256 devices in a mesh: span: 32 (over z, x), cross: 8 (over y, core).
Axes of the slice: x: 4, y: 4, z: 8, core: 2. Of those that a mesh axis runs over, the one named last changes fastest.
Arguments:
- velocity: float32 [3, 2048, 32, 128], P(None, 'span', 'cross'), may hold values from -6 to 6
- viscosity: float32 [2048, 32, 128], P('span', 'cross'), may hold values from 0.02 to 0.4
Outputs:
- advanced: float32 [3, 2048, 32, 128], P(None, 'span', 'cross')
The draws below stay inside these ranges and needn't reach their ends.
All inputs are finite; a program needn't handle non-finite values.
Results may differ from the reference program's by a relative error of at most 0.0001.
Values sent between devices are 32-bit elements; how exact they have to be, the bound alone decides.
No kernel may reach another device: no remote copies, remote signals or barrier semaphores. Data moves between devices by JAX's collectives and lax.ppermute only.
A program may use at most 64 MiB of HBM per device.

```python
import math
import jax
import jax.numpy as jnp

NX = 128
SWEEPS = 4
NZ = 2048
NY = 32


def steps_of(stream_key, shape, cuts, low, high):
    def one(axis_at, parts):
        steps = jax.random.uniform(jax.random.fold_in(jax.random.fold_in(stream_key, 6), axis_at), (parts,), jnp.float32, low / len(cuts), high / len(cuts))
        return jnp.repeat(jnp.exp(steps), shape[axis_at] // parts).reshape((-1,) + (1,) * (len(shape) - axis_at - 1))

    gain = one(*cuts[0])
    for cut in cuts[1:]:
        gain = gain * one(*cut)
    return gain


def gaussian(key, extent, scale, limit, shards=(), kind=jnp.bfloat16):
    array = jax.random.normal(key, extent, jnp.float32) * scale
    if len(shards) > 0:
        array = steps_of(key, extent, shards, -0.22, 0.18) * array
    return jnp.clip(array, min=-limit, max=limit).astype(kind)


def setup_inputs(seed: int = 0) -> dict:
    key_list = jax.random.split(jax.random.key(seed), 3)
    velocity = gaussian(key_list[0], (3, NZ, NY, NX), 1.0, 6.0, ((1, 32), (2, 8)), jnp.float32)
    viscosity = jnp.clip(jnp.exp(math.log(0.4) - 2.9957323 * jax.random.uniform(key_list[1], (NZ, NY, NX), jnp.float32) ** steps_of(key_list[1], (NZ, NY, NX), ((0, 32), (1, 8)), -0.2, 0.2)), 0.02, 0.4)
    return {"velocity": velocity, "viscosity": viscosity}


time_step = 0.1


def first_wave(number, length):
    angles = number * (2.0 * math.pi / length)
    return (14.0 / 9.0 * jnp.sin(angles) + 1.0 / 18.0 * jnp.sin(2.0 * angles)) / (1.0 + 2.0 / 3.0 * jnp.cos(angles))


def second_wave(number, length):
    angles = number * (2.0 * math.pi / length)
    return (24.0 / 11.0 * (1.0 - jnp.cos(angles)) + 3.0 / 22.0 * (1.0 - jnp.cos(2.0 * angles))) / (1.0 + 4.0 / 11.0 * jnp.cos(angles))


def stream_first(values):
    up_one = jnp.roll(values, -1, axis=-1)
    down_one = jnp.roll(values, 1, axis=-1)
    up_two = jnp.roll(values, -2, axis=-1)
    down_two = jnp.roll(values, 2, axis=-1)
    return (8.0 * (up_one - down_one) - (up_two - down_two)) / 12.0


def stream_curve(values):
    up_one = jnp.roll(values, -1, axis=-1)
    down_one = jnp.roll(values, 1, axis=-1)
    up_two = jnp.roll(values, -2, axis=-1)
    down_two = jnp.roll(values, 2, axis=-1)
    return (16.0 * (up_one + down_one) - (up_two + down_two) - 30.0 * values) / 12.0


def cross_pad(values):
    return jnp.pad(values, ((0, 0), (2, 2), (0, 0)))


def cross_slope(padded):
    return (8.0 * (padded[..., 3:-1, :] - padded[..., 1:-3, :]) - (padded[..., 4:, :] - padded[..., :-4, :])) / 12.0


def cross_curve(padded):
    return (16.0 * (padded[..., 3:-1, :] + padded[..., 1:-3, :]) - (padded[..., 4:, :] + padded[..., :-4, :]) - 30.0 * padded[..., 2:-2, :]) / 12.0


def span_pair(values):
    spectrum = jnp.fft.rfft(values, axis=0)
    number = jnp.arange(NZ // 2 + 1).astype(jnp.float32)[:, None, None]
    first_slope = jnp.fft.irfft(1j * first_wave(number, NZ) * spectrum, n=NZ, axis=0).astype(jnp.float32)
    second_slope = jnp.fft.irfft(-second_wave(number, NZ) * spectrum, n=NZ, axis=0).astype(jnp.float32)
    return first_slope, second_slope


def tendency(velocity, viscosity):
    results = []
    for component in range(3):
        values = velocity[component]
        padded = cross_pad(values)
        slope_z, curve_z = span_pair(values)
        carried = velocity[0] * stream_first(values) + velocity[1] * cross_slope(padded) + velocity[2] * slope_z
        results.append(viscosity * (stream_curve(values) + cross_curve(padded) + curve_z) - carried)
    return jnp.stack(results)


def project(section):
    joined = stream_first(section[0]) + cross_slope(cross_pad(section[1]))
    number = jnp.arange(NZ // 2 + 1).astype(jnp.float32)[:, None, None]
    source = jnp.fft.rfft(joined, axis=0) + 1j * first_wave(number, NZ) * jnp.fft.rfft(section[2], axis=0)
    diagonal = 4.0 + second_wave(number, NZ)
    potential = -source / diagonal
    for sweep_index in range(SWEEPS - 1):
        padded = jnp.pad(potential, ((0, 0), (1, 1), (0, 0)))
        beside_all = jnp.roll(potential, 1, axis=2) + jnp.roll(potential, -1, axis=2) + padded[:, 2:] + padded[:, :-2]
        potential = (beside_all - source) / diagonal
    scalar = jnp.fft.irfft(potential, n=NZ, axis=0).astype(jnp.float32)
    span_grad = jnp.fft.irfft(1j * first_wave(number, NZ) * potential, n=NZ, axis=0).astype(jnp.float32)
    return section - jnp.stack([stream_first(scalar), cross_slope(cross_pad(scalar)), span_grad])


def reference(velocity, viscosity):
    section_one = velocity + time_step * tendency(velocity, viscosity)
    first_pass = project(section_one)
    section_two = 0.5 * velocity + 0.5 * (first_pass + time_step * tendency(first_pass, viscosity))
    return project(section_two)
```

```python
import functools

import jax
import jax.numpy as jnp
import numpy as np
from jax import lax
from jax.experimental import pallas as pl
from jax.experimental.pallas import tpu as pltpu
from jax.sharding import PartitionSpec as P

SWEEPS = 4
ROWS = 4
LANES = 128
REACH = SWEEPS + 1
time_step = 0.1
highest = lax.Precision.HIGHEST
PAD_V = 16
PAD_S = 16
PAD_M = 8


def symbols(length):
    w = 2.0 * np.pi * np.arange(length) / length
    first = (14.0 / 9.0 * np.sin(w) + np.sin(2.0 * w) / 18.0) / (1.0 + 2.0 / 3.0 * np.cos(w))
    second = (24.0 / 11.0 * (1.0 - np.cos(w)) + 3.0 / 22.0 * (1.0 - np.cos(2.0 * w))) / (
        1.0 + 4.0 / 11.0 * np.cos(w)
    )
    return 1j * first, -second, 1.0 / (4.0 + second)


def block_of(symbol, cells, offset):
    kernel = np.fft.ifft(symbol).real
    at = np.arange(cells)
    return kernel[(at[:, None] - (at[None, :] + offset * cells)) % len(kernel)]


def low_rank(stack, rank):
    left, scale, right = np.linalg.svd(stack, full_matrices=False)
    return left[:, :rank] * scale[:rank], right[:rank]


@functools.lru_cache(None)
def tables(length, cells):
    first, second, inverse = symbols(length)
    at = lambda symbol, offset: block_of(symbol, cells, offset)
    slope_rank = 3
    from_left, take_left = low_rank(np.concatenate([at(first, -1), at(second, -1)]), slope_rank)
    from_right, take_right = low_rank(np.concatenate([at(first, 1), at(second, 1)]), slope_rank)
    own = np.concatenate([at(first, 0), at(second, 0)])
    slopes = np.zeros((3, 2 * cells, cells + 2 * PAD_V))
    moments = np.zeros((2 * PAD_V, 3 * cells))
    for c in range(3):
        rows = slice(slope_rank * c, slope_rank * (c + 1))
        slopes[c, :, :cells] = own
        slopes[c, :, cells:][:, rows] = from_left
        slopes[c, :, cells + PAD_V :][:, rows] = from_right
        moments[rows, cells * c : cells * (c + 1)] = take_left
        moments[PAD_V:][rows, cells * c : cells * (c + 1)] = take_right
    rank_m = 2
    m_left, t_left = low_rank(at(first, -1), rank_m)
    m_right, t_right = low_rank(at(first, 1), rank_m)
    lateral = np.zeros((cells + PAD_M, cells))
    lateral[:cells] = at(first, 0)
    lateral[cells : cells + rank_m] = t_left
    lateral[cells + rank_m : cells + 2 * rank_m] = t_right
    powers = [inverse ** (j + 1) for j in range(SWEEPS)]
    stacked = [p for p in powers] + [first * p for p in powers]
    rank_s = 2 * SWEEPS + 1
    s_left, q_left = low_rank(np.concatenate([at(p, -1) for p in stacked]), rank_s)
    s_right, q_right = low_rank(np.concatenate([at(p, 1) for p in stacked]), rank_s)
    source = np.zeros((2 * PAD_S, cells + PAD_M))
    source[:rank_s, :cells] = q_left
    source[rank_s : rank_s + rank_m, cells : cells + rank_m] = np.eye(rank_m)
    source[PAD_S : PAD_S + rank_s, :cells] = q_right
    source[PAD_S + rank_s : PAD_S + rank_s + rank_m, cells + rank_m : cells + 2 * rank_m] = np.eye(rank_m)
    depth = cells + 2 * PAD_S + PAD_M
    solve = np.zeros((2 * cells, SWEEPS * depth))
    for j in range(SWEEPS):
        for half in range(2):
            index = half * SWEEPS + j
            rows = slice(cells * index, cells * (index + 1))
            part = np.zeros((cells, depth))
            center = at(stacked[index], 0)
            part[:, :cells] = center
            low, high, mine = cells, cells + PAD_S, cells + 2 * PAD_S
            part[:, low : low + rank_s] = s_left[rows]
            part[:, low + rank_s : low + rank_s + rank_m] = center @ m_left
            part[:, high : high + rank_s] = s_right[rows]
            part[:, high + rank_s : high + rank_s + rank_m] = center @ m_right
            part[:, mine : mine + rank_m] = s_right[rows] @ (q_right @ m_left)
            part[:, mine + rank_m : mine + 2 * rank_m] = s_left[rows] @ (q_left @ m_right)
            solve[cells * half : cells * (half + 1), depth * j : depth * (j + 1)] = -part
    return tuple(x.astype(np.float32) for x in (slopes, moments, lateral, source, solve))


def dot(a, b):
    return jnp.dot(a, b, precision=highest, preferred_element_type=jnp.float32)


def lane(r, count=1):
    return slice(r * LANES, (r + count) * LANES)


def turned(tile, step):
    return pltpu.roll(tile, (-step) % LANES, 1)


def edge_masks():
    at = lax.axis_index("cross")
    last = lax.axis_size("cross") - 1
    flag = lambda test: jnp.where(test, 1.0, 0.0).astype(jnp.float32)
    return (flag(at >= 1), flag(at >= 2), flag(at <= last - 1), flag(at <= last - 2))


def masked(tile, e, masks):
    if e < -ROWS:
        return tile * masks[1]
    if e < 0:
        return tile * masks[0]
    if e >= 2 * ROWS:
        return tile * masks[3]
    if e >= ROWS:
        return tile * masks[2]
    return tile


def first_diff(up_one, down_one, up_two, down_two):
    return (8.0 * (up_one - down_one) - (up_two - down_two)) * (1.0 / 12.0)


def second_diff(middle, up_one, down_one, up_two, down_two):
    return (16.0 * (up_one + down_one) - (up_two + down_two) - 30.0 * middle) * (1.0 / 12.0)


def stream_slope(tile):
    return first_diff(turned(tile, 1), turned(tile, -1), turned(tile, 2), turned(tile, -2))


def open_kernel(cells, velocity, viscosity, moments, flat, thick, to_right, to_left, upward, downward):
    for r in range(ROWS):
        thick[:, lane(r)] = viscosity[:, r, :]
        for c in range(3):
            flat[cells * c : cells * (c + 1), lane(r)] = velocity[c, :, r, :]
    edges_kernel(flat, moments, to_right, to_left, upward, downward)


def edges_kernel(flat, moments, to_right, to_left, upward, downward):
    upward[...] = flat[:, lane(ROWS - 2, 2)]
    downward[...] = flat[:, lane(0, 2)]
    both = dot(moments[...], flat[...])
    to_right[...] = both[:PAD_V]
    to_left[...] = both[PAD_V:]


def tendency_kernel(cells, second, *refs):
    if second:
        base, *refs = refs
    flat, thick, left, right, low, high, slopes, lateral, section, near, up_far, down_far = refs
    masks = edge_masks()

    def tile(c, r):
        rows = slice(cells * c, cells * (c + 1))
        if r < 0:
            return masked(low[rows, lane(r + 2)], r, masks)
        if r >= ROWS:
            return masked(high[rows, lane(r - ROWS)], r, masks)
        return flat[rows, lane(r)]

    sides = jnp.concatenate([left[...], right[...]], axis=0)
    for c in range(3):
        rows = slice(cells * c, cells * (c + 1))
        spanned = dot(slopes[c], jnp.concatenate([flat[rows, :], sides], axis=0))
        for r in range(ROWS):
            here = tile(c, r)
            up_one, down_one = turned(here, 1), turned(here, -1)
            up_two, down_two = turned(here, 2), turned(here, -2)
            above_one, below_one = tile(c, r + 1), tile(c, r - 1)
            above_two, below_two = tile(c, r + 2), tile(c, r - 2)
            carried = (
                tile(0, r) * first_diff(up_one, down_one, up_two, down_two)
                + tile(1, r) * first_diff(above_one, below_one, above_two, below_two)
                + tile(2, r) * spanned[:cells, lane(r)]
            )
            spread = (
                second_diff(here, up_one, down_one, up_two, down_two)
                + second_diff(here, above_one, below_one, above_two, below_two)
                + spanned[cells:, lane(r)]
            )
            moved = here + time_step * (thick[:, lane(r)] * spread - carried)
            if second:
                moved = 0.5 * base[rows, lane(r)] + 0.5 * moved
            section[rows, lane(r)] = moved
            if c == 0:
                near[:cells, lane(r)] = stream_slope(moved)
            if c == 1:
                near[:cells, lane(ROWS + r)] = moved
    side = dot(lateral[...], section[2 * cells :, :])
    near[:cells, : ROWS * LANES] += side[:cells]
    near[cells:, : ROWS * LANES] = side[cells:]
    near[cells:, ROWS * LANES :] = jnp.zeros_like(near[cells:, ROWS * LANES :])
    up_far[:, lane(0)] = near[:, lane(ROWS - 1)]
    up_far[:, lane(1, 3)] = near[:, lane(ROWS + 1, 3)]
    down_far[:, lane(0)] = near[:, lane(0)]
    down_far[:, lane(1, 3)] = near[:, lane(ROWS, 3)]


def source_kernel(cells, near, low_one, high_one, low_two, high_two, source, ext, to_right, to_left):
    masks = edge_masks()

    def joined(e, rows):
        if e < -ROWS:
            return low_two[rows, lane(e + REACH)]
        if e < 0:
            return low_one[rows, lane(e + ROWS)]
        if e >= 2 * ROWS:
            return high_two[rows, lane(e - 2 * ROWS)]
        if e >= ROWS:
            return high_one[rows, lane(e - ROWS)]
        return near[rows, lane(e)]

    def across(e):
        rows = slice(0, cells)
        if e < -ROWS:
            return masked(low_two[rows, lane(e + 2 * ROWS)], e, masks)
        if e < 0:
            return masked(low_one[rows, lane(e + 2 * ROWS)], e, masks)
        if e >= 2 * ROWS:
            return masked(high_two[rows, lane(1 + e - 2 * ROWS)], e, masks)
        if e >= ROWS:
            return masked(high_one[rows, lane(e)], e, masks)
        return near[rows, lane(ROWS + e)]

    for e in range(-REACH, ROWS + REACH):
        total = joined(e, slice(0, cells)) + first_diff(
            across(e + 1), across(e - 1), across(e + 2), across(e - 2)
        )
        ext[:cells, lane(e + REACH)] = masked(total, e, masks)
        ext[cells:, lane(e + REACH)] = masked(joined(e, slice(cells, cells + PAD_M)), e, masks)
    both = dot(source[...], ext[...])
    to_right[...] = both[:PAD_S]
    to_left[...] = both[PAD_S:]


def solve_kernel(cells, last, ext, left, right, section, solve, *refs):
    if last:
        out, levels = refs
    else:
        moments, flat, to_right, to_left, upward, downward, levels = refs
    masks = edge_masks()
    depth = cells + 2 * PAD_S + PAD_M
    levels[:cells, :] = ext[:cells, :]
    levels[cells : cells + PAD_S, :] = left[...]
    levels[cells + PAD_S : cells + 2 * PAD_S, :] = right[...]
    levels[cells + 2 * PAD_S : depth, :] = ext[cells:, :]
    for j in range(1, SWEEPS):
        before = slice(depth * (j - 1), depth * j)
        after = slice(depth * j, depth * (j + 1))
        for e in range(-REACH + j, ROWS + REACH - j):
            here = levels[before, lane(e + REACH)]
            beside = (
                turned(here, 1)
                + turned(here, -1)
                + levels[before, lane(e + REACH + 1)]
                + levels[before, lane(e + REACH - 1)]
            )
            levels[after, lane(e + REACH)] = masked(beside, e, masks)
    found = dot(solve[...], levels[:, lane(REACH - 2, ROWS + 4)])
    phi = lambda r: masked(found[:cells, lane(r + 2)], r, masks)
    for r in range(ROWS):
        gradient = (
            stream_slope(phi(r)),
            first_diff(phi(r + 1), phi(r - 1), phi(r + 2), phi(r - 2)),
            found[cells:, lane(r + 2)],
        )
        for c in range(3):
            rows = slice(cells * c, cells * (c + 1))
            value = section[rows, lane(r)] - gradient[c]
            if last:
                out[c, :, r, :] = value
            else:
                flat[rows, lane(r)] = value
    if not last:
        edges_kernel(flat, moments, to_right, to_left, upward, downward)


def call(body, shapes, *args, scratch=()):
    return pl.pallas_call(
        body,
        out_shape=[jax.ShapeDtypeStruct(s, jnp.float32) for s in shapes],
        scratch_shapes=scratch,
        compiler_params=pltpu.CompilerParams(vmem_limit_bytes=40 * 1024 * 1024),
    )(*args)


def shifted(block, axis, step):
    count = lax.axis_size(axis)
    return lax.ppermute(block, axis, [(i, (i + step) % count) for i in range(count)])


def per_device(velocity, viscosity):
    components, cells, row_cells, columns = velocity.shape
    slopes, moments, lateral, source, solve = (
        jnp.asarray(t) for t in tables(cells * lax.axis_size("span"), cells)
    )
    width = row_cells * columns
    wide = (row_cells + 2 * REACH) * columns
    depth = cells + 2 * PAD_S + PAD_M
    edges = [(PAD_V, width), (PAD_V, width), (3 * cells, 2 * columns), (3 * cells, 2 * columns)]
    start, thick, to_right, to_left, upward, downward = call(
        functools.partial(open_kernel, cells),
        [(3 * cells, width), (cells, width)] + edges,
        velocity, viscosity, moments,
    )
    flat = start
    for second in (False, True):
        left = shifted(to_right, "span", 1)
        right = shifted(to_left, "span", -1)
        low = shifted(upward, "cross", 1)
        high = shifted(downward, "cross", -1)
        base = (start,) if second else ()
        section, near, up_far, down_far = call(
            functools.partial(tendency_kernel, cells, second),
            [(3 * cells, width), (cells + PAD_M, 2 * width), (cells + PAD_M, width), (cells + PAD_M, width)],
            *base, flat, thick, left, right, low, high, slopes, lateral,
        )
        low_one = shifted(near, "cross", 1)
        high_one = shifted(near, "cross", -1)
        low_two = shifted(up_far, "cross", 2)
        high_two = shifted(down_far, "cross", -2)
        ext, to_right, to_left = call(
            functools.partial(source_kernel, cells),
            [(cells + PAD_M, wide), (PAD_S, wide), (PAD_S, wide)],
            near, low_one, high_one, low_two, high_two, source,
        )
        left = shifted(to_right, "span", 1)
        right = shifted(to_left, "span", -1)
        scratch = [pltpu.VMEM((SWEEPS * depth, wide), jnp.float32)]
        if second:
            (out,) = call(
                functools.partial(solve_kernel, cells, True),
                [velocity.shape],
                ext, left, right, section, solve,
                scratch=scratch,
            )
        else:
            flat, to_right, to_left, upward, downward = call(
                functools.partial(solve_kernel, cells, False),
                [(3 * cells, width)] + edges,
                ext, left, right, section, solve, moments,
                scratch=scratch,
            )
    return out


def solution(mesh):
    in_specs = (P(None, "span", "cross", None), P("span", "cross", None))
    out_specs = P(None, "span", "cross", None)
    return jax.shard_map(
        per_device, mesh=mesh, in_specs=in_specs, out_specs=out_specs, check_vma=False
    )
```

```python
import functools

import jax
import jax.numpy as jnp
import numpy as np
from jax import lax
from jax.experimental import pallas as pl
from jax.experimental.pallas import tpu as pltpu
from jax.sharding import PartitionSpec as P

SWEEPS = 4
ROWS = 4
LANES = 128
REACH = SWEEPS + 1
time_step = 0.1
highest = lax.Precision.HIGHEST
PAD_V = 16
PAD_S = 16
PAD_M = 8
GROUP = 8
RANK_V = 3
RANK_M = 2
RANK_S = 2 * SWEEPS + 3


def symbols(length):
    w = 2.0 * np.pi * np.arange(length) / length
    first = (14.0 / 9.0 * np.sin(w) + np.sin(2.0 * w) / 18.0) / (1.0 + 2.0 / 3.0 * np.cos(w))
    second = (24.0 / 11.0 * (1.0 - np.cos(w)) + 3.0 / 22.0 * (1.0 - np.cos(2.0 * w))) / (
        1.0 + 4.0 / 11.0 * np.cos(w)
    )
    return 1j * first, -second, 1.0 / (4.0 + second)


def block_of(symbol, cells, offset):
    kernel = np.fft.ifft(symbol).real
    at = np.arange(cells)
    return kernel[(at[:, None] - (at[None, :] + offset * cells)) % len(kernel)]


def low_rank(stack, rank):
    left, scale, right = np.linalg.svd(stack, full_matrices=False)
    return left[:, :rank] * scale[:rank], right[:rank]


@functools.lru_cache(None)
def tables(length, cells):
    first, second, inverse = symbols(length)
    at = lambda symbol, offset: block_of(symbol, cells, offset)
    from_left, take_left = low_rank(np.concatenate([at(first, -1), at(second, -1)]), RANK_V)
    from_right, take_right = low_rank(np.concatenate([at(first, 1), at(second, 1)]), RANK_V)
    own = np.concatenate([at(first, 0), at(second, 0)])
    slopes = np.zeros((3, 2 * cells, cells + 2 * PAD_V))
    moments = np.zeros((2 * PAD_V, 3 * cells))
    for c in range(3):
        rows = slice(RANK_V * c, RANK_V * (c + 1))
        slopes[c, :, :cells] = own
        slopes[c, :, cells:][:, rows] = from_left
        slopes[c, :, cells + PAD_V :][:, rows] = from_right
        moments[rows, cells * c : cells * (c + 1)] = take_left
        moments[PAD_V:][rows, cells * c : cells * (c + 1)] = take_right
    m_left, t_left = low_rank(at(first, -1), RANK_M)
    m_right, t_right = low_rank(at(first, 1), RANK_M)
    lateral = np.zeros((cells + PAD_M, cells))
    lateral[:cells] = at(first, 0)
    lateral[cells : cells + RANK_M] = t_left
    lateral[cells + RANK_M : cells + 2 * RANK_M] = t_right
    powers = [inverse ** (j + 1) for j in range(SWEEPS)]
    stacked = [p for p in powers] + [first * p for p in powers]
    count = len(stacked)
    s_left, q_left = low_rank(
        np.concatenate([at(p, -1) for p in stacked] + [take_left @ at(p, 0) for p in stacked]), RANK_S
    )
    s_right, q_right = low_rank(
        np.concatenate([at(p, 1) for p in stacked] + [take_right @ at(p, 0) for p in stacked]), RANK_S
    )
    e_left, e_right = s_left[count * cells :], s_right[count * cells :]
    source = np.zeros((2 * PAD_S, cells + PAD_M))
    source[:RANK_S, :cells] = q_left
    source[RANK_S : RANK_S + RANK_M, cells : cells + RANK_M] = np.eye(RANK_M)
    source[PAD_S : PAD_S + RANK_S, :cells] = q_right
    source[PAD_S + RANK_S : PAD_S + RANK_S + RANK_M, cells + RANK_M : cells + 2 * RANK_M] = np.eye(RANK_M)
    near, wide = cells + PAD_M, 2 * PAD_S
    height = 2 * cells + 4 * GROUP
    solve_own = np.zeros((height, SWEEPS * near))
    solve_sides = np.zeros((height, SWEEPS * wide))
    for j in range(SWEEPS):
        for half in range(2):
            index = half * SWEEPS + j
            rows = slice(cells * index, cells * (index + 1))
            edge = slice(RANK_V * index, RANK_V * (index + 1))
            center = at(stacked[index], 0)
            by_left, by_right = s_left[rows], s_right[rows]
            mine, sides = np.zeros((cells, near)), np.zeros((cells, wide))
            mine[:, :cells] = center
            mine[:, cells : cells + RANK_M] = by_right @ (q_right @ m_left)
            mine[:, cells + RANK_M : cells + 2 * RANK_M] = by_left @ (q_left @ m_right)
            sides[:, :RANK_S] = by_left
            sides[:, RANK_S : RANK_S + RANK_M] = center @ m_left
            sides[:, PAD_S : PAD_S + RANK_S] = by_right
            sides[:, PAD_S + RANK_S : PAD_S + RANK_S + RANK_M] = center @ m_right
            solve_own[cells * half : cells * (half + 1), near * j : near * (j + 1)] = -mine
            solve_sides[cells * half : cells * (half + 1), wide * j : wide * (j + 1)] = -sides
            for side in range(2):
                mine, sides = np.zeros((RANK_V, near)), np.zeros((RANK_V, wide))
                if side == 0:
                    back = take_left @ by_right @ q_right
                    mine[:, cells + RANK_M : cells + 2 * RANK_M] = take_left @ center @ m_right
                    sides[:, :RANK_S] = e_left[edge]
                else:
                    back = take_right @ by_left @ q_left
                    mine[:, cells : cells + RANK_M] = take_right @ center @ m_left
                    sides[:, PAD_S : PAD_S + RANK_S] = e_right[edge]
                mine[:, :cells] = back
                sides[:, RANK_S : RANK_S + RANK_M] = back @ m_left
                sides[:, PAD_S + RANK_S : PAD_S + RANK_S + RANK_M] = back @ m_right
                top = 2 * cells + GROUP * (2 * side + half)
                solve_own[top : top + RANK_V, near * j : near * (j + 1)] = -mine
                solve_sides[top : top + RANK_V, wide * j : wide * (j + 1)] = -sides
    return tuple(
        x.astype(np.float32) for x in (slopes, moments, lateral, source, solve_own, solve_sides)
    )


def dot(a, b):
    return jnp.dot(a, b, precision=highest, preferred_element_type=jnp.float32)


DIFFERENCE = ((1, 2.0 / 3.0), (-1, -2.0 / 3.0), (2, -1.0 / 12.0), (-2, 1.0 / 12.0))


def lane(r, count=1):
    return slice(r * LANES, (r + count) * LANES)


def turned(tile, step):
    return pltpu.roll(tile, (-step) % LANES, 1)


def edge_masks():
    at = lax.axis_index("cross")
    last = lax.axis_size("cross") - 1
    flag = lambda test: jnp.where(test, 1.0, 0.0).astype(jnp.float32)
    return (flag(at >= 1), flag(at >= 2), flag(at <= last - 1), flag(at <= last - 2))


def masked(tile, e, masks):
    if e < -ROWS:
        return tile * masks[1]
    if e < 0:
        return tile * masks[0]
    if e >= 2 * ROWS:
        return tile * masks[3]
    if e >= ROWS:
        return tile * masks[2]
    return tile


def first_diff(up_one, down_one, up_two, down_two):
    return (8.0 * (up_one - down_one) - (up_two - down_two)) * (1.0 / 12.0)


def second_diff(middle, up_one, down_one, up_two, down_two):
    return (16.0 * (up_one + down_one) - (up_two + down_two) - 30.0 * middle) * (1.0 / 12.0)


def stream_slope(tile):
    return first_diff(turned(tile, 1), turned(tile, -1), turned(tile, 2), turned(tile, -2))


def open_kernel(cells, velocity, moments, flat, to_right, to_left, upward, downward, landed, weights, sems):
    copies = (
        pltpu.make_async_copy(velocity, landed, sems.at[0]),
        pltpu.make_async_copy(moments, weights, sems.at[1]),
    )
    for copy in copies:
        copy.start()
    for copy in copies:
        copy.wait()
    for r in range(ROWS):
        for c in range(3):
            flat[cells * c : cells * (c + 1), lane(r)] = landed[c, :, r, :]
    upward[...] = flat[:, lane(ROWS - 2, 2)]
    downward[...] = flat[:, lane(0, 2)]
    both = dot(weights[...], flat[...])
    to_right[...] = both[:PAD_V]
    to_left[...] = both[PAD_V:]


def tendency_kernel(cells, second, *refs):
    if second:
        base, *refs = refs
    flat, thick, left, right, low, high, slopes, lateral, section, parts, up_near, down_near, up_far, down_far = refs
    masks = edge_masks()

    def tile(c, r):
        rows = slice(cells * c, cells * (c + 1))
        if r < 0:
            return masked(low[rows, lane(r + 2)], r, masks)
        if r >= ROWS:
            return masked(high[rows, lane(r - ROWS)], r, masks)
        return flat[rows, lane(r)]

    sides = jnp.concatenate([left[...], right[...]], axis=0)
    for c in range(3):
        rows = slice(cells * c, cells * (c + 1))
        spanned = dot(slopes[c], jnp.concatenate([flat[rows, :], sides], axis=0))
        for r in range(ROWS):
            here = tile(c, r)
            up_one, down_one = turned(here, 1), turned(here, -1)
            up_two, down_two = turned(here, 2), turned(here, -2)
            above_one, below_one = tile(c, r + 1), tile(c, r - 1)
            above_two, below_two = tile(c, r + 2), tile(c, r - 2)
            carried = (
                tile(0, r) * first_diff(up_one, down_one, up_two, down_two)
                + tile(1, r) * first_diff(above_one, below_one, above_two, below_two)
                + tile(2, r) * spanned[:cells, lane(r)]
            )
            spread = (
                second_diff(here, up_one, down_one, up_two, down_two)
                + second_diff(here, above_one, below_one, above_two, below_two)
                + spanned[cells:, lane(r)]
            )
            moved = here + time_step * (thick[:, r, :] * spread - carried)
            if second:
                moved = 0.5 * base[rows, lane(r)] + 0.5 * moved
            section[rows, lane(r)] = moved
    side = dot(lateral[...], section[2 * cells :, :])
    span = slice(0, cells)
    at = lambda r: section[cells : 2 * cells, lane(r)]
    for r in range(ROWS):
        total = stream_slope(section[:cells, lane(r)]) + side[:cells, lane(r)]
        for reach, factor in DIFFERENCE:
            if 0 <= r + reach < ROWS:
                total = total + factor * at(r + reach)
        parts[span, lane(r)] = total
        up_near[span, lane(r)] = total
        down_near[span, lane(r)] = total
    tail = slice(cells, cells + PAD_M)
    parts[tail, :] = side[cells:]
    for near in (up_near, down_near):
        near[tail, lane(0, ROWS)] = side[cells:]
        near[tail, lane(ROWS, 3)] = jnp.zeros((PAD_M, 3 * LANES), jnp.float32)
    for far, r in ((up_far, ROWS - 1), (down_far, 0)):
        far[:, lane(0)] = parts[:, lane(r)]
        far[tail, lane(1, 2)] = jnp.zeros((PAD_M, 2 * LANES), jnp.float32)
    for k in range(2):
        up_near[span, lane(ROWS + k)] = at(ROWS - 2 + k)
        up_far[span, lane(1 + k)] = at(ROWS - 2 + k)
        down_near[span, lane(ROWS + k)] = at(k)
        down_far[span, lane(1 + k)] = at(k)
    up_near[span, lane(ROWS + 2)] = (2.0 / 3.0) * at(0) - (1.0 / 12.0) * at(1)
    down_near[span, lane(ROWS + 2)] = (1.0 / 12.0) * at(ROWS - 2) - (2.0 / 3.0) * at(ROWS - 1)


def source_kernel(cells, keep, parts, section, low_one, high_one, low_two, high_two, source, *refs):
    if keep:
        moments, ext, to_right, to_left = refs
    else:
        ext, to_right, to_left = refs
    masks = edge_masks()
    span, tail = slice(0, cells), slice(cells, cells + PAD_M)

    def joined(e):
        if e < -ROWS:
            return low_two[:, lane(e + REACH)]
        if e < 0:
            return low_one[:, lane(e + ROWS)]
        if e >= 2 * ROWS:
            return high_two[:, lane(e - 2 * ROWS)]
        if e >= ROWS:
            return high_one[:, lane(e - ROWS)]
        return parts[:, lane(e)]

    def across(e, home):
        owner = lambda x: x // ROWS
        if owner(e) == owner(home):
            return None
        if owner(home) == -2 or owner(home) == 2:
            return None
        if -ROWS - 2 <= e < -ROWS:
            return masked(low_two[span, lane(1 + e + ROWS + 2)], e, masks)
        if -2 <= e < 0:
            return masked(low_one[span, lane(ROWS + e + 2)], e, masks)
        if 0 <= e < ROWS:
            return section[cells : 2 * cells, lane(e)]
        if ROWS <= e < ROWS + 2:
            return masked(high_one[span, lane(e)], e, masks)
        return masked(high_two[span, lane(1 + e - 2 * ROWS)], e, masks)

    for e in range(-REACH, ROWS + REACH):
        both = joined(e)
        total = both[:cells]
        if e == -REACH:
            total = total + low_one[span, lane(ROWS + 2)]
        if e == ROWS + REACH - 1:
            total = total + high_one[span, lane(ROWS + 2)]
        for reach, factor in DIFFERENCE:
            other = across(e + reach, e)
            if other is not None:
                total = total + factor * other
        ext[span, lane(e + REACH)] = masked(total, e, masks)
        ext[tail, lane(e + REACH)] = masked(both[cells:], e, masks)
    wide = ext.shape[1]
    both = dot(source[...], ext[...])
    to_right[:, :wide] = both[:PAD_S]
    to_left[:, :wide] = both[PAD_S:]
    if keep:
        both = dot(moments[...], section[...])
        to_right[:, wide:] = both[:PAD_V]
        to_left[:, wide:] = both[PAD_V:]


def climb(levels, depth, masks):
    for j in range(1, SWEEPS):
        before = slice(depth * (j - 1), depth * j)
        after = slice(depth * j, depth * (j + 1))
        for e in range(-REACH + j, ROWS + REACH - j):
            here = levels[before, lane(e + REACH)]
            beside = (
                turned(here, 1)
                + turned(here, -1)
                + levels[before, lane(e + REACH + 1)]
                + levels[before, lane(e + REACH - 1)]
            )
            levels[after, lane(e + REACH)] = masked(beside, e, masks)
    return levels[:, lane(REACH - 2, ROWS + 4)]


def home_kernel(ext, solve, partial, levels):
    depth = ext.shape[0]
    levels[:depth, :] = ext[...]
    partial[...] = dot(solve[...], climb(levels, depth, edge_masks()))


def solve_kernel(cells, last, partial, left, right, section, solve, *refs):
    if last:
        out, levels = refs
    else:
        flat, next_left, next_right, upward, downward, levels = refs
    masks = edge_masks()
    wide = levels.shape[1]
    levels[:PAD_S, :] = left[:, :wide]
    levels[PAD_S : 2 * PAD_S, :] = right[:, :wide]
    found = partial[...] + dot(solve[...], climb(levels, 2 * PAD_S, masks))

    def gradient(rows, slope_rows, r):
        phi = lambda r: masked(found[rows, lane(r + 2)], r, masks)
        return (
            stream_slope(phi(r)),
            first_diff(phi(r + 1), phi(r - 1), phi(r + 2), phi(r - 2)),
            found[slope_rows, lane(r + 2)],
        )

    for r in range(ROWS):
        slopes = gradient(slice(0, cells), slice(cells, 2 * cells), r)
        for c in range(3):
            rows = slice(cells * c, cells * (c + 1))
            value = section[rows, lane(r)] - slopes[c]
            if last:
                out[c, :, r, :] = value
            else:
                flat[rows, lane(r)] = value
                if r < 2:
                    downward[rows, lane(r)] = value
                if r >= ROWS - 2:
                    upward[rows, lane(r - ROWS + 2)] = value
    if not last:
        for side, (given, target) in enumerate(((left, next_left), (right, next_right))):
            top = 2 * cells + 2 * GROUP * side
            target[...] = given[:, wide:]
            for r in range(ROWS):
                slopes = gradient(slice(top, top + GROUP), slice(top + GROUP, top + 2 * GROUP), r)
                for c in range(3):
                    rows = slice(RANK_V * c, RANK_V * (c + 1))
                    target[rows, lane(r)] = given[rows, wide + r * LANES : wide + (r + 1) * LANES] - slopes[c][:RANK_V]


def call(body, shapes, *args, scratch=(), **options):
    return pl.pallas_call(
        body,
        out_shape=[jax.ShapeDtypeStruct(s, jnp.float32) for s in shapes],
        scratch_shapes=scratch,
        compiler_params=pltpu.CompilerParams(vmem_limit_bytes=40 * 1024 * 1024),
        **options,
    )(*args)


def shifted(block, axis, step):
    count = lax.axis_size(axis)
    return lax.ppermute(block, axis, [(i, (i + step) % count) for i in range(count)])


def per_device(velocity, viscosity):
    components, cells, row_cells, columns = velocity.shape
    slopes, moments, lateral, source, solve_own, solve_sides = (
        jnp.asarray(t) for t in tables(cells * lax.axis_size("span"), cells)
    )
    width = row_cells * columns
    wide = (row_cells + 2 * REACH) * columns
    near = cells + PAD_M
    edge, rim = (PAD_V, width), (components * cells, 2 * columns)
    start, to_right, to_left, upward, downward = call(
        functools.partial(open_kernel, cells),
        [(components * cells, width), edge, edge, rim, rim],
        velocity, moments,
        in_specs=[pl.BlockSpec(memory_space=pltpu.HBM)] * 2,
        scratch=[
            pltpu.VMEM(velocity.shape, jnp.float32),
            pltpu.VMEM(moments.shape, jnp.float32),
            pltpu.SemaphoreType.DMA((2,)),
        ],
    )
    left = shifted(to_right, "span", 1)
    right = shifted(to_left, "span", -1)
    flat = start
    for second in (False, True):
        low = shifted(upward, "cross", 1)
        high = shifted(downward, "cross", -1)
        base = (start,) if second else ()
        section, parts, up_near, down_near, up_far, down_far = call(
            functools.partial(tendency_kernel, cells, second),
            [(components * cells, width), (near, width)] + [(near, 7 * columns)] * 2 + [(near, 3 * columns)] * 2,
            *base, flat, viscosity, left, right, low, high, slopes, lateral,
        )
        low_one = shifted(up_near, "cross", 1)
        high_one = shifted(down_near, "cross", -1)
        low_two = shifted(up_far, "cross", 2)
        high_two = shifted(down_far, "cross", -2)
        sent = (PAD_S, wide if second else wide + width)
        extra = () if second else (moments,)
        ext, to_right, to_left = call(
            functools.partial(source_kernel, cells, not second),
            [(near, wide), sent, sent],
            parts, section, low_one, high_one, low_two, high_two, source, *extra,
        )
        left = shifted(to_right, "span", 1)
        right = shifted(to_left, "span", -1)
        height = 2 * cells if second else solve_own.shape[0]
        (partial,) = call(
            home_kernel,
            [(height, (row_cells + 4) * columns)],
            ext, solve_own[:height],
            scratch=[pltpu.VMEM((SWEEPS * near, wide), jnp.float32)],
        )
        scratch = [pltpu.VMEM((SWEEPS * 2 * PAD_S, wide), jnp.float32)]
        given = (partial, left, right, section, solve_sides[:height])
        body = functools.partial(solve_kernel, cells, second)
        if second:
            (out,) = call(body, [velocity.shape], *given, scratch=scratch)
        else:
            flat, left, right, upward, downward = call(
                body, [(components * cells, width), edge, edge, rim, rim], *given, scratch=scratch
            )
    return out


def solution(mesh):
    in_specs = (P(None, "span", "cross", None), P("span", "cross", None))
    out_specs = P(None, "span", "cross", None)
    return jax.shard_map(
        per_device, mesh=mesh, in_specs=in_specs, out_specs=out_specs, check_vma=False
    )
```

```python
import functools

import jax
import jax.numpy as jnp
import numpy as np
from jax import lax
from jax.experimental import pallas as pl
from jax.experimental.pallas import tpu as pltpu
from jax.sharding import PartitionSpec as P

SWEEPS = 4
ROWS = 4
LANES = 128
REACH = SWEEPS + 1
time_step = 0.1
highest = lax.Precision.HIGHEST
PAD_V = 16
PAD_S = 16
PAD_M = 8
GROUP = 8
RANK_V = 3
RANK_M = 2


def symbols(length):
    w = 2.0 * np.pi * np.arange(length) / length
    first = (14.0 / 9.0 * np.sin(w) + np.sin(2.0 * w) / 18.0) / (1.0 + 2.0 / 3.0 * np.cos(w))
    second = (24.0 / 11.0 * (1.0 - np.cos(w)) + 3.0 / 22.0 * (1.0 - np.cos(2.0 * w))) / (
        1.0 + 4.0 / 11.0 * np.cos(w)
    )
    return 1j * first, -second, 1.0 / (4.0 + second)


def block_of(symbol, cells, offset):
    kernel = np.fft.ifft(symbol).real
    at = np.arange(cells)
    return kernel[(at[:, None] - (at[None, :] + offset * cells)) % len(kernel)]


def low_rank(stack, rank):
    left, scale, right = np.linalg.svd(stack, full_matrices=False)
    return left[:, :rank] * scale[:rank], right[:rank]


@functools.lru_cache(None)
def tables(length, cells, last):
    first, second, inverse = symbols(length)
    at = lambda symbol, offset: block_of(symbol, cells, offset)
    from_left, take_left = low_rank(np.concatenate([at(first, -1), at(second, -1)]), RANK_V)
    from_right, take_right = low_rank(np.concatenate([at(first, 1), at(second, 1)]), RANK_V)
    own = np.concatenate([at(first, 0), at(second, 0)])
    slopes = np.zeros((3, 2 * cells, cells + 2 * PAD_V))
    moments = np.zeros((2 * PAD_V, 3 * cells))
    for c in range(3):
        rows = slice(RANK_V * c, RANK_V * (c + 1))
        slopes[c, :, :cells] = own
        slopes[c, :, cells:][:, rows] = from_left
        slopes[c, :, cells + PAD_V :][:, rows] = from_right
        moments[rows, cells * c : cells * (c + 1)] = take_left
        moments[PAD_V:][rows, cells * c : cells * (c + 1)] = take_right
    m_left, t_left = low_rank(at(first, -1), RANK_M)
    m_right, t_right = low_rank(at(first, 1), RANK_M)
    lateral = np.zeros((cells + PAD_M, cells))
    lateral[:cells] = at(first, 0)
    lateral[cells : cells + RANK_M] = t_left
    lateral[cells + RANK_M : cells + 2 * RANK_M] = t_right
    powers = [inverse ** (j + 1) for j in range(SWEEPS)]
    stacked = [p for p in powers] + [first * p for p in powers]
    count = len(stacked)
    RANK_S = 2 * SWEEPS + (1 if last else 3)
    kept = [] if last else stacked
    s_left, q_left = low_rank(
        np.concatenate([at(p, -1) for p in stacked] + [take_left @ at(p, 0) for p in kept]), RANK_S
    )
    s_right, q_right = low_rank(
        np.concatenate([at(p, 1) for p in stacked] + [take_right @ at(p, 0) for p in kept]), RANK_S
    )
    e_left, e_right = s_left[count * cells :], s_right[count * cells :]
    source = np.zeros((8 * GROUP, cells + PAD_M))
    for side, q in enumerate((q_left, q_right)):
        rows = np.zeros((PAD_S, cells + PAD_M))
        rows[:RANK_S, :cells] = q
        at_m = cells + RANK_M * side
        rows[RANK_S : RANK_S + RANK_M, at_m : at_m + RANK_M] = np.eye(RANK_M)
        top = 4 * GROUP * side
        source[top : top + 8] = rows[:8]
        source[top + 8 : top + 12] = rows[8:12]
        source[top + 20 : top + 24] = rows[8:12]
        source[top + 24] = rows[12]
    near, wide = cells + PAD_M, 2 * PAD_S
    height = 2 * cells + (0 if last else 4 * GROUP)
    solve_own = np.zeros((height, SWEEPS * near))
    solve_sides = np.zeros((height, SWEEPS * wide))
    for j in range(SWEEPS):
        for half in range(2):
            index = half * SWEEPS + j
            rows = slice(cells * index, cells * (index + 1))
            edge = slice(RANK_V * index, RANK_V * (index + 1))
            center = at(stacked[index], 0)
            by_left, by_right = s_left[rows], s_right[rows]
            mine, sides = np.zeros((cells, near)), np.zeros((cells, wide))
            mine[:, :cells] = center
            mine[:, cells : cells + RANK_M] = by_right @ (q_right @ m_left)
            mine[:, cells + RANK_M : cells + 2 * RANK_M] = by_left @ (q_left @ m_right)
            sides[:, :RANK_S] = by_left
            sides[:, RANK_S : RANK_S + RANK_M] = center @ m_left
            sides[:, PAD_S : PAD_S + RANK_S] = by_right
            sides[:, PAD_S + RANK_S : PAD_S + RANK_S + RANK_M] = center @ m_right
            solve_own[cells * half : cells * (half + 1), near * j : near * (j + 1)] = -mine
            solve_sides[cells * half : cells * (half + 1), wide * j : wide * (j + 1)] = -sides
            for side in range(0 if last else 2):
                mine, sides = np.zeros((RANK_V, near)), np.zeros((RANK_V, wide))
                if side == 0:
                    back = take_left @ by_right @ q_right
                    mine[:, cells + RANK_M : cells + 2 * RANK_M] = take_left @ center @ m_right
                    sides[:, :RANK_S] = e_left[edge]
                else:
                    back = take_right @ by_left @ q_left
                    mine[:, cells : cells + RANK_M] = take_right @ center @ m_left
                    sides[:, PAD_S : PAD_S + RANK_S] = e_right[edge]
                mine[:, :cells] = back
                sides[:, RANK_S : RANK_S + RANK_M] = back @ m_left
                sides[:, PAD_S + RANK_S : PAD_S + RANK_S + RANK_M] = back @ m_right
                top = 2 * cells + GROUP * (2 * side + half)
                solve_own[top : top + RANK_V, near * j : near * (j + 1)] = -mine
                solve_sides[top : top + RANK_V, wide * j : wide * (j + 1)] = -sides
    return tuple(
        x.astype(np.float32) for x in (slopes, moments, lateral, source, solve_own, solve_sides)
    )


def dot(a, b):
    return jnp.dot(a, b, precision=highest, preferred_element_type=jnp.float32)


BREADTH = ROWS + 2 * REACH
PACKED = BREADTH + BREADTH // 2

DIFFERENCE = ((1, 2.0 / 3.0), (-1, -2.0 / 3.0), (2, -1.0 / 12.0), (-2, 1.0 / 12.0))


def lane(r, count=1):
    return slice(r * LANES, (r + count) * LANES)


def turned(tile, step):
    return pltpu.roll(tile, (-step) % LANES, 1)


def edge_masks():
    at = lax.axis_index("cross")
    last = lax.axis_size("cross") - 1
    flag = lambda test: jnp.where(test, 1.0, 0.0).astype(jnp.float32)
    return (flag(at >= 1), flag(at >= 2), flag(at <= last - 1), flag(at <= last - 2))


def masked(tile, e, masks):
    if e < -ROWS:
        return tile * masks[1]
    if e < 0:
        return tile * masks[0]
    if e >= 2 * ROWS:
        return tile * masks[3]
    if e >= ROWS:
        return tile * masks[2]
    return tile


def first_diff(up_one, down_one, up_two, down_two):
    return (8.0 * (up_one - down_one) - (up_two - down_two)) * (1.0 / 12.0)


def second_diff(middle, up_one, down_one, up_two, down_two):
    return (16.0 * (up_one + down_one) - (up_two + down_two) - 30.0 * middle) * (1.0 / 12.0)


def stream_slope(tile):
    return first_diff(turned(tile, 1), turned(tile, -1), turned(tile, 2), turned(tile, -2))


def open_kernel(cells, velocity, moments, flat, to_right, to_left, upward, downward, landed, weights, sems):
    copies = [pltpu.make_async_copy(velocity.at[c], landed.at[c], sems.at[c]) for c in range(3)]
    copies.append(pltpu.make_async_copy(moments, weights, sems.at[3]))
    for copy in copies:
        copy.start()
    for c in range(3):
        copies[c].wait()
        rows = slice(cells * c, cells * (c + 1))
        for r in range(ROWS):
            flat[rows, lane(r)] = landed[c, :, r, :]
        upward[rows, :] = flat[rows, lane(ROWS - 2, 2)]
        downward[rows, :] = flat[rows, lane(0, 2)]
    copies[3].wait()
    both = dot(weights[...], flat[...])
    to_right[...] = both[:PAD_V]
    to_left[...] = both[PAD_V:]


def tendency_kernel(cells, second, *refs):
    if second:
        base, *refs = refs
    flat, thick, left, right, low, high, slopes, lateral, section, parts, up_near, down_near, up_far, down_far = refs
    masks = edge_masks()

    def tile(c, r):
        rows = slice(cells * c, cells * (c + 1))
        if r < 0:
            return masked(low[rows, lane(r + 2)], r, masks)
        if r >= ROWS:
            return masked(high[rows, lane(r - ROWS)], r, masks)
        return flat[rows, lane(r)]

    sides = jnp.concatenate([left[...], right[...]], axis=0)
    for c in range(3):
        rows = slice(cells * c, cells * (c + 1))
        spanned = dot(slopes[c], jnp.concatenate([flat[rows, :], sides], axis=0))
        for r in range(ROWS):
            here = tile(c, r)
            up_one, down_one = turned(here, 1), turned(here, -1)
            up_two, down_two = turned(here, 2), turned(here, -2)
            above_one, below_one = tile(c, r + 1), tile(c, r - 1)
            above_two, below_two = tile(c, r + 2), tile(c, r - 2)
            carried = (
                tile(0, r) * first_diff(up_one, down_one, up_two, down_two)
                + tile(1, r) * first_diff(above_one, below_one, above_two, below_two)
                + tile(2, r) * spanned[:cells, lane(r)]
            )
            spread = (
                second_diff(here, up_one, down_one, up_two, down_two)
                + second_diff(here, above_one, below_one, above_two, below_two)
                + spanned[cells:, lane(r)]
            )
            moved = here + time_step * (thick[:, r, :] * spread - carried)
            if second:
                moved = 0.5 * base[rows, lane(r)] + 0.5 * moved
            section[rows, lane(r)] = moved
    side = dot(lateral[...], section[2 * cells :, :])
    span = slice(0, cells)
    at = lambda r: section[cells : 2 * cells, lane(r)]
    for r in range(ROWS):
        total = stream_slope(section[:cells, lane(r)]) + side[:cells, lane(r)]
        for reach, factor in DIFFERENCE:
            if 0 <= r + reach < ROWS:
                total = total + factor * at(r + reach)
        parts[span, lane(r)] = total
        for block in (up_near, down_near):
            block[cells * r : cells * (r + 1), :] = total
            block[7 * cells + PAD_M * r : 7 * cells + PAD_M * (r + 1), :] = side[cells:, lane(r)]
    tail = slice(cells, cells + PAD_M)
    parts[tail, :] = side[cells:]
    for far, r in ((up_far, ROWS - 1), (down_far, 0)):
        far[:cells, :] = parts[span, lane(r)]
        far[3 * cells :, :] = parts[tail, lane(r)]
    for k in range(2):
        near_rows = slice(cells * (ROWS + k), cells * (ROWS + k + 1))
        far_rows = slice(cells * (1 + k), cells * (2 + k))
        up_near[near_rows, :] = at(ROWS - 2 + k)
        up_far[far_rows, :] = at(ROWS - 2 + k)
        down_near[near_rows, :] = at(k)
        down_far[far_rows, :] = at(k)
    rest = slice(6 * cells, 7 * cells)
    up_near[rest, :] = (2.0 / 3.0) * at(0) - (1.0 / 12.0) * at(1)
    down_near[rest, :] = (1.0 / 12.0) * at(ROWS - 2) - (2.0 / 3.0) * at(ROWS - 1)


def source_kernel(cells, keep, parts, section, low_one, high_one, low_two, high_two, source, *refs):
    if keep:
        moments, ext, to_right, to_left = refs
    else:
        ext, to_right, to_left = refs
    masks = edge_masks()
    span, tail = slice(0, cells), slice(cells, cells + PAD_M)
    pick = lambda ref, k: ref[cells * k : cells * (k + 1), :]

    def joined(e):
        if e < -ROWS:
            return low_two[:cells, :], low_two[3 * cells :, :]
        if e >= 2 * ROWS:
            return high_two[:cells, :], high_two[3 * cells :, :]
        if 0 <= e < ROWS:
            return parts[span, lane(e)], parts[tail, lane(e)]
        near, r = (low_one, e + ROWS) if e < 0 else (high_one, e - ROWS)
        top = 7 * cells + PAD_M * r
        return pick(near, r), near[top : top + PAD_M, :]

    def across(e, home):
        if e // ROWS == home // ROWS or home // ROWS in (-2, 2):
            return None
        if e < -ROWS:
            return masked(pick(low_two, 1 + e + ROWS + 2), e, masks)
        if e < 0:
            return masked(pick(low_one, ROWS + e + 2), e, masks)
        if e < ROWS:
            return section[cells : 2 * cells, lane(e)]
        if e < 2 * ROWS:
            return masked(pick(high_one, e), e, masks)
        return masked(pick(high_two, 1 + e - 2 * ROWS), e, masks)

    for e in range(-REACH, ROWS + REACH):
        total, side = joined(e)
        if e == -REACH:
            total = total + pick(low_one, 6)
        if e == ROWS + REACH - 1:
            total = total + pick(high_one, 6)
        for reach, factor in DIFFERENCE:
            other = across(e + reach, e)
            if other is not None:
                total = total + factor * other
        ext[span, lane(e + REACH)] = masked(total, e, masks)
        ext[tail, lane(e + REACH)] = masked(side, e, masks)
    both = dot(source[...], ext[...])
    if keep:
        held = dot(moments[...], section[...])
    for side, out in enumerate((to_right, to_left)):
        top = 4 * GROUP * side
        out[:, lane(0, BREADTH)] = both[top : top + 8]
        for k in range(BREADTH // 2):
            out[:, lane(BREADTH + k)] = (
                both[top + 8 : top + 16, lane(2 * k)] + both[top + 16 : top + 24, lane(2 * k + 1)]
            )
        if keep:
            base = PAD_V * side
            out[:, lane(PACKED, ROWS)] = held[base : base + 8]
            out[:, lane(PACKED + ROWS, 3)] = jnp.zeros((GROUP, 3 * LANES), jnp.float32)
            for e in range(BREADTH + ROWS):
                value = (
                    both[top + 24 : top + 25, lane(e)]
                    if e < BREADTH
                    else held[base + 8 : base + 9, lane(e - BREADTH)]
                )
                row, tile = e % GROUP, PACKED + ROWS + e // GROUP
                out[row : row + 1, lane(tile)] = value


def climb(levels, depth, masks):
    for j in range(1, SWEEPS):
        before = slice(depth * (j - 1), depth * j)
        after = slice(depth * j, depth * (j + 1))
        for e in range(-REACH + j, ROWS + REACH - j):
            here = levels[before, lane(e + REACH)]
            beside = (
                turned(here, 1)
                + turned(here, -1)
                + levels[before, lane(e + REACH + 1)]
                + levels[before, lane(e + REACH - 1)]
            )
            levels[after, lane(e + REACH)] = masked(beside, e, masks)
    return levels[:, lane(REACH - 2, ROWS + 4)]


def home_kernel(ext, solve, partial, levels):
    depth = ext.shape[0]
    levels[:depth, :] = ext[...]
    partial[...] = dot(solve[...], climb(levels, depth, edge_masks()))


def solve_kernel(cells, last, partial, left, right, section, solve, *refs):
    if last:
        out, levels, staged, sems = refs
    else:
        flat, next_left, next_right, upward, downward, levels = refs
    masks = edge_masks()

    def spare(given, e):
        row, tile = e % GROUP, PACKED + ROWS + e // GROUP
        return given[row : row + 1, lane(tile)]

    for side, given in enumerate((left, right)):
        top = PAD_S * side
        levels[top : top + 8, :] = given[:, lane(0, BREADTH)]
        for e in range(BREADTH):
            tile = given[:, lane(BREADTH + e // 2)]
            levels[top + 8 : top + 16, lane(e)] = pltpu.roll(tile, 4, 0) if e % 2 else tile
            if not last:
                levels[top + 12 : top + 13, lane(e)] = spare(given, e)
    found = partial[...] + dot(solve[...], climb(levels, 2 * PAD_S, masks))

    def slope(c, rows, slope_rows, r):
        phi = lambda r: masked(found[rows, lane(r + 2)], r, masks)
        if c == 0:
            return stream_slope(phi(r))
        if c == 1:
            return first_diff(phi(r + 1), phi(r - 1), phi(r + 2), phi(r - 2))
        return found[slope_rows, lane(r + 2)]

    copies = []
    for c in range(3):
        rows = slice(cells * c, cells * (c + 1))
        for r in range(ROWS):
            value = section[rows, lane(r)] - slope(c, slice(0, cells), slice(cells, 2 * cells), r)
            if last:
                staged[c, :, r, :] = value
                continue
            flat[rows, lane(r)] = value
            if r < 2:
                downward[rows, lane(r)] = value
            if r >= ROWS - 2:
                upward[rows, lane(r - ROWS + 2)] = value
        if last:
            copies.append(pltpu.make_async_copy(staged.at[c], out.at[c], sems.at[c]))
            copies[c].start()
    for copy in copies:
        copy.wait()
    if not last:
        for side, (given, target) in enumerate(((left, next_left), (right, next_right))):
            top = 2 * cells + 2 * GROUP * side
            phi_rows, slope_rows = slice(top, top + GROUP), slice(top + GROUP, top + 2 * GROUP)
            target[:GROUP, :] = given[:, lane(PACKED, ROWS)]
            target[GROUP:, :] = jnp.zeros((PAD_V - GROUP, ROWS * LANES), jnp.float32)
            for r in range(ROWS):
                target[GROUP : GROUP + 1, lane(r)] = spare(given, BREADTH + r)
                for c in range(3):
                    rows = slice(RANK_V * c, RANK_V * (c + 1))
                    target[rows, lane(r)] = target[rows, lane(r)] - slope(c, phi_rows, slope_rows, r)[:RANK_V]


def call(body, shapes, *args, scratch=(), **options):
    return pl.pallas_call(
        body,
        out_shape=[jax.ShapeDtypeStruct(s, jnp.float32) for s in shapes],
        scratch_shapes=scratch,
        compiler_params=pltpu.CompilerParams(vmem_limit_bytes=40 * 1024 * 1024),
        **options,
    )(*args)


def shifted(block, axis, step):
    count = lax.axis_size(axis)
    return lax.ppermute(block, axis, [(i, (i + step) % count) for i in range(count)])


def per_device(velocity, viscosity):
    components, cells, row_cells, columns = velocity.shape
    length = cells * lax.axis_size("span")
    slopes, moments, lateral, *first_tables = (jnp.asarray(t) for t in tables(length, cells, False))
    last_tables = [jnp.asarray(t) for t in tables(length, cells, True)[3:]]
    width = row_cells * columns
    wide = (row_cells + 2 * REACH) * columns
    near = cells + PAD_M
    edge, rim = (PAD_V, width), (components * cells, 2 * columns)
    start, to_right, to_left, upward, downward = call(
        functools.partial(open_kernel, cells),
        [(components * cells, width), edge, edge, rim, rim],
        pltpu.with_memory_space_constraint(velocity, pltpu.HBM),
        pltpu.with_memory_space_constraint(moments, pltpu.HBM),
        in_specs=[pl.BlockSpec(memory_space=pltpu.HBM)] * 2,
        scratch=[
            pltpu.VMEM(velocity.shape, jnp.float32),
            pltpu.VMEM(moments.shape, jnp.float32),
            pltpu.SemaphoreType.DMA((4,)),
        ],
    )
    left = shifted(to_right, "span", 1)
    right = shifted(to_left, "span", -1)
    flat = start
    for second in (False, True):
        low = shifted(upward, "cross", 1)
        high = shifted(downward, "cross", -1)
        base = (start,) if second else ()
        source, solve_own, solve_sides = last_tables if second else first_tables
        section, parts, up_near, down_near, up_far, down_far = call(
            functools.partial(tendency_kernel, cells, second),
            [(components * cells, width), (near, width)] + [(7 * cells + 4 * PAD_M, columns)] * 2 + [(3 * cells + PAD_M, columns)] * 2,
            *base, flat, viscosity, left, right, low, high, slopes, lateral,
        )
        low_one = shifted(up_near, "cross", 1)
        high_one = shifted(down_near, "cross", -1)
        low_two = shifted(up_far, "cross", 2)
        high_two = shifted(down_far, "cross", -2)
        sent = (GROUP, (PACKED if second else PACKED + ROWS + 3) * columns)
        extra = () if second else (moments,)
        ext, to_right, to_left = call(
            functools.partial(source_kernel, cells, not second),
            [(near, wide), sent, sent],
            parts, section, low_one, high_one, low_two, high_two, source, *extra,
        )
        left = shifted(to_right, "span", 1)
        right = shifted(to_left, "span", -1)
        (partial,) = call(
            home_kernel,
            [(solve_own.shape[0], (row_cells + 4) * columns)],
            ext, solve_own,
            scratch=[pltpu.VMEM((SWEEPS * near, wide), jnp.float32)],
        )
        scratch = [pltpu.VMEM((SWEEPS * 2 * PAD_S, wide), jnp.float32)]
        given = (partial, left, right, section, solve_sides)
        body = functools.partial(solve_kernel, cells, second)
        if second:
            (out,) = call(
                body, [velocity.shape], *given,
                scratch=scratch + [pltpu.VMEM(velocity.shape, jnp.float32), pltpu.SemaphoreType.DMA((3,))],
                out_specs=[pl.BlockSpec(memory_space=pltpu.HBM)],
            )
        else:
            flat, left, right, upward, downward = call(
                body, [(components * cells, width), edge, edge, rim, rim], *given, scratch=scratch
            )
    return out


def solution(mesh):
    in_specs = (P(None, "span", "cross", None), P("span", "cross", None))
    out_specs = P(None, "span", "cross", None)
    return jax.shard_map(
        per_device, mesh=mesh, in_specs=in_specs, out_specs=out_specs, check_vma=False
    )
```

```python
import functools

import jax
import jax.numpy as jnp
import numpy as np
from jax import lax
from jax.experimental import pallas as pl
from jax.experimental.pallas import tpu as pltpu
from jax.sharding import PartitionSpec as P

SWEEPS = 4
ROWS = 4
LANES = 128
REACH = SWEEPS + 1
time_step = 0.1
highest = lax.Precision.HIGHEST
PAD_V = 16
PAD_S = 16
PAD_M = 8
GROUP = 8
RANK_V = 3
RANK_M = 2


def symbols(length):
    w = 2.0 * np.pi * np.arange(length) / length
    first = (14.0 / 9.0 * np.sin(w) + np.sin(2.0 * w) / 18.0) / (1.0 + 2.0 / 3.0 * np.cos(w))
    second = (24.0 / 11.0 * (1.0 - np.cos(w)) + 3.0 / 22.0 * (1.0 - np.cos(2.0 * w))) / (
        1.0 + 4.0 / 11.0 * np.cos(w)
    )
    return 1j * first, -second, 1.0 / (4.0 + second)


def block_of(symbol, cells, offset):
    kernel = np.fft.ifft(symbol).real
    at = np.arange(cells)
    return kernel[(at[:, None] - (at[None, :] + offset * cells)) % len(kernel)]


def low_rank(stack, rank):
    left, scale, right = np.linalg.svd(stack, full_matrices=False)
    return left[:, :rank] * scale[:rank], right[:rank]


@functools.lru_cache(None)
def tables(length, cells, last):
    first, second, inverse = symbols(length)
    at = lambda symbol, offset: block_of(symbol, cells, offset)
    from_left, take_left = low_rank(np.concatenate([at(first, -1), at(second, -1)]), RANK_V)
    from_right, take_right = low_rank(np.concatenate([at(first, 1), at(second, 1)]), RANK_V)
    own = np.concatenate([at(first, 0), at(second, 0)])
    slopes = np.zeros((3, 2 * cells, 2 * PAD_V))
    moments = np.zeros((2 * PAD_V, 3 * cells))
    for c in range(3):
        rows = slice(RANK_V * c, RANK_V * (c + 1))
        slopes[c, :, :PAD_V][:, rows] = from_left
        slopes[c, :, PAD_V:][:, rows] = from_right
        moments[rows, cells * c : cells * (c + 1)] = take_left
        moments[PAD_V:][rows, cells * c : cells * (c + 1)] = take_right
    m_left, t_left = low_rank(at(first, -1), RANK_M)
    m_right, t_right = low_rank(at(first, 1), RANK_M)
    lateral = np.zeros((cells + PAD_M, cells))
    lateral[:cells] = at(first, 0)
    lateral[cells : cells + RANK_M] = t_left
    lateral[cells + RANK_M : cells + 2 * RANK_M] = t_right
    powers = [inverse ** (j + 1) for j in range(SWEEPS)]
    stacked = [p for p in powers] + [first * p for p in powers]
    count = len(stacked)
    RANK_S = 2 * SWEEPS + (1 if last else 3)
    kept = [] if last else stacked
    s_left, q_left = low_rank(
        np.concatenate([at(p, -1) for p in stacked] + [take_left @ at(p, 0) for p in kept]), RANK_S
    )
    s_right, q_right = low_rank(
        np.concatenate([at(p, 1) for p in stacked] + [take_right @ at(p, 0) for p in kept]), RANK_S
    )
    e_left, e_right = s_left[count * cells :], s_right[count * cells :]
    source = np.zeros((8 * GROUP, cells + PAD_M))
    for side, q in enumerate((q_left, q_right)):
        rows = np.zeros((PAD_S, cells + PAD_M))
        rows[:RANK_S, :cells] = q
        at_m = cells + RANK_M * side
        rows[RANK_S : RANK_S + RANK_M, at_m : at_m + RANK_M] = np.eye(RANK_M)
        top = 4 * GROUP * side
        source[top : top + 8] = rows[:8]
        source[top + 8 : top + 12] = rows[8:12]
        source[top + 20 : top + 24] = rows[8:12]
        source[top + 24] = rows[12]
    near, wide = cells + PAD_M, 2 * PAD_S
    height = 2 * cells + (0 if last else 4 * GROUP)
    solve_own = np.zeros((height, SWEEPS * near))
    solve_sides = np.zeros((height, SWEEPS * wide))
    for j in range(SWEEPS):
        for half in range(2):
            index = half * SWEEPS + j
            rows = slice(cells * index, cells * (index + 1))
            edge = slice(RANK_V * index, RANK_V * (index + 1))
            center = at(stacked[index], 0)
            by_left, by_right = s_left[rows], s_right[rows]
            mine, sides = np.zeros((cells, near)), np.zeros((cells, wide))
            mine[:, :cells] = center
            mine[:, cells : cells + RANK_M] = by_right @ (q_right @ m_left)
            mine[:, cells + RANK_M : cells + 2 * RANK_M] = by_left @ (q_left @ m_right)
            sides[:, :RANK_S] = by_left
            sides[:, RANK_S : RANK_S + RANK_M] = center @ m_left
            sides[:, PAD_S : PAD_S + RANK_S] = by_right
            sides[:, PAD_S + RANK_S : PAD_S + RANK_S + RANK_M] = center @ m_right
            solve_own[cells * half : cells * (half + 1), near * j : near * (j + 1)] = -mine
            solve_sides[cells * half : cells * (half + 1), wide * j : wide * (j + 1)] = -sides
            for side in range(0 if last else 2):
                mine, sides = np.zeros((RANK_V, near)), np.zeros((RANK_V, wide))
                if side == 0:
                    back = take_left @ by_right @ q_right
                    mine[:, cells + RANK_M : cells + 2 * RANK_M] = take_left @ center @ m_right
                    sides[:, :RANK_S] = e_left[edge]
                else:
                    back = take_right @ by_left @ q_left
                    mine[:, cells : cells + RANK_M] = take_right @ center @ m_left
                    sides[:, PAD_S : PAD_S + RANK_S] = e_right[edge]
                mine[:, :cells] = back
                sides[:, RANK_S : RANK_S + RANK_M] = back @ m_left
                sides[:, PAD_S + RANK_S : PAD_S + RANK_S + RANK_M] = back @ m_right
                top = 2 * cells + GROUP * (2 * side + half)
                solve_own[top : top + RANK_V, near * j : near * (j + 1)] = -mine
                solve_sides[top : top + RANK_V, wide * j : wide * (j + 1)] = -sides
    return tuple(
        x.astype(np.float32) for x in (own, slopes, moments, lateral, source, solve_own, solve_sides)
    )


def dot(a, b):
    return jnp.dot(a, b, precision=highest, preferred_element_type=jnp.float32)


BREADTH = ROWS + 2 * REACH
PACKED = BREADTH + BREADTH // 2

DIFFERENCE = ((1, 2.0 / 3.0), (-1, -2.0 / 3.0), (2, -1.0 / 12.0), (-2, 1.0 / 12.0))
CURVE = ((1, 4.0 / 3.0), (-1, 4.0 / 3.0), (2, -1.0 / 12.0), (-2, -1.0 / 12.0))


def lane(r, count=1):
    return slice(r * LANES, (r + count) * LANES)


def turned(tile, step):
    return pltpu.roll(tile, (-step) % LANES, 1)


def edge_masks():
    at = lax.axis_index("cross")
    last = lax.axis_size("cross") - 1
    flag = lambda test: jnp.where(test, 1.0, 0.0).astype(jnp.float32)
    return (flag(at >= 1), flag(at >= 2), flag(at <= last - 1), flag(at <= last - 2))


def masked(tile, e, masks):
    if e < -ROWS:
        return tile * masks[1]
    if e < 0:
        return tile * masks[0]
    if e >= 2 * ROWS:
        return tile * masks[3]
    if e >= ROWS:
        return tile * masks[2]
    return tile


def first_diff(up_one, down_one, up_two, down_two):
    return (8.0 * (up_one - down_one) - (up_two - down_two)) * (1.0 / 12.0)


def second_diff(middle, up_one, down_one, up_two, down_two):
    return (16.0 * (up_one + down_one) - (up_two + down_two) - 30.0 * middle) * (1.0 / 12.0)


def stream_slope(tile):
    return first_diff(turned(tile, 1), turned(tile, -1), turned(tile, 2), turned(tile, -2))


def open_kernel(
    cells, velocity, viscosity, moments, flat, thick, to_right, to_left, upward, downward, weights, sems
):
    copies = [pltpu.make_async_copy(moments, weights, sems.at[0])]
    for c in range(3):
        rows = slice(cells * c, cells * (c + 1))
        for r in range(ROWS):
            copies.append(
                pltpu.make_async_copy(velocity.at[c, :, r, :], flat.at[rows, lane(r)], sems.at[len(copies)])
            )
    apart = len(copies)
    for r in range(ROWS):
        copies.append(pltpu.make_async_copy(viscosity.at[:, r, :], thick.at[:, lane(r)], sems.at[len(copies)]))
    for copy in copies:
        copy.start()
    for copy in copies[:apart]:
        copy.wait()
    upward[...] = flat[:, lane(ROWS - 2, 2)]
    downward[...] = flat[:, lane(0, 2)]
    both = dot(weights[...], flat[...])
    to_right[...] = both[:PAD_V]
    to_left[...] = both[PAD_V:]
    for copy in copies[apart:]:
        copy.wait()


def weighed(weights, value_at, r, home):
    total = None
    for reach, factor in weights:
        if (0 <= r + reach < ROWS) == home:
            part = factor * value_at(r + reach)
            total = part if total is None else total + part
    return total


def rough_kernel(cells, second, *refs):
    if second:
        base, *refs = refs
    flat, thick, own, rough = refs
    for c in range(3):
        rows = slice(cells * c, cells * (c + 1))
        at = lambda r: flat[rows, lane(r)]
        spanned = dot(own[...], flat[rows, :])
        for r in range(ROWS):
            here = at(r)
            up_one, down_one = turned(here, 1), turned(here, -1)
            up_two, down_two = turned(here, 2), turned(here, -2)
            carried = (
                flat[:cells, lane(r)] * first_diff(up_one, down_one, up_two, down_two)
                + flat[cells : 2 * cells, lane(r)] * weighed(DIFFERENCE, at, r, True)
                + flat[2 * cells :, lane(r)] * spanned[:cells, lane(r)]
            )
            spread = (
                (4.0 / 3.0) * (up_one + down_one)
                - (1.0 / 12.0) * (up_two + down_two)
                - 5.0 * here
                + weighed(CURVE, at, r, True)
                + spanned[cells:, lane(r)]
            )
            moved = here + time_step * (thick[:, lane(r)] * spread - carried)
            if second:
                moved = 0.5 * base[rows, lane(r)] + 0.5 * moved
            rough[rows, lane(r)] = moved


def tendency_kernel(
    cells, scale, rough, flat, thick, left, right, low, high, slopes, lateral,
    section, parts, up_near, down_near, up_far, down_far,
):
    masks = edge_masks()
    sides = jnp.concatenate([left[...], right[...]], axis=0)
    for c in range(3):
        rows = slice(cells * c, cells * (c + 1))
        spanned = dot(slopes[c], sides)

        def beyond(r):
            if r < 0:
                return masked(low[rows, lane(r + 2)], r, masks)
            return masked(high[rows, lane(r - ROWS)], r, masks)

        for r in range(ROWS):
            spread = spanned[cells:, lane(r)] + weighed(CURVE, beyond, r, False)
            carried = flat[cells : 2 * cells, lane(r)] * weighed(DIFFERENCE, beyond, r, False)
            carried = carried + flat[2 * cells :, lane(r)] * spanned[:cells, lane(r)]
            section[rows, lane(r)] = rough[rows, lane(r)] + scale * (thick[:, lane(r)] * spread - carried)
    side = dot(lateral[...], section[2 * cells :, :])
    span = slice(0, cells)
    at = lambda r: section[cells : 2 * cells, lane(r)]
    for r in range(ROWS):
        total = stream_slope(section[:cells, lane(r)]) + side[:cells, lane(r)]
        for reach, factor in DIFFERENCE:
            if 0 <= r + reach < ROWS:
                total = total + factor * at(r + reach)
        parts[span, lane(r)] = total
        for block in (up_near, down_near):
            block[cells * r : cells * (r + 1), :] = total
            block[7 * cells + PAD_M * r : 7 * cells + PAD_M * (r + 1), :] = side[cells:, lane(r)]
    tail = slice(cells, cells + PAD_M)
    parts[tail, :] = side[cells:]
    for far, r in ((up_far, ROWS - 1), (down_far, 0)):
        far[:cells, :] = parts[span, lane(r)]
        far[3 * cells :, :] = parts[tail, lane(r)]
    for k in range(2):
        near_rows = slice(cells * (ROWS + k), cells * (ROWS + k + 1))
        far_rows = slice(cells * (1 + k), cells * (2 + k))
        up_near[near_rows, :] = at(ROWS - 2 + k)
        up_far[far_rows, :] = at(ROWS - 2 + k)
        down_near[near_rows, :] = at(k)
        down_far[far_rows, :] = at(k)
    rest = slice(6 * cells, 7 * cells)
    up_near[rest, :] = (2.0 / 3.0) * at(0) - (1.0 / 12.0) * at(1)
    down_near[rest, :] = (1.0 / 12.0) * at(ROWS - 2) - (2.0 / 3.0) * at(ROWS - 1)


def source_kernel(cells, keep, parts, section, low_one, high_one, low_two, high_two, source, *refs):
    if keep:
        moments, ext, to_right, to_left = refs
    else:
        ext, to_right, to_left = refs
    masks = edge_masks()
    span, tail = slice(0, cells), slice(cells, cells + PAD_M)
    pick = lambda ref, k: ref[cells * k : cells * (k + 1), :]

    def joined(e):
        if e < -ROWS:
            return low_two[:cells, :], low_two[3 * cells :, :]
        if e >= 2 * ROWS:
            return high_two[:cells, :], high_two[3 * cells :, :]
        if 0 <= e < ROWS:
            return parts[span, lane(e)], parts[tail, lane(e)]
        near, r = (low_one, e + ROWS) if e < 0 else (high_one, e - ROWS)
        top = 7 * cells + PAD_M * r
        return pick(near, r), near[top : top + PAD_M, :]

    def across(e, home):
        if e // ROWS == home // ROWS or home // ROWS in (-2, 2):
            return None
        if e < -ROWS:
            return masked(pick(low_two, 1 + e + ROWS + 2), e, masks)
        if e < 0:
            return masked(pick(low_one, ROWS + e + 2), e, masks)
        if e < ROWS:
            return section[cells : 2 * cells, lane(e)]
        if e < 2 * ROWS:
            return masked(pick(high_one, e), e, masks)
        return masked(pick(high_two, 1 + e - 2 * ROWS), e, masks)

    for e in range(-REACH, ROWS + REACH):
        total, side = joined(e)
        if e == -REACH:
            total = total + pick(low_one, 6)
        if e == ROWS + REACH - 1:
            total = total + pick(high_one, 6)
        for reach, factor in DIFFERENCE:
            other = across(e + reach, e)
            if other is not None:
                total = total + factor * other
        ext[span, lane(e + REACH)] = masked(total, e, masks)
        ext[tail, lane(e + REACH)] = masked(side, e, masks)
    both = dot(source[...], ext[...])
    if keep:
        held = dot(moments[...], section[...])
    for side, out in enumerate((to_right, to_left)):
        top = 4 * GROUP * side
        out[:, lane(0, BREADTH)] = both[top : top + 8]
        for k in range(BREADTH // 2):
            out[:, lane(BREADTH + k)] = (
                both[top + 8 : top + 16, lane(2 * k)] + both[top + 16 : top + 24, lane(2 * k + 1)]
            )
        if keep:
            base = PAD_V * side
            out[:, lane(PACKED, ROWS)] = held[base : base + 8]
            out[:, lane(PACKED + ROWS, 3)] = jnp.zeros((GROUP, 3 * LANES), jnp.float32)
            for e in range(BREADTH + ROWS):
                value = (
                    both[top + 24 : top + 25, lane(e)]
                    if e < BREADTH
                    else held[base + 8 : base + 9, lane(e - BREADTH)]
                )
                row, tile = e % GROUP, PACKED + ROWS + e // GROUP
                out[row : row + 1, lane(tile)] = value


def climb(levels, depth, masks):
    for j in range(1, SWEEPS):
        before = slice(depth * (j - 1), depth * j)
        after = slice(depth * j, depth * (j + 1))
        for e in range(-REACH + j, ROWS + REACH - j):
            here = levels[before, lane(e + REACH)]
            beside = (
                turned(here, 1)
                + turned(here, -1)
                + levels[before, lane(e + REACH + 1)]
                + levels[before, lane(e + REACH - 1)]
            )
            levels[after, lane(e + REACH)] = masked(beside, e, masks)
    return levels[:, lane(REACH - 2, ROWS + 4)]


def home_kernel(ext, solve, partial, levels):
    depth = ext.shape[0]
    levels[:depth, :] = ext[...]
    partial[...] = dot(solve[...], climb(levels, depth, edge_masks()))


def solve_kernel(cells, last, partial, left, right, section, solve, *refs):
    if last:
        out, levels, staged, sems = refs
    else:
        flat, next_left, next_right, upward, downward, levels = refs
    masks = edge_masks()

    def spare(given, e):
        row, tile = e % GROUP, PACKED + ROWS + e // GROUP
        return given[row : row + 1, lane(tile)]

    for side, given in enumerate((left, right)):
        top = PAD_S * side
        levels[top : top + 8, :] = given[:, lane(0, BREADTH)]
        for e in range(BREADTH):
            tile = given[:, lane(BREADTH + e // 2)]
            levels[top + 8 : top + 16, lane(e)] = pltpu.roll(tile, 4, 0) if e % 2 else tile
            if not last:
                levels[top + 12 : top + 13, lane(e)] = spare(given, e)
    found = partial[...] + dot(solve[...], climb(levels, 2 * PAD_S, masks))

    def slope(c, rows, slope_rows, r):
        phi = lambda r: masked(found[rows, lane(r + 2)], r, masks)
        if c == 0:
            return stream_slope(phi(r))
        if c == 1:
            return first_diff(phi(r + 1), phi(r - 1), phi(r + 2), phi(r - 2))
        return found[slope_rows, lane(r + 2)]

    copies = []
    for c in range(3):
        rows = slice(cells * c, cells * (c + 1))
        for r in range(ROWS):
            value = section[rows, lane(r)] - slope(c, slice(0, cells), slice(cells, 2 * cells), r)
            if last:
                staged[rows, lane(r)] = value
                copies.append(
                    pltpu.make_async_copy(staged.at[rows, lane(r)], out.at[c, :, r, :], sems.at[len(copies)])
                )
                copies[-1].start()
                continue
            flat[rows, lane(r)] = value
            if r < 2:
                downward[rows, lane(r)] = value
            if r >= ROWS - 2:
                upward[rows, lane(r - ROWS + 2)] = value
    for copy in copies:
        copy.wait()
    if not last:
        for side, (given, target) in enumerate(((left, next_left), (right, next_right))):
            top = 2 * cells + 2 * GROUP * side
            phi_rows, slope_rows = slice(top, top + GROUP), slice(top + GROUP, top + 2 * GROUP)
            target[:GROUP, :] = given[:, lane(PACKED, ROWS)]
            target[GROUP:, :] = jnp.zeros((PAD_V - GROUP, ROWS * LANES), jnp.float32)
            for r in range(ROWS):
                target[GROUP : GROUP + 1, lane(r)] = spare(given, BREADTH + r)
                for c in range(3):
                    rows = slice(RANK_V * c, RANK_V * (c + 1))
                    target[rows, lane(r)] = target[rows, lane(r)] - slope(c, phi_rows, slope_rows, r)[:RANK_V]


def call(body, shapes, *args, scratch=(), **options):
    return pl.pallas_call(
        body,
        out_shape=[jax.ShapeDtypeStruct(s, jnp.float32) for s in shapes],
        scratch_shapes=scratch,
        compiler_params=pltpu.CompilerParams(vmem_limit_bytes=40 * 1024 * 1024),
        **options,
    )(*args)


def shifted(block, axis, step):
    count = lax.axis_size(axis)
    return lax.ppermute(block, axis, [(i, (i + step) % count) for i in range(count)])


def per_device(velocity, viscosity):
    components, cells, row_cells, columns = velocity.shape
    length = cells * lax.axis_size("span")
    own, slopes, moments, lateral, *first_tables = (jnp.asarray(t) for t in tables(length, cells, False))
    last_tables = [jnp.asarray(t) for t in tables(length, cells, True)[4:]]
    width = row_cells * columns
    wide = (row_cells + 2 * REACH) * columns
    near = cells + PAD_M
    edge, rim = (PAD_V, width), (components * cells, 2 * columns)
    start, thick, to_right, to_left, upward, downward = call(
        functools.partial(open_kernel, cells),
        [(components * cells, width), (cells, width), edge, edge, rim, rim],
        *(pltpu.with_memory_space_constraint(x, pltpu.HBM) for x in (velocity, viscosity, moments)),
        in_specs=[pl.BlockSpec(memory_space=pltpu.HBM)] * 3,
        scratch=[
            pltpu.VMEM(moments.shape, jnp.float32),
            pltpu.SemaphoreType.DMA((1 + 4 * ROWS,)),
        ],
    )
    left = shifted(to_right, "span", 1)
    right = shifted(to_left, "span", -1)
    flat = start
    for second in (False, True):
        low = shifted(upward, "cross", 1)
        high = shifted(downward, "cross", -1)
        base = (start,) if second else ()
        source, solve_own, solve_sides = last_tables if second else first_tables
        (rough,) = call(
            functools.partial(rough_kernel, cells, second), [(components * cells, width)], *base, flat, thick, own
        )
        section, parts, up_near, down_near, up_far, down_far = call(
            functools.partial(tendency_kernel, cells, 0.5 * time_step if second else time_step),
            [(components * cells, width), (near, width)] + [(7 * cells + 4 * PAD_M, columns)] * 2 + [(3 * cells + PAD_M, columns)] * 2,
            rough, flat, thick, left, right, low, high, slopes, lateral,
        )
        low_one = shifted(up_near, "cross", 1)
        high_one = shifted(down_near, "cross", -1)
        low_two = shifted(up_far, "cross", 2)
        high_two = shifted(down_far, "cross", -2)
        sent = (GROUP, (PACKED if second else PACKED + ROWS + 3) * columns)
        extra = () if second else (moments,)
        ext, to_right, to_left = call(
            functools.partial(source_kernel, cells, not second),
            [(near, wide), sent, sent],
            parts, section, low_one, high_one, low_two, high_two, source, *extra,
        )
        left = shifted(to_right, "span", 1)
        right = shifted(to_left, "span", -1)
        (partial,) = call(
            home_kernel,
            [(solve_own.shape[0], (row_cells + 4) * columns)],
            ext, solve_own,
            scratch=[pltpu.VMEM((SWEEPS * near, wide), jnp.float32)],
        )
        scratch = [pltpu.VMEM((SWEEPS * 2 * PAD_S, wide), jnp.float32)]
        given = (partial, left, right, section, solve_sides)
        body = functools.partial(solve_kernel, cells, second)
        if second:
            (out,) = call(
                body, [velocity.shape], *given,
                scratch=scratch + [pltpu.VMEM((components * cells, width), jnp.float32), pltpu.SemaphoreType.DMA((3 * ROWS,))],
                out_specs=[pl.BlockSpec(memory_space=pltpu.HBM)],
            )
        else:
            flat, left, right, upward, downward = call(
                body, [(components * cells, width), edge, edge, rim, rim], *given, scratch=scratch
            )
    return out


def solution(mesh):
    in_specs = (P(None, "span", "cross", None), P("span", "cross", None))
    out_specs = P(None, "span", "cross", None)
    return jax.shard_map(
        per_device, mesh=mesh, in_specs=in_specs, out_specs=out_specs, check_vma=False
    )
```

```python
import functools

import jax
import jax.numpy as jnp
import ml_dtypes
import numpy as np
from jax import lax
from jax.experimental import pallas as pl
from jax.experimental.pallas import tpu as pltpu
from jax.sharding import PartitionSpec as P

SWEEPS = 4
ROWS = 4
LANES = 128
REACH = SWEEPS + 1
time_step = 0.1
highest = lax.Precision.HIGHEST
PAD_V = 16
PAD_S = 16
PAD_M = 8
GROUP = 8
PACK = 16
RANK_V = 3
RANK_M = 2


def symbols(length):
    w = 2.0 * np.pi * np.arange(length) / length
    first = (14.0 / 9.0 * np.sin(w) + np.sin(2.0 * w) / 18.0) / (1.0 + 2.0 / 3.0 * np.cos(w))
    second = (24.0 / 11.0 * (1.0 - np.cos(w)) + 3.0 / 22.0 * (1.0 - np.cos(2.0 * w))) / (
        1.0 + 4.0 / 11.0 * np.cos(w)
    )
    return 1j * first, -second, 1.0 / (4.0 + second)


def block_of(symbol, cells, offset):
    kernel = np.fft.ifft(symbol).real
    at = np.arange(cells)
    return kernel[(at[:, None] - (at[None, :] + offset * cells)) % len(kernel)]


def low_rank(stack, rank):
    left, scale, right = np.linalg.svd(stack, full_matrices=False)
    return left[:, :rank] * scale[:rank], right[:rank]


@functools.lru_cache(None)
def tables(length, cells, last):
    first, second, inverse = symbols(length)
    at = lambda symbol, offset: block_of(symbol, cells, offset)
    from_left, take_left = low_rank(np.concatenate([at(first, -1), at(second, -1)]), RANK_V)
    from_right, take_right = low_rank(np.concatenate([at(first, 1), at(second, 1)]), RANK_V)
    own = np.concatenate([at(first, 0), at(second, 0)])
    slopes = np.zeros((3, 2 * cells, 2 * PAD_V))
    moments = np.zeros((2 * PAD_V, 3 * cells))
    for c in range(3):
        rows = slice(RANK_V * c, RANK_V * (c + 1))
        slopes[c, :, :PAD_V][:, rows] = from_left
        slopes[c, :, PAD_V:][:, rows] = from_right
        moments[rows, cells * c : cells * (c + 1)] = take_left
        moments[PAD_V:][rows, cells * c : cells * (c + 1)] = take_right
    m_left, t_left = low_rank(at(first, -1), RANK_M)
    m_right, t_right = low_rank(at(first, 1), RANK_M)
    lateral = np.zeros((cells + PAD_M, cells))
    lateral[:cells] = at(first, 0)
    lateral[cells : cells + RANK_M] = t_left
    lateral[cells + RANK_M : cells + 2 * RANK_M] = t_right
    powers = [inverse ** (j + 1) for j in range(SWEEPS)]
    stacked = [p for p in powers] + [first * p for p in powers]
    count = len(stacked)
    RANK_S = 2 * SWEEPS + (1 if last else 3)
    kept = [] if last else stacked
    s_left, q_left = low_rank(
        np.concatenate([at(p, -1) for p in stacked] + [take_left @ at(p, 0) for p in kept]), RANK_S
    )
    s_right, q_right = low_rank(
        np.concatenate([at(p, 1) for p in stacked] + [take_right @ at(p, 0) for p in kept]), RANK_S
    )
    e_left, e_right = s_left[count * cells :], s_right[count * cells :]
    source = np.zeros((8 * GROUP, cells + PAD_M))
    for side, q in enumerate((q_left, q_right)):
        rows = np.zeros((PAD_S, cells + PAD_M))
        rows[:RANK_S, :cells] = q
        at_m = cells + RANK_M * side
        rows[RANK_S : RANK_S + RANK_M, at_m : at_m + RANK_M] = np.eye(RANK_M)
        top = 4 * GROUP * side
        source[top : top + 8] = rows[:8]
        source[top + 8 : top + 12] = rows[8:12]
        source[top + 20 : top + 24] = rows[8:12]
        source[top + 24] = rows[12]
    near, wide = cells + PAD_M, 2 * PAD_S
    height = 2 * cells + (0 if last else 4 * GROUP)
    solve_own = np.zeros((height, SWEEPS * near))
    solve_sides = np.zeros((height, SWEEPS * wide))
    for j in range(SWEEPS):
        for half in range(2):
            index = half * SWEEPS + j
            rows = slice(cells * index, cells * (index + 1))
            edge = slice(RANK_V * index, RANK_V * (index + 1))
            center = at(stacked[index], 0)
            by_left, by_right = s_left[rows], s_right[rows]
            mine, sides = np.zeros((cells, near)), np.zeros((cells, wide))
            mine[:, :cells] = center
            mine[:, cells : cells + RANK_M] = by_right @ (q_right @ m_left)
            mine[:, cells + RANK_M : cells + 2 * RANK_M] = by_left @ (q_left @ m_right)
            sides[:, :RANK_S] = by_left
            sides[:, RANK_S : RANK_S + RANK_M] = center @ m_left
            sides[:, PAD_S : PAD_S + RANK_S] = by_right
            sides[:, PAD_S + RANK_S : PAD_S + RANK_S + RANK_M] = center @ m_right
            solve_own[cells * half : cells * (half + 1), near * j : near * (j + 1)] = -mine
            solve_sides[cells * half : cells * (half + 1), wide * j : wide * (j + 1)] = -sides
            for side in range(0 if last else 2):
                mine, sides = np.zeros((RANK_V, near)), np.zeros((RANK_V, wide))
                if side == 0:
                    back = take_left @ by_right @ q_right
                    mine[:, cells + RANK_M : cells + 2 * RANK_M] = take_left @ center @ m_right
                    sides[:, :RANK_S] = e_left[edge]
                else:
                    back = take_right @ by_left @ q_left
                    mine[:, cells : cells + RANK_M] = take_right @ center @ m_left
                    sides[:, PAD_S : PAD_S + RANK_S] = e_right[edge]
                mine[:, :cells] = back
                sides[:, RANK_S : RANK_S + RANK_M] = back @ m_left
                sides[:, PAD_S + RANK_S : PAD_S + RANK_S + RANK_M] = back @ m_right
                top = 2 * cells + GROUP * (2 * side + half)
                solve_own[top : top + RANK_V, near * j : near * (j + 1)] = -mine
                solve_sides[top : top + RANK_V, wide * j : wide * (j + 1)] = -sides
    plain, split = (own, solve_own), (slopes, moments, lateral, source, solve_sides)
    return [x.astype(np.float32) for x in plain] + [split_table(x.astype(np.float32)) for x in split]


def dot(a, b):
    return jnp.dot(a, b, precision=highest, preferred_element_type=jnp.float32)


def halves(x):
    high = x.astype(jnp.bfloat16)
    return high, (x - high.astype(jnp.float32)).astype(jnp.bfloat16)


def split_table(table):
    gap = -table.shape[-1] % PACK
    table = np.pad(table, [(0, 0)] * (table.ndim - 1) + [(0, gap)])
    high = table.astype(ml_dtypes.bfloat16)
    low = (table - high.astype(np.float32)).astype(ml_dtypes.bfloat16)
    return np.concatenate([high, high, low], axis=-1)


def split_dot(table, x):
    gap = -x.shape[0] % PACK
    if gap:
        x = jnp.concatenate([x, jnp.zeros((gap, x.shape[1]), x.dtype)], axis=0)
    high, low = halves(x)
    return jnp.dot(table, jnp.concatenate([high, low, high], axis=0), preferred_element_type=jnp.float32)


BREADTH = ROWS + 2 * REACH
PACKED = BREADTH + BREADTH // 2

DIFFERENCE = ((1, 2.0 / 3.0), (-1, -2.0 / 3.0), (2, -1.0 / 12.0), (-2, 1.0 / 12.0))
CURVE = ((1, 4.0 / 3.0), (-1, 4.0 / 3.0), (2, -1.0 / 12.0), (-2, -1.0 / 12.0))


def lane(r, count=1):
    return slice(r * LANES, (r + count) * LANES)


def turned(tile, step):
    return pltpu.roll(tile, (-step) % LANES, 1)


def edge_masks():
    at = lax.axis_index("cross")
    last = lax.axis_size("cross") - 1
    flag = lambda test: jnp.where(test, 1.0, 0.0).astype(jnp.float32)
    return (flag(at >= 1), flag(at >= 2), flag(at <= last - 1), flag(at <= last - 2))


def masked(tile, e, masks):
    if e < -ROWS:
        return tile * masks[1]
    if e < 0:
        return tile * masks[0]
    if e >= 2 * ROWS:
        return tile * masks[3]
    if e >= ROWS:
        return tile * masks[2]
    return tile


def first_diff(up_one, down_one, up_two, down_two):
    return (8.0 * (up_one - down_one) - (up_two - down_two)) * (1.0 / 12.0)


def second_diff(middle, up_one, down_one, up_two, down_two):
    return (16.0 * (up_one + down_one) - (up_two + down_two) - 30.0 * middle) * (1.0 / 12.0)


def stream_slope(tile):
    return first_diff(turned(tile, 1), turned(tile, -1), turned(tile, 2), turned(tile, -2))


def open_kernel(
    cells, velocity, viscosity, moments, flat, thick, to_right, to_left, upward, downward, weights, sems
):
    copies = [pltpu.make_async_copy(moments, weights, sems.at[0])]
    for c in range(3):
        rows = slice(cells * c, cells * (c + 1))
        for r in range(ROWS):
            copies.append(
                pltpu.make_async_copy(velocity.at[c, :, r, :], flat.at[rows, lane(r)], sems.at[len(copies)])
            )
    apart = len(copies)
    for r in range(ROWS):
        copies.append(pltpu.make_async_copy(viscosity.at[:, r, :], thick.at[:, lane(r)], sems.at[len(copies)]))
    for copy in copies:
        copy.start()
    for copy in copies[:apart]:
        copy.wait()
    upward[...] = flat[:, lane(ROWS - 2, 2)]
    downward[...] = flat[:, lane(0, 2)]
    both = split_dot(weights[...], flat[...])
    to_right[...] = both[:PAD_V]
    to_left[...] = both[PAD_V:]
    for copy in copies[apart:]:
        copy.wait()


def weighed(weights, value_at, r, home):
    total = None
    for reach, factor in weights:
        if (0 <= r + reach < ROWS) == home:
            part = factor * value_at(r + reach)
            total = part if total is None else total + part
    return total


def rough_kernel(cells, second, *refs):
    if second:
        base, *refs = refs
    flat, thick, own, rough = refs
    for c in range(3):
        rows = slice(cells * c, cells * (c + 1))
        at = lambda r: flat[rows, lane(r)]
        spanned = dot(own[...], flat[rows, :])
        for r in range(ROWS):
            here = at(r)
            up_one, down_one = turned(here, 1), turned(here, -1)
            up_two, down_two = turned(here, 2), turned(here, -2)
            carried = (
                flat[:cells, lane(r)] * first_diff(up_one, down_one, up_two, down_two)
                + flat[cells : 2 * cells, lane(r)] * weighed(DIFFERENCE, at, r, True)
                + flat[2 * cells :, lane(r)] * spanned[:cells, lane(r)]
            )
            spread = (
                (4.0 / 3.0) * (up_one + down_one)
                - (1.0 / 12.0) * (up_two + down_two)
                - 5.0 * here
                + weighed(CURVE, at, r, True)
                + spanned[cells:, lane(r)]
            )
            moved = here + time_step * (thick[:, lane(r)] * spread - carried)
            if second:
                moved = 0.5 * base[rows, lane(r)] + 0.5 * moved
            rough[rows, lane(r)] = moved


def tendency_kernel(
    cells, scale, rough, flat, thick, left, right, low, high, slopes, lateral,
    section, parts, up_near, down_near, up_far, down_far,
):
    masks = edge_masks()
    sides = jnp.concatenate([left[...], right[...]], axis=0)
    for c in range(3):
        rows = slice(cells * c, cells * (c + 1))
        spanned = split_dot(slopes[c], sides)

        def beyond(r):
            if r < 0:
                return masked(low[rows, lane(r + 2)], r, masks)
            return masked(high[rows, lane(r - ROWS)], r, masks)

        for r in range(ROWS):
            spread = spanned[cells:, lane(r)] + weighed(CURVE, beyond, r, False)
            carried = flat[cells : 2 * cells, lane(r)] * weighed(DIFFERENCE, beyond, r, False)
            carried = carried + flat[2 * cells :, lane(r)] * spanned[:cells, lane(r)]
            section[rows, lane(r)] = rough[rows, lane(r)] + scale * (thick[:, lane(r)] * spread - carried)
    side = split_dot(lateral[...], section[2 * cells :, :])
    span = slice(0, cells)
    at = lambda r: section[cells : 2 * cells, lane(r)]
    for r in range(ROWS):
        total = stream_slope(section[:cells, lane(r)]) + side[:cells, lane(r)]
        for reach, factor in DIFFERENCE:
            if 0 <= r + reach < ROWS:
                total = total + factor * at(r + reach)
        parts[span, lane(r)] = total
        for block in (up_near, down_near):
            block[cells * r : cells * (r + 1), :] = total
            block[7 * cells + PAD_M * r : 7 * cells + PAD_M * (r + 1), :] = side[cells:, lane(r)]
    tail = slice(cells, cells + PAD_M)
    parts[tail, :] = side[cells:]
    for far, r in ((up_far, ROWS - 1), (down_far, 0)):
        far[:cells, :] = parts[span, lane(r)]
        far[3 * cells :, :] = parts[tail, lane(r)]
    for k in range(2):
        near_rows = slice(cells * (ROWS + k), cells * (ROWS + k + 1))
        far_rows = slice(cells * (1 + k), cells * (2 + k))
        up_near[near_rows, :] = at(ROWS - 2 + k)
        up_far[far_rows, :] = at(ROWS - 2 + k)
        down_near[near_rows, :] = at(k)
        down_far[far_rows, :] = at(k)
    rest = slice(6 * cells, 7 * cells)
    up_near[rest, :] = (2.0 / 3.0) * at(0) - (1.0 / 12.0) * at(1)
    down_near[rest, :] = (1.0 / 12.0) * at(ROWS - 2) - (2.0 / 3.0) * at(ROWS - 1)


def source_kernel(cells, keep, parts, section, low_one, high_one, low_two, high_two, source, *refs):
    if keep:
        moments, ext, to_right, to_left = refs
    else:
        ext, to_right, to_left = refs
    masks = edge_masks()
    span, tail = slice(0, cells), slice(cells, cells + PAD_M)
    pick = lambda ref, k: ref[cells * k : cells * (k + 1), :]

    def joined(e):
        if e < -ROWS:
            return low_two[:cells, :], low_two[3 * cells :, :]
        if e >= 2 * ROWS:
            return high_two[:cells, :], high_two[3 * cells :, :]
        if 0 <= e < ROWS:
            return parts[span, lane(e)], parts[tail, lane(e)]
        near, r = (low_one, e + ROWS) if e < 0 else (high_one, e - ROWS)
        top = 7 * cells + PAD_M * r
        return pick(near, r), near[top : top + PAD_M, :]

    def across(e, home):
        if e // ROWS == home // ROWS or home // ROWS in (-2, 2):
            return None
        if e < -ROWS:
            return masked(pick(low_two, 1 + e + ROWS + 2), e, masks)
        if e < 0:
            return masked(pick(low_one, ROWS + e + 2), e, masks)
        if e < ROWS:
            return section[cells : 2 * cells, lane(e)]
        if e < 2 * ROWS:
            return masked(pick(high_one, e), e, masks)
        return masked(pick(high_two, 1 + e - 2 * ROWS), e, masks)

    for e in range(-REACH, ROWS + REACH):
        total, side = joined(e)
        if e == -REACH:
            total = total + pick(low_one, 6)
        if e == ROWS + REACH - 1:
            total = total + pick(high_one, 6)
        for reach, factor in DIFFERENCE:
            other = across(e + reach, e)
            if other is not None:
                total = total + factor * other
        ext[span, lane(e + REACH)] = masked(total, e, masks)
        ext[tail, lane(e + REACH)] = masked(side, e, masks)
    both = split_dot(source[...], ext[...])
    if keep:
        held = split_dot(moments[...], section[...])
    for side, out in enumerate((to_right, to_left)):
        top = 4 * GROUP * side
        out[:, lane(0, BREADTH)] = both[top : top + 8]
        for k in range(BREADTH // 2):
            out[:, lane(BREADTH + k)] = (
                both[top + 8 : top + 16, lane(2 * k)] + both[top + 16 : top + 24, lane(2 * k + 1)]
            )
        if keep:
            base = PAD_V * side
            out[:, lane(PACKED, ROWS)] = held[base : base + 8]
            out[:, lane(PACKED + ROWS, 3)] = jnp.zeros((GROUP, 3 * LANES), jnp.float32)
            for e in range(BREADTH + ROWS):
                value = (
                    both[top + 24 : top + 25, lane(e)]
                    if e < BREADTH
                    else held[base + 8 : base + 9, lane(e - BREADTH)]
                )
                row, tile = e % GROUP, PACKED + ROWS + e // GROUP
                out[row : row + 1, lane(tile)] = value


def climb(levels, depth, masks):
    for j in range(1, SWEEPS):
        before = slice(depth * (j - 1), depth * j)
        after = slice(depth * j, depth * (j + 1))
        for e in range(-REACH + j, ROWS + REACH - j):
            here = levels[before, lane(e + REACH)]
            beside = (
                turned(here, 1)
                + turned(here, -1)
                + levels[before, lane(e + REACH + 1)]
                + levels[before, lane(e + REACH - 1)]
            )
            levels[after, lane(e + REACH)] = masked(beside, e, masks)
    return levels[:, lane(REACH - 2, ROWS + 4)]


def home_kernel(ext, solve, partial, levels):
    depth = ext.shape[0]
    levels[:depth, :] = ext[...]
    partial[...] = dot(solve[...], climb(levels, depth, edge_masks()))


def solve_kernel(cells, last, partial, left, right, section, solve, *refs):
    if last:
        out, levels, staged, sems = refs
    else:
        flat, next_left, next_right, upward, downward, levels = refs
    masks = edge_masks()

    def spare(given, e):
        row, tile = e % GROUP, PACKED + ROWS + e // GROUP
        return given[row : row + 1, lane(tile)]

    for side, given in enumerate((left, right)):
        top = PAD_S * side
        levels[top : top + 8, :] = given[:, lane(0, BREADTH)]
        for e in range(BREADTH):
            tile = given[:, lane(BREADTH + e // 2)]
            levels[top + 8 : top + 16, lane(e)] = pltpu.roll(tile, 4, 0) if e % 2 else tile
            if not last:
                levels[top + 12 : top + 13, lane(e)] = spare(given, e)
    found = partial[...] + split_dot(solve[...], climb(levels, 2 * PAD_S, masks))

    def slope(c, rows, slope_rows, r):
        phi = lambda r: masked(found[rows, lane(r + 2)], r, masks)
        if c == 0:
            return stream_slope(phi(r))
        if c == 1:
            return first_diff(phi(r + 1), phi(r - 1), phi(r + 2), phi(r - 2))
        return found[slope_rows, lane(r + 2)]

    copies = []
    for c in range(3):
        rows = slice(cells * c, cells * (c + 1))
        for r in range(ROWS):
            value = section[rows, lane(r)] - slope(c, slice(0, cells), slice(cells, 2 * cells), r)
            if last:
                staged[rows, lane(r)] = value
                copies.append(
                    pltpu.make_async_copy(staged.at[rows, lane(r)], out.at[c, :, r, :], sems.at[len(copies)])
                )
                copies[-1].start()
                continue
            flat[rows, lane(r)] = value
            if r < 2:
                downward[rows, lane(r)] = value
            if r >= ROWS - 2:
                upward[rows, lane(r - ROWS + 2)] = value
    for copy in copies:
        copy.wait()
    if not last:
        for side, (given, target) in enumerate(((left, next_left), (right, next_right))):
            top = 2 * cells + 2 * GROUP * side
            phi_rows, slope_rows = slice(top, top + GROUP), slice(top + GROUP, top + 2 * GROUP)
            target[:GROUP, :] = given[:, lane(PACKED, ROWS)]
            target[GROUP:, :] = jnp.zeros((PAD_V - GROUP, ROWS * LANES), jnp.float32)
            for r in range(ROWS):
                target[GROUP : GROUP + 1, lane(r)] = spare(given, BREADTH + r)
                for c in range(3):
                    rows = slice(RANK_V * c, RANK_V * (c + 1))
                    target[rows, lane(r)] = target[rows, lane(r)] - slope(c, phi_rows, slope_rows, r)[:RANK_V]


def call(body, shapes, *args, scratch=(), **options):
    return pl.pallas_call(
        body,
        out_shape=[jax.ShapeDtypeStruct(s, jnp.float32) for s in shapes],
        scratch_shapes=scratch,
        compiler_params=pltpu.CompilerParams(vmem_limit_bytes=40 * 1024 * 1024),
        **options,
    )(*args)


def shifted(block, axis, step):
    count = lax.axis_size(axis)
    return lax.ppermute(block, axis, [(i, (i + step) % count) for i in range(count)])


def per_device(velocity, viscosity):
    components, cells, row_cells, columns = velocity.shape
    length = cells * lax.axis_size("span")
    own, first_own, slopes, moments, lateral, *first = (jnp.asarray(t) for t in tables(length, cells, False))
    _, last_own, _, _, _, *last = (jnp.asarray(t) for t in tables(length, cells, True))
    width = row_cells * columns
    wide = (row_cells + 2 * REACH) * columns
    near = cells + PAD_M
    edge, rim = (PAD_V, width), (components * cells, 2 * columns)
    start, thick, to_right, to_left, upward, downward = call(
        functools.partial(open_kernel, cells),
        [(components * cells, width), (cells, width), edge, edge, rim, rim],
        *(pltpu.with_memory_space_constraint(x, pltpu.HBM) for x in (velocity, viscosity, moments)),
        in_specs=[pl.BlockSpec(memory_space=pltpu.HBM)] * 3,
        scratch=[
            pltpu.VMEM(moments.shape, moments.dtype),
            pltpu.SemaphoreType.DMA((1 + 4 * ROWS,)),
        ],
    )
    left = shifted(to_right, "span", 1)
    right = shifted(to_left, "span", -1)
    flat = start
    for second in (False, True):
        low = shifted(upward, "cross", 1)
        high = shifted(downward, "cross", -1)
        base = (start,) if second else ()
        source, solve_sides = last if second else first
        solve_own = last_own if second else first_own
        (rough,) = call(
            functools.partial(rough_kernel, cells, second), [(components * cells, width)], *base, flat, thick, own
        )
        section, parts, up_near, down_near, up_far, down_far = call(
            functools.partial(tendency_kernel, cells, 0.5 * time_step if second else time_step),
            [(components * cells, width), (near, width)] + [(7 * cells + 4 * PAD_M, columns)] * 2 + [(3 * cells + PAD_M, columns)] * 2,
            rough, flat, thick, left, right, low, high, slopes, lateral,
        )
        low_one = shifted(up_near, "cross", 1)
        high_one = shifted(down_near, "cross", -1)
        low_two = shifted(up_far, "cross", 2)
        high_two = shifted(down_far, "cross", -2)
        sent = (GROUP, (PACKED if second else PACKED + ROWS + 3) * columns)
        extra = () if second else (moments,)
        ext, to_right, to_left = call(
            functools.partial(source_kernel, cells, not second),
            [(near, wide), sent, sent],
            parts, section, low_one, high_one, low_two, high_two, source, *extra,
        )
        left = shifted(to_right, "span", 1)
        right = shifted(to_left, "span", -1)
        (partial,) = call(
            home_kernel,
            [(solve_own.shape[0], (row_cells + 4) * columns)],
            ext, solve_own,
            scratch=[pltpu.VMEM((SWEEPS * near, wide), jnp.float32)],
        )
        scratch = [pltpu.VMEM((SWEEPS * 2 * PAD_S, wide), jnp.float32)]
        given = (partial, left, right, section, solve_sides)
        body = functools.partial(solve_kernel, cells, second)
        if second:
            (out,) = call(
                body, [velocity.shape], *given,
                scratch=scratch + [pltpu.VMEM((components * cells, width), jnp.float32), pltpu.SemaphoreType.DMA((3 * ROWS,))],
                out_specs=[pl.BlockSpec(memory_space=pltpu.HBM)],
            )
        else:
            flat, left, right, upward, downward = call(
                body, [(components * cells, width), edge, edge, rim, rim], *given, scratch=scratch
            )
    return out


def solution(mesh):
    in_specs = (P(None, "span", "cross", None), P("span", "cross", None))
    out_specs = P(None, "span", "cross", None)
    return jax.shard_map(
        per_device, mesh=mesh, in_specs=in_specs, out_specs=out_specs, check_vma=False
    )
```

```python
import functools

import jax
import jax.numpy as jnp
import ml_dtypes
import numpy as np
from jax import lax
from jax.experimental import pallas as pl
from jax.experimental.pallas import tpu as pltpu
from jax.sharding import PartitionSpec as P

SWEEPS = 4
ROWS = 4
LANES = 128
REACH = SWEEPS + 1
time_step = 0.1
highest = lax.Precision.HIGHEST
PAD_V = 16
PAD_S = 16
PAD_M = 8
GROUP = 8
PACK = 16
RANK_V = 3
RANK_M = 2


def symbols(length):
    w = 2.0 * np.pi * np.arange(length) / length
    first = (14.0 / 9.0 * np.sin(w) + np.sin(2.0 * w) / 18.0) / (1.0 + 2.0 / 3.0 * np.cos(w))
    second = (24.0 / 11.0 * (1.0 - np.cos(w)) + 3.0 / 22.0 * (1.0 - np.cos(2.0 * w))) / (
        1.0 + 4.0 / 11.0 * np.cos(w)
    )
    return 1j * first, -second, 1.0 / (4.0 + second)


def block_of(symbol, cells, offset):
    kernel = np.fft.ifft(symbol).real
    at = np.arange(cells)
    return kernel[(at[:, None] - (at[None, :] + offset * cells)) % len(kernel)]


def low_rank(stack, rank):
    left, scale, right = np.linalg.svd(stack, full_matrices=False)
    return left[:, :rank] * scale[:rank], right[:rank]


@functools.lru_cache(None)
def tables(length, cells, last):
    first, second, inverse = symbols(length)
    at = lambda symbol, offset: block_of(symbol, cells, offset)
    from_left, take_left = low_rank(np.concatenate([at(first, -1), at(second, -1)]), RANK_V)
    from_right, take_right = low_rank(np.concatenate([at(first, 1), at(second, 1)]), RANK_V)
    own = np.concatenate([at(first, 0), at(second, 0)])
    slopes = np.zeros((3, 2 * cells, 2 * PAD_V))
    moments = np.zeros((2 * PAD_V, 3 * cells))
    for c in range(3):
        rows = slice(RANK_V * c, RANK_V * (c + 1))
        slopes[c, :, :PAD_V][:, rows] = from_left
        slopes[c, :, PAD_V:][:, rows] = from_right
        moments[rows, cells * c : cells * (c + 1)] = take_left
        moments[PAD_V:][rows, cells * c : cells * (c + 1)] = take_right
    m_left, t_left = low_rank(at(first, -1), RANK_M)
    m_right, t_right = low_rank(at(first, 1), RANK_M)
    lateral = np.zeros((cells + PAD_M, cells))
    lateral[:cells] = at(first, 0)
    lateral[cells : cells + RANK_M] = t_left
    lateral[cells + RANK_M : cells + 2 * RANK_M] = t_right
    powers = [inverse ** (j + 1) for j in range(SWEEPS)]
    stacked = [p for p in powers] + [first * p for p in powers]
    count = len(stacked)
    RANK_S = 2 * SWEEPS + (1 if last else 3)
    kept = [] if last else stacked
    s_left, q_left = low_rank(
        np.concatenate([at(p, -1) for p in stacked] + [take_left @ at(p, 0) for p in kept]), RANK_S
    )
    s_right, q_right = low_rank(
        np.concatenate([at(p, 1) for p in stacked] + [take_right @ at(p, 0) for p in kept]), RANK_S
    )
    e_left, e_right = s_left[count * cells :], s_right[count * cells :]
    source = np.zeros((8 * GROUP, cells + PAD_M))
    for side, q in enumerate((q_left, q_right)):
        rows = np.zeros((PAD_S, cells + PAD_M))
        rows[:RANK_S, :cells] = q
        at_m = cells + RANK_M * side
        rows[RANK_S : RANK_S + RANK_M, at_m : at_m + RANK_M] = np.eye(RANK_M)
        top = 4 * GROUP * side
        source[top : top + 8] = rows[:8]
        source[top + 8 : top + 12] = rows[8:12]
        source[top + 20 : top + 24] = rows[8:12]
        source[top + 24] = rows[12]
    near, wide = cells + PAD_M, 2 * PAD_S
    height = 2 * cells + (0 if last else 4 * GROUP)
    solve_own = np.zeros((height, SWEEPS * near))
    solve_sides = np.zeros((height, SWEEPS * wide))
    for j in range(SWEEPS):
        for half in range(2):
            index = half * SWEEPS + j
            rows = slice(cells * index, cells * (index + 1))
            edge = slice(RANK_V * index, RANK_V * (index + 1))
            center = at(stacked[index], 0)
            by_left, by_right = s_left[rows], s_right[rows]
            mine, sides = np.zeros((cells, near)), np.zeros((cells, wide))
            mine[:, :cells] = center
            mine[:, cells : cells + RANK_M] = by_right @ (q_right @ m_left)
            mine[:, cells + RANK_M : cells + 2 * RANK_M] = by_left @ (q_left @ m_right)
            sides[:, :RANK_S] = by_left
            sides[:, RANK_S : RANK_S + RANK_M] = center @ m_left
            sides[:, PAD_S : PAD_S + RANK_S] = by_right
            sides[:, PAD_S + RANK_S : PAD_S + RANK_S + RANK_M] = center @ m_right
            solve_own[cells * half : cells * (half + 1), near * j : near * (j + 1)] = -mine
            solve_sides[cells * half : cells * (half + 1), wide * j : wide * (j + 1)] = -sides
            for side in range(0 if last else 2):
                mine, sides = np.zeros((RANK_V, near)), np.zeros((RANK_V, wide))
                if side == 0:
                    back = take_left @ by_right @ q_right
                    mine[:, cells + RANK_M : cells + 2 * RANK_M] = take_left @ center @ m_right
                    sides[:, :RANK_S] = e_left[edge]
                else:
                    back = take_right @ by_left @ q_left
                    mine[:, cells : cells + RANK_M] = take_right @ center @ m_left
                    sides[:, PAD_S : PAD_S + RANK_S] = e_right[edge]
                mine[:, :cells] = back
                sides[:, RANK_S : RANK_S + RANK_M] = back @ m_left
                sides[:, PAD_S + RANK_S : PAD_S + RANK_S + RANK_M] = back @ m_right
                top = 2 * cells + GROUP * (2 * side + half)
                solve_own[top : top + RANK_V, near * j : near * (j + 1)] = -mine
                solve_sides[top : top + RANK_V, wide * j : wide * (j + 1)] = -sides
    rim = np.concatenate([own, from_left, from_right], axis=1)
    plain, split = (own, solve_own), (slopes, rim, moments, lateral, source, solve_sides)
    return [x.astype(np.float32) for x in plain] + [split_table(x.astype(np.float32)) for x in split]


def dot(a, b):
    return jnp.dot(a, b, precision=highest, preferred_element_type=jnp.float32)


def halves(x):
    high = x.astype(jnp.bfloat16)
    return high, (x - high.astype(jnp.float32)).astype(jnp.bfloat16)


def split_table(table):
    gap = -table.shape[-1] % PACK
    table = np.pad(table, [(0, 0)] * (table.ndim - 1) + [(0, gap)])
    high = table.astype(ml_dtypes.bfloat16)
    low = (table - high.astype(np.float32)).astype(ml_dtypes.bfloat16)
    return np.concatenate([high, high, low], axis=-1)


def split_dot(table, x):
    gap = -x.shape[0] % PACK
    if gap:
        x = jnp.concatenate([x, jnp.zeros((gap, x.shape[1]), x.dtype)], axis=0)
    high, low = halves(x)
    return jnp.dot(table, jnp.concatenate([high, low, high], axis=0), preferred_element_type=jnp.float32)


BREADTH = ROWS + 2 * REACH
PACKED = BREADTH + BREADTH // 2

DIFFERENCE = ((1, 2.0 / 3.0), (-1, -2.0 / 3.0), (2, -1.0 / 12.0), (-2, 1.0 / 12.0))
CURVE = ((1, 4.0 / 3.0), (-1, 4.0 / 3.0), (2, -1.0 / 12.0), (-2, -1.0 / 12.0))


def lane(r, count=1):
    return slice(r * LANES, (r + count) * LANES)


def turned(tile, step):
    return pltpu.roll(tile, (-step) % LANES, 1)


def edge_masks():
    at = lax.axis_index("cross")
    last = lax.axis_size("cross") - 1
    flag = lambda test: jnp.where(test, 1.0, 0.0).astype(jnp.float32)
    return (flag(at >= 1), flag(at >= 2), flag(at <= last - 1), flag(at <= last - 2))


def masked(tile, e, masks):
    if e < -ROWS:
        return tile * masks[1]
    if e < 0:
        return tile * masks[0]
    if e >= 2 * ROWS:
        return tile * masks[3]
    if e >= ROWS:
        return tile * masks[2]
    return tile


def first_diff(up_one, down_one, up_two, down_two):
    return (8.0 * (up_one - down_one) - (up_two - down_two)) * (1.0 / 12.0)


def second_diff(middle, up_one, down_one, up_two, down_two):
    return (16.0 * (up_one + down_one) - (up_two + down_two) - 30.0 * middle) * (1.0 / 12.0)


def stream_slope(tile):
    return first_diff(turned(tile, 1), turned(tile, -1), turned(tile, 2), turned(tile, -2))


def open_kernel(
    cells, velocity, viscosity, moments, flat, thick, to_right, to_left, upward, downward, weights, sems
):
    copies = [pltpu.make_async_copy(moments, weights, sems.at[0])]
    for c in range(3):
        rows = slice(cells * c, cells * (c + 1))
        for r in range(ROWS):
            copies.append(
                pltpu.make_async_copy(velocity.at[c, :, r, :], flat.at[rows, lane(r)], sems.at[len(copies)])
            )
    for r in range(ROWS):
        copies.append(pltpu.make_async_copy(viscosity.at[:, r, :], thick.at[:, lane(r)], sems.at[len(copies)]))
    for copy in copies:
        copy.start()
    for copy in copies:
        copy.wait()
    upward[: 3 * cells, :] = flat[:, lane(ROWS - 2, 2)]
    downward[: 3 * cells, :] = flat[:, lane(0, 2)]
    upward[3 * cells :, :] = thick[:, lane(ROWS - 2, 2)]
    downward[3 * cells :, :] = thick[:, lane(0, 2)]
    both = split_dot(weights[...], flat[...])
    to_right[...] = both[:PAD_V]
    to_left[...] = both[PAD_V:]


def weighed(weights, value_at, r, home):
    total = None
    for reach, factor in weights:
        if (0 <= r + reach < ROWS) == home:
            part = factor * value_at(r + reach)
            total = part if total is None else total + part
    return total


def rough_kernel(cells, second, *refs):
    if second:
        base, *refs = refs
    flat, thick, own, rough = refs
    for c in range(3):
        rows = slice(cells * c, cells * (c + 1))
        at = lambda r: flat[rows, lane(r)]
        spanned = dot(own[...], flat[rows, :])
        for r in range(ROWS):
            here = at(r)
            up_one, down_one = turned(here, 1), turned(here, -1)
            up_two, down_two = turned(here, 2), turned(here, -2)
            carried = (
                flat[:cells, lane(r)] * first_diff(up_one, down_one, up_two, down_two)
                + flat[cells : 2 * cells, lane(r)] * weighed(DIFFERENCE, at, r, True)
                + flat[2 * cells :, lane(r)] * spanned[:cells, lane(r)]
            )
            spread = (
                (4.0 / 3.0) * (up_one + down_one)
                - (1.0 / 12.0) * (up_two + down_two)
                - 5.0 * here
                + weighed(CURVE, at, r, True)
                + spanned[cells:, lane(r)]
            )
            moved = here + time_step * (thick[:, lane(r)] * spread - carried)
            if second:
                moved = 0.5 * base[rows, lane(r)] + 0.5 * moved
            rough[rows, lane(r)] = moved


def beyond_rows(cells, low, high, stacked, masks):
    def value(c, r):
        given, k = (low, r + ROWS) if r < 0 else (high, r - ROWS)
        if not stacked:
            tile = given[cells * c : cells * (c + 1), lane(k % 2)]
        else:
            slot = k if c == 1 else ROWS + c + k % 2
            tile = given[cells * slot : cells * (slot + 1), :]
        return masked(tile, r, masks)

    return value


def add_beyond(cells, scale, rough, flat, thick, left, right, slopes, beyond, section):
    sides = jnp.concatenate([left[...], right[...]], axis=0)
    for c in range(3):
        rows = slice(cells * c, cells * (c + 1))
        spanned = split_dot(slopes[c], sides)
        value = lambda r: beyond(c, r)
        for r in range(ROWS):
            spread = spanned[cells:, lane(r)] + weighed(CURVE, value, r, False)
            carried = flat[cells : 2 * cells, lane(r)] * weighed(DIFFERENCE, value, r, False)
            carried = carried + flat[2 * cells :, lane(r)] * spanned[:cells, lane(r)]
            section[rows, lane(r)] = rough[rows, lane(r)] + scale * (thick[:, lane(r)] * spread - carried)


def tendency_kernel(
    cells, rough, flat, thick, left, right, low, high, slopes, lateral,
    section, parts, up_near, down_near, up_far, down_far,
):
    beyond = beyond_rows(cells, low, high, False, edge_masks())
    add_beyond(cells, time_step, rough, flat, thick, left, right, slopes, beyond, section)
    side = split_dot(lateral[...], section[2 * cells :, :])
    span = slice(0, cells)
    at = lambda r: section[cells : 2 * cells, lane(r)]
    for r in range(ROWS):
        total = stream_slope(section[:cells, lane(r)]) + side[:cells, lane(r)]
        for reach, factor in DIFFERENCE:
            if 0 <= r + reach < ROWS:
                total = total + factor * at(r + reach)
        parts[span, lane(r)] = total
        for block in (up_near, down_near):
            block[cells * r : cells * (r + 1), :] = total
            block[7 * cells + PAD_M * r : 7 * cells + PAD_M * (r + 1), :] = side[cells:, lane(r)]
    tail = slice(cells, cells + PAD_M)
    parts[tail, :] = side[cells:]
    for far, r in ((up_far, ROWS - 1), (down_far, 0)):
        far[:cells, :] = parts[span, lane(r)]
        far[3 * cells :, :] = parts[tail, lane(r)]
    for k in range(2):
        near_rows = slice(cells * (ROWS + k), cells * (ROWS + k + 1))
        far_rows = slice(cells * (1 + k), cells * (2 + k))
        up_near[near_rows, :] = at(ROWS - 2 + k)
        up_far[far_rows, :] = at(ROWS - 2 + k)
        down_near[near_rows, :] = at(k)
        down_far[far_rows, :] = at(k)
    rest = slice(6 * cells, 7 * cells)
    up_near[rest, :] = (2.0 / 3.0) * at(0) - (1.0 / 12.0) * at(1)
    down_near[rest, :] = (1.0 / 12.0) * at(ROWS - 2) - (2.0 / 3.0) * at(ROWS - 1)


def last_tendency_kernel(
    cells, rough, flat, thick, left, right, low, high, first_low, first_high, slopes, rim, lateral,
    section, near, up_far, down_far,
):
    masks = edge_masks()
    beyond = beyond_rows(cells, low, high, True, masks)
    base = beyond_rows(cells, first_low, first_high, False, masks)
    add_beyond(cells, 0.5 * time_step, rough, flat, thick, left, right, slopes, beyond, section)
    outer = (-2, -1, ROWS, ROWS + 1)
    v1 = lambda r: flat[cells : 2 * cells, lane(r)] if 0 <= r < ROWS else beyond(1, r)

    def rim_moments(r):
        given, k = (low, r + 2) if r < 0 else (high, r - ROWS)
        return given[8 * cells + GROUP * k : 8 * cells + GROUP * (k + 1), :]

    columns = [jnp.concatenate([v1(r), rim_moments(r)], axis=0) for r in outer]
    spanned = split_dot(rim[...], jnp.concatenate(columns, axis=1))
    moved = {}
    for k, r in enumerate(outer):
        here = v1(r)
        up_one, down_one = turned(here, 1), turned(here, -1)
        up_two, down_two = turned(here, 2), turned(here, -2)
        slope = sum(factor * v1(r + reach) for reach, factor in DIFFERENCE)
        curve = sum(factor * v1(r + reach) for reach, factor in CURVE)
        carried = (
            beyond(0, r) * first_diff(up_one, down_one, up_two, down_two)
            + here * slope
            + beyond(2, r) * spanned[:cells, lane(k)]
        )
        spread = (
            (4.0 / 3.0) * (up_one + down_one)
            - (1.0 / 12.0) * (up_two + down_two)
            - 5.0 * here
            + curve
            + spanned[cells:, lane(k)]
        )
        value = 0.5 * base(1, r) + 0.5 * (here + time_step * (base(3, r) * spread - carried))
        moved[r] = masked(value, r, masks)
    side = split_dot(lateral[...], section[2 * cells :, :])
    at = lambda r: section[cells : 2 * cells, lane(r)] if 0 <= r < ROWS else moved[r]
    for r in range(ROWS):
        total = stream_slope(section[:cells, lane(r)]) + side[:cells, lane(r)]
        for reach, factor in DIFFERENCE:
            total = total + factor * at(r + reach)
        tail = slice(ROWS * cells + PAD_M * r, ROWS * cells + PAD_M * (r + 1))
        near[cells * r : cells * (r + 1), :] = total
        near[tail, :] = side[cells:, lane(r)]
        for far, row in ((up_far, ROWS - 1), (down_far, 0)):
            if r == row:
                far[:cells, :] = total
                far[cells:, :] = side[cells:, lane(r)]


def last_source_kernel(cells, near, low_one, high_one, low_two, high_two, source, ext, to_right, to_left):
    masks = edge_masks()
    span, tail = slice(0, cells), slice(cells, cells + PAD_M)
    for e in range(-REACH, ROWS + REACH):
        if e < -ROWS or e >= 2 * ROWS:
            given = low_two if e < 0 else high_two
            total, side = given[span, :], given[tail, :]
        else:
            given = low_one if e < 0 else near if e < ROWS else high_one
            r = e % ROWS
            total = given[cells * r : cells * (r + 1), :]
            side = given[ROWS * cells + PAD_M * r : ROWS * cells + PAD_M * (r + 1), :]
        ext[span, lane(e + REACH)] = masked(total, e, masks)
        ext[tail, lane(e + REACH)] = masked(side, e, masks)
    pack_moments(split_dot(source[...], ext[...]), to_right, to_left)


def pack_moments(both, to_right, to_left):
    for side, out in enumerate((to_right, to_left)):
        top = 4 * GROUP * side
        out[:, lane(0, BREADTH)] = both[top : top + 8]
        for k in range(BREADTH // 2):
            out[:, lane(BREADTH + k)] = (
                both[top + 8 : top + 16, lane(2 * k)] + both[top + 16 : top + 24, lane(2 * k + 1)]
            )


def source_kernel(
    cells, parts, section, low_one, high_one, low_two, high_two, source, moments, ext, to_right, to_left
):
    masks = edge_masks()
    span, tail = slice(0, cells), slice(cells, cells + PAD_M)
    pick = lambda ref, k: ref[cells * k : cells * (k + 1), :]

    def joined(e):
        if e < -ROWS:
            return low_two[:cells, :], low_two[3 * cells :, :]
        if e >= 2 * ROWS:
            return high_two[:cells, :], high_two[3 * cells :, :]
        if 0 <= e < ROWS:
            return parts[span, lane(e)], parts[tail, lane(e)]
        near, r = (low_one, e + ROWS) if e < 0 else (high_one, e - ROWS)
        top = 7 * cells + PAD_M * r
        return pick(near, r), near[top : top + PAD_M, :]

    def across(e, home):
        if e // ROWS == home // ROWS or home // ROWS in (-2, 2):
            return None
        if e < -ROWS:
            return masked(pick(low_two, 1 + e + ROWS + 2), e, masks)
        if e < 0:
            return masked(pick(low_one, ROWS + e + 2), e, masks)
        if e < ROWS:
            return section[cells : 2 * cells, lane(e)]
        if e < 2 * ROWS:
            return masked(pick(high_one, e), e, masks)
        return masked(pick(high_two, 1 + e - 2 * ROWS), e, masks)

    for e in range(-REACH, ROWS + REACH):
        total, side = joined(e)
        if e == -REACH:
            total = total + pick(low_one, 6)
        if e == ROWS + REACH - 1:
            total = total + pick(high_one, 6)
        for reach, factor in DIFFERENCE:
            other = across(e + reach, e)
            if other is not None:
                total = total + factor * other
        ext[span, lane(e + REACH)] = masked(total, e, masks)
        ext[tail, lane(e + REACH)] = masked(side, e, masks)
    both = split_dot(source[...], ext[...])
    pack_moments(both, to_right, to_left)
    held = split_dot(moments[...], section[...])
    for side, out in enumerate((to_right, to_left)):
        top, base = 4 * GROUP * side, PAD_V * side
        out[:, lane(PACKED, ROWS)] = held[base : base + 8]
        out[:, lane(PACKED + ROWS, 3)] = jnp.zeros((GROUP, 3 * LANES), jnp.float32)
        for e in range(BREADTH + ROWS):
            value = (
                both[top + 24 : top + 25, lane(e)]
                if e < BREADTH
                else held[base + 8 : base + 9, lane(e - BREADTH)]
            )
            row, tile = e % GROUP, PACKED + ROWS + e // GROUP
            out[row : row + 1, lane(tile)] = value


def climb(levels, depth, masks):
    for j in range(1, SWEEPS):
        before = slice(depth * (j - 1), depth * j)
        after = slice(depth * j, depth * (j + 1))
        for e in range(-REACH + j, ROWS + REACH - j):
            here = levels[before, lane(e + REACH)]
            beside = (
                turned(here, 1)
                + turned(here, -1)
                + levels[before, lane(e + REACH + 1)]
                + levels[before, lane(e + REACH - 1)]
            )
            levels[after, lane(e + REACH)] = masked(beside, e, masks)
    return levels[:, lane(REACH - 2, ROWS + 4)]


def home_kernel(ext, solve, partial, levels):
    depth = ext.shape[0]
    levels[:depth, :] = ext[...]
    partial[...] = dot(solve[...], climb(levels, depth, edge_masks()))


def solve_kernel(cells, last, partial, left, right, section, solve, *refs):
    if last:
        out, levels, staged, sems = refs
    else:
        flat, next_left, next_right, upward, downward, levels = refs
    masks = edge_masks()

    def spare(given, e):
        row, tile = e % GROUP, PACKED + ROWS + e // GROUP
        return given[row : row + 1, lane(tile)]

    for side, given in enumerate((left, right)):
        top = PAD_S * side
        levels[top : top + 8, :] = given[:, lane(0, BREADTH)]
        for e in range(BREADTH):
            tile = given[:, lane(BREADTH + e // 2)]
            levels[top + 8 : top + 16, lane(e)] = pltpu.roll(tile, 4, 0) if e % 2 else tile
            if not last:
                levels[top + 12 : top + 13, lane(e)] = spare(given, e)
    found = partial[...] + split_dot(solve[...], climb(levels, 2 * PAD_S, masks))

    def slope(c, rows, slope_rows, r):
        phi = lambda r: masked(found[rows, lane(r + 2)], r, masks)
        if c == 0:
            return stream_slope(phi(r))
        if c == 1:
            return first_diff(phi(r + 1), phi(r - 1), phi(r + 2), phi(r - 2))
        return found[slope_rows, lane(r + 2)]

    copies = []
    for c in range(3):
        rows = slice(cells * c, cells * (c + 1))
        for r in range(ROWS):
            value = section[rows, lane(r)] - slope(c, slice(0, cells), slice(cells, 2 * cells), r)
            if last:
                staged[rows, lane(r)] = value
                copies.append(
                    pltpu.make_async_copy(staged.at[rows, lane(r)], out.at[c, :, r, :], sems.at[len(copies)])
                )
                copies[-1].start()
                continue
            flat[rows, lane(r)] = value
            if c == 1:
                upward[cells * r : cells * (r + 1), :] = value
                downward[cells * r : cells * (r + 1), :] = value
            else:
                slot = ROWS + c + r % 2
                target = downward if r < 2 else upward
                target[cells * slot : cells * (slot + 1), :] = value
    for copy in copies:
        copy.wait()
    if not last:
        for side, (given, target) in enumerate(((left, next_left), (right, next_right))):
            top = 2 * cells + 2 * GROUP * side
            phi_rows, slope_rows = slice(top, top + GROUP), slice(top + GROUP, top + 2 * GROUP)
            target[:GROUP, :] = given[:, lane(PACKED, ROWS)]
            target[GROUP:, :] = jnp.zeros((PAD_V - GROUP, ROWS * LANES), jnp.float32)
            for r in range(ROWS):
                target[GROUP : GROUP + 1, lane(r)] = spare(given, BREADTH + r)
                for c in range(3):
                    rows = slice(RANK_V * c, RANK_V * (c + 1))
                    target[rows, lane(r)] = target[rows, lane(r)] - slope(c, phi_rows, slope_rows, r)[:RANK_V]
        for sent, first in ((downward, 0), (upward, ROWS - 2)):
            sent[8 * cells :, :] = jnp.zeros((2 * GROUP, LANES), jnp.float32)
            for k in range(2):
                top = 8 * cells + GROUP * k
                sent[top : top + RANK_V, :] = next_left[RANK_V : 2 * RANK_V, lane(first + k)]
                sent[top + RANK_V : top + 2 * RANK_V, :] = next_right[RANK_V : 2 * RANK_V, lane(first + k)]


def call(body, shapes, *args, scratch=(), **options):
    return pl.pallas_call(
        body,
        out_shape=[jax.ShapeDtypeStruct(s, jnp.float32) for s in shapes],
        scratch_shapes=scratch,
        compiler_params=pltpu.CompilerParams(vmem_limit_bytes=40 * 1024 * 1024),
        **options,
    )(*args)


def shifted(block, axis, step):
    count = lax.axis_size(axis)
    return lax.ppermute(block, axis, [(i, (i + step) % count) for i in range(count)])


def per_device(velocity, viscosity):
    components, cells, row_cells, columns = velocity.shape
    length = cells * lax.axis_size("span")
    own, first_own, slopes, rim, moments, lateral, *first = (
        jnp.asarray(t) for t in tables(length, cells, False)
    )
    _, last_own, _, _, _, _, *last = (jnp.asarray(t) for t in tables(length, cells, True))
    width = row_cells * columns
    wide = (row_cells + 2 * REACH) * columns
    near = cells + PAD_M
    whole, edge = (components * cells, width), (PAD_V, width)
    start, thick, to_right, to_left, upward, downward = call(
        functools.partial(open_kernel, cells),
        [whole, (cells, width), edge, edge] + [((components + 1) * cells, 2 * columns)] * 2,
        *(pltpu.with_memory_space_constraint(x, pltpu.HBM) for x in (velocity, viscosity, moments)),
        in_specs=[pl.BlockSpec(memory_space=pltpu.HBM)] * 3,
        scratch=[pltpu.VMEM(moments.shape, moments.dtype), pltpu.SemaphoreType.DMA((1 + 4 * ROWS,))],
    )
    left = shifted(to_right, "span", 1)
    right = shifted(to_left, "span", -1)
    first_low = shifted(upward, "cross", 1)
    first_high = shifted(downward, "cross", -1)

    (rough,) = call(functools.partial(rough_kernel, cells, False), [whole], start, thick, own)
    section, parts, up_near, down_near, up_far, down_far = call(
        functools.partial(tendency_kernel, cells),
        [whole, (near, width)]
        + [(7 * cells + 4 * PAD_M, columns)] * 2
        + [(3 * cells + PAD_M, columns)] * 2,
        rough, start, thick, left, right, first_low, first_high, slopes, lateral,
    )
    low_one = shifted(up_near, "cross", 1)
    high_one = shifted(down_near, "cross", -1)
    low_two = shifted(up_far, "cross", 2)
    high_two = shifted(down_far, "cross", -2)
    ext, to_right, to_left = call(
        functools.partial(source_kernel, cells),
        [(near, wide)] + [(GROUP, (PACKED + ROWS + 3) * columns)] * 2,
        parts, section, low_one, high_one, low_two, high_two, first[0], moments,
    )
    levels = pltpu.VMEM((SWEEPS * near, wide), jnp.float32)
    side_levels = pltpu.VMEM((SWEEPS * 2 * PAD_S, wide), jnp.float32)
    found = (row_cells + 4) * columns
    left = shifted(to_right, "span", 1)
    right = shifted(to_left, "span", -1)
    (partial,) = call(home_kernel, [(first_own.shape[0], found)], ext, first_own, scratch=[levels])
    flat, left, right, upward, downward = call(
        functools.partial(solve_kernel, cells, False),
        [whole, edge, edge] + [(8 * cells + 2 * GROUP, columns)] * 2,
        partial, left, right, section, first[1],
        scratch=[side_levels],
    )

    low = shifted(upward, "cross", 1)
    high = shifted(downward, "cross", -1)
    (rough,) = call(functools.partial(rough_kernel, cells, True), [whole], start, flat, thick, own)
    section, sent, up_far, down_far = call(
        functools.partial(last_tendency_kernel, cells),
        [whole, (row_cells * near, columns)] + [(near, columns)] * 2,
        rough, flat, thick, left, right, low, high, first_low, first_high, slopes, rim, lateral,
    )
    low_one = shifted(sent, "cross", 1)
    high_one = shifted(sent, "cross", -1)
    low_two = shifted(up_far, "cross", 2)
    high_two = shifted(down_far, "cross", -2)
    ext, to_right, to_left = call(
        functools.partial(last_source_kernel, cells),
        [(near, wide)] + [(GROUP, PACKED * columns)] * 2,
        sent, low_one, high_one, low_two, high_two, last[0],
    )
    left = shifted(to_right, "span", 1)
    right = shifted(to_left, "span", -1)
    (partial,) = call(home_kernel, [(last_own.shape[0], found)], ext, last_own, scratch=[levels])
    (out,) = call(
        functools.partial(solve_kernel, cells, True),
        [velocity.shape],
        partial, left, right, section, last[1],
        scratch=[side_levels, pltpu.VMEM(whole, jnp.float32), pltpu.SemaphoreType.DMA((3 * ROWS,))],
        out_specs=[pl.BlockSpec(memory_space=pltpu.HBM)],
    )
    return out


def solution(mesh):
    in_specs = (P(None, "span", "cross", None), P("span", "cross", None))
    out_specs = P(None, "span", "cross", None)
    return jax.shard_map(
        per_device, mesh=mesh, in_specs=in_specs, out_specs=out_specs, check_vma=False
    )
```

```python
import functools

import jax
import jax.numpy as jnp
import ml_dtypes
import numpy as np
from jax import lax
from jax.experimental import pallas as pl
from jax.experimental.pallas import tpu as pltpu
from jax.sharding import PartitionSpec as P

SWEEPS = 4
ROWS = 4
LANES = 128
time_step = 0.1
highest = lax.Precision.HIGHEST
PAD_V = 16
PAD_S = 16
PAD_M = 8
GROUP = 8
PACK = 16
RANK_V = 3
RANK_M = 2


def symbols(length):
    w = 2.0 * np.pi * np.arange(length) / length
    first = (14.0 / 9.0 * np.sin(w) + np.sin(2.0 * w) / 18.0) / (1.0 + 2.0 / 3.0 * np.cos(w))
    second = (24.0 / 11.0 * (1.0 - np.cos(w)) + 3.0 / 22.0 * (1.0 - np.cos(2.0 * w))) / (
        1.0 + 4.0 / 11.0 * np.cos(w)
    )
    return 1j * first, -second, 1.0 / (4.0 + second)


def block_of(symbol, cells, offset):
    kernel = np.fft.ifft(symbol).real
    at = np.arange(cells)
    return kernel[(at[:, None] - (at[None, :] + offset * cells)) % len(kernel)]


def low_rank(stack, rank):
    left, scale, right = np.linalg.svd(stack, full_matrices=False)
    return left[:, :rank] * scale[:rank], right[:rank]


@functools.lru_cache(None)
def tables(length, cells, last):
    first, second, inverse = symbols(length)
    at = lambda symbol, offset: block_of(symbol, cells, offset)
    from_left, take_left = low_rank(np.concatenate([at(first, -1), at(second, -1)]), RANK_V)
    from_right, take_right = low_rank(np.concatenate([at(first, 1), at(second, 1)]), RANK_V)
    own = np.concatenate([at(first, 0), at(second, 0)])
    slopes = np.zeros((3, 2 * cells, 2 * PAD_V))
    moments = np.zeros((2 * PAD_V, 3 * cells))
    for c in range(3):
        rows = slice(RANK_V * c, RANK_V * (c + 1))
        slopes[c, :, :PAD_V][:, rows] = from_left
        slopes[c, :, PAD_V:][:, rows] = from_right
        moments[rows, cells * c : cells * (c + 1)] = take_left
        moments[PAD_V:][rows, cells * c : cells * (c + 1)] = take_right
    m_left, t_left = low_rank(at(first, -1), RANK_M)
    m_right, t_right = low_rank(at(first, 1), RANK_M)
    lateral = np.zeros((cells + PAD_M, cells))
    lateral[:cells] = at(first, 0)
    lateral[cells : cells + RANK_M] = t_left
    lateral[cells + RANK_M : cells + 2 * RANK_M] = t_right
    powers = [inverse ** (j + 1) for j in range(SWEEPS)]
    stacked = [p for p in powers] + [first * p for p in powers]
    count = len(stacked)
    RANK_S = 2 * SWEEPS + (1 if last else 3)
    kept = [] if last else stacked
    s_left, q_left = low_rank(
        np.concatenate([at(p, -1) for p in stacked] + [take_left @ at(p, 0) for p in kept]), RANK_S
    )
    s_right, q_right = low_rank(
        np.concatenate([at(p, 1) for p in stacked] + [take_right @ at(p, 0) for p in kept]), RANK_S
    )
    e_left, e_right = s_left[count * cells :], s_right[count * cells :]
    source = np.zeros((8 * GROUP, cells + PAD_M))
    for side, q in enumerate((q_left, q_right)):
        rows = np.zeros((PAD_S, cells + PAD_M))
        rows[:RANK_S, :cells] = q
        at_m = cells + RANK_M * side
        rows[RANK_S : RANK_S + RANK_M, at_m : at_m + RANK_M] = np.eye(RANK_M)
        top = 4 * GROUP * side
        source[top : top + 8] = rows[:8]
        source[top + 8 : top + 12] = rows[8:12]
        source[top + 20 : top + 24] = rows[8:12]
        source[top + 24] = rows[12]
    near, wide = cells + PAD_M, 2 * PAD_S
    height = 2 * cells + (0 if last else 4 * GROUP)
    solve_own = np.zeros((height, SWEEPS * near))
    solve_sides = np.zeros((height, SWEEPS * wide))
    for j in range(SWEEPS):
        for half in range(2):
            index = half * SWEEPS + j
            rows = slice(cells * index, cells * (index + 1))
            edge = slice(RANK_V * index, RANK_V * (index + 1))
            center = at(stacked[index], 0)
            by_left, by_right = s_left[rows], s_right[rows]
            mine, sides = np.zeros((cells, near)), np.zeros((cells, wide))
            mine[:, :cells] = center
            mine[:, cells : cells + RANK_M] = by_right @ (q_right @ m_left)
            mine[:, cells + RANK_M : cells + 2 * RANK_M] = by_left @ (q_left @ m_right)
            sides[:, :RANK_S] = by_left
            sides[:, RANK_S : RANK_S + RANK_M] = center @ m_left
            sides[:, PAD_S : PAD_S + RANK_S] = by_right
            sides[:, PAD_S + RANK_S : PAD_S + RANK_S + RANK_M] = center @ m_right
            solve_own[cells * half : cells * (half + 1), near * j : near * (j + 1)] = -mine
            solve_sides[cells * half : cells * (half + 1), wide * j : wide * (j + 1)] = -sides
            for side in range(0 if last else 2):
                mine, sides = np.zeros((RANK_V, near)), np.zeros((RANK_V, wide))
                if side == 0:
                    back = take_left @ by_right @ q_right
                    mine[:, cells + RANK_M : cells + 2 * RANK_M] = take_left @ center @ m_right
                    sides[:, :RANK_S] = e_left[edge]
                else:
                    back = take_right @ by_left @ q_left
                    mine[:, cells : cells + RANK_M] = take_right @ center @ m_left
                    sides[:, PAD_S : PAD_S + RANK_S] = e_right[edge]
                mine[:, :cells] = back
                sides[:, RANK_S : RANK_S + RANK_M] = back @ m_left
                sides[:, PAD_S + RANK_S : PAD_S + RANK_S + RANK_M] = back @ m_right
                top = 2 * cells + GROUP * (2 * side + half)
                solve_own[top : top + RANK_V, near * j : near * (j + 1)] = -mine
                solve_sides[top : top + RANK_V, wide * j : wide * (j + 1)] = -sides
    full = np.concatenate([np.broadcast_to(own, (3,) + own.shape), slopes], axis=2)
    plain, split = (own, solve_own), (slopes, full, moments, lateral, source, solve_sides)
    return [x.astype(np.float32) for x in plain] + [split_table(x.astype(np.float32)) for x in split]


def dot(a, b):
    return jnp.dot(a, b, precision=highest, preferred_element_type=jnp.float32)


def halves(x):
    high = x.astype(jnp.bfloat16)
    return high, (x - high.astype(jnp.float32)).astype(jnp.bfloat16)


def split_table(table):
    gap = -table.shape[-1] % PACK
    table = np.pad(table, [(0, 0)] * (table.ndim - 1) + [(0, gap)])
    high = table.astype(ml_dtypes.bfloat16)
    low = (table - high.astype(np.float32)).astype(ml_dtypes.bfloat16)
    return np.concatenate([high, high, low], axis=-1)


def split_dot(table, x):
    gap = -x.shape[0] % PACK
    if gap:
        x = jnp.concatenate([x, jnp.zeros((gap, x.shape[1]), x.dtype)], axis=0)
    high, low = halves(x)
    return jnp.dot(table, jnp.concatenate([high, low, high], axis=0), preferred_element_type=jnp.float32)


class Extent:
    def __init__(self, margin):
        self.margin = margin
        self.reach = margin + SWEEPS - 1
        self.breadth = ROWS + 2 * self.reach
        self.packed = self.breadth + self.breadth // 2
        self.found = ROWS + 2 * margin


FIRST, LAST = Extent(3), Extent(2)


DIFFERENCE = ((1, 2.0 / 3.0), (-1, -2.0 / 3.0), (2, -1.0 / 12.0), (-2, 1.0 / 12.0))
CURVE = ((1, 4.0 / 3.0), (-1, 4.0 / 3.0), (2, -1.0 / 12.0), (-2, -1.0 / 12.0))


def lane(r, count=1):
    return slice(r * LANES, (r + count) * LANES)


def turned(tile, step):
    return pltpu.roll(tile, (-step) % LANES, 1)


def edge_masks():
    at = lax.axis_index("cross")
    last = lax.axis_size("cross") - 1
    flag = lambda test: jnp.where(test, 1.0, 0.0).astype(jnp.float32)
    return (flag(at >= 1), flag(at >= 2), flag(at <= last - 1), flag(at <= last - 2))


def masked(tile, e, masks):
    if e < -ROWS:
        return tile * masks[1]
    if e < 0:
        return tile * masks[0]
    if e >= 2 * ROWS:
        return tile * masks[3]
    if e >= ROWS:
        return tile * masks[2]
    return tile


def first_diff(up_one, down_one, up_two, down_two):
    return (8.0 * (up_one - down_one) - (up_two - down_two)) * (1.0 / 12.0)


def second_diff(middle, up_one, down_one, up_two, down_two):
    return (16.0 * (up_one + down_one) - (up_two + down_two) - 30.0 * middle) * (1.0 / 12.0)


def stream_slope(tile):
    return first_diff(turned(tile, 1), turned(tile, -1), turned(tile, 2), turned(tile, -2))


def open_kernel(
    cells, velocity, viscosity, moments, flat, thick, to_right, to_left, upward, downward, weights, sems
):
    copies = [pltpu.make_async_copy(moments, weights, sems.at[0])]
    for c in range(3):
        rows = slice(cells * c, cells * (c + 1))
        for r in range(ROWS):
            copies.append(
                pltpu.make_async_copy(velocity.at[c, :, r, :], flat.at[rows, lane(r)], sems.at[len(copies)])
            )
    apart = len(copies)
    for r in range(ROWS):
        copies.append(pltpu.make_async_copy(viscosity.at[:, r, :], thick.at[:, lane(r)], sems.at[len(copies)]))
    for copy in copies:
        copy.start()
    for copy in copies[:apart]:
        copy.wait()
    upward[...] = flat[:, lane(ROWS - 2, 2)]
    downward[...] = flat[:, lane(0, 2)]
    both = split_dot(weights[...], flat[...])
    to_right[...] = both[:PAD_V]
    to_left[...] = both[PAD_V:]
    for copy in copies[apart:]:
        copy.wait()


def weighed(weights, value_at, r, home):
    total = None
    for reach, factor in weights:
        if (0 <= r + reach < ROWS) == home:
            part = factor * value_at(r + reach)
            total = part if total is None else total + part
    return total


def rough_kernel(cells, flat, thick, own, rough):
    for c in range(3):
        rows = slice(cells * c, cells * (c + 1))
        at = lambda r: flat[rows, lane(r)]
        spanned = dot(own[...], flat[rows, :])
        for r in range(ROWS):
            here = at(r)
            up_one, down_one = turned(here, 1), turned(here, -1)
            up_two, down_two = turned(here, 2), turned(here, -2)
            carried = (
                flat[:cells, lane(r)] * first_diff(up_one, down_one, up_two, down_two)
                + flat[cells : 2 * cells, lane(r)] * weighed(DIFFERENCE, at, r, True)
                + flat[2 * cells :, lane(r)] * spanned[:cells, lane(r)]
            )
            spread = (
                (4.0 / 3.0) * (up_one + down_one)
                - (1.0 / 12.0) * (up_two + down_two)
                - 5.0 * here
                + weighed(CURVE, at, r, True)
                + spanned[cells:, lane(r)]
            )
            rough[rows, lane(r)] = here + time_step * (thick[:, lane(r)] * spread - carried)


def add_beyond(cells, rough, flat, thick, left, right, low, high, slopes, section):
    masks = edge_masks()
    sides = jnp.concatenate([left[...], right[...]], axis=0)
    for c in range(3):
        rows = slice(cells * c, cells * (c + 1))
        spanned = split_dot(slopes[c], sides)

        def beyond(r):
            if r < 0:
                return masked(low[rows, lane(r + 2)], r, masks)
            return masked(high[rows, lane(r - ROWS)], r, masks)

        for r in range(ROWS):
            spread = spanned[cells:, lane(r)] + weighed(CURVE, beyond, r, False)
            carried = flat[cells : 2 * cells, lane(r)] * weighed(DIFFERENCE, beyond, r, False)
            carried = carried + flat[2 * cells :, lane(r)] * spanned[:cells, lane(r)]
            section[rows, lane(r)] = rough[rows, lane(r)] + time_step * (thick[:, lane(r)] * spread - carried)


def slot(ref, cells, k):
    return ref.at[cells * k : cells * (k + 1), :]


def fill_slots(ref, cells, blocks, moments):
    for k, block in enumerate(blocks):
        slot(ref, cells, k)[...] = block
    for k, block in enumerate(moments):
        top = cells * len(blocks) + PAD_M * k
        ref[top : top + PAD_M, :] = block


def own_source(cells, section, lateral, parts):
    side = split_dot(lateral[...], section[2 * cells :, :])
    at = lambda r: section[cells : 2 * cells, lane(r)]
    blocks = []
    for r in range(ROWS):
        total = stream_slope(section[:cells, lane(r)]) + side[:cells, lane(r)] + weighed(DIFFERENCE, at, r, True)
        parts[:cells, lane(r)] = total
        blocks.append(total)
    parts[cells:, :] = side[cells:]
    moments = [side[cells:, lane(r)] for r in range(ROWS)]
    up = (2.0 / 3.0) * at(0) - (1.0 / 12.0) * at(1)
    down = (1.0 / 12.0) * at(ROWS - 2) - (2.0 / 3.0) * at(ROWS - 1)
    return blocks, moments, at, up, down


def tendency_kernel(
    cells, rough, flat, thick, left, right, low, high, slopes, lateral,
    section, parts, up_near, down_near, up_far, down_far,
):
    add_beyond(cells, rough, flat, thick, left, right, low, high, slopes, section)
    blocks, moments, at, up, down = own_source(cells, section, lateral, parts)
    row = lambda c, r: section[cells * c : cells * (c + 1), lane(r)]
    fill_slots(
        up_near, cells,
        blocks + [at(2), at(3), up, at(0), row(0, 2), row(0, 3), row(2, 2), row(2, 3)], moments,
    )
    fill_slots(
        down_near, cells,
        blocks + [at(0), at(1), down, at(3), row(0, 0), row(0, 1), row(2, 0), row(2, 1)], moments,
    )
    fill_slots(up_far, cells, blocks[2:] + [at(2), at(3)], moments[2:])
    fill_slots(down_far, cells, blocks[:2] + [at(0), at(1)], moments[:2])


def extend_source(cells, extent, near_slots, far_slots, parts, section, arrived, extra, ext):
    low_one, high_one, low_two, high_two = arrived
    masks = edge_masks()
    span, tail = slice(0, cells), slice(cells, cells + PAD_M)
    outer = extent.reach - ROWS
    pick = lambda ref, k: slot(ref, cells, k)[...]

    def joined(e):
        if 0 <= e < ROWS:
            return parts[span, lane(e)], parts[tail, lane(e)]
        if e < -ROWS or e >= 2 * ROWS:
            given, k, count = (low_two, e + extent.reach, far_slots) if e < 0 else (high_two, e - 2 * ROWS, far_slots)
        else:
            given, k, count = (low_one, e + ROWS, near_slots) if e < 0 else (high_one, e - ROWS, near_slots)
        top = count * cells + PAD_M * k
        return pick(given, k), given[top : top + PAD_M, :]

    def across(e, home):
        if e // ROWS == home // ROWS or home // ROWS in (-2, 2):
            return None
        if e < -ROWS:
            return masked(pick(low_two, outer + e + ROWS + 2), e, masks)
        if e < 0:
            return masked(pick(low_one, ROWS + e + 2), e, masks)
        if e < ROWS:
            return section[cells : 2 * cells, lane(e)]
        if e < 2 * ROWS:
            return masked(pick(high_one, e), e, masks)
        return masked(pick(high_two, outer + e - 2 * ROWS), e, masks)

    for e in range(-extent.reach, ROWS + extent.reach):
        total, side = joined(e)
        if e == -ROWS - 1:
            total = total + pick(low_one, 6)
        if e == -ROWS - 2:
            total = total - (1.0 / 12.0) * pick(low_one, 7)
        if e == 2 * ROWS:
            total = total + pick(high_one, 6)
        if e == 2 * ROWS + 1:
            total = total + (1.0 / 12.0) * pick(high_one, 7)
        for reach, factor in DIFFERENCE:
            other = across(e + reach, e)
            if other is not None:
                total = total + factor * other
            if e + reach in extra:
                total = total + factor * extra[e + reach]
        ext[span, lane(e + extent.reach)] = masked(total, e, masks)
        ext[tail, lane(e + extent.reach)] = masked(side, e, masks)


def pack_moments(extent, both, to_right, to_left):
    for side, out in enumerate((to_right, to_left)):
        top = 4 * GROUP * side
        out[:, lane(0, extent.breadth)] = both[top : top + 8]
        for k in range(extent.breadth // 2):
            out[:, lane(extent.breadth + k)] = (
                both[top + 8 : top + 16, lane(2 * k)] + both[top + 16 : top + 24, lane(2 * k + 1)]
            )


def source_kernel(
    cells, parts, section, low_one, high_one, low_two, high_two, source, moments, ext, to_right, to_left
):
    extend_source(cells, FIRST, 12, 4, parts, section, (low_one, high_one, low_two, high_two), {}, ext)
    both = split_dot(source[...], ext[...])
    pack_moments(FIRST, both, to_right, to_left)
    held = split_dot(moments[...], section[...])
    for side, out in enumerate((to_right, to_left)):
        top, base = 4 * GROUP * side, PAD_V * side
        out[:, lane(FIRST.packed, ROWS)] = held[base : base + 8]
        out[:, lane(FIRST.packed + ROWS, 3)] = jnp.zeros((GROUP, 3 * LANES), jnp.float32)
        for e in range(FIRST.breadth + ROWS):
            value = (
                both[top + 24 : top + 25, lane(e)]
                if e < FIRST.breadth
                else held[base + 8 : base + 9, lane(e - FIRST.breadth)]
            )
            row, tile = e % GROUP, FIRST.packed + ROWS + e // GROUP
            out[row : row + 1, lane(tile)] = value


def last_source_kernel(
    cells, parts, section, mine, low_one, high_one, low_two, high_two, source, ext, fixed, to_right, to_left
):
    masks = edge_masks()
    pick = lambda ref, k: slot(ref, cells, k)[...]
    phi_first, phi_last, factor_first, factor_last = 7, 8, 9, 10
    below, above = masks[0], masks[2]
    below_two, above_two = masks[1], masks[3]
    extra = {
        0: pick(mine, factor_first) * pick(low_one, phi_first) * below,
        ROWS - 1: pick(mine, factor_last) * pick(high_one, phi_last) * above,
        -1: pick(low_one, factor_last) * pick(mine, phi_last) * below,
        -ROWS: pick(low_one, factor_first) * pick(low_two, 4) * below_two,
        -ROWS - 1: pick(low_two, 3) * pick(low_one, phi_last) * below_two,
        ROWS: pick(high_one, factor_first) * pick(mine, phi_first) * above,
        2 * ROWS - 1: pick(high_one, factor_last) * pick(high_two, 4) * above_two,
        2 * ROWS: pick(high_two, 3) * pick(high_one, phi_first) * above_two,
    }
    fixed[:cells, :] = extra[0]
    fixed[cells:, :] = extra[ROWS - 1]
    extend_source(cells, LAST, 11, 5, parts, section, (low_one, high_one, low_two, high_two), extra, ext)
    pack_moments(LAST, split_dot(source[...], ext[...]), to_right, to_left)


def climb(extent, levels, depth):
    masks = edge_masks()
    for j in range(1, SWEEPS):
        before = slice(depth * (j - 1), depth * j)
        after = slice(depth * j, depth * (j + 1))
        for e in range(-extent.reach + j, ROWS + extent.reach - j):
            k = e + extent.reach
            here = levels[before, lane(k)]
            beside = (
                turned(here, 1) + turned(here, -1) + levels[before, lane(k + 1)] + levels[before, lane(k - 1)]
            )
            levels[after, lane(k)] = masked(beside, e, masks)
    return levels[:, lane(SWEEPS - 1, extent.found)]


def home_kernel(extent, ext, solve, partial, levels):
    depth = ext.shape[0]
    levels[:depth, :] = ext[...]
    partial[...] = dot(solve[...], climb(extent, levels, depth))


def spare(given, e):
    row, tile = e % GROUP, FIRST.packed + ROWS + e // GROUP
    return given[row : row + 1, lane(tile)]


def finish(extent, partial, left, right, solve, levels):
    for side, given in enumerate((left, right)):
        top = PAD_S * side
        levels[top : top + 8, :] = given[:, lane(0, extent.breadth)]
        for e in range(extent.breadth):
            tile = given[:, lane(extent.breadth + e // 2)]
            levels[top + 8 : top + 16, lane(e)] = pltpu.roll(tile, 4, 0) if e % 2 else tile
            if extent is FIRST:
                levels[top + 12 : top + 13, lane(e)] = spare(given, e)
    return partial[...] + split_dot(solve[...], climb(extent, levels, 2 * PAD_S))


def gradient(extent, found, c, rows, slope_rows, r):
    masks = edge_masks()
    phi = lambda r: masked(found[rows, lane(r + extent.margin)], r, masks)
    if c == 0:
        return stream_slope(phi(r))
    if c == 1:
        inside = lambda r: -extent.margin <= r < ROWS + extent.margin
        return sum(factor * phi(r + reach) for reach, factor in DIFFERENCE if inside(r + reach))
    return found[slope_rows, lane(r + extent.margin)]


def middle_kernel(
    cells, partial, left, right, section, solve, low_one, high_one, start, thick, full, lateral,
    following, parts, up_near, down_near, up_far, down_far, levels, flat, rim, sides,
):
    masks = edge_masks()
    found = finish(FIRST, partial, left, right, solve, levels)
    home, home_slope = slice(0, cells), slice(cells, 2 * cells)
    outer = (-2, -1, ROWS, ROWS + 1)
    for c in range(3):
        rows = slice(cells * c, cells * (c + 1))
        for r in range(ROWS):
            flat[rows, lane(r)] = section[rows, lane(r)] - gradient(FIRST, found, c, home, home_slope, r)
        first = (8, 4, 10)[c]
        for k, r in enumerate(outer):
            value = slot(low_one if r < 0 else high_one, cells, first + k % 2)[...]
            value = value - gradient(FIRST, found, c, home, home_slope, r)
            rim[rows, lane(k)] = masked(value, r, masks)
    for side, given in enumerate((left, right)):
        base, top = PAD_V * side, 2 * cells + 2 * GROUP * side
        phi_rows, slope_rows = slice(top, top + GROUP), slice(top + GROUP, top + 2 * GROUP)
        sides[base : base + GROUP, :] = given[:, lane(FIRST.packed, ROWS)]
        sides[base + GROUP : base + PAD_V, :] = jnp.zeros((PAD_V - GROUP, ROWS * LANES), jnp.float32)
        for r in range(ROWS):
            sides[base + GROUP : base + GROUP + 1, lane(r)] = spare(given, FIRST.breadth + r)
            for c in range(3):
                rows = slice(base + RANK_V * c, base + RANK_V * (c + 1))
                change = gradient(FIRST, found, c, phi_rows, slope_rows, r)[:RANK_V]
                sides[rows, lane(r)] = sides[rows, lane(r)] - change

    def tile(c, r):
        rows = slice(cells * c, cells * (c + 1))
        return flat[rows, lane(r)] if 0 <= r < ROWS else rim[rows, lane(r + 2 if r < 0 else r - 2)]

    for c in range(3):
        rows = slice(cells * c, cells * (c + 1))
        spanned = split_dot(full[c], jnp.concatenate([flat[rows, :], sides[...]], axis=0))
        for r in range(ROWS):
            here = tile(c, r)
            up_one, down_one = turned(here, 1), turned(here, -1)
            up_two, down_two = turned(here, 2), turned(here, -2)
            carried = (
                tile(0, r) * first_diff(up_one, down_one, up_two, down_two)
                + tile(1, r) * sum(factor * tile(c, r + reach) for reach, factor in DIFFERENCE)
                + tile(2, r) * spanned[:cells, lane(r)]
            )
            spread = (
                (4.0 / 3.0) * (up_one + down_one)
                - (1.0 / 12.0) * (up_two + down_two)
                - 5.0 * here
                + sum(factor * tile(c, r + reach) for reach, factor in CURVE)
                + spanned[cells:, lane(r)]
            )
            moved = here + time_step * (thick[:, lane(r)] * spread - carried)
            following[rows, lane(r)] = 0.5 * start[rows, lane(r)] + 0.5 * moved
    blocks, moments, at, up, down = own_source(cells, following, lateral, parts)
    phi = lambda r: found[:cells, lane(r + FIRST.margin)]
    scale = 0.5 * time_step / 144.0
    first = scale * (thick[:, lane(0)] + tile(1, 0))
    last = scale * (tile(1, ROWS - 1) - thick[:, lane(ROWS - 1)])
    owed = [phi(0), phi(ROWS - 1), first, last]
    fill_slots(up_near, cells, blocks + [at(2), at(3), up] + owed, moments)
    fill_slots(down_near, cells, blocks + [at(0), at(1), down] + owed, moments)
    fill_slots(up_far, cells, [blocks[3], at(2), at(3), last, phi(0)], moments[3:])
    fill_slots(down_far, cells, [blocks[0], at(0), at(1), first, phi(ROWS - 1)], moments[:1])


def last_kernel(cells, partial, left, right, section, fixed, solve, out, levels, staged, sems):
    found = finish(LAST, partial, left, right, solve, levels)
    copies = []
    for c in range(3):
        rows = slice(cells * c, cells * (c + 1))
        for r in range(ROWS):
            value = section[rows, lane(r)]
            if c == 1 and r in (0, ROWS - 1):
                value = value + fixed[cells * (r > 0) : cells * (1 + (r > 0)), :]
            value = value - gradient(LAST, found, c, slice(0, cells), slice(cells, 2 * cells), r)
            staged[rows, lane(r)] = value
            copies.append(
                pltpu.make_async_copy(staged.at[rows, lane(r)], out.at[c, :, r, :], sems.at[len(copies)])
            )
            copies[-1].start()
    for copy in copies:
        copy.wait()


def call(body, shapes, *args, scratch=(), **options):
    return pl.pallas_call(
        body,
        out_shape=[jax.ShapeDtypeStruct(s, jnp.float32) for s in shapes],
        scratch_shapes=scratch,
        compiler_params=pltpu.CompilerParams(vmem_limit_bytes=40 * 1024 * 1024),
        **options,
    )(*args)


def shifted(block, axis, step):
    count = lax.axis_size(axis)
    return lax.ppermute(block, axis, [(i, (i + step) % count) for i in range(count)])


def per_device(velocity, viscosity):
    components, cells, row_cells, columns = velocity.shape
    length = cells * lax.axis_size("span")
    own, first_own, slopes, full, moments, lateral, *first = (
        jnp.asarray(t) for t in tables(length, cells, False)
    )
    _, last_own, _, _, _, _, *last = (jnp.asarray(t) for t in tables(length, cells, True))
    width = row_cells * columns
    near = cells + PAD_M
    whole, edge, rim = (components * cells, width), (PAD_V, width), (components * cells, 2 * columns)

    def across(up_near, down_near, up_far, down_far):
        return (
            shifted(up_near, "cross", 1), shifted(down_near, "cross", -1),
            shifted(up_far, "cross", 2), shifted(down_far, "cross", -2),
        )

    def message(near_slots, far_slots, far_rows):
        near_shape = (near_slots * cells + row_cells * PAD_M, columns)
        far_shape = (far_slots * cells + far_rows * PAD_M, columns)
        return [near_shape] * 2 + [far_shape] * 2

    def levels(extent, depth):
        return pltpu.VMEM((SWEEPS * depth, extent.breadth * columns), jnp.float32)

    start, thick, to_right, to_left, upward, downward = call(
        functools.partial(open_kernel, cells),
        [whole, (cells, width), edge, edge, rim, rim],
        *(pltpu.with_memory_space_constraint(x, pltpu.HBM) for x in (velocity, viscosity, moments)),
        in_specs=[pl.BlockSpec(memory_space=pltpu.HBM)] * 3,
        scratch=[pltpu.VMEM(moments.shape, moments.dtype), pltpu.SemaphoreType.DMA((1 + 4 * ROWS,))],
    )
    left = shifted(to_right, "span", 1)
    right = shifted(to_left, "span", -1)
    low = shifted(upward, "cross", 1)
    high = shifted(downward, "cross", -1)
    (rough,) = call(functools.partial(rough_kernel, cells), [whole], start, thick, own)
    section, parts, *sent = call(
        functools.partial(tendency_kernel, cells),
        [whole, (near, width)] + message(12, 4, 2),
        rough, start, thick, left, right, low, high, slopes, lateral,
    )
    arrived = across(*sent)
    ext, to_right, to_left = call(
        functools.partial(source_kernel, cells),
        [(near, FIRST.breadth * columns)] + [(GROUP, (FIRST.packed + ROWS + 3) * columns)] * 2,
        parts, section, *arrived, first[0], moments,
    )
    left = shifted(to_right, "span", 1)
    right = shifted(to_left, "span", -1)
    (partial,) = call(
        functools.partial(home_kernel, FIRST),
        [(first_own.shape[0], FIRST.found * columns)],
        ext, first_own,
        scratch=[levels(FIRST, near)],
    )

    section, parts, *sent = call(
        functools.partial(middle_kernel, cells),
        [whole, (near, width)] + message(11, 5, 1),
        partial, left, right, section, first[1], *arrived[:2], start, thick, full, lateral,
        scratch=[
            levels(FIRST, 2 * PAD_S),
            pltpu.VMEM(whole, jnp.float32),
            pltpu.VMEM((components * cells, 4 * columns), jnp.float32),
            pltpu.VMEM((2 * PAD_V, width), jnp.float32),
        ],
    )
    arrived = across(*sent)
    ext, fixed, to_right, to_left = call(
        functools.partial(last_source_kernel, cells),
        [(near, LAST.breadth * columns), (2 * cells, columns)] + [(GROUP, LAST.packed * columns)] * 2,
        parts, section, sent[0], *arrived, last[0],
    )
    left = shifted(to_right, "span", 1)
    right = shifted(to_left, "span", -1)
    (partial,) = call(
        functools.partial(home_kernel, LAST),
        [(last_own.shape[0], LAST.found * columns)],
        ext, last_own,
        scratch=[levels(LAST, near)],
    )
    (out,) = call(
        functools.partial(last_kernel, cells),
        [velocity.shape],
        partial, left, right, section, fixed, last[1],
        scratch=[
            levels(LAST, 2 * PAD_S),
            pltpu.VMEM(whole, jnp.float32),
            pltpu.SemaphoreType.DMA((3 * ROWS,)),
        ],
        out_specs=[pl.BlockSpec(memory_space=pltpu.HBM)],
    )
    return out


def solution(mesh):
    in_specs = (P(None, "span", "cross", None), P("span", "cross", None))
    out_specs = P(None, "span", "cross", None)
    return jax.shard_map(
        per_device, mesh=mesh, in_specs=in_specs, out_specs=out_specs, check_vma=False
    )
```

```python
import functools

import jax
import jax.numpy as jnp
import ml_dtypes
import numpy as np
from jax import lax
from jax.experimental import pallas as pl
from jax.experimental.pallas import tpu as pltpu
from jax.sharding import PartitionSpec as P

SWEEPS = 4
ROWS = 4
LANES = 128
time_step = 0.1
highest = lax.Precision.HIGHEST
PAD_V = 16
PAD_S = 16
PAD_M = 8
GROUP = 8
PACK = 16
RANK_V = 3
RANK_M = 2


def symbols(length):
    w = 2.0 * np.pi * np.arange(length) / length
    first = (14.0 / 9.0 * np.sin(w) + np.sin(2.0 * w) / 18.0) / (1.0 + 2.0 / 3.0 * np.cos(w))
    second = (24.0 / 11.0 * (1.0 - np.cos(w)) + 3.0 / 22.0 * (1.0 - np.cos(2.0 * w))) / (
        1.0 + 4.0 / 11.0 * np.cos(w)
    )
    return 1j * first, -second, 1.0 / (4.0 + second)


def block_of(symbol, cells, offset):
    kernel = np.fft.ifft(symbol).real
    at = np.arange(cells)
    return kernel[(at[:, None] - (at[None, :] + offset * cells)) % len(kernel)]


def low_rank(stack, rank):
    left, scale, right = np.linalg.svd(stack, full_matrices=False)
    return left[:, :rank] * scale[:rank], right[:rank]


@functools.lru_cache(None)
def tables(length, cells, last):
    first, second, inverse = symbols(length)
    at = lambda symbol, offset: block_of(symbol, cells, offset)
    from_left, take_left = low_rank(np.concatenate([at(first, -1), at(second, -1)]), RANK_V)
    from_right, take_right = low_rank(np.concatenate([at(first, 1), at(second, 1)]), RANK_V)
    own = np.concatenate([at(first, 0), at(second, 0)])
    slopes = np.zeros((3, 2 * cells, 2 * PAD_V))
    moments = np.zeros((2 * PAD_V, 3 * cells))
    for c in range(3):
        rows = slice(RANK_V * c, RANK_V * (c + 1))
        slopes[c, :, :PAD_V][:, rows] = from_left
        slopes[c, :, PAD_V:][:, rows] = from_right
        moments[rows, cells * c : cells * (c + 1)] = take_left
        moments[PAD_V:][rows, cells * c : cells * (c + 1)] = take_right
    m_left, t_left = low_rank(at(first, -1), RANK_M)
    m_right, t_right = low_rank(at(first, 1), RANK_M)
    lateral = np.zeros((cells + PAD_M, cells))
    lateral[:cells] = at(first, 0)
    lateral[cells : cells + RANK_M] = t_left
    lateral[cells + RANK_M : cells + 2 * RANK_M] = t_right
    powers = [inverse ** (j + 1) for j in range(SWEEPS)]
    stacked = [p for p in powers] + [first * p for p in powers]
    count = len(stacked)
    RANK_S = 2 * SWEEPS + (1 if last else 3)
    kept = [] if last else stacked
    s_left, q_left = low_rank(
        np.concatenate([at(p, -1) for p in stacked] + [take_left @ at(p, 0) for p in kept]), RANK_S
    )
    s_right, q_right = low_rank(
        np.concatenate([at(p, 1) for p in stacked] + [take_right @ at(p, 0) for p in kept]), RANK_S
    )
    e_left, e_right = s_left[count * cells :], s_right[count * cells :]
    source = np.zeros((8 * GROUP, cells + PAD_M))
    for side, q in enumerate((q_left, q_right)):
        rows = np.zeros((PAD_S, cells + PAD_M))
        rows[:RANK_S, :cells] = q
        at_m = cells + RANK_M * side
        rows[RANK_S : RANK_S + RANK_M, at_m : at_m + RANK_M] = np.eye(RANK_M)
        top = 4 * GROUP * side
        source[top : top + 8] = rows[:8]
        source[top + 8 : top + 12] = rows[8:12]
        source[top + 20 : top + 24] = rows[8:12]
        source[top + 24] = rows[12]
    near, wide = cells + PAD_M, 2 * PAD_S
    height = 2 * cells + (0 if last else 4 * GROUP)
    solve_own = np.zeros((height, SWEEPS * near))
    solve_sides = np.zeros((height, SWEEPS * wide))
    for j in range(SWEEPS):
        for half in range(2):
            index = half * SWEEPS + j
            rows = slice(cells * index, cells * (index + 1))
            edge = slice(RANK_V * index, RANK_V * (index + 1))
            center = at(stacked[index], 0)
            by_left, by_right = s_left[rows], s_right[rows]
            mine, sides = np.zeros((cells, near)), np.zeros((cells, wide))
            mine[:, :cells] = center
            mine[:, cells : cells + RANK_M] = by_right @ (q_right @ m_left)
            mine[:, cells + RANK_M : cells + 2 * RANK_M] = by_left @ (q_left @ m_right)
            sides[:, :RANK_S] = by_left
            sides[:, RANK_S : RANK_S + RANK_M] = center @ m_left
            sides[:, PAD_S : PAD_S + RANK_S] = by_right
            sides[:, PAD_S + RANK_S : PAD_S + RANK_S + RANK_M] = center @ m_right
            solve_own[cells * half : cells * (half + 1), near * j : near * (j + 1)] = -mine
            solve_sides[cells * half : cells * (half + 1), wide * j : wide * (j + 1)] = -sides
            for side in range(0 if last else 2):
                mine, sides = np.zeros((RANK_V, near)), np.zeros((RANK_V, wide))
                if side == 0:
                    back = take_left @ by_right @ q_right
                    mine[:, cells + RANK_M : cells + 2 * RANK_M] = take_left @ center @ m_right
                    sides[:, :RANK_S] = e_left[edge]
                else:
                    back = take_right @ by_left @ q_left
                    mine[:, cells : cells + RANK_M] = take_right @ center @ m_left
                    sides[:, PAD_S : PAD_S + RANK_S] = e_right[edge]
                mine[:, :cells] = back
                sides[:, RANK_S : RANK_S + RANK_M] = back @ m_left
                sides[:, PAD_S + RANK_S : PAD_S + RANK_S + RANK_M] = back @ m_right
                top = 2 * cells + GROUP * (2 * side + half)
                solve_own[top : top + RANK_V, near * j : near * (j + 1)] = -mine
                solve_sides[top : top + RANK_V, wide * j : wide * (j + 1)] = -sides
    full = np.concatenate([np.broadcast_to(own, (3,) + own.shape), slopes], axis=2)
    plain, split = (own, solve_own), (slopes, full, moments, lateral, source, solve_sides)
    return [x.astype(np.float32) for x in plain] + [split_table(x.astype(np.float32)) for x in split]


def dot(a, b):
    return jnp.dot(a, b, precision=highest, preferred_element_type=jnp.float32)


def halves(x):
    high = x.astype(jnp.bfloat16)
    return high, (x - high.astype(jnp.float32)).astype(jnp.bfloat16)


def split_table(table):
    gap = -table.shape[-1] % PACK
    table = np.pad(table, [(0, 0)] * (table.ndim - 1) + [(0, gap)])
    high = table.astype(ml_dtypes.bfloat16)
    low = (table - high.astype(np.float32)).astype(ml_dtypes.bfloat16)
    return np.concatenate([high, high, low], axis=-1)


def split_dot(table, x):
    gap = -x.shape[0] % PACK
    if gap:
        x = jnp.concatenate([x, jnp.zeros((gap, x.shape[1]), x.dtype)], axis=0)
    high, low = halves(x)
    return jnp.dot(table, jnp.concatenate([high, low, high], axis=0), preferred_element_type=jnp.float32)


class Extent:
    def __init__(self, margin):
        self.margin = margin
        self.reach = margin + SWEEPS - 1
        self.breadth = ROWS + 2 * self.reach
        self.packed = self.breadth + self.breadth // 2
        self.found = ROWS + 2 * margin


FIRST, LAST = Extent(3), Extent(2)


DIFFERENCE = ((1, 2.0 / 3.0), (-1, -2.0 / 3.0), (2, -1.0 / 12.0), (-2, 1.0 / 12.0))
CURVE = ((1, 4.0 / 3.0), (-1, 4.0 / 3.0), (2, -1.0 / 12.0), (-2, -1.0 / 12.0))


def lane(r, count=1):
    return slice(r * LANES, (r + count) * LANES)


def turned(tile, step):
    return pltpu.roll(tile, (-step) % LANES, 1)


def edge_masks():
    at = lax.axis_index("cross")
    last = lax.axis_size("cross") - 1
    flag = lambda test: jnp.where(test, 1.0, 0.0).astype(jnp.float32)
    return (flag(at >= 1), flag(at >= 2), flag(at <= last - 1), flag(at <= last - 2))


def masked(tile, e, masks):
    if e < -ROWS:
        return tile * masks[1]
    if e < 0:
        return tile * masks[0]
    if e >= 2 * ROWS:
        return tile * masks[3]
    if e >= ROWS:
        return tile * masks[2]
    return tile


def first_diff(up_one, down_one, up_two, down_two):
    return (8.0 * (up_one - down_one) - (up_two - down_two)) * (1.0 / 12.0)


def second_diff(middle, up_one, down_one, up_two, down_two):
    return (16.0 * (up_one + down_one) - (up_two + down_two) - 30.0 * middle) * (1.0 / 12.0)


def stream_slope(tile):
    return first_diff(turned(tile, 1), turned(tile, -1), turned(tile, 2), turned(tile, -2))


def open_kernel(
    cells, velocity, viscosity, moments, flat, thick, to_right, to_left, upward, downward, weights, sems
):
    copies = [pltpu.make_async_copy(moments, weights, sems.at[0])]
    for c in range(3):
        rows = slice(cells * c, cells * (c + 1))
        for r in range(ROWS):
            copies.append(
                pltpu.make_async_copy(velocity.at[c, :, r, :], flat.at[rows, lane(r)], sems.at[len(copies)])
            )
    for r in range(ROWS):
        copies.append(pltpu.make_async_copy(viscosity.at[:, r, :], thick.at[:, lane(r)], sems.at[len(copies)]))
    for copy in copies:
        copy.start()
    for copy in copies:
        copy.wait()
    row = lambda c, r: flat[cells * c : cells * (c + 1), lane(r)]
    fill_slots(upward, cells, [row(c, r) for c in range(3) for r in (2, 3)] + [thick[:, lane(3)]], [])
    fill_slots(downward, cells, [row(c, r) for c in range(3) for r in (0, 1)] + [thick[:, lane(0)]], [])
    both = split_dot(weights[...], flat[...])
    to_right[...] = both[:PAD_V]
    to_left[...] = both[PAD_V:]


def weighed(weights, value_at, r, home):
    total = None
    for reach, factor in weights:
        if (0 <= r + reach < ROWS) == home:
            part = factor * value_at(r + reach)
            total = part if total is None else total + part
    return total


def rough_kernel(cells, flat, thick, own, rough):
    for c in range(3):
        rows = slice(cells * c, cells * (c + 1))
        at = lambda r: flat[rows, lane(r)]
        spanned = dot(own[...], flat[rows, :])
        for r in range(ROWS):
            here = at(r)
            up_one, down_one = turned(here, 1), turned(here, -1)
            up_two, down_two = turned(here, 2), turned(here, -2)
            carried = (
                flat[:cells, lane(r)] * first_diff(up_one, down_one, up_two, down_two)
                + flat[cells : 2 * cells, lane(r)] * weighed(DIFFERENCE, at, r, True)
                + flat[2 * cells :, lane(r)] * spanned[:cells, lane(r)]
            )
            spread = (
                (4.0 / 3.0) * (up_one + down_one)
                - (1.0 / 12.0) * (up_two + down_two)
                - 5.0 * here
                + weighed(CURVE, at, r, True)
                + spanned[cells:, lane(r)]
            )
            rough[rows, lane(r)] = here + time_step * (thick[:, lane(r)] * spread - carried)


def add_beyond(cells, rough, flat, thick, left, right, low, high, slopes, section):
    masks = edge_masks()
    sides = jnp.concatenate([left[...], right[...]], axis=0)
    for c in range(3):
        rows = slice(cells * c, cells * (c + 1))
        spanned = split_dot(slopes[c], sides)

        def beyond(r):
            if r < 0:
                return masked(slot(low, cells, 2 * c + r + 2)[...], r, masks)
            return masked(slot(high, cells, 2 * c + r - ROWS)[...], r, masks)

        for r in range(ROWS):
            spread = spanned[cells:, lane(r)] + weighed(CURVE, beyond, r, False)
            carried = flat[cells : 2 * cells, lane(r)] * weighed(DIFFERENCE, beyond, r, False)
            carried = carried + flat[2 * cells :, lane(r)] * spanned[:cells, lane(r)]
            section[rows, lane(r)] = rough[rows, lane(r)] + time_step * (thick[:, lane(r)] * spread - carried)


def slot(ref, cells, k):
    return ref.at[cells * k : cells * (k + 1), :]


def fill_slots(ref, cells, blocks, moments):
    for k, block in enumerate(blocks):
        slot(ref, cells, k)[...] = block
    for k, block in enumerate(moments):
        top = cells * len(blocks) + PAD_M * k
        ref[top : top + PAD_M, :] = block


def own_source(cells, section, lateral, parts, owed={}):
    side = split_dot(lateral[...], section[2 * cells :, :])
    at = lambda r: section[cells : 2 * cells, lane(r)]
    blocks = []
    for r in range(ROWS):
        total = stream_slope(section[:cells, lane(r)]) + side[:cells, lane(r)] + weighed(DIFFERENCE, at, r, True)
        for reach, factor in DIFFERENCE:
            if r + reach in owed:
                total = total + factor * owed[r + reach]
        parts[:cells, lane(r)] = total
        blocks.append(total)
    parts[cells:, :] = side[cells:]
    moments = [side[cells:, lane(r)] for r in range(ROWS)]
    up = (2.0 / 3.0) * at(0) - (1.0 / 12.0) * at(1)
    down = (1.0 / 12.0) * at(ROWS - 2) - (2.0 / 3.0) * at(ROWS - 1)
    return blocks, moments, at, up, down


def tendency_kernel(
    cells, rough, flat, thick, left, right, low, high, slopes, lateral,
    section, parts, up_near, down_near, up_far, down_far,
):
    add_beyond(cells, rough, flat, thick, left, right, low, high, slopes, section)
    blocks, moments, at, _, _ = own_source(cells, section, lateral, parts)
    row = lambda c, r: section[cells * c : cells * (c + 1), lane(r)]
    every = [at(r) for r in range(ROWS)]
    for near, far, outer, inner in ((up_near, up_far, 0, 2), (down_near, down_far, 2, 0)):
        side = [row(c, inner + k) for c in (0, 2) for k in range(2)]
        fill_slots(near, cells, blocks[outer : outer + 2] + every + side, moments[outer : outer + 2])
        fill_slots(far, cells, blocks[inner : inner + 2] + [at(inner), at(inner + 1)], moments[inner : inner + 2])


def first_source(cells, parts, section, arrived, lateral, ext):
    low_one, high_one, low_two, high_two = arrived
    masks = edge_masks()
    span, tail = slice(0, cells), slice(cells, cells + PAD_M)
    pick = lambda ref, k: slot(ref, cells, k)[...]

    def across(e):
        if 0 <= e < ROWS:
            return section[cells : 2 * cells, lane(e)]
        if e < -ROWS or e >= 2 * ROWS:
            tile = pick(low_two, e + 8) if e < 0 else pick(high_two, e - 6)
        else:
            tile = pick(low_one, e + 6) if e < 0 else pick(high_one, e - 2)
        return masked(tile, e, masks)

    whole = (-2, -1, ROWS, ROWS + 1)
    given = [(low_one if e < 0 else high_one, e % 2) for e in whole]
    beside = split_dot(lateral[...], jnp.concatenate([pick(ref, 8 + k) for ref, k in given], axis=1))

    for e in range(-FIRST.reach, ROWS + FIRST.reach):
        if e in whole:
            at = whole.index(e)
            ref, k = given[at]
            total = stream_slope(pick(ref, 6 + k)) + beside[:cells, lane(at)]
            side = beside[cells:, lane(at)]
        elif 0 <= e < ROWS:
            total, side = parts[span, lane(e)], parts[tail, lane(e)]
        else:
            far = e < -ROWS or e >= 2 * ROWS
            ref = (low_two if e < 0 else high_two) if far else (low_one if e < 0 else high_one)
            top = (4 if far else 10) * cells + PAD_M * (e % 2)
            total, side = pick(ref, e % 2), ref[top : top + PAD_M, :]
        for reach, factor in DIFFERENCE:
            if e in whole or (e + reach) // ROWS != e // ROWS:
                total = total + factor * across(e + reach)
        ext[span, lane(e + FIRST.reach)] = masked(total, e, masks)
        ext[tail, lane(e + FIRST.reach)] = masked(side, e, masks)


def last_source(cells, parts, section, arrived, extra, ext):
    low_one, high_one, low_two, high_two = arrived
    masks = edge_masks()
    span, tail = slice(0, cells), slice(cells, cells + PAD_M)
    pick = lambda ref, k: slot(ref, cells, k)[...]

    def joined(e):
        if 0 <= e < ROWS:
            return parts[span, lane(e)], parts[tail, lane(e)]
        if e < -ROWS or e >= 2 * ROWS:
            ref = low_two if e < 0 else high_two
            return pick(ref, 0), ref[4 * cells :, :]
        ref, k = (low_one, e + ROWS) if e < 0 else (high_one, e - ROWS)
        top = 9 * cells + PAD_M * k
        return pick(ref, k), ref[top : top + PAD_M, :]

    def across(e, home):
        if e // ROWS == home // ROWS or home // ROWS in (-2, 2):
            return None
        if e < -ROWS:
            return masked(pick(low_two, 1 + e + ROWS + 2), e, masks)
        if e < 0:
            return masked(pick(low_one, ROWS + e + 2), e, masks)
        if e < ROWS:
            return section[cells : 2 * cells, lane(e)]
        if e < 2 * ROWS:
            return masked(pick(high_one, e), e, masks)
        return masked(pick(high_two, 1 + e - 2 * ROWS), e, masks)

    for e in range(-LAST.reach, ROWS + LAST.reach):
        total, side = joined(e)
        if e == -ROWS - 1:
            total = total + pick(low_one, 6)
        if e == 2 * ROWS:
            total = total + pick(high_one, 6)
        for reach, factor in DIFFERENCE:
            other = across(e + reach, e)
            if other is not None:
                total = total + factor * other
            if e + reach in extra and (e + reach) // ROWS == e // ROWS:
                total = total + factor * extra[e + reach]
        ext[span, lane(e + LAST.reach)] = masked(total, e, masks)
        ext[tail, lane(e + LAST.reach)] = masked(side, e, masks)


def pack_moments(extent, both, to_right, to_left):
    for side, out in enumerate((to_right, to_left)):
        top = 4 * GROUP * side
        out[:, lane(0, extent.breadth)] = both[top : top + 8]
        for k in range(extent.breadth // 2):
            out[:, lane(extent.breadth + k)] = (
                both[top + 8 : top + 16, lane(2 * k)] + both[top + 16 : top + 24, lane(2 * k + 1)]
            )


def source_kernel(
    cells, parts, section, low_one, high_one, low_two, high_two, lateral, source, moments, ext, to_right, to_left
):
    first_source(cells, parts, section, (low_one, high_one, low_two, high_two), lateral, ext)
    both = split_dot(source[...], ext[...])
    pack_moments(FIRST, both, to_right, to_left)
    held = split_dot(moments[...], section[...])
    for side, out in enumerate((to_right, to_left)):
        top, base = 4 * GROUP * side, PAD_V * side
        out[:, lane(FIRST.packed, ROWS)] = held[base : base + 8]
        out[:, lane(FIRST.packed + ROWS, 3)] = jnp.zeros((GROUP, 3 * LANES), jnp.float32)
        for e in range(FIRST.breadth + ROWS):
            value = (
                both[top + 24 : top + 25, lane(e)]
                if e < FIRST.breadth
                else held[base + 8 : base + 9, lane(e - FIRST.breadth)]
            )
            row, tile = e % GROUP, FIRST.packed + ROWS + e // GROUP
            out[row : row + 1, lane(tile)] = value


def last_source_kernel(
    cells, parts, section, up_near, down_near, debts, low_one, high_one, low_two, high_two, source,
    ext, fixed, to_right, to_left,
):
    masks = edge_masks()
    pick = lambda ref, k: slot(ref, cells, k)[...]
    phi, factor = 7, 8
    extra = {
        0: pick(up_near, factor) * pick(low_one, phi) * masks[0],
        ROWS - 1: pick(down_near, factor) * pick(high_one, phi) * masks[2],
        -1: pick(debts, 0),
        ROWS: pick(debts, 1),
        -ROWS: pick(low_one, factor) * pick(low_two, 3) * masks[1],
        2 * ROWS - 1: pick(high_one, factor) * pick(high_two, 3) * masks[3],
    }
    fixed[:cells, :] = extra[0]
    fixed[cells:, :] = extra[ROWS - 1]
    last_source(cells, parts, section, (low_one, high_one, low_two, high_two), extra, ext)
    pack_moments(LAST, split_dot(source[...], ext[...]), to_right, to_left)


def climb(extent, levels, depth):
    masks = edge_masks()
    for j in range(1, SWEEPS):
        before = slice(depth * (j - 1), depth * j)
        after = slice(depth * j, depth * (j + 1))
        for e in range(-extent.reach + j, ROWS + extent.reach - j):
            k = e + extent.reach
            here = levels[before, lane(k)]
            beside = (
                turned(here, 1) + turned(here, -1) + levels[before, lane(k + 1)] + levels[before, lane(k - 1)]
            )
            levels[after, lane(k)] = masked(beside, e, masks)
    return levels[:, lane(SWEEPS - 1, extent.found)]


def home_kernel(extent, ext, solve, partial, levels):
    depth = ext.shape[0]
    levels[:depth, :] = ext[...]
    partial[...] = dot(solve[...], climb(extent, levels, depth))


def spare(given, e):
    row, tile = e % GROUP, FIRST.packed + ROWS + e // GROUP
    return given[row : row + 1, lane(tile)]


def finish(extent, partial, left, right, solve, levels):
    for side, given in enumerate((left, right)):
        top = PAD_S * side
        levels[top : top + 8, :] = given[:, lane(0, extent.breadth)]
        for e in range(extent.breadth):
            tile = given[:, lane(extent.breadth + e // 2)]
            levels[top + 8 : top + 16, lane(e)] = pltpu.roll(tile, 4, 0) if e % 2 else tile
            if extent is FIRST:
                levels[top + 12 : top + 13, lane(e)] = spare(given, e)
    return partial[...] + split_dot(solve[...], climb(extent, levels, 2 * PAD_S))


def gradient(extent, found, c, rows, slope_rows, r):
    masks = edge_masks()
    phi = lambda r: masked(found[rows, lane(r + extent.margin)], r, masks)
    if c == 0:
        return stream_slope(phi(r))
    if c == 1:
        inside = lambda r: -extent.margin <= r < ROWS + extent.margin
        return sum(factor * phi(r + reach) for reach, factor in DIFFERENCE if inside(r + reach))
    return found[slope_rows, lane(r + extent.margin)]


def middle_kernel(
    cells, partial, left, right, section, solve, low_one, high_one, low, high, start, thick, full, lateral,
    following, parts, debts, up_near, down_near, up_far, down_far, levels, flat, rim, sides,
):
    masks = edge_masks()
    found = finish(FIRST, partial, left, right, solve, levels)
    home, home_slope = slice(0, cells), slice(cells, 2 * cells)
    outer = (-2, -1, ROWS, ROWS + 1)
    for c in range(3):
        rows = slice(cells * c, cells * (c + 1))
        for r in range(ROWS):
            flat[rows, lane(r)] = section[rows, lane(r)] - gradient(FIRST, found, c, home, home_slope, r)
        for k, r in enumerate(outer):
            first = (6, 4 if r < 0 else 2, 8)[c]
            value = slot(low_one if r < 0 else high_one, cells, first + k % 2)[...]
            value = value - gradient(FIRST, found, c, home, home_slope, r)
            rim[rows, lane(k)] = masked(value, r, masks)
    for side, given in enumerate((left, right)):
        base, top = PAD_V * side, 2 * cells + 2 * GROUP * side
        phi_rows, slope_rows = slice(top, top + GROUP), slice(top + GROUP, top + 2 * GROUP)
        sides[base : base + GROUP, :] = given[:, lane(FIRST.packed, ROWS)]
        sides[base + GROUP : base + PAD_V, :] = jnp.zeros((PAD_V - GROUP, ROWS * LANES), jnp.float32)
        for r in range(ROWS):
            sides[base + GROUP : base + GROUP + 1, lane(r)] = spare(given, FIRST.breadth + r)
            for c in range(3):
                rows = slice(base + RANK_V * c, base + RANK_V * (c + 1))
                change = gradient(FIRST, found, c, phi_rows, slope_rows, r)[:RANK_V]
                sides[rows, lane(r)] = sides[rows, lane(r)] - change

    def tile(c, r):
        rows = slice(cells * c, cells * (c + 1))
        return flat[rows, lane(r)] if 0 <= r < ROWS else rim[rows, lane(r + 2 if r < 0 else r - 2)]

    for c in range(3):
        rows = slice(cells * c, cells * (c + 1))
        spanned = split_dot(full[c], jnp.concatenate([flat[rows, :], sides[...]], axis=0))
        for r in range(ROWS):
            here = tile(c, r)
            up_one, down_one = turned(here, 1), turned(here, -1)
            up_two, down_two = turned(here, 2), turned(here, -2)
            carried = (
                tile(0, r) * first_diff(up_one, down_one, up_two, down_two)
                + tile(1, r) * sum(factor * tile(c, r + reach) for reach, factor in DIFFERENCE)
                + tile(2, r) * spanned[:cells, lane(r)]
            )
            spread = (
                (4.0 / 3.0) * (up_one + down_one)
                - (1.0 / 12.0) * (up_two + down_two)
                - 5.0 * here
                + sum(factor * tile(c, r + reach) for reach, factor in CURVE)
                + spanned[cells:, lane(r)]
            )
            moved = here + time_step * (thick[:, lane(r)] * spread - carried)
            following[rows, lane(r)] = 0.5 * start[rows, lane(r)] + 0.5 * moved
    phi = lambda r: found[:cells, lane(r + FIRST.margin)]
    scale = 0.5 * time_step / 144.0
    owed = {
        -1: scale * (tile(1, -1) - slot(low, cells, 6)[...]) * phi(ROWS - 1) * masks[0],
        ROWS: scale * (tile(1, ROWS) + slot(high, cells, 6)[...]) * phi(0) * masks[2],
    }
    slot(debts, cells, 0)[...] = owed[-1]
    slot(debts, cells, 1)[...] = owed[ROWS]
    blocks, moments, at, up, down = own_source(cells, following, lateral, parts, owed)
    first = scale * (thick[:, lane(0)] + tile(1, 0))
    last = scale * (tile(1, ROWS - 1) - thick[:, lane(ROWS - 1)])
    fill_slots(up_near, cells, blocks + [at(2), at(3), up, phi(0), first], moments)
    fill_slots(down_near, cells, blocks + [at(0), at(1), down, phi(ROWS - 1), last], moments)
    fill_slots(up_far, cells, [blocks[3], at(2), at(3), phi(0)], moments[3:])
    fill_slots(down_far, cells, [blocks[0], at(0), at(1), phi(ROWS - 1)], moments[:1])


def last_kernel(cells, partial, left, right, section, fixed, solve, out, levels, staged, sems):
    found = finish(LAST, partial, left, right, solve, levels)
    copies = []
    for c in range(3):
        rows = slice(cells * c, cells * (c + 1))
        for r in range(ROWS):
            value = section[rows, lane(r)]
            if c == 1 and r in (0, ROWS - 1):
                value = value + fixed[cells * (r > 0) : cells * (1 + (r > 0)), :]
            value = value - gradient(LAST, found, c, slice(0, cells), slice(cells, 2 * cells), r)
            staged[rows, lane(r)] = value
            copies.append(
                pltpu.make_async_copy(staged.at[rows, lane(r)], out.at[c, :, r, :], sems.at[len(copies)])
            )
            copies[-1].start()
    for copy in copies:
        copy.wait()


def call(body, shapes, *args, scratch=(), **options):
    return pl.pallas_call(
        body,
        out_shape=[jax.ShapeDtypeStruct(s, jnp.float32) for s in shapes],
        scratch_shapes=scratch,
        compiler_params=pltpu.CompilerParams(vmem_limit_bytes=40 * 1024 * 1024),
        **options,
    )(*args)


def shifted(block, axis, step):
    count = lax.axis_size(axis)
    return lax.ppermute(block, axis, [(i, (i + step) % count) for i in range(count)])


def per_device(velocity, viscosity):
    components, cells, row_cells, columns = velocity.shape
    length = cells * lax.axis_size("span")
    own, first_own, slopes, full, moments, lateral, *first = (
        jnp.asarray(t) for t in tables(length, cells, False)
    )
    _, last_own, _, _, _, _, *last = (jnp.asarray(t) for t in tables(length, cells, True))
    width = row_cells * columns
    near = cells + PAD_M
    whole, edge, rim = (components * cells, width), (PAD_V, width), (7 * cells, columns)

    def across(up_near, down_near, up_far, down_far):
        return (
            shifted(up_near, "cross", 1), shifted(down_near, "cross", -1),
            shifted(up_far, "cross", 2), shifted(down_far, "cross", -2),
        )

    def message(near_slots, near_rows, far_slots, far_rows):
        near_shape = (near_slots * cells + near_rows * PAD_M, columns)
        far_shape = (far_slots * cells + far_rows * PAD_M, columns)
        return [near_shape] * 2 + [far_shape] * 2

    def levels(extent, depth):
        return pltpu.VMEM((SWEEPS * depth, extent.breadth * columns), jnp.float32)

    start, thick, to_right, to_left, upward, downward = call(
        functools.partial(open_kernel, cells),
        [whole, (cells, width), edge, edge, rim, rim],
        *(pltpu.with_memory_space_constraint(x, pltpu.HBM) for x in (velocity, viscosity, moments)),
        in_specs=[pl.BlockSpec(memory_space=pltpu.HBM)] * 3,
        scratch=[pltpu.VMEM(moments.shape, moments.dtype), pltpu.SemaphoreType.DMA((1 + 4 * ROWS,))],
    )
    left = shifted(to_right, "span", 1)
    right = shifted(to_left, "span", -1)
    low = shifted(upward, "cross", 1)
    high = shifted(downward, "cross", -1)
    (rough,) = call(functools.partial(rough_kernel, cells), [whole], start, thick, own)
    section, parts, *sent = call(
        functools.partial(tendency_kernel, cells),
        [whole, (near, width)] + message(10, 2, 4, 2),
        rough, start, thick, left, right, low, high, slopes, lateral,
    )
    arrived = across(*sent)
    ext, to_right, to_left = call(
        functools.partial(source_kernel, cells),
        [(near, FIRST.breadth * columns)] + [(GROUP, (FIRST.packed + ROWS + 3) * columns)] * 2,
        parts, section, *arrived, lateral, first[0], moments,
    )
    left = shifted(to_right, "span", 1)
    right = shifted(to_left, "span", -1)
    (partial,) = call(
        functools.partial(home_kernel, FIRST),
        [(first_own.shape[0], FIRST.found * columns)],
        ext, first_own,
        scratch=[levels(FIRST, near)],
    )

    section, parts, debts, *sent = call(
        functools.partial(middle_kernel, cells),
        [whole, (near, width), (2 * cells, columns)] + message(9, 4, 4, 1),
        partial, left, right, section, first[1], *arrived[:2], low, high, start, thick, full, lateral,
        scratch=[
            levels(FIRST, 2 * PAD_S),
            pltpu.VMEM(whole, jnp.float32),
            pltpu.VMEM((components * cells, 4 * columns), jnp.float32),
            pltpu.VMEM((2 * PAD_V, width), jnp.float32),
        ],
    )
    arrived = across(*sent)
    ext, fixed, to_right, to_left = call(
        functools.partial(last_source_kernel, cells),
        [(near, LAST.breadth * columns), (2 * cells, columns)] + [(GROUP, LAST.packed * columns)] * 2,
        parts, section, *sent[:2], debts, *arrived, last[0],
    )
    left = shifted(to_right, "span", 1)
    right = shifted(to_left, "span", -1)
    (partial,) = call(
        functools.partial(home_kernel, LAST),
        [(last_own.shape[0], LAST.found * columns)],
        ext, last_own,
        scratch=[levels(LAST, near)],
    )
    (out,) = call(
        functools.partial(last_kernel, cells),
        [velocity.shape],
        partial, left, right, section, fixed, last[1],
        scratch=[
            levels(LAST, 2 * PAD_S),
            pltpu.VMEM(whole, jnp.float32),
            pltpu.SemaphoreType.DMA((3 * ROWS,)),
        ],
        out_specs=[pl.BlockSpec(memory_space=pltpu.HBM)],
    )
    return out


def solution(mesh):
    in_specs = (P(None, "span", "cross", None), P("span", "cross", None))
    out_specs = P(None, "span", "cross", None)
    return jax.shard_map(
        per_device, mesh=mesh, in_specs=in_specs, out_specs=out_specs, check_vma=False
    )
```

```python
import functools

import jax
import jax.numpy as jnp
import ml_dtypes
import numpy as np
from jax import lax
from jax.experimental import pallas as pl
from jax.experimental.pallas import tpu as pltpu
from jax.sharding import PartitionSpec as P

SWEEPS = 4
ROWS = 4
LANES = 128
time_step = 0.1
highest = lax.Precision.HIGHEST
PAD_V = 16
PAD_S = 16
PAD_M = 8
GROUP = 8
PACK = 16
RANK_V = 3
RANK_M = 2


def symbols(length):
    w = 2.0 * np.pi * np.arange(length) / length
    first = (14.0 / 9.0 * np.sin(w) + np.sin(2.0 * w) / 18.0) / (1.0 + 2.0 / 3.0 * np.cos(w))
    second = (24.0 / 11.0 * (1.0 - np.cos(w)) + 3.0 / 22.0 * (1.0 - np.cos(2.0 * w))) / (
        1.0 + 4.0 / 11.0 * np.cos(w)
    )
    return 1j * first, -second, 1.0 / (4.0 + second)


def block_of(symbol, cells, offset):
    kernel = np.fft.ifft(symbol).real
    at = np.arange(cells)
    return kernel[(at[:, None] - (at[None, :] + offset * cells)) % len(kernel)]


def low_rank(stack, rank):
    left, scale, right = np.linalg.svd(stack, full_matrices=False)
    return left[:, :rank] * scale[:rank], right[:rank]


@functools.lru_cache(None)
def tables(length, cells, last):
    first, second, inverse = symbols(length)
    at = lambda symbol, offset: block_of(symbol, cells, offset)
    from_left, take_left = low_rank(np.concatenate([at(first, -1), at(second, -1)]), RANK_V)
    from_right, take_right = low_rank(np.concatenate([at(first, 1), at(second, 1)]), RANK_V)
    own = np.concatenate([at(first, 0), at(second, 0)])
    slopes = np.zeros((3, 2 * cells, 2 * PAD_V))
    moments = np.zeros((2 * PAD_V, 3 * cells))
    for c in range(3):
        rows = slice(RANK_V * c, RANK_V * (c + 1))
        slopes[c, :, :PAD_V][:, rows] = from_left
        slopes[c, :, PAD_V:][:, rows] = from_right
        moments[rows, cells * c : cells * (c + 1)] = take_left
        moments[PAD_V:][rows, cells * c : cells * (c + 1)] = take_right
    m_left, t_left = low_rank(at(first, -1), RANK_M)
    m_right, t_right = low_rank(at(first, 1), RANK_M)
    lateral = np.zeros((cells + PAD_M, cells))
    lateral[:cells] = at(first, 0)
    lateral[cells : cells + RANK_M] = t_left
    lateral[cells + RANK_M : cells + 2 * RANK_M] = t_right
    powers = [inverse ** (j + 1) for j in range(SWEEPS)]
    stacked = [p for p in powers] + [first * p for p in powers]
    count = len(stacked)
    RANK_S = 2 * SWEEPS + (1 if last else 3)
    kept = [] if last else stacked
    s_left, q_left = low_rank(
        np.concatenate([at(p, -1) for p in stacked] + [take_left @ at(p, 0) for p in kept]), RANK_S
    )
    s_right, q_right = low_rank(
        np.concatenate([at(p, 1) for p in stacked] + [take_right @ at(p, 0) for p in kept]), RANK_S
    )
    e_left, e_right = s_left[count * cells :], s_right[count * cells :]
    source = np.zeros((8 * GROUP, cells + PAD_M))
    for side, q in enumerate((q_left, q_right)):
        rows = np.zeros((PAD_S, cells + PAD_M))
        rows[:RANK_S, :cells] = q
        at_m = cells + RANK_M * side
        rows[RANK_S : RANK_S + RANK_M, at_m : at_m + RANK_M] = np.eye(RANK_M)
        top = 4 * GROUP * side
        source[top : top + 8] = rows[:8]
        source[top + 8 : top + 12] = rows[8:12]
        source[top + 20 : top + 24] = rows[8:12]
        source[top + 24] = rows[12]
    near, wide = cells + PAD_M, 2 * PAD_S
    height = 2 * cells + (0 if last else 4 * GROUP)
    solve_own = np.zeros((height, SWEEPS * near))
    solve_sides = np.zeros((height, SWEEPS * wide))
    for j in range(SWEEPS):
        for half in range(2):
            index = half * SWEEPS + j
            rows = slice(cells * index, cells * (index + 1))
            edge = slice(RANK_V * index, RANK_V * (index + 1))
            center = at(stacked[index], 0)
            by_left, by_right = s_left[rows], s_right[rows]
            mine, sides = np.zeros((cells, near)), np.zeros((cells, wide))
            mine[:, :cells] = center
            mine[:, cells : cells + RANK_M] = by_right @ (q_right @ m_left)
            mine[:, cells + RANK_M : cells + 2 * RANK_M] = by_left @ (q_left @ m_right)
            sides[:, :RANK_S] = by_left
            sides[:, RANK_S : RANK_S + RANK_M] = center @ m_left
            sides[:, PAD_S : PAD_S + RANK_S] = by_right
            sides[:, PAD_S + RANK_S : PAD_S + RANK_S + RANK_M] = center @ m_right
            solve_own[cells * half : cells * (half + 1), near * j : near * (j + 1)] = -mine
            solve_sides[cells * half : cells * (half + 1), wide * j : wide * (j + 1)] = -sides
            for side in range(0 if last else 2):
                mine, sides = np.zeros((RANK_V, near)), np.zeros((RANK_V, wide))
                if side == 0:
                    back = take_left @ by_right @ q_right
                    mine[:, cells + RANK_M : cells + 2 * RANK_M] = take_left @ center @ m_right
                    sides[:, :RANK_S] = e_left[edge]
                else:
                    back = take_right @ by_left @ q_left
                    mine[:, cells : cells + RANK_M] = take_right @ center @ m_left
                    sides[:, PAD_S : PAD_S + RANK_S] = e_right[edge]
                mine[:, :cells] = back
                sides[:, RANK_S : RANK_S + RANK_M] = back @ m_left
                sides[:, PAD_S + RANK_S : PAD_S + RANK_S + RANK_M] = back @ m_right
                top = 2 * cells + GROUP * (2 * side + half)
                solve_own[top : top + RANK_V, near * j : near * (j + 1)] = -mine
                solve_sides[top : top + RANK_V, wide * j : wide * (j + 1)] = -sides
    full = np.concatenate([np.broadcast_to(own, (3,) + own.shape), slopes], axis=2)
    plain, split = (own, solve_own), (slopes, full, moments, lateral, source, solve_sides)
    return [x.astype(np.float32) for x in plain] + [split_table(x.astype(np.float32)) for x in split]


def dot(a, b):
    return jnp.dot(a, b, precision=highest, preferred_element_type=jnp.float32)


def halves(x):
    high = x.astype(jnp.bfloat16)
    return high, (x - high.astype(jnp.float32)).astype(jnp.bfloat16)


def split_table(table):
    gap = -table.shape[-1] % PACK
    table = np.pad(table, [(0, 0)] * (table.ndim - 1) + [(0, gap)])
    high = table.astype(ml_dtypes.bfloat16)
    low = (table - high.astype(np.float32)).astype(ml_dtypes.bfloat16)
    return np.concatenate([high, high, low], axis=-1)


def split_dot(table, x):
    gap = -x.shape[0] % PACK
    if gap:
        x = jnp.concatenate([x, jnp.zeros((gap, x.shape[1]), x.dtype)], axis=0)
    high, low = halves(x)
    return jnp.dot(table, jnp.concatenate([high, low, high], axis=0), preferred_element_type=jnp.float32)


class Extent:
    def __init__(self, margin):
        self.margin = margin
        self.reach = margin + SWEEPS - 1
        self.breadth = ROWS + 2 * self.reach
        self.packed = self.breadth + self.breadth // 2
        self.found = ROWS + 2 * margin


FIRST, LAST = Extent(3), Extent(2)


DIFFERENCE = ((1, 2.0 / 3.0), (-1, -2.0 / 3.0), (2, -1.0 / 12.0), (-2, 1.0 / 12.0))
CURVE = ((1, 4.0 / 3.0), (-1, 4.0 / 3.0), (2, -1.0 / 12.0), (-2, -1.0 / 12.0))


def lane(r, count=1):
    return slice(r * LANES, (r + count) * LANES)


def turned(tile, step):
    return pltpu.roll(tile, (-step) % LANES, 1)


def edge_masks():
    at = lax.axis_index("cross")
    last = lax.axis_size("cross") - 1
    flag = lambda test: jnp.where(test, 1.0, 0.0).astype(jnp.float32)
    return (flag(at >= 1), flag(at >= 2), flag(at <= last - 1), flag(at <= last - 2))


def masked(tile, e, masks):
    if e < -ROWS:
        return tile * masks[1]
    if e < 0:
        return tile * masks[0]
    if e >= 2 * ROWS:
        return tile * masks[3]
    if e >= ROWS:
        return tile * masks[2]
    return tile


def first_diff(up_one, down_one, up_two, down_two):
    return (8.0 * (up_one - down_one) - (up_two - down_two)) * (1.0 / 12.0)


def second_diff(middle, up_one, down_one, up_two, down_two):
    return (16.0 * (up_one + down_one) - (up_two + down_two) - 30.0 * middle) * (1.0 / 12.0)


def stream_slope(tile):
    return first_diff(turned(tile, 1), turned(tile, -1), turned(tile, 2), turned(tile, -2))


def open_kernel(
    cells, velocity, viscosity, moments, flat, thick, to_right, to_left, upward, downward, weights, sems
):
    copies = [pltpu.make_async_copy(moments, weights, sems.at[0])]
    for c in range(3):
        rows = slice(cells * c, cells * (c + 1))
        for r in range(ROWS):
            copies.append(
                pltpu.make_async_copy(velocity.at[c, :, r, :], flat.at[rows, lane(r)], sems.at[len(copies)])
            )
    for r in range(ROWS):
        copies.append(pltpu.make_async_copy(viscosity.at[:, r, :], thick.at[:, lane(r)], sems.at[len(copies)]))
    for copy in copies:
        copy.start()
    for copy in copies:
        copy.wait()
    row = lambda c, r: flat[cells * c : cells * (c + 1), lane(r)]
    fill_slots(upward, cells, [row(c, r) for c in range(3) for r in (2, 3)] + [thick[:, lane(3)]], [])
    fill_slots(downward, cells, [row(c, r) for c in range(3) for r in (0, 1)] + [thick[:, lane(0)]], [])
    both = split_dot(weights[...], flat[...])
    to_right[...] = both[:PAD_V]
    to_left[...] = both[PAD_V:]


def weighed(weights, value_at, r, home):
    total = None
    for reach, factor in weights:
        if (0 <= r + reach < ROWS) == home:
            part = factor * value_at(r + reach)
            total = part if total is None else total + part
    return total


def rough_kernel(cells, flat, thick, own, rough):
    for c in range(3):
        rows = slice(cells * c, cells * (c + 1))
        at = lambda r: flat[rows, lane(r)]
        spanned = dot(own[...], flat[rows, :])
        for r in range(ROWS):
            here = at(r)
            up_one, down_one = turned(here, 1), turned(here, -1)
            up_two, down_two = turned(here, 2), turned(here, -2)
            carried = (
                flat[:cells, lane(r)] * first_diff(up_one, down_one, up_two, down_two)
                + flat[cells : 2 * cells, lane(r)] * weighed(DIFFERENCE, at, r, True)
                + flat[2 * cells :, lane(r)] * spanned[:cells, lane(r)]
            )
            spread = (
                (4.0 / 3.0) * (up_one + down_one)
                - (1.0 / 12.0) * (up_two + down_two)
                - 5.0 * here
                + weighed(CURVE, at, r, True)
                + spanned[cells:, lane(r)]
            )
            rough[rows, lane(r)] = here + time_step * (thick[:, lane(r)] * spread - carried)


def add_beyond(cells, rough, flat, thick, left, right, low, high, slopes, section):
    masks = edge_masks()
    sides = jnp.concatenate([left[...], right[...]], axis=0)
    for c in range(3):
        rows = slice(cells * c, cells * (c + 1))
        spanned = split_dot(slopes[c], sides)

        def beyond(r):
            if r < 0:
                return masked(slot(low, cells, 2 * c + r + 2)[...], r, masks)
            return masked(slot(high, cells, 2 * c + r - ROWS)[...], r, masks)

        for r in range(ROWS):
            spread = spanned[cells:, lane(r)] + weighed(CURVE, beyond, r, False)
            carried = flat[cells : 2 * cells, lane(r)] * weighed(DIFFERENCE, beyond, r, False)
            carried = carried + flat[2 * cells :, lane(r)] * spanned[:cells, lane(r)]
            section[rows, lane(r)] = rough[rows, lane(r)] + time_step * (thick[:, lane(r)] * spread - carried)


def slot(ref, cells, k):
    return ref.at[cells * k : cells * (k + 1), :]


def fill_slots(ref, cells, blocks, moments):
    for k, block in enumerate(blocks):
        slot(ref, cells, k)[...] = block
    for k, block in enumerate(moments):
        top = cells * len(blocks) + PAD_M * k
        ref[top : top + PAD_M, :] = block


def own_source(cells, section, lateral, parts, owed={}):
    side = split_dot(lateral[...], section[2 * cells :, :])
    at = lambda r: section[cells : 2 * cells, lane(r)]
    blocks = []
    for r in range(ROWS):
        total = stream_slope(section[:cells, lane(r)]) + side[:cells, lane(r)] + weighed(DIFFERENCE, at, r, True)
        for reach, factor in DIFFERENCE:
            if r + reach in owed:
                total = total + factor * owed[r + reach]
        parts[:cells, lane(r)] = total
        blocks.append(total)
    parts[cells:, :] = side[cells:]
    moments = [side[cells:, lane(r)] for r in range(ROWS)]
    up = (2.0 / 3.0) * at(0) - (1.0 / 12.0) * at(1)
    down = (1.0 / 12.0) * at(ROWS - 2) - (2.0 / 3.0) * at(ROWS - 1)
    return blocks, moments, at, up, down


def tendency_kernel(
    cells, rough, flat, thick, left, right, low, high, slopes, lateral,
    section, parts, up_near, down_near, up_far, down_far,
):
    add_beyond(cells, rough, flat, thick, left, right, low, high, slopes, section)
    blocks, moments, at, _, _ = own_source(cells, section, lateral, parts)
    row = lambda c, r: section[cells * c : cells * (c + 1), lane(r)]
    every = [at(r) for r in range(ROWS)]
    for near, far, outer, inner in ((up_near, up_far, 0, 2), (down_near, down_far, 2, 0)):
        side = [row(c, inner + k) for c in (0, 2) for k in range(2)]
        fill_slots(near, cells, blocks[outer : outer + 2] + every + side, moments[outer : outer + 2])
        fill_slots(far, cells, blocks[inner : inner + 2] + [at(inner), at(inner + 1)], moments[inner : inner + 2])


def first_source(cells, parts, section, arrived, lateral, ext):
    low_one, high_one, low_two, high_two = arrived
    masks = edge_masks()
    span, tail = slice(0, cells), slice(cells, cells + PAD_M)
    pick = lambda ref, k: slot(ref, cells, k)[...]

    def across(e):
        if 0 <= e < ROWS:
            return section[cells : 2 * cells, lane(e)]
        if e < -ROWS or e >= 2 * ROWS:
            tile = pick(low_two, e + 8) if e < 0 else pick(high_two, e - 6)
        else:
            tile = pick(low_one, e + 6) if e < 0 else pick(high_one, e - 2)
        return masked(tile, e, masks)

    whole = (-2, -1, ROWS, ROWS + 1)
    given = [(low_one if e < 0 else high_one, e % 2) for e in whole]
    beside = split_dot(lateral[...], jnp.concatenate([pick(ref, 8 + k) for ref, k in given], axis=1))

    for e in range(-FIRST.reach, ROWS + FIRST.reach):
        if e in whole:
            at = whole.index(e)
            ref, k = given[at]
            total = stream_slope(pick(ref, 6 + k)) + beside[:cells, lane(at)]
            side = beside[cells:, lane(at)]
        elif 0 <= e < ROWS:
            total, side = parts[span, lane(e)], parts[tail, lane(e)]
        else:
            far = e < -ROWS or e >= 2 * ROWS
            ref = (low_two if e < 0 else high_two) if far else (low_one if e < 0 else high_one)
            top = (4 if far else 10) * cells + PAD_M * (e % 2)
            total, side = pick(ref, e % 2), ref[top : top + PAD_M, :]
        for reach, factor in DIFFERENCE:
            if e in whole or (e + reach) // ROWS != e // ROWS:
                total = total + factor * across(e + reach)
        ext[span, lane(e + FIRST.reach)] = masked(total, e, masks)
        ext[tail, lane(e + FIRST.reach)] = masked(side, e, masks)


def last_source(cells, parts, section, arrived, extra, ext):
    low_one, high_one, low_two, high_two = arrived
    masks = edge_masks()
    span, tail = slice(0, cells), slice(cells, cells + PAD_M)
    pick = lambda ref, k: slot(ref, cells, k)[...]

    def joined(e):
        if 0 <= e < ROWS:
            return parts[span, lane(e)], parts[tail, lane(e)]
        if e < -ROWS or e >= 2 * ROWS:
            ref = low_two if e < 0 else high_two
            return pick(ref, 0), ref[4 * cells :, :]
        ref, k = (low_one, e + ROWS) if e < 0 else (high_one, e - ROWS)
        top = 8 * cells + PAD_M * k
        return pick(ref, k), ref[top : top + PAD_M, :]

    def across(e, home):
        if e // ROWS == home // ROWS or home // ROWS in (-2, 2):
            return None
        if e < -ROWS:
            return masked(pick(low_two, 1 + e + ROWS + 2), e, masks)
        if e < 0:
            return masked(pick(low_one, ROWS + e + 2), e, masks)
        if e < ROWS:
            return section[cells : 2 * cells, lane(e)]
        if e < 2 * ROWS:
            return masked(pick(high_one, e), e, masks)
        return masked(pick(high_two, 1 + e - 2 * ROWS), e, masks)

    for e in range(-LAST.reach, ROWS + LAST.reach):
        total, side = joined(e)
        if e == -ROWS - 1:
            total = total + pick(low_one, 6)
        if e == 2 * ROWS:
            total = total + pick(high_one, 6)
        for reach, factor in DIFFERENCE:
            other = across(e + reach, e)
            if other is not None:
                total = total + factor * other
            if e + reach in extra and (e + reach) // ROWS == e // ROWS:
                total = total + factor * extra[e + reach]
        ext[span, lane(e + LAST.reach)] = masked(total, e, masks)
        ext[tail, lane(e + LAST.reach)] = masked(side, e, masks)


def pack_moments(extent, both, to_right, to_left):
    for side, out in enumerate((to_right, to_left)):
        top = 4 * GROUP * side
        out[:, lane(0, extent.breadth)] = both[top : top + 8]
        for k in range(extent.breadth // 2):
            out[:, lane(extent.breadth + k)] = (
                both[top + 8 : top + 16, lane(2 * k)] + both[top + 16 : top + 24, lane(2 * k + 1)]
            )


def source_kernel(
    cells, parts, section, low_one, high_one, low_two, high_two, lateral, source, moments, ext, to_right, to_left
):
    first_source(cells, parts, section, (low_one, high_one, low_two, high_two), lateral, ext)
    both = split_dot(source[...], ext[...])
    pack_moments(FIRST, both, to_right, to_left)
    held = split_dot(moments[...], section[...])
    for side, out in enumerate((to_right, to_left)):
        top, base = 4 * GROUP * side, PAD_V * side
        out[:, lane(FIRST.packed, ROWS)] = held[base : base + 8]
        out[:, lane(FIRST.packed + ROWS, 3)] = jnp.zeros((GROUP, 3 * LANES), jnp.float32)
        for e in range(FIRST.breadth + ROWS):
            value = (
                both[top + 24 : top + 25, lane(e)]
                if e < FIRST.breadth
                else held[base + 8 : base + 9, lane(e - FIRST.breadth)]
            )
            row, tile = e % GROUP, FIRST.packed + ROWS + e // GROUP
            out[row : row + 1, lane(tile)] = value


def last_source_kernel(
    cells, parts, section, debts, low_one, high_one, low_two, high_two, source,
    ext, fixed, to_right, to_left,
):
    masks = edge_masks()
    pick = lambda ref, k: slot(ref, cells, k)[...]
    extra = {
        0: pick(low_one, 7) * masks[0],
        ROWS - 1: pick(high_one, 7) * masks[2],
        -1: pick(debts, 0),
        ROWS: pick(debts, 1),
        -ROWS: pick(low_two, 3) * masks[1],
        2 * ROWS - 1: pick(high_two, 3) * masks[3],
    }
    fixed[:cells, :] = extra[0]
    fixed[cells:, :] = extra[ROWS - 1]
    last_source(cells, parts, section, (low_one, high_one, low_two, high_two), extra, ext)
    pack_moments(LAST, split_dot(source[...], ext[...]), to_right, to_left)


def climb(extent, levels, depth):
    masks = edge_masks()
    for j in range(1, SWEEPS):
        before = slice(depth * (j - 1), depth * j)
        after = slice(depth * j, depth * (j + 1))
        for e in range(-extent.reach + j, ROWS + extent.reach - j):
            k = e + extent.reach
            here = levels[before, lane(k)]
            beside = (
                turned(here, 1) + turned(here, -1) + levels[before, lane(k + 1)] + levels[before, lane(k - 1)]
            )
            levels[after, lane(k)] = masked(beside, e, masks)
    return levels[:, lane(SWEEPS - 1, extent.found)]


def home_kernel(extent, ext, solve, partial, levels):
    depth = ext.shape[0]
    levels[:depth, :] = ext[...]
    partial[...] = dot(solve[...], climb(extent, levels, depth))


def spare(given, e):
    row, tile = e % GROUP, FIRST.packed + ROWS + e // GROUP
    return given[row : row + 1, lane(tile)]


def finish(extent, partial, left, right, solve, levels):
    for side, given in enumerate((left, right)):
        top = PAD_S * side
        levels[top : top + 8, :] = given[:, lane(0, extent.breadth)]
        for e in range(extent.breadth):
            tile = given[:, lane(extent.breadth + e // 2)]
            levels[top + 8 : top + 16, lane(e)] = pltpu.roll(tile, 4, 0) if e % 2 else tile
            if extent is FIRST:
                levels[top + 12 : top + 13, lane(e)] = spare(given, e)
    return partial[...] + split_dot(solve[...], climb(extent, levels, 2 * PAD_S))


def gradient(extent, found, c, rows, slope_rows, r):
    masks = edge_masks()
    phi = lambda r: masked(found[rows, lane(r + extent.margin)], r, masks)
    if c == 0:
        return stream_slope(phi(r))
    if c == 1:
        inside = lambda r: -extent.margin <= r < ROWS + extent.margin
        return sum(factor * phi(r + reach) for reach, factor in DIFFERENCE if inside(r + reach))
    return found[slope_rows, lane(r + extent.margin)]


def middle_kernel(
    cells, partial, left, right, section, solve, low_one, high_one, low, high, start, thick, full, lateral,
    following, parts, debts, up_near, down_near, up_far, down_far, levels, flat, rim, sides,
):
    masks = edge_masks()
    found = finish(FIRST, partial, left, right, solve, levels)
    home, home_slope = slice(0, cells), slice(cells, 2 * cells)
    outer = (-2, -1, ROWS, ROWS + 1)
    for c in range(3):
        rows = slice(cells * c, cells * (c + 1))
        for r in range(ROWS):
            flat[rows, lane(r)] = section[rows, lane(r)] - gradient(FIRST, found, c, home, home_slope, r)
        for k, r in enumerate(outer):
            first = (6, 4 if r < 0 else 2, 8)[c]
            value = slot(low_one if r < 0 else high_one, cells, first + k % 2)[...]
            value = value - gradient(FIRST, found, c, home, home_slope, r)
            rim[rows, lane(k)] = masked(value, r, masks)
    for side, given in enumerate((left, right)):
        base, top = PAD_V * side, 2 * cells + 2 * GROUP * side
        phi_rows, slope_rows = slice(top, top + GROUP), slice(top + GROUP, top + 2 * GROUP)
        sides[base : base + GROUP, :] = given[:, lane(FIRST.packed, ROWS)]
        sides[base + GROUP : base + PAD_V, :] = jnp.zeros((PAD_V - GROUP, ROWS * LANES), jnp.float32)
        for r in range(ROWS):
            sides[base + GROUP : base + GROUP + 1, lane(r)] = spare(given, FIRST.breadth + r)
            for c in range(3):
                rows = slice(base + RANK_V * c, base + RANK_V * (c + 1))
                change = gradient(FIRST, found, c, phi_rows, slope_rows, r)[:RANK_V]
                sides[rows, lane(r)] = sides[rows, lane(r)] - change

    def tile(c, r):
        rows = slice(cells * c, cells * (c + 1))
        return flat[rows, lane(r)] if 0 <= r < ROWS else rim[rows, lane(r + 2 if r < 0 else r - 2)]

    for c in range(3):
        rows = slice(cells * c, cells * (c + 1))
        spanned = split_dot(full[c], jnp.concatenate([flat[rows, :], sides[...]], axis=0))
        for r in range(ROWS):
            here = tile(c, r)
            up_one, down_one = turned(here, 1), turned(here, -1)
            up_two, down_two = turned(here, 2), turned(here, -2)
            carried = (
                tile(0, r) * first_diff(up_one, down_one, up_two, down_two)
                + tile(1, r) * sum(factor * tile(c, r + reach) for reach, factor in DIFFERENCE)
                + tile(2, r) * spanned[:cells, lane(r)]
            )
            spread = (
                (4.0 / 3.0) * (up_one + down_one)
                - (1.0 / 12.0) * (up_two + down_two)
                - 5.0 * here
                + sum(factor * tile(c, r + reach) for reach, factor in CURVE)
                + spanned[cells:, lane(r)]
            )
            moved = here + time_step * (thick[:, lane(r)] * spread - carried)
            following[rows, lane(r)] = 0.5 * start[rows, lane(r)] + 0.5 * moved
    phi = lambda r: found[:cells, lane(r + FIRST.margin)]
    scale = 0.5 * time_step / 144.0
    owed = {
        -1: scale * (tile(1, -1) - slot(low, cells, 6)[...]) * phi(ROWS - 1) * masks[0],
        ROWS: scale * (tile(1, ROWS) + slot(high, cells, 6)[...]) * phi(0) * masks[2],
    }
    slot(debts, cells, 0)[...] = owed[-1]
    slot(debts, cells, 1)[...] = owed[ROWS]
    blocks, moments, at, up, down = own_source(cells, following, lateral, parts, owed)
    fill_slots(up_near, cells, blocks + [at(2), at(3), up, owed[ROWS]], moments)
    fill_slots(down_near, cells, blocks + [at(0), at(1), down, owed[-1]], moments)
    fill_slots(up_far, cells, [blocks[3], at(2), at(3), owed[ROWS]], moments[3:])
    fill_slots(down_far, cells, [blocks[0], at(0), at(1), owed[-1]], moments[:1])


def last_kernel(cells, partial, left, right, section, fixed, solve, out, levels, staged, sems):
    found = finish(LAST, partial, left, right, solve, levels)
    copies = []
    for c in range(3):
        rows = slice(cells * c, cells * (c + 1))
        for r in range(ROWS):
            value = section[rows, lane(r)]
            if c == 1 and r in (0, ROWS - 1):
                value = value + fixed[cells * (r > 0) : cells * (1 + (r > 0)), :]
            value = value - gradient(LAST, found, c, slice(0, cells), slice(cells, 2 * cells), r)
            staged[rows, lane(r)] = value
            copies.append(
                pltpu.make_async_copy(staged.at[rows, lane(r)], out.at[c, :, r, :], sems.at[len(copies)])
            )
            copies[-1].start()
    for copy in copies:
        copy.wait()


def call(body, shapes, *args, scratch=(), **options):
    return pl.pallas_call(
        body,
        out_shape=[jax.ShapeDtypeStruct(s, jnp.float32) for s in shapes],
        scratch_shapes=scratch,
        compiler_params=pltpu.CompilerParams(vmem_limit_bytes=40 * 1024 * 1024),
        **options,
    )(*args)


def shifted(block, axis, step):
    count = lax.axis_size(axis)
    return lax.ppermute(block, axis, [(i, (i + step) % count) for i in range(count)])


def per_device(velocity, viscosity):
    components, cells, row_cells, columns = velocity.shape
    length = cells * lax.axis_size("span")
    own, first_own, slopes, full, moments, lateral, *first = (
        jnp.asarray(t) for t in tables(length, cells, False)
    )
    _, last_own, _, _, _, _, *last = (jnp.asarray(t) for t in tables(length, cells, True))
    width = row_cells * columns
    near = cells + PAD_M
    whole, edge, rim = (components * cells, width), (PAD_V, width), (7 * cells, columns)

    def across(up_near, down_near, up_far, down_far):
        return (
            shifted(up_near, "cross", 1), shifted(down_near, "cross", -1),
            shifted(up_far, "cross", 2), shifted(down_far, "cross", -2),
        )

    def message(near_slots, near_rows, far_slots, far_rows):
        near_shape = (near_slots * cells + near_rows * PAD_M, columns)
        far_shape = (far_slots * cells + far_rows * PAD_M, columns)
        return [near_shape] * 2 + [far_shape] * 2

    def levels(extent, depth):
        return pltpu.VMEM((SWEEPS * depth, extent.breadth * columns), jnp.float32)

    start, thick, to_right, to_left, upward, downward = call(
        functools.partial(open_kernel, cells),
        [whole, (cells, width), edge, edge, rim, rim],
        *(pltpu.with_memory_space_constraint(x, pltpu.HBM) for x in (velocity, viscosity, moments)),
        in_specs=[pl.BlockSpec(memory_space=pltpu.HBM)] * 3,
        scratch=[pltpu.VMEM(moments.shape, moments.dtype), pltpu.SemaphoreType.DMA((1 + 4 * ROWS,))],
    )
    left = shifted(to_right, "span", 1)
    right = shifted(to_left, "span", -1)
    low = shifted(upward, "cross", 1)
    high = shifted(downward, "cross", -1)
    (rough,) = call(functools.partial(rough_kernel, cells), [whole], start, thick, own)
    section, parts, *sent = call(
        functools.partial(tendency_kernel, cells),
        [whole, (near, width)] + message(10, 2, 4, 2),
        rough, start, thick, left, right, low, high, slopes, lateral,
    )
    arrived = across(*sent)
    ext, to_right, to_left = call(
        functools.partial(source_kernel, cells),
        [(near, FIRST.breadth * columns)] + [(GROUP, (FIRST.packed + ROWS + 3) * columns)] * 2,
        parts, section, *arrived, lateral, first[0], moments,
    )
    left = shifted(to_right, "span", 1)
    right = shifted(to_left, "span", -1)
    (partial,) = call(
        functools.partial(home_kernel, FIRST),
        [(first_own.shape[0], FIRST.found * columns)],
        ext, first_own,
        scratch=[levels(FIRST, near)],
    )

    section, parts, debts, *sent = call(
        functools.partial(middle_kernel, cells),
        [whole, (near, width), (2 * cells, columns)] + message(8, 4, 4, 1),
        partial, left, right, section, first[1], *arrived[:2], low, high, start, thick, full, lateral,
        scratch=[
            levels(FIRST, 2 * PAD_S),
            pltpu.VMEM(whole, jnp.float32),
            pltpu.VMEM((components * cells, 4 * columns), jnp.float32),
            pltpu.VMEM((2 * PAD_V, width), jnp.float32),
        ],
    )
    arrived = across(*sent)
    ext, fixed, to_right, to_left = call(
        functools.partial(last_source_kernel, cells),
        [(near, LAST.breadth * columns), (2 * cells, columns)] + [(GROUP, LAST.packed * columns)] * 2,
        parts, section, debts, *arrived, last[0],
    )
    left = shifted(to_right, "span", 1)
    right = shifted(to_left, "span", -1)
    (partial,) = call(
        functools.partial(home_kernel, LAST),
        [(last_own.shape[0], LAST.found * columns)],
        ext, last_own,
        scratch=[levels(LAST, near)],
    )
    (out,) = call(
        functools.partial(last_kernel, cells),
        [velocity.shape],
        partial, left, right, section, fixed, last[1],
        scratch=[
            levels(LAST, 2 * PAD_S),
            pltpu.VMEM(whole, jnp.float32),
            pltpu.SemaphoreType.DMA((3 * ROWS,)),
        ],
        out_specs=[pl.BlockSpec(memory_space=pltpu.HBM)],
    )
    return out


def solution(mesh):
    in_specs = (P(None, "span", "cross", None), P("span", "cross", None))
    out_specs = P(None, "span", "cross", None)
    return jax.shard_map(
        per_device, mesh=mesh, in_specs=in_specs, out_specs=out_specs, check_vma=False
    )
```

```python
import functools

import jax
import jax.numpy as jnp
import ml_dtypes
import numpy as np
from jax import lax
from jax.experimental import pallas as pl
from jax.experimental.pallas import tpu as pltpu
from jax.sharding import PartitionSpec as P

SWEEPS = 4
ROWS = 4
LANES = 128
time_step = 0.1
highest = lax.Precision.HIGHEST
PAD_V = 16
PAD_S = 16
PAD_M = 8
GROUP = 8
PACK = 16
RANK_V = 3
RANK_M = 2


def symbols(length):
    w = 2.0 * np.pi * np.arange(length) / length
    first = (14.0 / 9.0 * np.sin(w) + np.sin(2.0 * w) / 18.0) / (1.0 + 2.0 / 3.0 * np.cos(w))
    second = (24.0 / 11.0 * (1.0 - np.cos(w)) + 3.0 / 22.0 * (1.0 - np.cos(2.0 * w))) / (
        1.0 + 4.0 / 11.0 * np.cos(w)
    )
    return 1j * first, -second, 1.0 / (4.0 + second)


def block_of(symbol, cells, offset):
    kernel = np.fft.ifft(symbol).real
    at = np.arange(cells)
    return kernel[(at[:, None] - (at[None, :] + offset * cells)) % len(kernel)]


def low_rank(stack, rank):
    left, scale, right = np.linalg.svd(stack, full_matrices=False)
    return left[:, :rank] * scale[:rank], right[:rank]


@functools.lru_cache(None)
def tables(length, cells, last):
    first, second, inverse = symbols(length)
    at = lambda symbol, offset: block_of(symbol, cells, offset)
    from_left, take_left = low_rank(np.concatenate([at(first, -1), at(second, -1)]), RANK_V)
    from_right, take_right = low_rank(np.concatenate([at(first, 1), at(second, 1)]), RANK_V)
    own = np.concatenate([at(first, 0), at(second, 0)])
    slopes = np.zeros((3, 2 * cells, 2 * PAD_V))
    moments = np.zeros((3, 2 * PAD_V, cells))
    for c in range(3):
        rows = slice(RANK_V * c, RANK_V * (c + 1))
        slopes[c, :, :PAD_V][:, rows] = from_left
        slopes[c, :, PAD_V:][:, rows] = from_right
        moments[c, rows] = take_left
        moments[c, PAD_V:][rows] = take_right
    m_left, t_left = low_rank(at(first, -1), RANK_M)
    m_right, t_right = low_rank(at(first, 1), RANK_M)
    lateral = np.zeros((cells + PAD_M, cells))
    lateral[:cells] = at(first, 0)
    lateral[cells : cells + RANK_M] = t_left
    lateral[cells + RANK_M : cells + 2 * RANK_M] = t_right
    powers = [inverse ** (j + 1) for j in range(SWEEPS)]
    stacked = [p for p in powers] + [first * p for p in powers]
    count = len(stacked)
    RANK_S = 2 * SWEEPS + (1 if last else 3)
    kept = [] if last else stacked
    s_left, q_left = low_rank(
        np.concatenate([at(p, -1) for p in stacked] + [take_left @ at(p, 0) for p in kept]), RANK_S
    )
    s_right, q_right = low_rank(
        np.concatenate([at(p, 1) for p in stacked] + [take_right @ at(p, 0) for p in kept]), RANK_S
    )
    e_left, e_right = s_left[count * cells :], s_right[count * cells :]
    source = np.zeros((8 * GROUP, cells + PAD_M))
    for side, q in enumerate((q_left, q_right)):
        rows = np.zeros((PAD_S, cells + PAD_M))
        rows[:RANK_S, :cells] = q
        at_m = cells + RANK_M * side
        rows[RANK_S : RANK_S + RANK_M, at_m : at_m + RANK_M] = np.eye(RANK_M)
        top = 4 * GROUP * side
        source[top : top + 8] = rows[:8]
        source[top + 8 : top + 12] = rows[8:12]
        source[top + 20 : top + 24] = rows[8:12]
        source[top + 24] = rows[12]
    near, wide = cells + PAD_M, 2 * PAD_S
    height = 2 * cells + (0 if last else 4 * GROUP)
    solve_own = np.zeros((height, SWEEPS * near))
    solve_sides = np.zeros((height, SWEEPS * wide))
    for j in range(SWEEPS):
        for half in range(2):
            index = half * SWEEPS + j
            rows = slice(cells * index, cells * (index + 1))
            edge = slice(RANK_V * index, RANK_V * (index + 1))
            center = at(stacked[index], 0)
            by_left, by_right = s_left[rows], s_right[rows]
            mine, sides = np.zeros((cells, near)), np.zeros((cells, wide))
            mine[:, :cells] = center
            mine[:, cells : cells + RANK_M] = by_right @ (q_right @ m_left)
            mine[:, cells + RANK_M : cells + 2 * RANK_M] = by_left @ (q_left @ m_right)
            sides[:, :RANK_S] = by_left
            sides[:, RANK_S : RANK_S + RANK_M] = center @ m_left
            sides[:, PAD_S : PAD_S + RANK_S] = by_right
            sides[:, PAD_S + RANK_S : PAD_S + RANK_S + RANK_M] = center @ m_right
            solve_own[cells * half : cells * (half + 1), near * j : near * (j + 1)] = -mine
            solve_sides[cells * half : cells * (half + 1), wide * j : wide * (j + 1)] = -sides
            for side in range(0 if last else 2):
                mine, sides = np.zeros((RANK_V, near)), np.zeros((RANK_V, wide))
                if side == 0:
                    back = take_left @ by_right @ q_right
                    mine[:, cells + RANK_M : cells + 2 * RANK_M] = take_left @ center @ m_right
                    sides[:, :RANK_S] = e_left[edge]
                else:
                    back = take_right @ by_left @ q_left
                    mine[:, cells : cells + RANK_M] = take_right @ center @ m_left
                    sides[:, PAD_S : PAD_S + RANK_S] = e_right[edge]
                mine[:, :cells] = back
                sides[:, RANK_S : RANK_S + RANK_M] = back @ m_left
                sides[:, PAD_S + RANK_S : PAD_S + RANK_S + RANK_M] = back @ m_right
                top = 2 * cells + GROUP * (2 * side + half)
                solve_own[top : top + RANK_V, near * j : near * (j + 1)] = -mine
                solve_sides[top : top + RANK_V, wide * j : wide * (j + 1)] = -sides
    full = np.concatenate([np.broadcast_to(own, (3,) + own.shape), slopes], axis=2)
    plain, split = (own, solve_own), (slopes, full, moments, lateral, source, solve_sides)
    return [x.astype(np.float32) for x in plain] + [split_table(x.astype(np.float32)) for x in split]


def dot(a, b):
    return jnp.dot(a, b, precision=highest, preferred_element_type=jnp.float32)


def halves(x):
    high = x.astype(jnp.bfloat16)
    return high, (x - high.astype(jnp.float32)).astype(jnp.bfloat16)


def split_table(table):
    gap = -table.shape[-1] % PACK
    table = np.pad(table, [(0, 0)] * (table.ndim - 1) + [(0, gap)])
    high = table.astype(ml_dtypes.bfloat16)
    low = (table - high.astype(np.float32)).astype(ml_dtypes.bfloat16)
    return np.concatenate([high, high, low], axis=-1)


def split_dot(table, x):
    gap = -x.shape[0] % PACK
    if gap:
        x = jnp.concatenate([x, jnp.zeros((gap, x.shape[1]), x.dtype)], axis=0)
    high, low = halves(x)
    return jnp.dot(table, jnp.concatenate([high, low, high], axis=0), preferred_element_type=jnp.float32)


class Extent:
    def __init__(self, margin):
        self.margin = margin
        self.reach = margin + SWEEPS - 1
        self.breadth = ROWS + 2 * self.reach
        self.packed = self.breadth + self.breadth // 2
        self.found = ROWS + 2 * margin


FIRST, LAST = Extent(3), Extent(2)


DIFFERENCE = ((1, 2.0 / 3.0), (-1, -2.0 / 3.0), (2, -1.0 / 12.0), (-2, 1.0 / 12.0))
CURVE = ((1, 4.0 / 3.0), (-1, 4.0 / 3.0), (2, -1.0 / 12.0), (-2, -1.0 / 12.0))


def lane(r, count=1):
    return slice(r * LANES, (r + count) * LANES)


def turned(tile, step):
    return pltpu.roll(tile, (-step) % LANES, 1)


def edge_masks():
    at = lax.axis_index("cross")
    last = lax.axis_size("cross") - 1
    flag = lambda test: jnp.where(test, 1.0, 0.0).astype(jnp.float32)
    return (flag(at >= 1), flag(at >= 2), flag(at <= last - 1), flag(at <= last - 2))


def masked(tile, e, masks):
    if e < -ROWS:
        return tile * masks[1]
    if e < 0:
        return tile * masks[0]
    if e >= 2 * ROWS:
        return tile * masks[3]
    if e >= ROWS:
        return tile * masks[2]
    return tile


def first_diff(up_one, down_one, up_two, down_two):
    return (8.0 * (up_one - down_one) - (up_two - down_two)) * (1.0 / 12.0)


def second_diff(middle, up_one, down_one, up_two, down_two):
    return (16.0 * (up_one + down_one) - (up_two + down_two) - 30.0 * middle) * (1.0 / 12.0)


def stream_slope(tile):
    return first_diff(turned(tile, 1), turned(tile, -1), turned(tile, 2), turned(tile, -2))


def open_kernel(
    cells, velocity, viscosity, moments, flat, thick, to_right, to_left, upward, downward, weights, sems
):
    copies = [pltpu.make_async_copy(moments, weights, sems.at[0])]
    for c in range(3):
        rows = slice(cells * c, cells * (c + 1))
        for r in range(ROWS):
            copies.append(
                pltpu.make_async_copy(velocity.at[c, :, r, :], flat.at[rows, lane(r)], sems.at[len(copies)])
            )
    for r in range(ROWS):
        copies.append(pltpu.make_async_copy(viscosity.at[:, r, :], thick.at[:, lane(r)], sems.at[len(copies)]))
    for copy in copies:
        copy.start()
    copies[0].wait()
    both = None
    for c in range(3):
        for copy in copies[1 + ROWS * c : 1 + ROWS * (c + 1)]:
            copy.wait()
        rows = slice(cells * c, cells * (c + 1))
        for k in range(2):
            slot(upward, cells, 2 * c + k)[...] = flat[rows, lane(2 + k)]
            slot(downward, cells, 2 * c + k)[...] = flat[rows, lane(k)]
        part = split_dot(weights[c], flat[rows, :])
        both = part if both is None else both + part
    to_right[...] = both[:PAD_V]
    to_left[...] = both[PAD_V:]
    for copy in copies[1 + 3 * ROWS :]:
        copy.wait()
    slot(upward, cells, 6)[...] = thick[:, lane(ROWS - 1)]
    slot(downward, cells, 6)[...] = thick[:, lane(0)]


def weighed(weights, value_at, r, home):
    total = None
    for reach, factor in weights:
        if (0 <= r + reach < ROWS) == home:
            part = factor * value_at(r + reach)
            total = part if total is None else total + part
    return total


def rough_kernel(cells, flat, thick, own, rough):
    for c in range(3):
        rows = slice(cells * c, cells * (c + 1))
        at = lambda r: flat[rows, lane(r)]
        spanned = dot(own[...], flat[rows, :])
        for r in range(ROWS):
            here = at(r)
            up_one, down_one = turned(here, 1), turned(here, -1)
            up_two, down_two = turned(here, 2), turned(here, -2)
            carried = (
                flat[:cells, lane(r)] * first_diff(up_one, down_one, up_two, down_two)
                + flat[cells : 2 * cells, lane(r)] * weighed(DIFFERENCE, at, r, True)
                + flat[2 * cells :, lane(r)] * spanned[:cells, lane(r)]
            )
            spread = (
                (4.0 / 3.0) * (up_one + down_one)
                - (1.0 / 12.0) * (up_two + down_two)
                - 5.0 * here
                + weighed(CURVE, at, r, True)
                + spanned[cells:, lane(r)]
            )
            rough[rows, lane(r)] = here + time_step * (thick[:, lane(r)] * spread - carried)


def add_beyond(cells, rough, flat, thick, left, right, low, high, slopes, section):
    masks = edge_masks()
    sides = jnp.concatenate([left[...], right[...]], axis=0)
    for c in range(3):
        rows = slice(cells * c, cells * (c + 1))
        spanned = split_dot(slopes[c], sides)

        def beyond(r):
            if r < 0:
                return masked(slot(low, cells, 2 * c + r + 2)[...], r, masks)
            return masked(slot(high, cells, 2 * c + r - ROWS)[...], r, masks)

        for r in range(ROWS):
            spread = spanned[cells:, lane(r)] + weighed(CURVE, beyond, r, False)
            carried = flat[cells : 2 * cells, lane(r)] * weighed(DIFFERENCE, beyond, r, False)
            carried = carried + flat[2 * cells :, lane(r)] * spanned[:cells, lane(r)]
            section[rows, lane(r)] = rough[rows, lane(r)] + time_step * (thick[:, lane(r)] * spread - carried)


def slot(ref, cells, k):
    return ref.at[cells * k : cells * (k + 1), :]


def fill_slots(ref, cells, blocks, moments):
    for k, block in enumerate(blocks):
        slot(ref, cells, k)[...] = block
    for k, block in enumerate(moments):
        top = cells * len(blocks) + PAD_M * k
        ref[top : top + PAD_M, :] = block


def own_source(cells, section, lateral, parts, owed={}):
    side = split_dot(lateral[...], section[2 * cells :, :])
    at = lambda r: section[cells : 2 * cells, lane(r)]
    blocks = []
    for r in range(ROWS):
        total = stream_slope(section[:cells, lane(r)]) + side[:cells, lane(r)] + weighed(DIFFERENCE, at, r, True)
        for reach, factor in DIFFERENCE:
            if r + reach in owed:
                total = total + factor * owed[r + reach]
        parts[:cells, lane(r)] = total
        blocks.append(total)
    parts[cells:, :] = side[cells:]
    moments = [side[cells:, lane(r)] for r in range(ROWS)]
    up = (2.0 / 3.0) * at(0) - (1.0 / 12.0) * at(1)
    down = (1.0 / 12.0) * at(ROWS - 2) - (2.0 / 3.0) * at(ROWS - 1)
    return blocks, moments, at, up, down


def tendency_kernel(
    cells, rough, flat, thick, left, right, low, high, slopes, lateral,
    section, parts, up_near, down_near, up_far, down_far,
):
    add_beyond(cells, rough, flat, thick, left, right, low, high, slopes, section)
    blocks, moments, at, _, _ = own_source(cells, section, lateral, parts)
    row = lambda c, r: section[cells * c : cells * (c + 1), lane(r)]
    every = [at(r) for r in range(ROWS)]
    for near, far, outer, inner in ((up_near, up_far, 0, 2), (down_near, down_far, 2, 0)):
        side = [row(c, inner + k) for c in (0, 2) for k in range(2)]
        fill_slots(near, cells, blocks[outer : outer + 2] + every + side, moments[outer : outer + 2])
        fill_slots(far, cells, blocks[inner : inner + 2] + [at(inner), at(inner + 1)], moments[inner : inner + 2])


def first_source(cells, parts, section, arrived, lateral, ext):
    low_one, high_one, low_two, high_two = arrived
    masks = edge_masks()
    span, tail = slice(0, cells), slice(cells, cells + PAD_M)
    pick = lambda ref, k: slot(ref, cells, k)[...]

    def across(e):
        if 0 <= e < ROWS:
            return section[cells : 2 * cells, lane(e)]
        if e < -ROWS or e >= 2 * ROWS:
            tile = pick(low_two, e + 8) if e < 0 else pick(high_two, e - 6)
        else:
            tile = pick(low_one, e + 6) if e < 0 else pick(high_one, e - 2)
        return masked(tile, e, masks)

    whole = (-2, -1, ROWS, ROWS + 1)
    given = [(low_one if e < 0 else high_one, e % 2) for e in whole]
    beside = split_dot(lateral[...], jnp.concatenate([pick(ref, 8 + k) for ref, k in given], axis=1))

    for e in range(-FIRST.reach, ROWS + FIRST.reach):
        if e in whole:
            at = whole.index(e)
            ref, k = given[at]
            total = stream_slope(pick(ref, 6 + k)) + beside[:cells, lane(at)]
            side = beside[cells:, lane(at)]
        elif 0 <= e < ROWS:
            total, side = parts[span, lane(e)], parts[tail, lane(e)]
        else:
            far = e < -ROWS or e >= 2 * ROWS
            ref = (low_two if e < 0 else high_two) if far else (low_one if e < 0 else high_one)
            top = (4 if far else 10) * cells + PAD_M * (e % 2)
            total, side = pick(ref, e % 2), ref[top : top + PAD_M, :]
        for reach, factor in DIFFERENCE:
            if e in whole or (e + reach) // ROWS != e // ROWS:
                total = total + factor * across(e + reach)
        ext[span, lane(e + FIRST.reach)] = masked(total, e, masks)
        ext[tail, lane(e + FIRST.reach)] = masked(side, e, masks)


def last_source(cells, parts, section, arrived, extra, ext):
    low_one, high_one, low_two, high_two = arrived
    masks = edge_masks()
    span, tail = slice(0, cells), slice(cells, cells + PAD_M)
    pick = lambda ref, k: slot(ref, cells, k)[...]

    def joined(e):
        if 0 <= e < ROWS:
            return parts[span, lane(e)], parts[tail, lane(e)]
        if e < -ROWS or e >= 2 * ROWS:
            ref = low_two if e < 0 else high_two
            return pick(ref, 0), ref[4 * cells :, :]
        ref, k = (low_one, e + ROWS) if e < 0 else (high_one, e - ROWS)
        top = 8 * cells + PAD_M * k
        return pick(ref, k), ref[top : top + PAD_M, :]

    def across(e, home):
        if e // ROWS == home // ROWS or home // ROWS in (-2, 2):
            return None
        if e < -ROWS:
            return masked(pick(low_two, 1 + e + ROWS + 2), e, masks)
        if e < 0:
            return masked(pick(low_one, ROWS + e + 2), e, masks)
        if e < ROWS:
            return section[cells : 2 * cells, lane(e)]
        if e < 2 * ROWS:
            return masked(pick(high_one, e), e, masks)
        return masked(pick(high_two, 1 + e - 2 * ROWS), e, masks)

    for e in range(-LAST.reach, ROWS + LAST.reach):
        total, side = joined(e)
        if e == -ROWS - 1:
            total = total + pick(low_one, 6)
        if e == 2 * ROWS:
            total = total + pick(high_one, 6)
        for reach, factor in DIFFERENCE:
            other = across(e + reach, e)
            if other is not None:
                total = total + factor * other
            if e + reach in extra and (e + reach) // ROWS == e // ROWS:
                total = total + factor * extra[e + reach]
        ext[span, lane(e + LAST.reach)] = masked(total, e, masks)
        ext[tail, lane(e + LAST.reach)] = masked(side, e, masks)


def pack_moments(extent, both, to_right, to_left):
    for side, out in enumerate((to_right, to_left)):
        top = 4 * GROUP * side
        out[:, lane(0, extent.breadth)] = both[top : top + 8]
        for k in range(extent.breadth // 2):
            out[:, lane(extent.breadth + k)] = (
                both[top + 8 : top + 16, lane(2 * k)] + both[top + 16 : top + 24, lane(2 * k + 1)]
            )


def source_kernel(
    cells, parts, section, low_one, high_one, low_two, high_two, lateral, source, moments, ext, to_right, to_left
):
    first_source(cells, parts, section, (low_one, high_one, low_two, high_two), lateral, ext)
    both = split_dot(source[...], ext[...])
    pack_moments(FIRST, both, to_right, to_left)
    held = sum(split_dot(moments[c], section[cells * c : cells * (c + 1), :]) for c in range(3))
    for side, out in enumerate((to_right, to_left)):
        top, base = 4 * GROUP * side, PAD_V * side
        out[:, lane(FIRST.packed, ROWS)] = held[base : base + 8]
        out[:, lane(FIRST.packed + ROWS, 3)] = jnp.zeros((GROUP, 3 * LANES), jnp.float32)
        for e in range(FIRST.breadth + ROWS):
            value = (
                both[top + 24 : top + 25, lane(e)]
                if e < FIRST.breadth
                else held[base + 8 : base + 9, lane(e - FIRST.breadth)]
            )
            row, tile = e % GROUP, FIRST.packed + ROWS + e // GROUP
            out[row : row + 1, lane(tile)] = value


def last_source_kernel(
    cells, parts, section, debts, low_one, high_one, low_two, high_two, source,
    ext, fixed, to_right, to_left,
):
    masks = edge_masks()
    pick = lambda ref, k: slot(ref, cells, k)[...]
    extra = {
        0: pick(low_one, 7) * masks[0],
        ROWS - 1: pick(high_one, 7) * masks[2],
        -1: pick(debts, 0),
        ROWS: pick(debts, 1),
        -ROWS: pick(low_two, 3) * masks[1],
        2 * ROWS - 1: pick(high_two, 3) * masks[3],
    }
    fixed[:cells, :] = extra[0]
    fixed[cells:, :] = extra[ROWS - 1]
    last_source(cells, parts, section, (low_one, high_one, low_two, high_two), extra, ext)
    pack_moments(LAST, split_dot(source[...], ext[...]), to_right, to_left)


def climb(extent, levels, depth):
    masks = edge_masks()
    for j in range(1, SWEEPS):
        before = slice(depth * (j - 1), depth * j)
        after = slice(depth * j, depth * (j + 1))
        for e in range(-extent.reach + j, ROWS + extent.reach - j):
            k = e + extent.reach
            here = levels[before, lane(k)]
            beside = (
                turned(here, 1) + turned(here, -1) + levels[before, lane(k + 1)] + levels[before, lane(k - 1)]
            )
            levels[after, lane(k)] = masked(beside, e, masks)
    return levels[:, lane(SWEEPS - 1, extent.found)]


def home_kernel(extent, ext, solve, partial, levels):
    depth = ext.shape[0]
    levels[:depth, :] = ext[...]
    partial[...] = dot(solve[...], climb(extent, levels, depth))


def spare(given, e):
    row, tile = e % GROUP, FIRST.packed + ROWS + e // GROUP
    return given[row : row + 1, lane(tile)]


def finish(extent, partial, left, right, solve, levels):
    for side, given in enumerate((left, right)):
        top = PAD_S * side
        levels[top : top + 8, :] = given[:, lane(0, extent.breadth)]
        for e in range(extent.breadth):
            tile = given[:, lane(extent.breadth + e // 2)]
            levels[top + 8 : top + 16, lane(e)] = pltpu.roll(tile, 4, 0) if e % 2 else tile
            if extent is FIRST:
                levels[top + 12 : top + 13, lane(e)] = spare(given, e)
    return partial[...] + split_dot(solve[...], climb(extent, levels, 2 * PAD_S))


def gradient(extent, found, c, rows, slope_rows, r):
    masks = edge_masks()
    phi = lambda r: masked(found[rows, lane(r + extent.margin)], r, masks)
    if c == 0:
        return stream_slope(phi(r))
    if c == 1:
        inside = lambda r: -extent.margin <= r < ROWS + extent.margin
        return sum(factor * phi(r + reach) for reach, factor in DIFFERENCE if inside(r + reach))
    return found[slope_rows, lane(r + extent.margin)]


def middle_kernel(
    cells, partial, left, right, section, solve, low_one, high_one, low, high, start, thick, full, lateral,
    following, parts, debts, up_near, down_near, up_far, down_far, levels, flat, rim, sides,
):
    masks = edge_masks()
    found = finish(FIRST, partial, left, right, solve, levels)
    home, home_slope = slice(0, cells), slice(cells, 2 * cells)
    outer = (-2, -1, ROWS, ROWS + 1)
    for c in range(3):
        rows = slice(cells * c, cells * (c + 1))
        for r in range(ROWS):
            flat[rows, lane(r)] = section[rows, lane(r)] - gradient(FIRST, found, c, home, home_slope, r)
        for k, r in enumerate(outer):
            first = (6, 4 if r < 0 else 2, 8)[c]
            value = slot(low_one if r < 0 else high_one, cells, first + k % 2)[...]
            value = value - gradient(FIRST, found, c, home, home_slope, r)
            rim[rows, lane(k)] = masked(value, r, masks)
    for side, given in enumerate((left, right)):
        base, top = PAD_V * side, 2 * cells + 2 * GROUP * side
        phi_rows, slope_rows = slice(top, top + GROUP), slice(top + GROUP, top + 2 * GROUP)
        sides[base : base + GROUP, :] = given[:, lane(FIRST.packed, ROWS)]
        sides[base + GROUP : base + PAD_V, :] = jnp.zeros((PAD_V - GROUP, ROWS * LANES), jnp.float32)
        for r in range(ROWS):
            sides[base + GROUP : base + GROUP + 1, lane(r)] = spare(given, FIRST.breadth + r)
            for c in range(3):
                rows = slice(base + RANK_V * c, base + RANK_V * (c + 1))
                change = gradient(FIRST, found, c, phi_rows, slope_rows, r)[:RANK_V]
                sides[rows, lane(r)] = sides[rows, lane(r)] - change

    def tile(c, r):
        rows = slice(cells * c, cells * (c + 1))
        return flat[rows, lane(r)] if 0 <= r < ROWS else rim[rows, lane(r + 2 if r < 0 else r - 2)]

    for c in range(3):
        rows = slice(cells * c, cells * (c + 1))
        spanned = split_dot(full[c], jnp.concatenate([flat[rows, :], sides[...]], axis=0))
        for r in range(ROWS):
            here = tile(c, r)
            up_one, down_one = turned(here, 1), turned(here, -1)
            up_two, down_two = turned(here, 2), turned(here, -2)
            carried = (
                tile(0, r) * first_diff(up_one, down_one, up_two, down_two)
                + tile(1, r) * sum(factor * tile(c, r + reach) for reach, factor in DIFFERENCE)
                + tile(2, r) * spanned[:cells, lane(r)]
            )
            spread = (
                (4.0 / 3.0) * (up_one + down_one)
                - (1.0 / 12.0) * (up_two + down_two)
                - 5.0 * here
                + sum(factor * tile(c, r + reach) for reach, factor in CURVE)
                + spanned[cells:, lane(r)]
            )
            moved = here + time_step * (thick[:, lane(r)] * spread - carried)
            following[rows, lane(r)] = 0.5 * start[rows, lane(r)] + 0.5 * moved
    phi = lambda r: found[:cells, lane(r + FIRST.margin)]
    scale = 0.5 * time_step / 144.0
    owed = {
        -1: scale * (tile(1, -1) - slot(low, cells, 6)[...]) * phi(ROWS - 1) * masks[0],
        ROWS: scale * (tile(1, ROWS) + slot(high, cells, 6)[...]) * phi(0) * masks[2],
    }
    slot(debts, cells, 0)[...] = owed[-1]
    slot(debts, cells, 1)[...] = owed[ROWS]
    blocks, moments, at, up, down = own_source(cells, following, lateral, parts, owed)
    fill_slots(up_near, cells, blocks + [at(2), at(3), up, owed[ROWS]], moments)
    fill_slots(down_near, cells, blocks + [at(0), at(1), down, owed[-1]], moments)
    fill_slots(up_far, cells, [blocks[3], at(2), at(3), owed[ROWS]], moments[3:])
    fill_slots(down_far, cells, [blocks[0], at(0), at(1), owed[-1]], moments[:1])


def last_kernel(cells, partial, left, right, section, fixed, solve, out, levels, staged, sems):
    found = finish(LAST, partial, left, right, solve, levels)
    copies = []
    for c in (2, 0, 1):
        rows = slice(cells * c, cells * (c + 1))
        for r in range(ROWS):
            value = section[rows, lane(r)]
            if c == 1 and r in (0, ROWS - 1):
                value = value + fixed[cells * (r > 0) : cells * (1 + (r > 0)), :]
            value = value - gradient(LAST, found, c, slice(0, cells), slice(cells, 2 * cells), r)
            staged[rows, lane(r)] = value
            copies.append(
                pltpu.make_async_copy(staged.at[rows, lane(r)], out.at[c, :, r, :], sems.at[len(copies)])
            )
            copies[-1].start()
    for copy in copies:
        copy.wait()


def call(body, shapes, *args, scratch=(), **options):
    return pl.pallas_call(
        body,
        out_shape=[jax.ShapeDtypeStruct(s, jnp.float32) for s in shapes],
        scratch_shapes=scratch,
        compiler_params=pltpu.CompilerParams(vmem_limit_bytes=40 * 1024 * 1024),
        **options,
    )(*args)


def shifted(block, axis, step):
    count = lax.axis_size(axis)
    return lax.ppermute(block, axis, [(i, (i + step) % count) for i in range(count)])


def per_device(velocity, viscosity):
    components, cells, row_cells, columns = velocity.shape
    length = cells * lax.axis_size("span")
    own, first_own, slopes, full, moments, lateral, *first = (
        jnp.asarray(t) for t in tables(length, cells, False)
    )
    _, last_own, _, _, _, _, *last = (jnp.asarray(t) for t in tables(length, cells, True))
    width = row_cells * columns
    near = cells + PAD_M
    whole, edge, rim = (components * cells, width), (PAD_V, width), (7 * cells, columns)

    def across(up_near, down_near, up_far, down_far):
        return (
            shifted(up_near, "cross", 1), shifted(down_near, "cross", -1),
            shifted(up_far, "cross", 2), shifted(down_far, "cross", -2),
        )

    def message(near_slots, near_rows, far_slots, far_rows):
        near_shape = (near_slots * cells + near_rows * PAD_M, columns)
        far_shape = (far_slots * cells + far_rows * PAD_M, columns)
        return [near_shape] * 2 + [far_shape] * 2

    def levels(extent, depth):
        return pltpu.VMEM((SWEEPS * depth, extent.breadth * columns), jnp.float32)

    start, thick, to_right, to_left, upward, downward = call(
        functools.partial(open_kernel, cells),
        [whole, (cells, width), edge, edge, rim, rim],
        *(pltpu.with_memory_space_constraint(x, pltpu.HBM) for x in (velocity, viscosity, moments)),
        in_specs=[pl.BlockSpec(memory_space=pltpu.HBM)] * 3,
        scratch=[pltpu.VMEM(moments.shape, moments.dtype), pltpu.SemaphoreType.DMA((1 + 4 * ROWS,))],
    )
    left = shifted(to_right, "span", 1)
    right = shifted(to_left, "span", -1)
    low = shifted(upward, "cross", 1)
    high = shifted(downward, "cross", -1)
    (rough,) = call(functools.partial(rough_kernel, cells), [whole], start, thick, own)
    section, parts, *sent = call(
        functools.partial(tendency_kernel, cells),
        [whole, (near, width)] + message(10, 2, 4, 2),
        rough, start, thick, left, right, low, high, slopes, lateral,
    )
    arrived = across(*sent)
    ext, to_right, to_left = call(
        functools.partial(source_kernel, cells),
        [(near, FIRST.breadth * columns)] + [(GROUP, (FIRST.packed + ROWS + 3) * columns)] * 2,
        parts, section, *arrived, lateral, first[0], moments,
    )
    left = shifted(to_right, "span", 1)
    right = shifted(to_left, "span", -1)
    (partial,) = call(
        functools.partial(home_kernel, FIRST),
        [(first_own.shape[0], FIRST.found * columns)],
        ext, first_own,
        scratch=[levels(FIRST, near)],
    )

    section, parts, debts, *sent = call(
        functools.partial(middle_kernel, cells),
        [whole, (near, width), (2 * cells, columns)] + message(8, 4, 4, 1),
        partial, left, right, section, first[1], *arrived[:2], low, high, start, thick, full, lateral,
        scratch=[
            levels(FIRST, 2 * PAD_S),
            pltpu.VMEM(whole, jnp.float32),
            pltpu.VMEM((components * cells, 4 * columns), jnp.float32),
            pltpu.VMEM((2 * PAD_V, width), jnp.float32),
        ],
    )
    arrived = across(*sent)
    ext, fixed, to_right, to_left = call(
        functools.partial(last_source_kernel, cells),
        [(near, LAST.breadth * columns), (2 * cells, columns)] + [(GROUP, LAST.packed * columns)] * 2,
        parts, section, debts, *arrived, last[0],
    )
    left = shifted(to_right, "span", 1)
    right = shifted(to_left, "span", -1)
    (partial,) = call(
        functools.partial(home_kernel, LAST),
        [(last_own.shape[0], LAST.found * columns)],
        ext, last_own,
        scratch=[levels(LAST, near)],
    )
    (out,) = call(
        functools.partial(last_kernel, cells),
        [velocity.shape],
        partial, left, right, section, fixed, last[1],
        scratch=[
            levels(LAST, 2 * PAD_S),
            pltpu.VMEM(whole, jnp.float32),
            pltpu.SemaphoreType.DMA((3 * ROWS,)),
        ],
        out_specs=[pl.BlockSpec(memory_space=pltpu.HBM)],
    )
    return out


def solution(mesh):
    in_specs = (P(None, "span", "cross", None), P("span", "cross", None))
    out_specs = P(None, "span", "cross", None)
    return jax.shard_map(
        per_device, mesh=mesh, in_specs=in_specs, out_specs=out_specs, check_vma=False
    )
```

```python
import functools

import jax
import jax.numpy as jnp
import ml_dtypes
import numpy as np
from jax import lax
from jax.experimental import pallas as pl
from jax.experimental.pallas import tpu as pltpu
from jax.sharding import PartitionSpec as P

SWEEPS = 4
ROWS = 4
LANES = 128
time_step = 0.1
highest = lax.Precision.HIGHEST
PAD_V = 16
PAD_S = 16
PAD_M = 8
GROUP = 8
PACK = 16
RANK_V = 3
RANK_M = 2


def symbols(length):
    w = 2.0 * np.pi * np.arange(length) / length
    first = (14.0 / 9.0 * np.sin(w) + np.sin(2.0 * w) / 18.0) / (1.0 + 2.0 / 3.0 * np.cos(w))
    second = (24.0 / 11.0 * (1.0 - np.cos(w)) + 3.0 / 22.0 * (1.0 - np.cos(2.0 * w))) / (
        1.0 + 4.0 / 11.0 * np.cos(w)
    )
    return 1j * first, -second, 1.0 / (4.0 + second)


def block_of(symbol, cells, offset):
    kernel = np.fft.ifft(symbol).real
    at = np.arange(cells)
    return kernel[(at[:, None] - (at[None, :] + offset * cells)) % len(kernel)]


def low_rank(stack, rank):
    left, scale, right = np.linalg.svd(stack, full_matrices=False)
    return left[:, :rank] * scale[:rank], right[:rank]


@functools.lru_cache(None)
def tables(length, cells, last):
    first, second, inverse = symbols(length)
    at = lambda symbol, offset: block_of(symbol, cells, offset)
    from_left, take_left = low_rank(np.concatenate([at(first, -1), at(second, -1)]), RANK_V)
    from_right, take_right = low_rank(np.concatenate([at(first, 1), at(second, 1)]), RANK_V)
    own = np.concatenate([at(first, 0), at(second, 0)])
    slopes = np.zeros((3, 2 * cells, 2 * PAD_V))
    moments = np.zeros((3, 2 * PAD_V, cells))
    for c in range(3):
        rows = slice(RANK_V * c, RANK_V * (c + 1))
        slopes[c, :, :PAD_V][:, rows] = from_left
        slopes[c, :, PAD_V:][:, rows] = from_right
        moments[c, rows] = take_left
        moments[c, PAD_V:][rows] = take_right
    m_left, t_left = low_rank(at(first, -1), RANK_M)
    m_right, t_right = low_rank(at(first, 1), RANK_M)
    lateral = np.zeros((cells + PAD_M, cells))
    lateral[:cells] = at(first, 0)
    lateral[cells : cells + RANK_M] = t_left
    lateral[cells + RANK_M : cells + 2 * RANK_M] = t_right
    powers = [inverse ** (j + 1) for j in range(SWEEPS)]
    stacked = [p for p in powers] + [first * p for p in powers]
    count = len(stacked)
    RANK_S = 2 * SWEEPS + (1 if last else 3)
    kept = [] if last else stacked
    s_left, q_left = low_rank(
        np.concatenate([at(p, -1) for p in stacked] + [take_left @ at(p, 0) for p in kept]), RANK_S
    )
    s_right, q_right = low_rank(
        np.concatenate([at(p, 1) for p in stacked] + [take_right @ at(p, 0) for p in kept]), RANK_S
    )
    e_left, e_right = s_left[count * cells :], s_right[count * cells :]
    source = np.zeros((8 * GROUP, cells + PAD_M))
    for side, q in enumerate((q_left, q_right)):
        rows = np.zeros((PAD_S, cells + PAD_M))
        rows[:RANK_S, :cells] = q
        at_m = cells + RANK_M * side
        rows[RANK_S : RANK_S + RANK_M, at_m : at_m + RANK_M] = np.eye(RANK_M)
        top = 4 * GROUP * side
        source[top : top + 8] = rows[:8]
        source[top + 8 : top + 12] = rows[8:12]
        source[top + 20 : top + 24] = rows[8:12]
        source[top + 24] = rows[12]
    near, wide = cells + PAD_M, 2 * PAD_S
    height = 2 * cells + (0 if last else 4 * GROUP)
    solve_own = np.zeros((height, SWEEPS * near))
    solve_sides = np.zeros((height, SWEEPS * wide))
    for j in range(SWEEPS):
        for half in range(2):
            index = half * SWEEPS + j
            rows = slice(cells * index, cells * (index + 1))
            edge = slice(RANK_V * index, RANK_V * (index + 1))
            center = at(stacked[index], 0)
            by_left, by_right = s_left[rows], s_right[rows]
            mine, sides = np.zeros((cells, near)), np.zeros((cells, wide))
            mine[:, :cells] = center
            mine[:, cells : cells + RANK_M] = by_right @ (q_right @ m_left)
            mine[:, cells + RANK_M : cells + 2 * RANK_M] = by_left @ (q_left @ m_right)
            sides[:, :RANK_S] = by_left
            sides[:, RANK_S : RANK_S + RANK_M] = center @ m_left
            sides[:, PAD_S : PAD_S + RANK_S] = by_right
            sides[:, PAD_S + RANK_S : PAD_S + RANK_S + RANK_M] = center @ m_right
            solve_own[cells * half : cells * (half + 1), near * j : near * (j + 1)] = -mine
            solve_sides[cells * half : cells * (half + 1), wide * j : wide * (j + 1)] = -sides
            for side in range(0 if last else 2):
                mine, sides = np.zeros((RANK_V, near)), np.zeros((RANK_V, wide))
                if side == 0:
                    back = take_left @ by_right @ q_right
                    mine[:, cells + RANK_M : cells + 2 * RANK_M] = take_left @ center @ m_right
                    sides[:, :RANK_S] = e_left[edge]
                else:
                    back = take_right @ by_left @ q_left
                    mine[:, cells : cells + RANK_M] = take_right @ center @ m_left
                    sides[:, PAD_S : PAD_S + RANK_S] = e_right[edge]
                mine[:, :cells] = back
                sides[:, RANK_S : RANK_S + RANK_M] = back @ m_left
                sides[:, PAD_S + RANK_S : PAD_S + RANK_S + RANK_M] = back @ m_right
                top = 2 * cells + GROUP * (2 * side + half)
                solve_own[top : top + RANK_V, near * j : near * (j + 1)] = -mine
                solve_sides[top : top + RANK_V, wide * j : wide * (j + 1)] = -sides
    full = np.concatenate([own, from_left, from_right], axis=1)
    full = np.pad(full, [(0, 0), (0, GROUP - 2 * RANK_V)])
    plain, split = (own, solve_own), (slopes, full, moments, lateral, source, solve_sides)
    return [x.astype(np.float32) for x in plain] + [split_table(x.astype(np.float32)) for x in split]


def dot(a, b):
    return jnp.dot(a, b, precision=highest, preferred_element_type=jnp.float32)


def halves(x):
    high = x.astype(jnp.bfloat16)
    return high, (x - high.astype(jnp.float32)).astype(jnp.bfloat16)


def split_table(table):
    gap = -table.shape[-1] % PACK
    table = np.pad(table, [(0, 0)] * (table.ndim - 1) + [(0, gap)])
    high = table.astype(ml_dtypes.bfloat16)
    low = (table - high.astype(np.float32)).astype(ml_dtypes.bfloat16)
    return np.concatenate([high, high, low], axis=-1)


def split_dot(table, x):
    gap = -x.shape[0] % PACK
    if gap:
        x = jnp.concatenate([x, jnp.zeros((gap, x.shape[1]), x.dtype)], axis=0)
    high, low = halves(x)
    return jnp.dot(table, jnp.concatenate([high, low, high], axis=0), preferred_element_type=jnp.float32)


class Extent:
    def __init__(self, margin):
        self.margin = margin
        self.reach = margin + SWEEPS - 1
        self.breadth = ROWS + 2 * self.reach
        self.packed = self.breadth + self.breadth // 2
        self.found = ROWS + 2 * margin


FIRST, LAST = Extent(3), Extent(2)


DIFFERENCE = ((1, 2.0 / 3.0), (-1, -2.0 / 3.0), (2, -1.0 / 12.0), (-2, 1.0 / 12.0))
CURVE = ((1, 4.0 / 3.0), (-1, 4.0 / 3.0), (2, -1.0 / 12.0), (-2, -1.0 / 12.0))


def lane(r, count=1):
    return slice(r * LANES, (r + count) * LANES)


def turned(tile, step):
    return pltpu.roll(tile, (-step) % LANES, 1)


def edge_masks():
    at = lax.axis_index("cross")
    last = lax.axis_size("cross") - 1
    flag = lambda test: jnp.where(test, 1.0, 0.0).astype(jnp.float32)
    return (flag(at >= 1), flag(at >= 2), flag(at <= last - 1), flag(at <= last - 2))


def masked(tile, e, masks):
    if e < -ROWS:
        return tile * masks[1]
    if e < 0:
        return tile * masks[0]
    if e >= 2 * ROWS:
        return tile * masks[3]
    if e >= ROWS:
        return tile * masks[2]
    return tile


def first_diff(up_one, down_one, up_two, down_two):
    return (8.0 * (up_one - down_one) - (up_two - down_two)) * (1.0 / 12.0)


def second_diff(middle, up_one, down_one, up_two, down_two):
    return (16.0 * (up_one + down_one) - (up_two + down_two) - 30.0 * middle) * (1.0 / 12.0)


def stream_slope(tile):
    return first_diff(turned(tile, 1), turned(tile, -1), turned(tile, 2), turned(tile, -2))


def open_kernel(
    cells, velocity, viscosity, moments, flat, thick, to_right, to_left, upward, downward, weights, sems
):
    copies = [pltpu.make_async_copy(moments, weights, sems.at[0])]
    for c in range(3):
        rows = slice(cells * c, cells * (c + 1))
        for r in range(ROWS):
            copies.append(
                pltpu.make_async_copy(velocity.at[c, :, r, :], flat.at[rows, lane(r)], sems.at[len(copies)])
            )
    for r in range(ROWS):
        copies.append(pltpu.make_async_copy(viscosity.at[:, r, :], thick.at[:, lane(r)], sems.at[len(copies)]))
    for copy in copies:
        copy.start()
    copies[0].wait()
    both = None
    for c in range(3):
        for copy in copies[1 + ROWS * c : 1 + ROWS * (c + 1)]:
            copy.wait()
        rows = slice(cells * c, cells * (c + 1))
        for k in range(2):
            slot(upward, cells, 2 * c + k)[...] = flat[rows, lane(2 + k)]
            slot(downward, cells, 2 * c + k)[...] = flat[rows, lane(k)]
        part = split_dot(weights[c], flat[rows, :])
        both = part if both is None else both + part
    to_right[...] = both[:PAD_V]
    to_left[...] = both[PAD_V:]
    for copy in copies[1 + 3 * ROWS :]:
        copy.wait()
    slot(upward, cells, 6)[...] = thick[:, lane(ROWS - 1)]
    slot(downward, cells, 6)[...] = thick[:, lane(0)]


def weighed(weights, value_at, r, home):
    total = None
    for reach, factor in weights:
        if (0 <= r + reach < ROWS) == home:
            part = factor * value_at(r + reach)
            total = part if total is None else total + part
    return total


def rough_kernel(cells, flat, thick, own, rough):
    for c in range(3):
        rows = slice(cells * c, cells * (c + 1))
        at = lambda r: flat[rows, lane(r)]
        spanned = dot(own[...], flat[rows, :])
        for r in range(ROWS):
            here = at(r)
            up_one, down_one = turned(here, 1), turned(here, -1)
            up_two, down_two = turned(here, 2), turned(here, -2)
            carried = (
                flat[:cells, lane(r)] * first_diff(up_one, down_one, up_two, down_two)
                + flat[cells : 2 * cells, lane(r)] * weighed(DIFFERENCE, at, r, True)
                + flat[2 * cells :, lane(r)] * spanned[:cells, lane(r)]
            )
            spread = (
                (4.0 / 3.0) * (up_one + down_one)
                - (1.0 / 12.0) * (up_two + down_two)
                - 5.0 * here
                + weighed(CURVE, at, r, True)
                + spanned[cells:, lane(r)]
            )
            rough[rows, lane(r)] = here + time_step * (thick[:, lane(r)] * spread - carried)


def add_beyond(cells, rough, flat, thick, left, right, low, high, slopes, section):
    masks = edge_masks()
    sides = jnp.concatenate([left[...], right[...]], axis=0)
    for c in range(3):
        rows = slice(cells * c, cells * (c + 1))
        spanned = split_dot(slopes[c], sides)

        def beyond(r):
            if r < 0:
                return masked(slot(low, cells, 2 * c + r + 2)[...], r, masks)
            return masked(slot(high, cells, 2 * c + r - ROWS)[...], r, masks)

        for r in range(ROWS):
            spread = spanned[cells:, lane(r)] + weighed(CURVE, beyond, r, False)
            carried = flat[cells : 2 * cells, lane(r)] * weighed(DIFFERENCE, beyond, r, False)
            carried = carried + flat[2 * cells :, lane(r)] * spanned[:cells, lane(r)]
            section[rows, lane(r)] = rough[rows, lane(r)] + time_step * (thick[:, lane(r)] * spread - carried)


def slot(ref, cells, k):
    return ref.at[cells * k : cells * (k + 1), :]


def fill_slots(ref, cells, blocks, moments):
    for k, block in enumerate(blocks):
        slot(ref, cells, k)[...] = block
    for k, block in enumerate(moments):
        top = cells * len(blocks) + PAD_M * k
        ref[top : top + PAD_M, :] = block


def own_source(cells, section, lateral, parts, owed={}):
    side = split_dot(lateral[...], section[2 * cells :, :])
    at = lambda r: section[cells : 2 * cells, lane(r)]
    blocks = []
    for r in range(ROWS):
        total = stream_slope(section[:cells, lane(r)]) + side[:cells, lane(r)] + weighed(DIFFERENCE, at, r, True)
        for reach, factor in DIFFERENCE:
            if r + reach in owed:
                total = total + factor * owed[r + reach]
        parts[:cells, lane(r)] = total
        blocks.append(total)
    parts[cells:, :] = side[cells:]
    moments = [side[cells:, lane(r)] for r in range(ROWS)]
    up = (2.0 / 3.0) * at(0) - (1.0 / 12.0) * at(1)
    down = (1.0 / 12.0) * at(ROWS - 2) - (2.0 / 3.0) * at(ROWS - 1)
    return blocks, moments, at, up, down


def tendency_kernel(
    cells, rough, flat, thick, left, right, low, high, slopes, lateral,
    section, parts, up_near, down_near, up_far, down_far,
):
    add_beyond(cells, rough, flat, thick, left, right, low, high, slopes, section)
    blocks, moments, at, _, _ = own_source(cells, section, lateral, parts)
    row = lambda c, r: section[cells * c : cells * (c + 1), lane(r)]
    every = [at(r) for r in range(ROWS)]
    for near, far, outer, inner in ((up_near, up_far, 0, 2), (down_near, down_far, 2, 0)):
        side = [row(c, inner + k) for c in (0, 2) for k in range(2)]
        fill_slots(near, cells, blocks[outer : outer + 2] + every + side, moments[outer : outer + 2])
        fill_slots(far, cells, blocks[inner : inner + 2] + [at(inner), at(inner + 1)], moments[inner : inner + 2])


WHOLE = (-2, -1, ROWS, ROWS + 1)


def row_across(cells, section, arrived):
    low_one, high_one, low_two, high_two = arrived
    masks = edge_masks()

    def value(e):
        if 0 <= e < ROWS:
            return section[cells : 2 * cells, lane(e)]
        if e < -ROWS or e >= 2 * ROWS:
            ref, k = (low_two, e + 8) if e < 0 else (high_two, e - 6)
        else:
            ref, k = (low_one, e + 6) if e < 0 else (high_one, e - 2)
        return masked(slot(ref, cells, k)[...], e, masks)

    return value


def near_source_kernel(cells, parts, section, low_one, high_one, lateral, moments, middle, held):
    masks = edge_masks()
    across = row_across(cells, section, (low_one, high_one, None, None))
    pick = lambda ref, k: slot(ref, cells, k)[...]
    given = [(low_one if e < 0 else high_one, e % 2) for e in WHOLE]
    beside = split_dot(lateral[...], jnp.concatenate([pick(ref, 8 + k) for ref, k in given], axis=1))
    for e in range(-2, ROWS + 2):
        if e in WHOLE:
            at = WHOLE.index(e)
            ref, k = given[at]
            total = stream_slope(pick(ref, 6 + k)) + beside[:cells, lane(at)]
            side = beside[cells:, lane(at)]
        else:
            total, side = parts[:cells, lane(e)], parts[cells:, lane(e)]
        for reach, factor in DIFFERENCE:
            if e in WHOLE or not 0 <= e + reach < ROWS:
                total = total + factor * across(e + reach)
        middle[:cells, lane(e + 2)] = masked(total, e, masks)
        middle[cells:, lane(e + 2)] = masked(side, e, masks)
    held[...] = sum(split_dot(moments[c], section[cells * c : cells * (c + 1), :]) for c in range(3))


def first_source(cells, middle, arrived, ext):
    low_one, high_one, low_two, high_two = arrived
    masks = edge_masks()
    across = row_across(cells, None, arrived)
    ext[:, lane(FIRST.reach - 2, ROWS + 4)] = middle[...]
    for e in range(-FIRST.reach, ROWS + FIRST.reach):
        if -2 <= e < ROWS + 2:
            continue
        far = e < -ROWS or e >= 2 * ROWS
        ref = (low_two if e < 0 else high_two) if far else (low_one if e < 0 else high_one)
        top = (4 if far else 10) * cells + PAD_M * (e % 2)
        total, side = slot(ref, cells, e % 2)[...], ref[top : top + PAD_M, :]
        for reach, factor in DIFFERENCE:
            if (e + reach) // ROWS != e // ROWS:
                total = total + factor * across(e + reach)
        ext[:cells, lane(e + FIRST.reach)] = masked(total, e, masks)
        ext[cells:, lane(e + FIRST.reach)] = masked(side, e, masks)


def last_source(cells, parts, section, arrived, extra, ext):
    low_one, high_one, low_two, high_two = arrived
    masks = edge_masks()
    span, tail = slice(0, cells), slice(cells, cells + PAD_M)
    pick = lambda ref, k: slot(ref, cells, k)[...]

    def joined(e):
        if 0 <= e < ROWS:
            return parts[span, lane(e)], parts[tail, lane(e)]
        if e < -ROWS or e >= 2 * ROWS:
            ref = low_two if e < 0 else high_two
            return pick(ref, 0), ref[4 * cells :, :]
        ref, k = (low_one, e + ROWS) if e < 0 else (high_one, e - ROWS)
        top = 8 * cells + PAD_M * k
        return pick(ref, k), ref[top : top + PAD_M, :]

    def across(e, home):
        if e // ROWS == home // ROWS or home // ROWS in (-2, 2):
            return None
        if e < -ROWS:
            return masked(pick(low_two, 1 + e + ROWS + 2), e, masks)
        if e < 0:
            return masked(pick(low_one, ROWS + e + 2), e, masks)
        if e < ROWS:
            return section[cells : 2 * cells, lane(e)]
        if e < 2 * ROWS:
            return masked(pick(high_one, e), e, masks)
        return masked(pick(high_two, 1 + e - 2 * ROWS), e, masks)

    for e in range(-LAST.reach, ROWS + LAST.reach):
        total, side = joined(e)
        if e == -ROWS - 1:
            total = total + pick(low_one, 6)
        if e == 2 * ROWS:
            total = total + pick(high_one, 6)
        for reach, factor in DIFFERENCE:
            other = across(e + reach, e)
            if other is not None:
                total = total + factor * other
            if e + reach in extra and (e + reach) // ROWS == e // ROWS:
                total = total + factor * extra[e + reach]
        ext[span, lane(e + LAST.reach)] = masked(total, e, masks)
        ext[tail, lane(e + LAST.reach)] = masked(side, e, masks)


def pack_moments(extent, both, to_right, to_left):
    for side, out in enumerate((to_right, to_left)):
        top = 4 * GROUP * side
        out[:, lane(0, extent.breadth)] = both[top : top + 8]
        for k in range(extent.breadth // 2):
            out[:, lane(extent.breadth + k)] = (
                both[top + 8 : top + 16, lane(2 * k)] + both[top + 16 : top + 24, lane(2 * k + 1)]
            )


def source_kernel(
    cells, middle, held, low_one, high_one, low_two, high_two, source, ext, to_right, to_left
):
    first_source(cells, middle, (low_one, high_one, low_two, high_two), ext)
    both = split_dot(source[...], ext[...])
    pack_moments(FIRST, both, to_right, to_left)
    for side, out in enumerate((to_right, to_left)):
        top, base = 4 * GROUP * side, PAD_V * side
        out[:, lane(FIRST.packed, ROWS)] = held[base : base + 8]
        out[:, lane(FIRST.packed + ROWS, 3)] = jnp.zeros((GROUP, 3 * LANES), jnp.float32)
        for e in range(FIRST.breadth + ROWS):
            value = (
                both[top + 24 : top + 25, lane(e)]
                if e < FIRST.breadth
                else held[base + 8 : base + 9, lane(e - FIRST.breadth)]
            )
            row, tile = e % GROUP, FIRST.packed + ROWS + e // GROUP
            out[row : row + 1, lane(tile)] = value


def last_source_kernel(
    cells, parts, section, debts, low_one, high_one, low_two, high_two, source,
    ext, fixed, to_right, to_left,
):
    masks = edge_masks()
    pick = lambda ref, k: slot(ref, cells, k)[...]
    extra = {
        0: pick(low_one, 7) * masks[0],
        ROWS - 1: pick(high_one, 7) * masks[2],
        -1: pick(debts, 0),
        ROWS: pick(debts, 1),
        -ROWS: pick(low_two, 3) * masks[1],
        2 * ROWS - 1: pick(high_two, 3) * masks[3],
    }
    fixed[:cells, :] = extra[0]
    fixed[cells:, :] = extra[ROWS - 1]
    last_source(cells, parts, section, (low_one, high_one, low_two, high_two), extra, ext)
    pack_moments(LAST, split_dot(source[...], ext[...]), to_right, to_left)


def climb(extent, levels, depth):
    masks = edge_masks()
    for j in range(1, SWEEPS):
        before = slice(depth * (j - 1), depth * j)
        after = slice(depth * j, depth * (j + 1))
        for e in range(-extent.reach + j, ROWS + extent.reach - j):
            k = e + extent.reach
            here = levels[before, lane(k)]
            beside = (
                turned(here, 1) + turned(here, -1) + levels[before, lane(k + 1)] + levels[before, lane(k - 1)]
            )
            levels[after, lane(k)] = masked(beside, e, masks)
    return levels[:, lane(SWEEPS - 1, extent.found)]


def home_kernel(extent, ext, solve, partial, levels):
    depth = ext.shape[0]
    levels[:depth, :] = ext[...]
    partial[...] = dot(solve[...], climb(extent, levels, depth))


def spare(given, e):
    row, tile = e % GROUP, FIRST.packed + ROWS + e // GROUP
    return given[row : row + 1, lane(tile)]


def finish(extent, partial, left, right, solve, levels):
    for side, given in enumerate((left, right)):
        top = PAD_S * side
        levels[top : top + 8, :] = given[:, lane(0, extent.breadth)]
        for e in range(extent.breadth):
            tile = given[:, lane(extent.breadth + e // 2)]
            levels[top + 8 : top + 16, lane(e)] = pltpu.roll(tile, 4, 0) if e % 2 else tile
            if extent is FIRST:
                levels[top + 12 : top + 13, lane(e)] = spare(given, e)
    return partial[...] + split_dot(solve[...], climb(extent, levels, 2 * PAD_S))


def gradient(extent, found, c, rows, slope_rows, r):
    masks = edge_masks()
    phi = lambda r: masked(found[rows, lane(r + extent.margin)], r, masks)
    if c == 0:
        return stream_slope(phi(r))
    if c == 1:
        inside = lambda r: -extent.margin <= r < ROWS + extent.margin
        return sum(factor * phi(r + reach) for reach, factor in DIFFERENCE if inside(r + reach))
    return found[slope_rows, lane(r + extent.margin)]


def middle_kernel(
    cells, partial, left, right, section, solve, low_one, high_one, low, high, start, thick, full, lateral,
    following, parts, debts, up_near, down_near, up_far, down_far, levels, flat, rim, sides,
):
    masks = edge_masks()
    found = finish(FIRST, partial, left, right, solve, levels)
    home, home_slope = slice(0, cells), slice(cells, 2 * cells)
    outer = (-2, -1, ROWS, ROWS + 1)
    for c in range(3):
        rows = slice(cells * c, cells * (c + 1))
        for r in range(ROWS):
            flat[rows, lane(r)] = section[rows, lane(r)] - gradient(FIRST, found, c, home, home_slope, r)
        for k, r in enumerate(outer):
            first = (6, 4 if r < 0 else 2, 8)[c]
            value = slot(low_one if r < 0 else high_one, cells, first + k % 2)[...]
            value = value - gradient(FIRST, found, c, home, home_slope, r)
            rim[rows, lane(k)] = masked(value, r, masks)
    sides[...] = jnp.zeros(sides.shape, jnp.float32)
    for side, given in enumerate((left, right)):
        top = 2 * cells + 2 * GROUP * side
        phi_rows, slope_rows = slice(top, top + GROUP), slice(top + GROUP, top + 2 * GROUP)
        for r in range(ROWS):
            for c in range(3):
                change = gradient(FIRST, found, c, phi_rows, slope_rows, r)
                base = GROUP * c + RANK_V * side
                count = min(RANK_V, GROUP - RANK_V * c)
                held = given[RANK_V * c : RANK_V * c + count, lane(FIRST.packed + r)]
                sides[base : base + count, lane(r)] = held - change[:count]
                if count < RANK_V:
                    held = spare(given, FIRST.breadth + r)
                    sides[base + count : base + RANK_V, lane(r)] = held - change[count:RANK_V]

    def tile(c, r):
        rows = slice(cells * c, cells * (c + 1))
        return flat[rows, lane(r)] if 0 <= r < ROWS else rim[rows, lane(r + 2 if r < 0 else r - 2)]

    for c in range(3):
        rows = slice(cells * c, cells * (c + 1))
        spanned = split_dot(
            full[...], jnp.concatenate([flat[rows, :], sides[GROUP * c : GROUP * (c + 1), :]], axis=0)
        )
        for r in range(ROWS):
            here = tile(c, r)
            up_one, down_one = turned(here, 1), turned(here, -1)
            up_two, down_two = turned(here, 2), turned(here, -2)
            carried = (
                tile(0, r) * first_diff(up_one, down_one, up_two, down_two)
                + tile(1, r) * sum(factor * tile(c, r + reach) for reach, factor in DIFFERENCE)
                + tile(2, r) * spanned[:cells, lane(r)]
            )
            spread = (
                (4.0 / 3.0) * (up_one + down_one)
                - (1.0 / 12.0) * (up_two + down_two)
                - 5.0 * here
                + sum(factor * tile(c, r + reach) for reach, factor in CURVE)
                + spanned[cells:, lane(r)]
            )
            moved = here + time_step * (thick[:, lane(r)] * spread - carried)
            following[rows, lane(r)] = 0.5 * start[rows, lane(r)] + 0.5 * moved
    phi = lambda r: found[:cells, lane(r + FIRST.margin)]
    scale = 0.5 * time_step / 144.0
    owed = {
        -1: scale * (tile(1, -1) - slot(low, cells, 6)[...]) * phi(ROWS - 1) * masks[0],
        ROWS: scale * (tile(1, ROWS) + slot(high, cells, 6)[...]) * phi(0) * masks[2],
    }
    slot(debts, cells, 0)[...] = owed[-1]
    slot(debts, cells, 1)[...] = owed[ROWS]
    blocks, moments, at, up, down = own_source(cells, following, lateral, parts, owed)
    fill_slots(up_near, cells, blocks + [at(2), at(3), up, owed[ROWS]], moments)
    fill_slots(down_near, cells, blocks + [at(0), at(1), down, owed[-1]], moments)
    fill_slots(up_far, cells, [blocks[3], at(2), at(3), owed[ROWS]], moments[3:])
    fill_slots(down_far, cells, [blocks[0], at(0), at(1), owed[-1]], moments[:1])


def last_kernel(cells, partial, left, right, section, fixed, solve, out, levels, staged, sems):
    found = finish(LAST, partial, left, right, solve, levels)
    copies = []
    for c in (2, 0, 1):
        rows = slice(cells * c, cells * (c + 1))
        for r in range(ROWS):
            value = section[rows, lane(r)]
            if c == 1 and r in (0, ROWS - 1):
                value = value + fixed[cells * (r > 0) : cells * (1 + (r > 0)), :]
            value = value - gradient(LAST, found, c, slice(0, cells), slice(cells, 2 * cells), r)
            staged[rows, lane(r)] = value
            copies.append(
                pltpu.make_async_copy(staged.at[rows, lane(r)], out.at[c, :, r, :], sems.at[len(copies)])
            )
            copies[-1].start()
    for copy in copies:
        copy.wait()


def call(body, shapes, *args, scratch=(), **options):
    return pl.pallas_call(
        body,
        out_shape=[jax.ShapeDtypeStruct(s, jnp.float32) for s in shapes],
        scratch_shapes=scratch,
        compiler_params=pltpu.CompilerParams(vmem_limit_bytes=40 * 1024 * 1024),
        **options,
    )(*args)


def shifted(block, axis, step):
    count = lax.axis_size(axis)
    return lax.ppermute(block, axis, [(i, (i + step) % count) for i in range(count)])


def per_device(velocity, viscosity):
    components, cells, row_cells, columns = velocity.shape
    length = cells * lax.axis_size("span")
    own, first_own, slopes, full, moments, lateral, *first = (
        jnp.asarray(t) for t in tables(length, cells, False)
    )
    _, last_own, _, _, _, _, *last = (jnp.asarray(t) for t in tables(length, cells, True))
    width = row_cells * columns
    near = cells + PAD_M
    whole, edge, rim = (components * cells, width), (PAD_V, width), (7 * cells, columns)

    def across(up_near, down_near, up_far, down_far):
        return (
            shifted(up_near, "cross", 1), shifted(down_near, "cross", -1),
            shifted(up_far, "cross", 2), shifted(down_far, "cross", -2),
        )

    def message(near_slots, near_rows, far_slots, far_rows):
        near_shape = (near_slots * cells + near_rows * PAD_M, columns)
        far_shape = (far_slots * cells + far_rows * PAD_M, columns)
        return [near_shape] * 2 + [far_shape] * 2

    def levels(extent, depth):
        return pltpu.VMEM((SWEEPS * depth, extent.breadth * columns), jnp.float32)

    start, thick, to_right, to_left, upward, downward = call(
        functools.partial(open_kernel, cells),
        [whole, (cells, width), edge, edge, rim, rim],
        *(pltpu.with_memory_space_constraint(x, pltpu.HBM) for x in (velocity, viscosity, moments)),
        in_specs=[pl.BlockSpec(memory_space=pltpu.HBM)] * 3,
        scratch=[pltpu.VMEM(moments.shape, moments.dtype), pltpu.SemaphoreType.DMA((1 + 4 * ROWS,))],
    )
    left = shifted(to_right, "span", 1)
    right = shifted(to_left, "span", -1)
    low = shifted(upward, "cross", 1)
    high = shifted(downward, "cross", -1)
    (rough,) = call(functools.partial(rough_kernel, cells), [whole], start, thick, own)
    section, parts, *sent = call(
        functools.partial(tendency_kernel, cells),
        [whole, (near, width)] + message(10, 2, 4, 2),
        rough, start, thick, left, right, low, high, slopes, lateral,
    )
    arrived = across(*sent)
    middle, held = call(
        functools.partial(near_source_kernel, cells),
        [(near, 2 * width), (2 * PAD_V, width)],
        parts, section, *arrived[:2], lateral, moments,
    )
    ext, to_right, to_left = call(
        functools.partial(source_kernel, cells),
        [(near, FIRST.breadth * columns)] + [(GROUP, (FIRST.packed + ROWS + 3) * columns)] * 2,
        middle, held, *arrived, first[0],
    )
    left = shifted(to_right, "span", 1)
    right = shifted(to_left, "span", -1)
    (partial,) = call(
        functools.partial(home_kernel, FIRST),
        [(first_own.shape[0], FIRST.found * columns)],
        ext, first_own,
        scratch=[levels(FIRST, near)],
    )

    section, parts, debts, *sent = call(
        functools.partial(middle_kernel, cells),
        [whole, (near, width), (2 * cells, columns)] + message(8, 4, 4, 1),
        partial, left, right, section, first[1], *arrived[:2], low, high, start, thick, full, lateral,
        scratch=[
            levels(FIRST, 2 * PAD_S),
            pltpu.VMEM(whole, jnp.float32),
            pltpu.VMEM((components * cells, 4 * columns), jnp.float32),
            pltpu.VMEM((components * GROUP, width), jnp.float32),
        ],
    )
    arrived = across(*sent)
    ext, fixed, to_right, to_left = call(
        functools.partial(last_source_kernel, cells),
        [(near, LAST.breadth * columns), (2 * cells, columns)] + [(GROUP, LAST.packed * columns)] * 2,
        parts, section, debts, *arrived, last[0],
    )
    left = shifted(to_right, "span", 1)
    right = shifted(to_left, "span", -1)
    (partial,) = call(
        functools.partial(home_kernel, LAST),
        [(last_own.shape[0], LAST.found * columns)],
        ext, last_own,
        scratch=[levels(LAST, near)],
    )
    (out,) = call(
        functools.partial(last_kernel, cells),
        [velocity.shape],
        partial, left, right, section, fixed, last[1],
        scratch=[
            levels(LAST, 2 * PAD_S),
            pltpu.VMEM(whole, jnp.float32),
            pltpu.SemaphoreType.DMA((3 * ROWS,)),
        ],
        out_specs=[pl.BlockSpec(memory_space=pltpu.HBM)],
    )
    return out


def solution(mesh):
    in_specs = (P(None, "span", "cross", None), P("span", "cross", None))
    out_specs = P(None, "span", "cross", None)
    return jax.shard_map(
        per_device, mesh=mesh, in_specs=in_specs, out_specs=out_specs, check_vma=False
    )
```

```python
import functools

import jax
import jax.numpy as jnp
import ml_dtypes
import numpy as np
from jax import lax
from jax.experimental import pallas as pl
from jax.experimental.pallas import tpu as pltpu
from jax.sharding import PartitionSpec as P

SWEEPS = 4
ROWS = 4
LANES = 128
time_step = 0.1
highest = lax.Precision.HIGHEST
PAD_V = 16
PAD_S = 16
PAD_M = 8
GROUP = 8
PACK = 16
RANK_V = 3
RANK_M = 2


def symbols(length):
    w = 2.0 * np.pi * np.arange(length) / length
    first = (14.0 / 9.0 * np.sin(w) + np.sin(2.0 * w) / 18.0) / (1.0 + 2.0 / 3.0 * np.cos(w))
    second = (24.0 / 11.0 * (1.0 - np.cos(w)) + 3.0 / 22.0 * (1.0 - np.cos(2.0 * w))) / (
        1.0 + 4.0 / 11.0 * np.cos(w)
    )
    return 1j * first, -second, 1.0 / (4.0 + second)


def block_of(symbol, cells, offset):
    kernel = np.fft.ifft(symbol).real
    at = np.arange(cells)
    return kernel[(at[:, None] - (at[None, :] + offset * cells)) % len(kernel)]


def low_rank(stack, rank):
    left, scale, right = np.linalg.svd(stack, full_matrices=False)
    return left[:, :rank] * scale[:rank], right[:rank]


@functools.lru_cache(None)
def tables(length, cells, last):
    first, second, inverse = symbols(length)
    at = lambda symbol, offset: block_of(symbol, cells, offset)
    from_left, take_left = low_rank(np.concatenate([at(first, -1), at(second, -1)]), RANK_V)
    from_right, take_right = low_rank(np.concatenate([at(first, 1), at(second, 1)]), RANK_V)
    own = np.concatenate([at(first, 0), at(second, 0)])
    slopes = np.zeros((3, 2 * cells, 2 * PAD_V))
    moments = np.zeros((3, 2 * PAD_V, cells))
    for c in range(3):
        rows = slice(RANK_V * c, RANK_V * (c + 1))
        slopes[c, :, :PAD_V][:, rows] = from_left
        slopes[c, :, PAD_V:][:, rows] = from_right
        moments[c, rows] = take_left
        moments[c, PAD_V:][rows] = take_right
    m_left, t_left = low_rank(at(first, -1), RANK_M)
    m_right, t_right = low_rank(at(first, 1), RANK_M)
    lateral = np.zeros((cells + PAD_M, cells))
    lateral[:cells] = at(first, 0)
    lateral[cells : cells + RANK_M] = t_left
    lateral[cells + RANK_M : cells + 2 * RANK_M] = t_right
    powers = [inverse ** (j + 1) for j in range(SWEEPS)]
    stacked = [p for p in powers] + [first * p for p in powers]
    count = len(stacked)
    RANK_S = 2 * SWEEPS + (1 if last else 3)
    kept = [] if last else stacked
    s_left, q_left = low_rank(
        np.concatenate([at(p, -1) for p in stacked] + [take_left @ at(p, 0) for p in kept]), RANK_S
    )
    s_right, q_right = low_rank(
        np.concatenate([at(p, 1) for p in stacked] + [take_right @ at(p, 0) for p in kept]), RANK_S
    )
    e_left, e_right = s_left[count * cells :], s_right[count * cells :]
    source = np.zeros((8 * GROUP, cells + PAD_M))
    for side, q in enumerate((q_left, q_right)):
        rows = np.zeros((PAD_S, cells + PAD_M))
        rows[:RANK_S, :cells] = q
        at_m = cells + RANK_M * side
        rows[RANK_S : RANK_S + RANK_M, at_m : at_m + RANK_M] = np.eye(RANK_M)
        top = 4 * GROUP * side
        source[top : top + 8] = rows[:8]
        source[top + 8 : top + 12] = rows[8:12]
        source[top + 20 : top + 24] = rows[8:12]
        source[top + 24] = rows[12]
    near, wide = cells + PAD_M, 2 * PAD_S
    height = 2 * cells + (0 if last else 4 * GROUP)
    solve_own = np.zeros((height, SWEEPS * near))
    solve_sides = np.zeros((height, SWEEPS * wide))
    for j in range(SWEEPS):
        for half in range(2):
            index = half * SWEEPS + j
            rows = slice(cells * index, cells * (index + 1))
            edge = slice(RANK_V * index, RANK_V * (index + 1))
            center = at(stacked[index], 0)
            by_left, by_right = s_left[rows], s_right[rows]
            mine, sides = np.zeros((cells, near)), np.zeros((cells, wide))
            mine[:, :cells] = center
            mine[:, cells : cells + RANK_M] = by_right @ (q_right @ m_left)
            mine[:, cells + RANK_M : cells + 2 * RANK_M] = by_left @ (q_left @ m_right)
            sides[:, :RANK_S] = by_left
            sides[:, RANK_S : RANK_S + RANK_M] = center @ m_left
            sides[:, PAD_S : PAD_S + RANK_S] = by_right
            sides[:, PAD_S + RANK_S : PAD_S + RANK_S + RANK_M] = center @ m_right
            solve_own[cells * half : cells * (half + 1), near * j : near * (j + 1)] = -mine
            solve_sides[cells * half : cells * (half + 1), wide * j : wide * (j + 1)] = -sides
            for side in range(0 if last else 2):
                mine, sides = np.zeros((RANK_V, near)), np.zeros((RANK_V, wide))
                if side == 0:
                    back = take_left @ by_right @ q_right
                    mine[:, cells + RANK_M : cells + 2 * RANK_M] = take_left @ center @ m_right
                    sides[:, :RANK_S] = e_left[edge]
                else:
                    back = take_right @ by_left @ q_left
                    mine[:, cells : cells + RANK_M] = take_right @ center @ m_left
                    sides[:, PAD_S : PAD_S + RANK_S] = e_right[edge]
                mine[:, :cells] = back
                sides[:, RANK_S : RANK_S + RANK_M] = back @ m_left
                sides[:, PAD_S + RANK_S : PAD_S + RANK_S + RANK_M] = back @ m_right
                top = 2 * cells + GROUP * (2 * side + half)
                solve_own[top : top + RANK_V, near * j : near * (j + 1)] = -mine
                solve_sides[top : top + RANK_V, wide * j : wide * (j + 1)] = -sides
    full = np.concatenate([own, from_left, from_right], axis=1)
    full = np.pad(full, [(0, 0), (0, GROUP - 2 * RANK_V)])
    split = (solve_own, slopes, full, moments, lateral, source, solve_sides)
    return [own.astype(np.float32)] + [split_table(x.astype(np.float32)) for x in split]


def dot(a, b):
    return jnp.dot(a, b, precision=highest, preferred_element_type=jnp.float32)


def halves(x):
    high = x.astype(jnp.bfloat16)
    return high, (x - high.astype(jnp.float32)).astype(jnp.bfloat16)


def split_table(table):
    gap = -table.shape[-1] % PACK
    table = np.pad(table, [(0, 0)] * (table.ndim - 1) + [(0, gap)])
    high = table.astype(ml_dtypes.bfloat16)
    low = (table - high.astype(np.float32)).astype(ml_dtypes.bfloat16)
    return np.concatenate([high, high, low], axis=-1)


def split_dot(table, x):
    gap = -x.shape[0] % PACK
    if gap:
        x = jnp.concatenate([x, jnp.zeros((gap, x.shape[1]), x.dtype)], axis=0)
    high, low = halves(x)
    return jnp.dot(table, jnp.concatenate([high, low, high], axis=0), preferred_element_type=jnp.float32)


class Extent:
    def __init__(self, margin):
        self.margin = margin
        self.reach = margin + SWEEPS - 1
        self.breadth = ROWS + 2 * self.reach
        self.packed = self.breadth + self.breadth // 2
        self.found = ROWS + 2 * margin


FIRST, LAST = Extent(3), Extent(2)


DIFFERENCE = ((1, 2.0 / 3.0), (-1, -2.0 / 3.0), (2, -1.0 / 12.0), (-2, 1.0 / 12.0))
CURVE = ((1, 4.0 / 3.0), (-1, 4.0 / 3.0), (2, -1.0 / 12.0), (-2, -1.0 / 12.0))


def lane(r, count=1):
    return slice(r * LANES, (r + count) * LANES)


def turned(tile, step):
    return pltpu.roll(tile, (-step) % LANES, 1)


def edge_masks():
    at = lax.axis_index("cross")
    last = lax.axis_size("cross") - 1
    flag = lambda test: jnp.where(test, 1.0, 0.0).astype(jnp.float32)
    return (flag(at >= 1), flag(at >= 2), flag(at <= last - 1), flag(at <= last - 2))


def masked(tile, e, masks):
    if e < -ROWS:
        return tile * masks[1]
    if e < 0:
        return tile * masks[0]
    if e >= 2 * ROWS:
        return tile * masks[3]
    if e >= ROWS:
        return tile * masks[2]
    return tile


def first_diff(up_one, down_one, up_two, down_two):
    return (8.0 * (up_one - down_one) - (up_two - down_two)) * (1.0 / 12.0)


def second_diff(middle, up_one, down_one, up_two, down_two):
    return (16.0 * (up_one + down_one) - (up_two + down_two) - 30.0 * middle) * (1.0 / 12.0)


def stream_slope(tile):
    return first_diff(turned(tile, 1), turned(tile, -1), turned(tile, 2), turned(tile, -2))


def open_kernel(
    cells, velocity, viscosity, moments, flat, thick, to_right, to_left, upward, downward, weights, sems
):
    copies = [pltpu.make_async_copy(moments, weights, sems.at[0])]
    for c in range(3):
        rows = slice(cells * c, cells * (c + 1))
        for r in range(ROWS):
            copies.append(
                pltpu.make_async_copy(velocity.at[c, :, r, :], flat.at[rows, lane(r)], sems.at[len(copies)])
            )
    for r in range(ROWS):
        copies.append(pltpu.make_async_copy(viscosity.at[:, r, :], thick.at[:, lane(r)], sems.at[len(copies)]))
    for copy in copies:
        copy.start()
    copies[0].wait()
    both = None
    for c in range(3):
        for copy in copies[1 + ROWS * c : 1 + ROWS * (c + 1)]:
            copy.wait()
        rows = slice(cells * c, cells * (c + 1))
        for k in range(2):
            slot(upward, cells, 2 * c + k)[...] = flat[rows, lane(2 + k)]
            slot(downward, cells, 2 * c + k)[...] = flat[rows, lane(k)]
        part = split_dot(weights[c], flat[rows, :])
        both = part if both is None else both + part
    to_right[...] = both[:PAD_V]
    to_left[...] = both[PAD_V:]
    for copy in copies[1 + 3 * ROWS :]:
        copy.wait()
    slot(upward, cells, 6)[...] = thick[:, lane(ROWS - 1)]
    slot(downward, cells, 6)[...] = thick[:, lane(0)]


def weighed(weights, value_at, r, home):
    total = None
    for reach, factor in weights:
        if (0 <= r + reach < ROWS) == home:
            part = factor * value_at(r + reach)
            total = part if total is None else total + part
    return total


def rough_kernel(cells, flat, thick, own, rough):
    for c in range(3):
        rows = slice(cells * c, cells * (c + 1))
        at = lambda r: flat[rows, lane(r)]
        spanned = dot(own[...], flat[rows, :])
        for r in range(ROWS):
            here = at(r)
            up_one, down_one = turned(here, 1), turned(here, -1)
            up_two, down_two = turned(here, 2), turned(here, -2)
            carried = (
                flat[:cells, lane(r)] * first_diff(up_one, down_one, up_two, down_two)
                + flat[cells : 2 * cells, lane(r)] * weighed(DIFFERENCE, at, r, True)
                + flat[2 * cells :, lane(r)] * spanned[:cells, lane(r)]
            )
            spread = (
                (4.0 / 3.0) * (up_one + down_one)
                - (1.0 / 12.0) * (up_two + down_two)
                - 5.0 * here
                + weighed(CURVE, at, r, True)
                + spanned[cells:, lane(r)]
            )
            rough[rows, lane(r)] = here + time_step * (thick[:, lane(r)] * spread - carried)


def add_beyond(cells, rough, flat, thick, left, right, low, high, slopes, section):
    masks = edge_masks()
    sides = jnp.concatenate([left[...], right[...]], axis=0)
    for c in range(3):
        rows = slice(cells * c, cells * (c + 1))
        spanned = split_dot(slopes[c], sides)

        def beyond(r):
            if r < 0:
                return masked(slot(low, cells, 2 * c + r + 2)[...], r, masks)
            return masked(slot(high, cells, 2 * c + r - ROWS)[...], r, masks)

        for r in range(ROWS):
            spread = spanned[cells:, lane(r)] + weighed(CURVE, beyond, r, False)
            carried = flat[cells : 2 * cells, lane(r)] * weighed(DIFFERENCE, beyond, r, False)
            carried = carried + flat[2 * cells :, lane(r)] * spanned[:cells, lane(r)]
            section[rows, lane(r)] = rough[rows, lane(r)] + time_step * (thick[:, lane(r)] * spread - carried)


def slot(ref, cells, k):
    return ref.at[cells * k : cells * (k + 1), :]


def fill_slots(ref, cells, blocks, moments):
    for k, block in enumerate(blocks):
        slot(ref, cells, k)[...] = block
    for k, block in enumerate(moments):
        top = cells * len(blocks) + PAD_M * k
        ref[top : top + PAD_M, :] = block


def own_source(cells, section, lateral, parts, owed={}):
    side = split_dot(lateral[...], section[2 * cells :, :])
    at = lambda r: section[cells : 2 * cells, lane(r)]
    blocks = []
    for r in range(ROWS):
        total = stream_slope(section[:cells, lane(r)]) + side[:cells, lane(r)] + weighed(DIFFERENCE, at, r, True)
        for reach, factor in DIFFERENCE:
            if r + reach in owed:
                total = total + factor * owed[r + reach]
        parts[:cells, lane(r)] = total
        blocks.append(total)
    parts[cells:, :] = side[cells:]
    moments = [side[cells:, lane(r)] for r in range(ROWS)]
    up = (2.0 / 3.0) * at(0) - (1.0 / 12.0) * at(1)
    down = (1.0 / 12.0) * at(ROWS - 2) - (2.0 / 3.0) * at(ROWS - 1)
    return blocks, moments, at, up, down


def tendency_kernel(
    cells, rough, flat, thick, left, right, low, high, slopes, lateral,
    section, parts, up_near, down_near, up_far, down_far,
):
    add_beyond(cells, rough, flat, thick, left, right, low, high, slopes, section)
    blocks, moments, at, _, _ = own_source(cells, section, lateral, parts)
    row = lambda c, r: section[cells * c : cells * (c + 1), lane(r)]
    every = [at(r) for r in range(ROWS)]
    for near, far, outer, inner in ((up_near, up_far, 0, 2), (down_near, down_far, 2, 0)):
        side = [row(c, inner + k) for c in (0, 2) for k in range(2)]
        fill_slots(near, cells, blocks[outer : outer + 2] + every + side, moments[outer : outer + 2])
        fill_slots(far, cells, blocks[inner : inner + 2] + [at(inner), at(inner + 1)], moments[inner : inner + 2])


WHOLE = (-2, -1, ROWS, ROWS + 1)


def row_across(cells, section, arrived):
    low_one, high_one, low_two, high_two = arrived
    masks = edge_masks()

    def value(e):
        if 0 <= e < ROWS:
            return section[cells : 2 * cells, lane(e)]
        if e < -ROWS or e >= 2 * ROWS:
            ref, k = (low_two, e + 8) if e < 0 else (high_two, e - 6)
        else:
            ref, k = (low_one, e + 6) if e < 0 else (high_one, e - 2)
        return masked(slot(ref, cells, k)[...], e, masks)

    return value


def near_source_kernel(cells, parts, section, low_one, high_one, lateral, moments, middle, held):
    masks = edge_masks()
    across = row_across(cells, section, (low_one, high_one, None, None))
    pick = lambda ref, k: slot(ref, cells, k)[...]
    given = [(low_one if e < 0 else high_one, e % 2) for e in WHOLE]
    beside = split_dot(lateral[...], jnp.concatenate([pick(ref, 8 + k) for ref, k in given], axis=1))
    for e in range(-2, ROWS + 2):
        if e in WHOLE:
            at = WHOLE.index(e)
            ref, k = given[at]
            total = stream_slope(pick(ref, 6 + k)) + beside[:cells, lane(at)]
            side = beside[cells:, lane(at)]
        else:
            total, side = parts[:cells, lane(e)], parts[cells:, lane(e)]
        for reach, factor in DIFFERENCE:
            if e in WHOLE or not 0 <= e + reach < ROWS:
                total = total + factor * across(e + reach)
        middle[:cells, lane(e + 2)] = masked(total, e, masks)
        middle[cells:, lane(e + 2)] = masked(side, e, masks)
    held[...] = sum(split_dot(moments[c], section[cells * c : cells * (c + 1), :]) for c in range(3))


def first_source(cells, middle, arrived, ext):
    low_one, high_one, low_two, high_two = arrived
    masks = edge_masks()
    across = row_across(cells, None, arrived)
    ext[:, lane(FIRST.reach - 2, ROWS + 4)] = middle[...]
    for e in range(-FIRST.reach, ROWS + FIRST.reach):
        if -2 <= e < ROWS + 2:
            continue
        far = e < -ROWS or e >= 2 * ROWS
        ref = (low_two if e < 0 else high_two) if far else (low_one if e < 0 else high_one)
        top = (4 if far else 10) * cells + PAD_M * (e % 2)
        total, side = slot(ref, cells, e % 2)[...], ref[top : top + PAD_M, :]
        for reach, factor in DIFFERENCE:
            if (e + reach) // ROWS != e // ROWS:
                total = total + factor * across(e + reach)
        ext[:cells, lane(e + FIRST.reach)] = masked(total, e, masks)
        ext[cells:, lane(e + FIRST.reach)] = masked(side, e, masks)


def last_source(cells, parts, section, arrived, extra, ext):
    low_one, high_one, low_two, high_two = arrived
    masks = edge_masks()
    span, tail = slice(0, cells), slice(cells, cells + PAD_M)
    pick = lambda ref, k: slot(ref, cells, k)[...]

    def joined(e):
        if 0 <= e < ROWS:
            return parts[span, lane(e)], parts[tail, lane(e)]
        if e < -ROWS or e >= 2 * ROWS:
            ref = low_two if e < 0 else high_two
            return pick(ref, 0), ref[4 * cells :, :]
        ref, k = (low_one, e + ROWS) if e < 0 else (high_one, e - ROWS)
        top = 8 * cells + PAD_M * k
        return pick(ref, k), ref[top : top + PAD_M, :]

    def across(e, home):
        if e // ROWS == home // ROWS or home // ROWS in (-2, 2):
            return None
        if e < -ROWS:
            return masked(pick(low_two, 1 + e + ROWS + 2), e, masks)
        if e < 0:
            return masked(pick(low_one, ROWS + e + 2), e, masks)
        if e < ROWS:
            return section[cells : 2 * cells, lane(e)]
        if e < 2 * ROWS:
            return masked(pick(high_one, e), e, masks)
        return masked(pick(high_two, 1 + e - 2 * ROWS), e, masks)

    for e in range(-LAST.reach, ROWS + LAST.reach):
        total, side = joined(e)
        if e == -ROWS - 1:
            total = total + pick(low_one, 6)
        if e == 2 * ROWS:
            total = total + pick(high_one, 6)
        for reach, factor in DIFFERENCE:
            other = across(e + reach, e)
            if other is not None:
                total = total + factor * other
            if e + reach in extra and (e + reach) // ROWS == e // ROWS:
                total = total + factor * extra[e + reach]
        ext[span, lane(e + LAST.reach)] = masked(total, e, masks)
        ext[tail, lane(e + LAST.reach)] = masked(side, e, masks)


def pack_moments(extent, both, to_right, to_left):
    for side, out in enumerate((to_right, to_left)):
        top = 4 * GROUP * side
        out[:, lane(0, extent.breadth)] = both[top : top + 8]
        for k in range(extent.breadth // 2):
            out[:, lane(extent.breadth + k)] = (
                both[top + 8 : top + 16, lane(2 * k)] + both[top + 16 : top + 24, lane(2 * k + 1)]
            )


def source_kernel(
    cells, middle, held, low_one, high_one, low_two, high_two, source, ext, to_right, to_left
):
    first_source(cells, middle, (low_one, high_one, low_two, high_two), ext)
    both = split_dot(source[...], ext[...])
    pack_moments(FIRST, both, to_right, to_left)
    for side, out in enumerate((to_right, to_left)):
        top, base = 4 * GROUP * side, PAD_V * side
        out[:, lane(FIRST.packed, ROWS)] = held[base : base + 8]
        out[:, lane(FIRST.packed + ROWS, 3)] = jnp.zeros((GROUP, 3 * LANES), jnp.float32)
        for e in range(FIRST.breadth + ROWS):
            value = (
                both[top + 24 : top + 25, lane(e)]
                if e < FIRST.breadth
                else held[base + 8 : base + 9, lane(e - FIRST.breadth)]
            )
            row, tile = e % GROUP, FIRST.packed + ROWS + e // GROUP
            out[row : row + 1, lane(tile)] = value


def last_source_kernel(
    cells, parts, section, debts, low_one, high_one, low_two, high_two, source,
    ext, fixed, to_right, to_left,
):
    masks = edge_masks()
    pick = lambda ref, k: slot(ref, cells, k)[...]
    extra = {
        0: pick(low_one, 7) * masks[0],
        ROWS - 1: pick(high_one, 7) * masks[2],
        -1: pick(debts, 0),
        ROWS: pick(debts, 1),
        -ROWS: pick(low_two, 3) * masks[1],
        2 * ROWS - 1: pick(high_two, 3) * masks[3],
    }
    fixed[:cells, :] = extra[0]
    fixed[cells:, :] = extra[ROWS - 1]
    last_source(cells, parts, section, (low_one, high_one, low_two, high_two), extra, ext)
    pack_moments(LAST, split_dot(source[...], ext[...]), to_right, to_left)


def climb(extent, levels, depth):
    masks = edge_masks()
    for j in range(1, SWEEPS):
        before = slice(depth * (j - 1), depth * j)
        after = slice(depth * j, depth * (j + 1))
        for e in range(-extent.reach + j, ROWS + extent.reach - j):
            k = e + extent.reach
            here = levels[before, lane(k)]
            beside = (
                turned(here, 1) + turned(here, -1) + levels[before, lane(k + 1)] + levels[before, lane(k - 1)]
            )
            levels[after, lane(k)] = masked(beside, e, masks)
    return levels[:, lane(SWEEPS - 1, extent.found)]


def home_kernel(extent, ext, solve, partial, levels):
    depth = ext.shape[0]
    levels[:depth, :] = ext[...]
    partial[...] = split_dot(solve[...], climb(extent, levels, depth))


def spare(given, e):
    row, tile = e % GROUP, FIRST.packed + ROWS + e // GROUP
    return given[row : row + 1, lane(tile)]


def finish(extent, partial, left, right, solve, levels):
    for side, given in enumerate((left, right)):
        top = PAD_S * side
        levels[top : top + 8, :] = given[:, lane(0, extent.breadth)]
        for e in range(extent.breadth):
            tile = given[:, lane(extent.breadth + e // 2)]
            levels[top + 8 : top + 16, lane(e)] = pltpu.roll(tile, 4, 0) if e % 2 else tile
            if extent is FIRST:
                levels[top + 12 : top + 13, lane(e)] = spare(given, e)
    return partial[...] + split_dot(solve[...], climb(extent, levels, 2 * PAD_S))


def gradient(extent, found, c, rows, slope_rows, r):
    masks = edge_masks()
    phi = lambda r: masked(found[rows, lane(r + extent.margin)], r, masks)
    if c == 0:
        return stream_slope(phi(r))
    if c == 1:
        inside = lambda r: -extent.margin <= r < ROWS + extent.margin
        return sum(factor * phi(r + reach) for reach, factor in DIFFERENCE if inside(r + reach))
    return found[slope_rows, lane(r + extent.margin)]


def middle_kernel(
    cells, partial, left, right, section, solve, low_one, high_one, low, high, start, thick, full, lateral,
    following, parts, debts, up_near, down_near, up_far, down_far, levels, flat, rim, sides,
):
    masks = edge_masks()
    found = finish(FIRST, partial, left, right, solve, levels)
    home, home_slope = slice(0, cells), slice(cells, 2 * cells)
    outer = (-2, -1, ROWS, ROWS + 1)
    for c in range(3):
        rows = slice(cells * c, cells * (c + 1))
        for r in range(ROWS):
            flat[rows, lane(r)] = section[rows, lane(r)] - gradient(FIRST, found, c, home, home_slope, r)
        for k, r in enumerate(outer):
            first = (6, 4 if r < 0 else 2, 8)[c]
            value = slot(low_one if r < 0 else high_one, cells, first + k % 2)[...]
            value = value - gradient(FIRST, found, c, home, home_slope, r)
            rim[rows, lane(k)] = masked(value, r, masks)
    sides[...] = jnp.zeros(sides.shape, jnp.float32)
    for side, given in enumerate((left, right)):
        top = 2 * cells + 2 * GROUP * side
        phi_rows, slope_rows = slice(top, top + GROUP), slice(top + GROUP, top + 2 * GROUP)
        for r in range(ROWS):
            for c in range(3):
                change = gradient(FIRST, found, c, phi_rows, slope_rows, r)
                base = GROUP * c + RANK_V * side
                count = min(RANK_V, GROUP - RANK_V * c)
                held = given[RANK_V * c : RANK_V * c + count, lane(FIRST.packed + r)]
                sides[base : base + count, lane(r)] = held - change[:count]
                if count < RANK_V:
                    held = spare(given, FIRST.breadth + r)
                    sides[base + count : base + RANK_V, lane(r)] = held - change[count:RANK_V]

    def tile(c, r):
        rows = slice(cells * c, cells * (c + 1))
        return flat[rows, lane(r)] if 0 <= r < ROWS else rim[rows, lane(r + 2 if r < 0 else r - 2)]

    for c in range(3):
        rows = slice(cells * c, cells * (c + 1))
        spanned = split_dot(
            full[...], jnp.concatenate([flat[rows, :], sides[GROUP * c : GROUP * (c + 1), :]], axis=0)
        )
        for r in range(ROWS):
            here = tile(c, r)
            up_one, down_one = turned(here, 1), turned(here, -1)
            up_two, down_two = turned(here, 2), turned(here, -2)
            carried = (
                tile(0, r) * first_diff(up_one, down_one, up_two, down_two)
                + tile(1, r) * sum(factor * tile(c, r + reach) for reach, factor in DIFFERENCE)
                + tile(2, r) * spanned[:cells, lane(r)]
            )
            spread = (
                (4.0 / 3.0) * (up_one + down_one)
                - (1.0 / 12.0) * (up_two + down_two)
                - 5.0 * here
                + sum(factor * tile(c, r + reach) for reach, factor in CURVE)
                + spanned[cells:, lane(r)]
            )
            moved = here + time_step * (thick[:, lane(r)] * spread - carried)
            following[rows, lane(r)] = 0.5 * start[rows, lane(r)] + 0.5 * moved
    phi = lambda r: found[:cells, lane(r + FIRST.margin)]
    scale = 0.5 * time_step / 144.0
    owed = {
        -1: scale * (tile(1, -1) - slot(low, cells, 6)[...]) * phi(ROWS - 1) * masks[0],
        ROWS: scale * (tile(1, ROWS) + slot(high, cells, 6)[...]) * phi(0) * masks[2],
    }
    slot(debts, cells, 0)[...] = owed[-1]
    slot(debts, cells, 1)[...] = owed[ROWS]
    blocks, moments, at, up, down = own_source(cells, following, lateral, parts, owed)
    fill_slots(up_near, cells, blocks + [at(2), at(3), up, owed[ROWS]], moments)
    fill_slots(down_near, cells, blocks + [at(0), at(1), down, owed[-1]], moments)
    fill_slots(up_far, cells, [blocks[3], at(2), at(3), owed[ROWS]], moments[3:])
    fill_slots(down_far, cells, [blocks[0], at(0), at(1), owed[-1]], moments[:1])


def last_kernel(cells, partial, left, right, section, fixed, solve, out, levels, staged, sems):
    found = finish(LAST, partial, left, right, solve, levels)
    copies = []
    for c in (2, 0, 1):
        rows = slice(cells * c, cells * (c + 1))
        for r in range(ROWS):
            value = section[rows, lane(r)]
            if c == 1 and r in (0, ROWS - 1):
                value = value + fixed[cells * (r > 0) : cells * (1 + (r > 0)), :]
            value = value - gradient(LAST, found, c, slice(0, cells), slice(cells, 2 * cells), r)
            staged[rows, lane(r)] = value
            copies.append(
                pltpu.make_async_copy(staged.at[rows, lane(r)], out.at[c, :, r, :], sems.at[len(copies)])
            )
            copies[-1].start()
    for copy in copies:
        copy.wait()


def call(body, shapes, *args, scratch=(), **options):
    return pl.pallas_call(
        body,
        out_shape=[jax.ShapeDtypeStruct(s, jnp.float32) for s in shapes],
        scratch_shapes=scratch,
        compiler_params=pltpu.CompilerParams(vmem_limit_bytes=40 * 1024 * 1024),
        **options,
    )(*args)


def shifted(block, axis, step):
    count = lax.axis_size(axis)
    return lax.ppermute(block, axis, [(i, (i + step) % count) for i in range(count)])


def per_device(velocity, viscosity):
    components, cells, row_cells, columns = velocity.shape
    length = cells * lax.axis_size("span")
    own, first_own, slopes, full, moments, lateral, *first = (
        jnp.asarray(t) for t in tables(length, cells, False)
    )
    _, last_own, _, _, _, _, *last = (jnp.asarray(t) for t in tables(length, cells, True))
    width = row_cells * columns
    near = cells + PAD_M
    whole, edge, rim = (components * cells, width), (PAD_V, width), (7 * cells, columns)

    def across(up_near, down_near, up_far, down_far):
        return (
            shifted(up_near, "cross", 1), shifted(down_near, "cross", -1),
            shifted(up_far, "cross", 2), shifted(down_far, "cross", -2),
        )

    def message(near_slots, near_rows, far_slots, far_rows):
        near_shape = (near_slots * cells + near_rows * PAD_M, columns)
        far_shape = (far_slots * cells + far_rows * PAD_M, columns)
        return [near_shape] * 2 + [far_shape] * 2

    def levels(extent, depth):
        return pltpu.VMEM((SWEEPS * depth, extent.breadth * columns), jnp.float32)

    start, thick, to_right, to_left, upward, downward = call(
        functools.partial(open_kernel, cells),
        [whole, (cells, width), edge, edge, rim, rim],
        *(pltpu.with_memory_space_constraint(x, pltpu.HBM) for x in (velocity, viscosity, moments)),
        in_specs=[pl.BlockSpec(memory_space=pltpu.HBM)] * 3,
        scratch=[pltpu.VMEM(moments.shape, moments.dtype), pltpu.SemaphoreType.DMA((1 + 4 * ROWS,))],
    )
    left = shifted(to_right, "span", 1)
    right = shifted(to_left, "span", -1)
    low = shifted(upward, "cross", 1)
    high = shifted(downward, "cross", -1)
    (rough,) = call(functools.partial(rough_kernel, cells), [whole], start, thick, own)
    section, parts, *sent = call(
        functools.partial(tendency_kernel, cells),
        [whole, (near, width)] + message(10, 2, 4, 2),
        rough, start, thick, left, right, low, high, slopes, lateral,
    )
    arrived = across(*sent)
    middle, held = call(
        functools.partial(near_source_kernel, cells),
        [(near, 2 * width), (2 * PAD_V, width)],
        parts, section, *arrived[:2], lateral, moments,
    )
    ext, to_right, to_left = call(
        functools.partial(source_kernel, cells),
        [(near, FIRST.breadth * columns)] + [(GROUP, (FIRST.packed + ROWS + 3) * columns)] * 2,
        middle, held, *arrived, first[0],
    )
    left = shifted(to_right, "span", 1)
    right = shifted(to_left, "span", -1)
    (partial,) = call(
        functools.partial(home_kernel, FIRST),
        [(first_own.shape[0], FIRST.found * columns)],
        ext, first_own,
        scratch=[levels(FIRST, near)],
    )

    section, parts, debts, *sent = call(
        functools.partial(middle_kernel, cells),
        [whole, (near, width), (2 * cells, columns)] + message(8, 4, 4, 1),
        partial, left, right, section, first[1], *arrived[:2], low, high, start, thick, full, lateral,
        scratch=[
            levels(FIRST, 2 * PAD_S),
            pltpu.VMEM(whole, jnp.float32),
            pltpu.VMEM((components * cells, 4 * columns), jnp.float32),
            pltpu.VMEM((components * GROUP, width), jnp.float32),
        ],
    )
    arrived = across(*sent)
    ext, fixed, to_right, to_left = call(
        functools.partial(last_source_kernel, cells),
        [(near, LAST.breadth * columns), (2 * cells, columns)] + [(GROUP, LAST.packed * columns)] * 2,
        parts, section, debts, *arrived, last[0],
    )
    left = shifted(to_right, "span", 1)
    right = shifted(to_left, "span", -1)
    (partial,) = call(
        functools.partial(home_kernel, LAST),
        [(last_own.shape[0], LAST.found * columns)],
        ext, last_own,
        scratch=[levels(LAST, near)],
    )
    (out,) = call(
        functools.partial(last_kernel, cells),
        [velocity.shape],
        partial, left, right, section, fixed, last[1],
        scratch=[
            levels(LAST, 2 * PAD_S),
            pltpu.VMEM(whole, jnp.float32),
            pltpu.SemaphoreType.DMA((3 * ROWS,)),
        ],
        out_specs=[pl.BlockSpec(memory_space=pltpu.HBM)],
    )
    return out


def solution(mesh):
    in_specs = (P(None, "span", "cross", None), P("span", "cross", None))
    out_specs = P(None, "span", "cross", None)
    return jax.shard_map(
        per_device, mesh=mesh, in_specs=in_specs, out_specs=out_specs, check_vma=False
    )
```

```python
import functools

import jax
import jax.numpy as jnp
import ml_dtypes
import numpy as np
from jax import lax
from jax.experimental import pallas as pl
from jax.experimental.pallas import tpu as pltpu
from jax.sharding import PartitionSpec as P

SWEEPS = 4
ROWS = 4
LANES = 128
time_step = 0.1
highest = lax.Precision.HIGHEST
PAD_V = 16
PAD_S = 16
PAD_M = 8
GROUP = 8
PACK = 16
RANK_V = 3
RANK_M = 2


def symbols(length):
    w = 2.0 * np.pi * np.arange(length) / length
    first = (14.0 / 9.0 * np.sin(w) + np.sin(2.0 * w) / 18.0) / (1.0 + 2.0 / 3.0 * np.cos(w))
    second = (24.0 / 11.0 * (1.0 - np.cos(w)) + 3.0 / 22.0 * (1.0 - np.cos(2.0 * w))) / (
        1.0 + 4.0 / 11.0 * np.cos(w)
    )
    return 1j * first, -second, 1.0 / (4.0 + second)


def block_of(symbol, cells, offset):
    kernel = np.fft.ifft(symbol).real
    at = np.arange(cells)
    return kernel[(at[:, None] - (at[None, :] + offset * cells)) % len(kernel)]


def low_rank(stack, rank):
    left, scale, right = np.linalg.svd(stack, full_matrices=False)
    return left[:, :rank] * scale[:rank], right[:rank]


@functools.lru_cache(None)
def tables(length, cells, last):
    first, second, inverse = symbols(length)
    at = lambda symbol, offset: block_of(symbol, cells, offset)
    from_left, take_left = low_rank(np.concatenate([at(first, -1), at(second, -1)]), RANK_V)
    from_right, take_right = low_rank(np.concatenate([at(first, 1), at(second, 1)]), RANK_V)
    own = np.concatenate([at(first, 0), at(second, 0)])
    slopes = np.zeros((3, 2 * cells, 2 * PAD_V))
    moments = np.zeros((3, 2 * PAD_V, cells))
    for c in range(3):
        rows = slice(RANK_V * c, RANK_V * (c + 1))
        slopes[c, :, :PAD_V][:, rows] = from_left
        slopes[c, :, PAD_V:][:, rows] = from_right
        moments[c, rows] = take_left
        moments[c, PAD_V:][rows] = take_right
    m_left, t_left = low_rank(at(first, -1), RANK_M)
    m_right, t_right = low_rank(at(first, 1), RANK_M)
    lateral = np.zeros((cells + PAD_M, cells))
    lateral[:cells] = at(first, 0)
    lateral[cells : cells + RANK_M] = t_left
    lateral[cells + RANK_M : cells + 2 * RANK_M] = t_right
    powers = [inverse ** (j + 1) for j in range(SWEEPS)]
    stacked = [p for p in powers] + [first * p for p in powers]
    count = len(stacked)
    RANK_S = 2 * SWEEPS + (1 if last else 3)
    kept = [] if last else stacked
    s_left, q_left = low_rank(
        np.concatenate([at(p, -1) for p in stacked] + [take_left @ at(p, 0) for p in kept]), RANK_S
    )
    s_right, q_right = low_rank(
        np.concatenate([at(p, 1) for p in stacked] + [take_right @ at(p, 0) for p in kept]), RANK_S
    )
    e_left, e_right = s_left[count * cells :], s_right[count * cells :]
    source = np.zeros((8 * GROUP, cells + PAD_M))
    for side, q in enumerate((q_left, q_right)):
        rows = np.zeros((PAD_S, cells + PAD_M))
        rows[:RANK_S, :cells] = q
        at_m = cells + RANK_M * side
        rows[RANK_S : RANK_S + RANK_M, at_m : at_m + RANK_M] = np.eye(RANK_M)
        top = 4 * GROUP * side
        source[top : top + 8] = rows[:8]
        source[top + 8 : top + 12] = rows[8:12]
        source[top + 20 : top + 24] = rows[8:12]
        source[top + 24] = rows[12]
    near, wide = cells + PAD_M, 2 * PAD_S
    height = 2 * cells + (0 if last else 4 * GROUP)
    solve_own = np.zeros((height, SWEEPS * near))
    solve_sides = np.zeros((height, SWEEPS * wide))
    for j in range(SWEEPS):
        for half in range(2):
            index = half * SWEEPS + j
            rows = slice(cells * index, cells * (index + 1))
            edge = slice(RANK_V * index, RANK_V * (index + 1))
            center = at(stacked[index], 0)
            by_left, by_right = s_left[rows], s_right[rows]
            mine, sides = np.zeros((cells, near)), np.zeros((cells, wide))
            mine[:, :cells] = center
            mine[:, cells : cells + RANK_M] = by_right @ (q_right @ m_left)
            mine[:, cells + RANK_M : cells + 2 * RANK_M] = by_left @ (q_left @ m_right)
            sides[:, :RANK_S] = by_left
            sides[:, RANK_S : RANK_S + RANK_M] = center @ m_left
            sides[:, PAD_S : PAD_S + RANK_S] = by_right
            sides[:, PAD_S + RANK_S : PAD_S + RANK_S + RANK_M] = center @ m_right
            solve_own[cells * half : cells * (half + 1), near * j : near * (j + 1)] = -mine
            solve_sides[cells * half : cells * (half + 1), wide * j : wide * (j + 1)] = -sides
            for side in range(0 if last else 2):
                mine, sides = np.zeros((RANK_V, near)), np.zeros((RANK_V, wide))
                if side == 0:
                    back = take_left @ by_right @ q_right
                    mine[:, cells + RANK_M : cells + 2 * RANK_M] = take_left @ center @ m_right
                    sides[:, :RANK_S] = e_left[edge]
                else:
                    back = take_right @ by_left @ q_left
                    mine[:, cells : cells + RANK_M] = take_right @ center @ m_left
                    sides[:, PAD_S : PAD_S + RANK_S] = e_right[edge]
                mine[:, :cells] = back
                sides[:, RANK_S : RANK_S + RANK_M] = back @ m_left
                sides[:, PAD_S + RANK_S : PAD_S + RANK_S + RANK_M] = back @ m_right
                top = 2 * cells + GROUP * (2 * side + half)
                solve_own[top : top + RANK_V, near * j : near * (j + 1)] = -mine
                solve_sides[top : top + RANK_V, wide * j : wide * (j + 1)] = -sides
    full = np.concatenate([own, from_left, from_right], axis=1)
    full = np.pad(full, [(0, 0), (0, GROUP - 2 * RANK_V)])
    plain, split = (own, solve_own), (slopes, full, moments, lateral, source, solve_sides)
    return [x.astype(np.float32) for x in plain] + [split_table(x.astype(np.float32)) for x in split]


def dot(a, b):
    return jnp.dot(a, b, precision=highest, preferred_element_type=jnp.float32)


def halves(x):
    high = x.astype(jnp.bfloat16)
    return high, (x - high.astype(jnp.float32)).astype(jnp.bfloat16)


def split_table(table):
    gap = -table.shape[-1] % PACK
    table = np.pad(table, [(0, 0)] * (table.ndim - 1) + [(0, gap)])
    high = table.astype(ml_dtypes.bfloat16)
    low = (table - high.astype(np.float32)).astype(ml_dtypes.bfloat16)
    return np.concatenate([high, high, low], axis=-1)


def split_dot(table, x):
    gap = -x.shape[0] % PACK
    if gap:
        x = jnp.concatenate([x, jnp.zeros((gap, x.shape[1]), x.dtype)], axis=0)
    high, low = halves(x)
    return jnp.dot(table, jnp.concatenate([high, low, high], axis=0), preferred_element_type=jnp.float32)


class Extent:
    def __init__(self, margin):
        self.margin = margin
        self.reach = margin + SWEEPS - 1
        self.breadth = ROWS + 2 * self.reach
        self.packed = self.breadth + self.breadth // 2
        self.found = ROWS + 2 * margin


FIRST, LAST = Extent(3), Extent(2)


DIFFERENCE = ((1, 2.0 / 3.0), (-1, -2.0 / 3.0), (2, -1.0 / 12.0), (-2, 1.0 / 12.0))
CURVE = ((1, 4.0 / 3.0), (-1, 4.0 / 3.0), (2, -1.0 / 12.0), (-2, -1.0 / 12.0))


def lane(r, count=1):
    return slice(r * LANES, (r + count) * LANES)


def turned(tile, step):
    return pltpu.roll(tile, (-step) % LANES, 1)


def edge_masks():
    at = lax.axis_index("cross")
    last = lax.axis_size("cross") - 1
    flag = lambda test: jnp.where(test, 1.0, 0.0).astype(jnp.float32)
    return (flag(at >= 1), flag(at >= 2), flag(at <= last - 1), flag(at <= last - 2))


def masked(tile, e, masks):
    if e < -ROWS:
        return tile * masks[1]
    if e < 0:
        return tile * masks[0]
    if e >= 2 * ROWS:
        return tile * masks[3]
    if e >= ROWS:
        return tile * masks[2]
    return tile


def first_diff(up_one, down_one, up_two, down_two):
    return (8.0 * (up_one - down_one) - (up_two - down_two)) * (1.0 / 12.0)


def second_diff(middle, up_one, down_one, up_two, down_two):
    return (16.0 * (up_one + down_one) - (up_two + down_two) - 30.0 * middle) * (1.0 / 12.0)


def stream_slope(tile):
    return first_diff(turned(tile, 1), turned(tile, -1), turned(tile, 2), turned(tile, -2))


def open_kernel(
    cells, velocity, viscosity, moments, flat, thick, to_right, to_left, upward, downward, weights, sems
):
    copies = [pltpu.make_async_copy(moments, weights, sems.at[0])]
    for c in range(3):
        rows = slice(cells * c, cells * (c + 1))
        for r in range(ROWS):
            copies.append(
                pltpu.make_async_copy(velocity.at[c, :, r, :], flat.at[rows, lane(r)], sems.at[len(copies)])
            )
    for r in range(ROWS):
        copies.append(pltpu.make_async_copy(viscosity.at[:, r, :], thick.at[:, lane(r)], sems.at[len(copies)]))
    for copy in copies:
        copy.start()
    copies[0].wait()
    both = None
    for c in range(3):
        for copy in copies[1 + ROWS * c : 1 + ROWS * (c + 1)]:
            copy.wait()
        rows = slice(cells * c, cells * (c + 1))
        for k in range(2):
            slot(upward, cells, 2 * c + k)[...] = flat[rows, lane(2 + k)]
            slot(downward, cells, 2 * c + k)[...] = flat[rows, lane(k)]
        part = split_dot(weights[c], flat[rows, :])
        both = part if both is None else both + part
    to_right[...] = both[:PAD_V]
    to_left[...] = both[PAD_V:]
    for copy in copies[1 + 3 * ROWS :]:
        copy.wait()
    slot(upward, cells, 6)[...] = thick[:, lane(ROWS - 1)]
    slot(downward, cells, 6)[...] = thick[:, lane(0)]


def weighed(weights, value_at, r, home):
    total = None
    for reach, factor in weights:
        if (0 <= r + reach < ROWS) == home:
            part = factor * value_at(r + reach)
            total = part if total is None else total + part
    return total


def rough_kernel(cells, flat, thick, own, rough):
    for c in range(3):
        rows = slice(cells * c, cells * (c + 1))
        at = lambda r: flat[rows, lane(r)]
        spanned = dot(own[...], flat[rows, :])
        for r in range(ROWS):
            here = at(r)
            up_one, down_one = turned(here, 1), turned(here, -1)
            up_two, down_two = turned(here, 2), turned(here, -2)
            carried = (
                flat[:cells, lane(r)] * first_diff(up_one, down_one, up_two, down_two)
                + flat[cells : 2 * cells, lane(r)] * weighed(DIFFERENCE, at, r, True)
                + flat[2 * cells :, lane(r)] * spanned[:cells, lane(r)]
            )
            spread = (
                (4.0 / 3.0) * (up_one + down_one)
                - (1.0 / 12.0) * (up_two + down_two)
                - 5.0 * here
                + weighed(CURVE, at, r, True)
                + spanned[cells:, lane(r)]
            )
            rough[rows, lane(r)] = here + time_step * (thick[:, lane(r)] * spread - carried)


def add_beyond(cells, rough, flat, thick, left, right, low, high, slopes, section):
    masks = edge_masks()
    sides = jnp.concatenate([left[...], right[...]], axis=0)
    for c in range(3):
        rows = slice(cells * c, cells * (c + 1))
        spanned = split_dot(slopes[c], sides)

        def beyond(r):
            if r < 0:
                return masked(slot(low, cells, 2 * c + r + 2)[...], r, masks)
            return masked(slot(high, cells, 2 * c + r - ROWS)[...], r, masks)

        for r in range(ROWS):
            spread = spanned[cells:, lane(r)] + weighed(CURVE, beyond, r, False)
            carried = flat[cells : 2 * cells, lane(r)] * weighed(DIFFERENCE, beyond, r, False)
            carried = carried + flat[2 * cells :, lane(r)] * spanned[:cells, lane(r)]
            section[rows, lane(r)] = rough[rows, lane(r)] + time_step * (thick[:, lane(r)] * spread - carried)


def slot(ref, cells, k):
    return ref.at[cells * k : cells * (k + 1), :]


def fill_slots(ref, cells, blocks, moments):
    for k, block in enumerate(blocks):
        slot(ref, cells, k)[...] = block
    for k, block in enumerate(moments):
        top = cells * len(blocks) + PAD_M * k
        ref[top : top + PAD_M, :] = block


def own_source(cells, section, lateral, parts, owed={}):
    side = split_dot(lateral[...], section[2 * cells :, :])
    at = lambda r: section[cells : 2 * cells, lane(r)]
    blocks = []
    for r in range(ROWS):
        total = stream_slope(section[:cells, lane(r)]) + side[:cells, lane(r)] + weighed(DIFFERENCE, at, r, True)
        for reach, factor in DIFFERENCE:
            if r + reach in owed:
                total = total + factor * owed[r + reach]
        parts[:cells, lane(r)] = total
        blocks.append(total)
    parts[cells:, :] = side[cells:]
    moments = [side[cells:, lane(r)] for r in range(ROWS)]
    up = (2.0 / 3.0) * at(0) - (1.0 / 12.0) * at(1)
    down = (1.0 / 12.0) * at(ROWS - 2) - (2.0 / 3.0) * at(ROWS - 1)
    return blocks, moments, at, up, down


def tendency_kernel(
    cells, rough, flat, thick, left, right, low, high, slopes, lateral,
    section, parts, up_near, down_near, up_far, down_far,
):
    add_beyond(cells, rough, flat, thick, left, right, low, high, slopes, section)
    blocks, moments, at, _, _ = own_source(cells, section, lateral, parts)
    row = lambda c, r: section[cells * c : cells * (c + 1), lane(r)]
    every = [at(r) for r in range(ROWS)]
    for near, far, outer, inner in ((up_near, up_far, 0, 2), (down_near, down_far, 2, 0)):
        side = [row(c, inner + k) for c in (0, 2) for k in range(2)]
        fill_slots(near, cells, blocks[outer : outer + 2] + every + side, moments[outer : outer + 2])
        fill_slots(far, cells, blocks[inner : inner + 2] + [at(inner), at(inner + 1)], moments[inner : inner + 2])


WHOLE = (-2, -1, ROWS, ROWS + 1)


def row_across(cells, section, arrived):
    low_one, high_one, low_two, high_two = arrived
    masks = edge_masks()

    def value(e):
        if 0 <= e < ROWS:
            return section[cells : 2 * cells, lane(e)]
        if e < -ROWS or e >= 2 * ROWS:
            ref, k = (low_two, e + 8) if e < 0 else (high_two, e - 6)
        else:
            ref, k = (low_one, e + 6) if e < 0 else (high_one, e - 2)
        return masked(slot(ref, cells, k)[...], e, masks)

    return value


def near_source_kernel(cells, parts, section, low_one, high_one, lateral, middle):
    masks = edge_masks()
    across = row_across(cells, section, (low_one, high_one, None, None))
    pick = lambda ref, k: slot(ref, cells, k)[...]
    given = [(low_one if e < 0 else high_one, e % 2) for e in WHOLE]
    beside = split_dot(lateral[...], jnp.concatenate([pick(ref, 8 + k) for ref, k in given], axis=1))
    for e in range(-2, ROWS + 2):
        if e in WHOLE:
            at = WHOLE.index(e)
            ref, k = given[at]
            total = stream_slope(pick(ref, 6 + k)) + beside[:cells, lane(at)]
            side = beside[cells:, lane(at)]
        else:
            total, side = parts[:cells, lane(e)], parts[cells:, lane(e)]
        for reach, factor in DIFFERENCE:
            if e in WHOLE or not 0 <= e + reach < ROWS:
                total = total + factor * across(e + reach)
        middle[:cells, lane(e + 2)] = masked(total, e, masks)
        middle[cells:, lane(e + 2)] = masked(side, e, masks)

def held_kernel(cells, section, moments, to_right, to_left):
    held = sum(split_dot(moments[c], section[cells * c : cells * (c + 1), :]) for c in range(3))
    to_right[...] = held[:PAD_V]
    to_left[...] = held[PAD_V:]


def first_source(cells, middle, arrived, ext):
    low_one, high_one, low_two, high_two = arrived
    masks = edge_masks()
    across = row_across(cells, None, arrived)
    ext[:, lane(FIRST.reach - 2, ROWS + 4)] = middle[...]
    for e in range(-FIRST.reach, ROWS + FIRST.reach):
        if -2 <= e < ROWS + 2:
            continue
        far = e < -ROWS or e >= 2 * ROWS
        ref = (low_two if e < 0 else high_two) if far else (low_one if e < 0 else high_one)
        top = (4 if far else 10) * cells + PAD_M * (e % 2)
        total, side = slot(ref, cells, e % 2)[...], ref[top : top + PAD_M, :]
        for reach, factor in DIFFERENCE:
            if (e + reach) // ROWS != e // ROWS:
                total = total + factor * across(e + reach)
        ext[:cells, lane(e + FIRST.reach)] = masked(total, e, masks)
        ext[cells:, lane(e + FIRST.reach)] = masked(side, e, masks)


def last_source(cells, parts, section, arrived, extra, ext):
    low_one, high_one, low_two, high_two = arrived
    masks = edge_masks()
    span, tail = slice(0, cells), slice(cells, cells + PAD_M)
    pick = lambda ref, k: slot(ref, cells, k)[...]

    def joined(e):
        if 0 <= e < ROWS:
            return parts[span, lane(e)], parts[tail, lane(e)]
        if e < -ROWS or e >= 2 * ROWS:
            ref = low_two if e < 0 else high_two
            return pick(ref, 0), ref[4 * cells :, :]
        ref, k = (low_one, e + ROWS) if e < 0 else (high_one, e - ROWS)
        top = 8 * cells + PAD_M * k
        return pick(ref, k), ref[top : top + PAD_M, :]

    def across(e, home):
        if e // ROWS == home // ROWS or home // ROWS in (-2, 2):
            return None
        if e < -ROWS:
            return masked(pick(low_two, 1 + e + ROWS + 2), e, masks)
        if e < 0:
            return masked(pick(low_one, ROWS + e + 2), e, masks)
        if e < ROWS:
            return section[cells : 2 * cells, lane(e)]
        if e < 2 * ROWS:
            return masked(pick(high_one, e), e, masks)
        return masked(pick(high_two, 1 + e - 2 * ROWS), e, masks)

    for e in range(-LAST.reach, ROWS + LAST.reach):
        total, side = joined(e)
        if e == -ROWS - 1:
            total = total + pick(low_one, 6)
        if e == 2 * ROWS:
            total = total + pick(high_one, 6)
        for reach, factor in DIFFERENCE:
            other = across(e + reach, e)
            if other is not None:
                total = total + factor * other
            if e + reach in extra and (e + reach) // ROWS == e // ROWS:
                total = total + factor * extra[e + reach]
        ext[span, lane(e + LAST.reach)] = masked(total, e, masks)
        ext[tail, lane(e + LAST.reach)] = masked(side, e, masks)


def pack_moments(extent, both, to_right, to_left):
    for side, out in enumerate((to_right, to_left)):
        top = 4 * GROUP * side
        out[:, lane(0, extent.breadth)] = both[top : top + 8]
        for k in range(extent.breadth // 2):
            out[:, lane(extent.breadth + k)] = (
                both[top + 8 : top + 16, lane(2 * k)] + both[top + 16 : top + 24, lane(2 * k + 1)]
            )


def source_kernel(
    cells, middle, low_one, high_one, low_two, high_two, source, ext, to_right, to_left
):
    first_source(cells, middle, (low_one, high_one, low_two, high_two), ext)
    both = split_dot(source[...], ext[...])
    pack_moments(FIRST, both, to_right, to_left)
    for side, out in enumerate((to_right, to_left)):
        top = 4 * GROUP * side
        for e in range(FIRST.breadth):
            row, tile = e % GROUP, FIRST.packed + e // GROUP
            out[row : row + 1, lane(tile)] = both[top + 24 : top + 25, lane(e)]


def last_source_kernel(
    cells, parts, section, debts, low_one, high_one, low_two, high_two, source,
    ext, fixed, to_right, to_left,
):
    masks = edge_masks()
    pick = lambda ref, k: slot(ref, cells, k)[...]
    extra = {
        0: pick(low_one, 7) * masks[0],
        ROWS - 1: pick(high_one, 7) * masks[2],
        -1: pick(debts, 0),
        ROWS: pick(debts, 1),
        -ROWS: pick(low_two, 3) * masks[1],
        2 * ROWS - 1: pick(high_two, 3) * masks[3],
    }
    fixed[:cells, :] = extra[0]
    fixed[cells:, :] = extra[ROWS - 1]
    last_source(cells, parts, section, (low_one, high_one, low_two, high_two), extra, ext)
    pack_moments(LAST, split_dot(source[...], ext[...]), to_right, to_left)


def climb(extent, levels, depth):
    masks = edge_masks()
    for j in range(1, SWEEPS):
        before = slice(depth * (j - 1), depth * j)
        after = slice(depth * j, depth * (j + 1))
        for e in range(-extent.reach + j, ROWS + extent.reach - j):
            k = e + extent.reach
            here = levels[before, lane(k)]
            beside = (
                turned(here, 1) + turned(here, -1) + levels[before, lane(k + 1)] + levels[before, lane(k - 1)]
            )
            levels[after, lane(k)] = masked(beside, e, masks)
    return levels[:, lane(SWEEPS - 1, extent.found)]


def home_kernel(extent, ext, solve, partial, levels):
    depth = ext.shape[0]
    levels[:depth, :] = ext[...]
    partial[...] = dot(solve[...], climb(extent, levels, depth))


def spare(given, e):
    row, tile = e % GROUP, FIRST.packed + e // GROUP
    return given[row : row + 1, lane(tile)]


def finish(extent, partial, left, right, solve, levels):
    for side, given in enumerate((left, right)):
        top = PAD_S * side
        levels[top : top + 8, :] = given[:, lane(0, extent.breadth)]
        for e in range(extent.breadth):
            tile = given[:, lane(extent.breadth + e // 2)]
            levels[top + 8 : top + 16, lane(e)] = pltpu.roll(tile, 4, 0) if e % 2 else tile
            if extent is FIRST:
                levels[top + 12 : top + 13, lane(e)] = spare(given, e)
    return partial[...] + split_dot(solve[...], climb(extent, levels, 2 * PAD_S))


def gradient(extent, found, c, rows, slope_rows, r):
    masks = edge_masks()
    phi = lambda r: masked(found[rows, lane(r + extent.margin)], r, masks)
    if c == 0:
        return stream_slope(phi(r))
    if c == 1:
        inside = lambda r: -extent.margin <= r < ROWS + extent.margin
        return sum(factor * phi(r + reach) for reach, factor in DIFFERENCE if inside(r + reach))
    return found[slope_rows, lane(r + extent.margin)]


def middle_kernel(
    cells, partial, left, right, held_left, held_right, section, solve, low_one, high_one, low, high, start,
    thick, full, lateral,
    following, parts, debts, up_near, down_near, up_far, down_far, levels, flat, rim, sides,
):
    masks = edge_masks()
    found = finish(FIRST, partial, left, right, solve, levels)
    home, home_slope = slice(0, cells), slice(cells, 2 * cells)
    outer = (-2, -1, ROWS, ROWS + 1)
    for c in range(3):
        rows = slice(cells * c, cells * (c + 1))
        for r in range(ROWS):
            flat[rows, lane(r)] = section[rows, lane(r)] - gradient(FIRST, found, c, home, home_slope, r)
        for k, r in enumerate(outer):
            first = (6, 4 if r < 0 else 2, 8)[c]
            value = slot(low_one if r < 0 else high_one, cells, first + k % 2)[...]
            value = value - gradient(FIRST, found, c, home, home_slope, r)
            rim[rows, lane(k)] = masked(value, r, masks)
    sides[...] = jnp.zeros(sides.shape, jnp.float32)
    for side, given in enumerate((held_left, held_right)):
        top = 2 * cells + 2 * GROUP * side
        phi_rows, slope_rows = slice(top, top + GROUP), slice(top + GROUP, top + 2 * GROUP)
        for r in range(ROWS):
            for c in range(3):
                change = gradient(FIRST, found, c, phi_rows, slope_rows, r)
                base = GROUP * c + RANK_V * side
                held = given[RANK_V * c : RANK_V * (c + 1), lane(r)]
                sides[base : base + RANK_V, lane(r)] = held - change[:RANK_V]

    def tile(c, r):
        rows = slice(cells * c, cells * (c + 1))
        return flat[rows, lane(r)] if 0 <= r < ROWS else rim[rows, lane(r + 2 if r < 0 else r - 2)]

    for c in range(3):
        rows = slice(cells * c, cells * (c + 1))
        spanned = split_dot(
            full[...], jnp.concatenate([flat[rows, :], sides[GROUP * c : GROUP * (c + 1), :]], axis=0)
        )
        for r in range(ROWS):
            here = tile(c, r)
            up_one, down_one = turned(here, 1), turned(here, -1)
            up_two, down_two = turned(here, 2), turned(here, -2)
            carried = (
                tile(0, r) * first_diff(up_one, down_one, up_two, down_two)
                + tile(1, r) * sum(factor * tile(c, r + reach) for reach, factor in DIFFERENCE)
                + tile(2, r) * spanned[:cells, lane(r)]
            )
            spread = (
                (4.0 / 3.0) * (up_one + down_one)
                - (1.0 / 12.0) * (up_two + down_two)
                - 5.0 * here
                + sum(factor * tile(c, r + reach) for reach, factor in CURVE)
                + spanned[cells:, lane(r)]
            )
            moved = here + time_step * (thick[:, lane(r)] * spread - carried)
            following[rows, lane(r)] = 0.5 * start[rows, lane(r)] + 0.5 * moved
    phi = lambda r: found[:cells, lane(r + FIRST.margin)]
    scale = 0.5 * time_step / 144.0
    owed = {
        -1: scale * (tile(1, -1) - slot(low, cells, 6)[...]) * phi(ROWS - 1) * masks[0],
        ROWS: scale * (tile(1, ROWS) + slot(high, cells, 6)[...]) * phi(0) * masks[2],
    }
    slot(debts, cells, 0)[...] = owed[-1]
    slot(debts, cells, 1)[...] = owed[ROWS]
    blocks, moments, at, up, down = own_source(cells, following, lateral, parts, owed)
    fill_slots(up_near, cells, blocks + [at(2), at(3), up, owed[ROWS]], moments)
    fill_slots(down_near, cells, blocks + [at(0), at(1), down, owed[-1]], moments)
    fill_slots(up_far, cells, [blocks[3], at(2), at(3), owed[ROWS]], moments[3:])
    fill_slots(down_far, cells, [blocks[0], at(0), at(1), owed[-1]], moments[:1])


def last_kernel(cells, partial, left, right, section, fixed, solve, out, levels, staged, sems):
    found = finish(LAST, partial, left, right, solve, levels)
    copies = []
    for c in (2, 0, 1):
        rows = slice(cells * c, cells * (c + 1))
        for r in range(ROWS):
            value = section[rows, lane(r)]
            if c == 1 and r in (0, ROWS - 1):
                value = value + fixed[cells * (r > 0) : cells * (1 + (r > 0)), :]
            value = value - gradient(LAST, found, c, slice(0, cells), slice(cells, 2 * cells), r)
            staged[rows, lane(r)] = value
            copies.append(
                pltpu.make_async_copy(staged.at[rows, lane(r)], out.at[c, :, r, :], sems.at[len(copies)])
            )
            copies[-1].start()
    for copy in copies:
        copy.wait()


def call(body, shapes, *args, scratch=(), **options):
    return pl.pallas_call(
        body,
        out_shape=[jax.ShapeDtypeStruct(s, jnp.float32) for s in shapes],
        scratch_shapes=scratch,
        compiler_params=pltpu.CompilerParams(vmem_limit_bytes=40 * 1024 * 1024),
        **options,
    )(*args)


def shifted(block, axis, step):
    count = lax.axis_size(axis)
    return lax.ppermute(block, axis, [(i, (i + step) % count) for i in range(count)])


def per_device(velocity, viscosity):
    components, cells, row_cells, columns = velocity.shape
    length = cells * lax.axis_size("span")
    own, first_own, slopes, full, moments, lateral, *first = (
        jnp.asarray(t) for t in tables(length, cells, False)
    )
    _, last_own, _, _, _, _, *last = (jnp.asarray(t) for t in tables(length, cells, True))
    width = row_cells * columns
    near = cells + PAD_M
    whole, edge, rim = (components * cells, width), (PAD_V, width), (7 * cells, columns)

    def across(up_near, down_near, up_far, down_far):
        return (
            shifted(up_near, "cross", 1), shifted(down_near, "cross", -1),
            shifted(up_far, "cross", 2), shifted(down_far, "cross", -2),
        )

    def message(near_slots, near_rows, far_slots, far_rows):
        near_shape = (near_slots * cells + near_rows * PAD_M, columns)
        far_shape = (far_slots * cells + far_rows * PAD_M, columns)
        return [near_shape] * 2 + [far_shape] * 2

    def levels(extent, depth):
        return pltpu.VMEM((SWEEPS * depth, extent.breadth * columns), jnp.float32)

    start, thick, to_right, to_left, upward, downward = call(
        functools.partial(open_kernel, cells),
        [whole, (cells, width), edge, edge, rim, rim],
        *(pltpu.with_memory_space_constraint(x, pltpu.HBM) for x in (velocity, viscosity, moments)),
        in_specs=[pl.BlockSpec(memory_space=pltpu.HBM)] * 3,
        scratch=[pltpu.VMEM(moments.shape, moments.dtype), pltpu.SemaphoreType.DMA((1 + 4 * ROWS,))],
    )
    left = shifted(to_right, "span", 1)
    right = shifted(to_left, "span", -1)
    low = shifted(upward, "cross", 1)
    high = shifted(downward, "cross", -1)
    (rough,) = call(functools.partial(rough_kernel, cells), [whole], start, thick, own)
    section, parts, *sent = call(
        functools.partial(tendency_kernel, cells),
        [whole, (near, width)] + message(10, 2, 4, 2),
        rough, start, thick, left, right, low, high, slopes, lateral,
    )
    arrived = across(*sent)
    to_right, to_left = call(functools.partial(held_kernel, cells), [edge, edge], section, moments)
    held_left = shifted(to_right, "span", 1)
    held_right = shifted(to_left, "span", -1)
    (middle,) = call(
        functools.partial(near_source_kernel, cells),
        [(near, 2 * width)],
        parts, section, *arrived[:2], lateral,
    )
    middle, held_left, held_right = lax.optimization_barrier((middle, held_left, held_right))
    ext, to_right, to_left = call(
        functools.partial(source_kernel, cells),
        [(near, FIRST.breadth * columns)] + [(GROUP, (FIRST.packed + 2) * columns)] * 2,
        middle, *arrived, first[0],
    )
    left = shifted(to_right, "span", 1)
    right = shifted(to_left, "span", -1)
    (partial,) = call(
        functools.partial(home_kernel, FIRST),
        [(first_own.shape[0], FIRST.found * columns)],
        ext, first_own,
        scratch=[levels(FIRST, near)],
    )

    section, parts, debts, *sent = call(
        functools.partial(middle_kernel, cells),
        [whole, (near, width), (2 * cells, columns)] + message(8, 4, 4, 1),
        partial, left, right, held_left, held_right, section, first[1], *arrived[:2], low, high, start, thick, full, lateral,
        scratch=[
            levels(FIRST, 2 * PAD_S),
            pltpu.VMEM(whole, jnp.float32),
            pltpu.VMEM((components * cells, 4 * columns), jnp.float32),
            pltpu.VMEM((components * GROUP, width), jnp.float32),
        ],
    )
    arrived = across(*sent)
    ext, fixed, to_right, to_left = call(
        functools.partial(last_source_kernel, cells),
        [(near, LAST.breadth * columns), (2 * cells, columns)] + [(GROUP, LAST.packed * columns)] * 2,
        parts, section, debts, *arrived, last[0],
    )
    left = shifted(to_right, "span", 1)
    right = shifted(to_left, "span", -1)
    (partial,) = call(
        functools.partial(home_kernel, LAST),
        [(last_own.shape[0], LAST.found * columns)],
        ext, last_own,
        scratch=[levels(LAST, near)],
    )
    (out,) = call(
        functools.partial(last_kernel, cells),
        [velocity.shape],
        partial, left, right, section, fixed, last[1],
        scratch=[
            levels(LAST, 2 * PAD_S),
            pltpu.VMEM(whole, jnp.float32),
            pltpu.SemaphoreType.DMA((3 * ROWS,)),
        ],
        out_specs=[pl.BlockSpec(memory_space=pltpu.HBM)],
    )
    return out


def solution(mesh):
    in_specs = (P(None, "span", "cross", None), P("span", "cross", None))
    out_specs = P(None, "span", "cross", None)
    return jax.shard_map(
        per_device, mesh=mesh, in_specs=in_specs, out_specs=out_specs, check_vma=False
    )
```

```python
import functools

import jax
import jax.numpy as jnp
import ml_dtypes
import numpy as np
from jax import lax
from jax.experimental import pallas as pl
from jax.experimental.pallas import tpu as pltpu
from jax.sharding import PartitionSpec as P

SWEEPS = 4
ROWS = 4
LANES = 128
time_step = 0.1
highest = lax.Precision.HIGHEST
PAD_V = 16
PAD_S = 16
PAD_M = 8
GROUP = 8
PACK = 16
RANK_V = 3
RANK_M = 2


def symbols(length):
    w = 2.0 * np.pi * np.arange(length) / length
    first = (14.0 / 9.0 * np.sin(w) + np.sin(2.0 * w) / 18.0) / (1.0 + 2.0 / 3.0 * np.cos(w))
    second = (24.0 / 11.0 * (1.0 - np.cos(w)) + 3.0 / 22.0 * (1.0 - np.cos(2.0 * w))) / (
        1.0 + 4.0 / 11.0 * np.cos(w)
    )
    return 1j * first, -second, 1.0 / (4.0 + second)


def block_of(symbol, cells, offset):
    kernel = np.fft.ifft(symbol).real
    at = np.arange(cells)
    return kernel[(at[:, None] - (at[None, :] + offset * cells)) % len(kernel)]


def low_rank(stack, rank):
    left, scale, right = np.linalg.svd(stack, full_matrices=False)
    return left[:, :rank] * scale[:rank], right[:rank]


@functools.lru_cache(None)
def tables(length, cells, last):
    first, second, inverse = symbols(length)
    at = lambda symbol, offset: block_of(symbol, cells, offset)
    from_left, take_left = low_rank(np.concatenate([at(first, -1), at(second, -1)]), RANK_V)
    from_right, take_right = low_rank(np.concatenate([at(first, 1), at(second, 1)]), RANK_V)
    own = np.concatenate([at(first, 0), at(second, 0)])
    slopes = np.zeros((3, 2 * cells, 2 * PAD_V))
    moments = np.zeros((3, 2 * PAD_V, cells))
    for c in range(3):
        rows = slice(RANK_V * c, RANK_V * (c + 1))
        slopes[c, :, :PAD_V][:, rows] = from_left
        slopes[c, :, PAD_V:][:, rows] = from_right
        moments[c, rows] = take_left
        moments[c, PAD_V:][rows] = take_right
    m_left, t_left = low_rank(at(first, -1), RANK_M)
    m_right, t_right = low_rank(at(first, 1), RANK_M)
    lateral = np.zeros((cells + PAD_M, cells))
    lateral[:cells] = at(first, 0)
    lateral[cells : cells + RANK_M] = t_left
    lateral[cells + RANK_M : cells + 2 * RANK_M] = t_right
    powers = [inverse ** (j + 1) for j in range(SWEEPS)]
    stacked = [p for p in powers] + [first * p for p in powers]
    count = len(stacked)
    RANK_S = 2 * SWEEPS + (1 if last else 3)
    kept = [] if last else stacked
    s_left, q_left = low_rank(
        np.concatenate([at(p, -1) for p in stacked] + [take_left @ at(p, 0) for p in kept]), RANK_S
    )
    s_right, q_right = low_rank(
        np.concatenate([at(p, 1) for p in stacked] + [take_right @ at(p, 0) for p in kept]), RANK_S
    )
    e_left, e_right = s_left[count * cells :], s_right[count * cells :]
    source = np.zeros((8 * GROUP, cells + PAD_M))
    for side, q in enumerate((q_left, q_right)):
        rows = np.zeros((PAD_S, cells + PAD_M))
        rows[:RANK_S, :cells] = q
        at_m = cells + RANK_M * side
        rows[RANK_S : RANK_S + RANK_M, at_m : at_m + RANK_M] = np.eye(RANK_M)
        top = 4 * GROUP * side
        source[top : top + 8] = rows[:8]
        source[top + 8 : top + 12] = rows[8:12]
        source[top + 20 : top + 24] = rows[8:12]
        source[top + 24] = rows[12]
    near, wide = cells + PAD_M, 2 * PAD_S
    height = 2 * cells + (0 if last else 4 * GROUP)
    solve_own = np.zeros((height, SWEEPS * near))
    solve_sides = np.zeros((height, SWEEPS * wide))
    for j in range(SWEEPS):
        for half in range(2):
            index = half * SWEEPS + j
            rows = slice(cells * index, cells * (index + 1))
            edge = slice(RANK_V * index, RANK_V * (index + 1))
            center = at(stacked[index], 0)
            by_left, by_right = s_left[rows], s_right[rows]
            mine, sides = np.zeros((cells, near)), np.zeros((cells, wide))
            mine[:, :cells] = center
            mine[:, cells : cells + RANK_M] = by_right @ (q_right @ m_left)
            mine[:, cells + RANK_M : cells + 2 * RANK_M] = by_left @ (q_left @ m_right)
            sides[:, :RANK_S] = by_left
            sides[:, RANK_S : RANK_S + RANK_M] = center @ m_left
            sides[:, PAD_S : PAD_S + RANK_S] = by_right
            sides[:, PAD_S + RANK_S : PAD_S + RANK_S + RANK_M] = center @ m_right
            solve_own[cells * half : cells * (half + 1), near * j : near * (j + 1)] = -mine
            solve_sides[cells * half : cells * (half + 1), wide * j : wide * (j + 1)] = -sides
            for side in range(0 if last else 2):
                mine, sides = np.zeros((RANK_V, near)), np.zeros((RANK_V, wide))
                if side == 0:
                    back = take_left @ by_right @ q_right
                    mine[:, cells + RANK_M : cells + 2 * RANK_M] = take_left @ center @ m_right
                    sides[:, :RANK_S] = e_left[edge]
                else:
                    back = take_right @ by_left @ q_left
                    mine[:, cells : cells + RANK_M] = take_right @ center @ m_left
                    sides[:, PAD_S : PAD_S + RANK_S] = e_right[edge]
                mine[:, :cells] = back
                sides[:, RANK_S : RANK_S + RANK_M] = back @ m_left
                sides[:, PAD_S + RANK_S : PAD_S + RANK_S + RANK_M] = back @ m_right
                top = 2 * cells + GROUP * (2 * side + half)
                solve_own[top : top + RANK_V, near * j : near * (j + 1)] = -mine
                solve_sides[top : top + RANK_V, wide * j : wide * (j + 1)] = -sides
    full = np.concatenate([own, from_left, from_right], axis=1)
    full = np.pad(full, [(0, 0), (0, GROUP - 2 * RANK_V)])
    plain, split = (own, solve_own), (slopes, full, moments, lateral, source, solve_sides)
    return [x.astype(np.float32) for x in plain] + [split_table(x.astype(np.float32)) for x in split]


def dot(a, b):
    return jnp.dot(a, b, precision=highest, preferred_element_type=jnp.float32)


def halves(x):
    high = x.astype(jnp.bfloat16)
    return high, (x - high.astype(jnp.float32)).astype(jnp.bfloat16)


def split_table(table):
    gap = -table.shape[-1] % PACK
    table = np.pad(table, [(0, 0)] * (table.ndim - 1) + [(0, gap)])
    high = table.astype(ml_dtypes.bfloat16)
    low = (table - high.astype(np.float32)).astype(ml_dtypes.bfloat16)
    return np.concatenate([high, high, low], axis=-1)


def split_dot(table, x):
    gap = -x.shape[0] % PACK
    if gap:
        x = jnp.concatenate([x, jnp.zeros((gap, x.shape[1]), x.dtype)], axis=0)
    high, low = halves(x)
    return jnp.dot(table, jnp.concatenate([high, low, high], axis=0), preferred_element_type=jnp.float32)


class Extent:
    def __init__(self, margin):
        self.margin = margin
        self.reach = margin + SWEEPS - 1
        self.breadth = ROWS + 2 * self.reach
        self.packed = self.breadth + self.breadth // 2
        self.found = ROWS + 2 * margin


FIRST, LAST = Extent(3), Extent(2)


DIFFERENCE = ((1, 2.0 / 3.0), (-1, -2.0 / 3.0), (2, -1.0 / 12.0), (-2, 1.0 / 12.0))
CURVE = ((1, 4.0 / 3.0), (-1, 4.0 / 3.0), (2, -1.0 / 12.0), (-2, -1.0 / 12.0))


def lane(r, count=1):
    return slice(r * LANES, (r + count) * LANES)


def turned(tile, step):
    return pltpu.roll(tile, (-step) % LANES, 1)


def edge_masks():
    at = lax.axis_index("cross")
    last = lax.axis_size("cross") - 1
    flag = lambda test: jnp.where(test, 1.0, 0.0).astype(jnp.float32)
    return (flag(at >= 1), flag(at >= 2), flag(at <= last - 1), flag(at <= last - 2))


def masked(tile, e, masks):
    if e < -ROWS:
        return tile * masks[1]
    if e < 0:
        return tile * masks[0]
    if e >= 2 * ROWS:
        return tile * masks[3]
    if e >= ROWS:
        return tile * masks[2]
    return tile


def first_diff(up_one, down_one, up_two, down_two):
    return (8.0 * (up_one - down_one) - (up_two - down_two)) * (1.0 / 12.0)


def second_diff(middle, up_one, down_one, up_two, down_two):
    return (16.0 * (up_one + down_one) - (up_two + down_two) - 30.0 * middle) * (1.0 / 12.0)


def stream_slope(tile):
    return first_diff(turned(tile, 1), turned(tile, -1), turned(tile, 2), turned(tile, -2))


def open_kernel(
    cells, velocity, viscosity, moments, flat, thick, to_right, to_left, upward, downward, weights, sems
):
    copies = [pltpu.make_async_copy(moments, weights, sems.at[0])]
    for c in range(3):
        rows = slice(cells * c, cells * (c + 1))
        for r in range(ROWS):
            copies.append(
                pltpu.make_async_copy(velocity.at[c, :, r, :], flat.at[rows, lane(r)], sems.at[len(copies)])
            )
    for r in range(ROWS):
        copies.append(pltpu.make_async_copy(viscosity.at[:, r, :], thick.at[:, lane(r)], sems.at[len(copies)]))
    for copy in copies:
        copy.start()
    copies[0].wait()
    both = None
    for c in range(3):
        for copy in copies[1 + ROWS * c : 1 + ROWS * (c + 1)]:
            copy.wait()
        rows = slice(cells * c, cells * (c + 1))
        for k in range(2):
            slot(upward, cells, 2 * c + k)[...] = flat[rows, lane(2 + k)]
            slot(downward, cells, 2 * c + k)[...] = flat[rows, lane(k)]
        part = split_dot(weights[c], flat[rows, :])
        both = part if both is None else both + part
    to_right[...] = both[:PAD_V]
    to_left[...] = both[PAD_V:]
    for copy in copies[1 + 3 * ROWS :]:
        copy.wait()
    slot(upward, cells, 6)[...] = thick[:, lane(ROWS - 1)]
    slot(downward, cells, 6)[...] = thick[:, lane(0)]


def added(parts):
    return functools.reduce(lambda a, b: a + b, parts)


def weighed(weights, value_at, r, home):
    total = None
    for reach, factor in weights:
        if (0 <= r + reach < ROWS) == home:
            part = factor * value_at(r + reach)
            total = part if total is None else total + part
    return total


def rough_kernel(cells, flat, thick, own, rough):
    for c in range(3):
        rows = slice(cells * c, cells * (c + 1))
        at = lambda r: flat[rows, lane(r)]
        spanned = dot(own[...], flat[rows, :])
        for r in range(ROWS):
            here = at(r)
            up_one, down_one = turned(here, 1), turned(here, -1)
            up_two, down_two = turned(here, 2), turned(here, -2)
            carried = (
                flat[:cells, lane(r)] * first_diff(up_one, down_one, up_two, down_two)
                + flat[cells : 2 * cells, lane(r)] * weighed(DIFFERENCE, at, r, True)
                + flat[2 * cells :, lane(r)] * spanned[:cells, lane(r)]
            )
            spread = (
                (4.0 / 3.0) * (up_one + down_one)
                - (1.0 / 12.0) * (up_two + down_two)
                - 5.0 * here
                + weighed(CURVE, at, r, True)
                + spanned[cells:, lane(r)]
            )
            rough[rows, lane(r)] = here + time_step * (thick[:, lane(r)] * spread - carried)


def add_beyond(cells, rough, flat, thick, left, right, low, high, slopes, section):
    masks = edge_masks()
    sides = jnp.concatenate([left[...], right[...]], axis=0)
    for c in range(3):
        rows = slice(cells * c, cells * (c + 1))
        spanned = split_dot(slopes[c], sides)

        def beyond(r):
            if r < 0:
                return masked(slot(low, cells, 2 * c + r + 2)[...], r, masks)
            return masked(slot(high, cells, 2 * c + r - ROWS)[...], r, masks)

        for r in range(ROWS):
            spread = spanned[cells:, lane(r)] + weighed(CURVE, beyond, r, False)
            carried = flat[cells : 2 * cells, lane(r)] * weighed(DIFFERENCE, beyond, r, False)
            carried = carried + flat[2 * cells :, lane(r)] * spanned[:cells, lane(r)]
            section[rows, lane(r)] = rough[rows, lane(r)] + time_step * (thick[:, lane(r)] * spread - carried)


def slot(ref, cells, k):
    return ref.at[cells * k : cells * (k + 1), :]


def fill_slots(ref, cells, blocks, moments):
    for k, block in enumerate(blocks):
        slot(ref, cells, k)[...] = block
    for k, block in enumerate(moments):
        top = cells * len(blocks) + PAD_M * k
        ref[top : top + PAD_M, :] = block


def own_source(cells, section, lateral, parts, owed={}):
    side = split_dot(lateral[...], section[2 * cells :, :])
    at = lambda r: section[cells : 2 * cells, lane(r)]
    blocks = []
    for r in range(ROWS):
        total = stream_slope(section[:cells, lane(r)]) + side[:cells, lane(r)] + weighed(DIFFERENCE, at, r, True)
        for reach, factor in DIFFERENCE:
            if r + reach in owed:
                total = total + factor * owed[r + reach]
        parts[:cells, lane(r)] = total
        blocks.append(total)
    parts[cells:, :] = side[cells:]
    moments = [side[cells:, lane(r)] for r in range(ROWS)]
    up = (2.0 / 3.0) * at(0) - (1.0 / 12.0) * at(1)
    down = (1.0 / 12.0) * at(ROWS - 2) - (2.0 / 3.0) * at(ROWS - 1)
    return blocks, moments, at, up, down


def tendency_kernel(
    cells, rough, flat, thick, left, right, low, high, slopes, lateral,
    section, parts, up_near, down_near, up_far, down_far,
):
    add_beyond(cells, rough, flat, thick, left, right, low, high, slopes, section)
    blocks, moments, at, _, _ = own_source(cells, section, lateral, parts)
    row = lambda c, r: section[cells * c : cells * (c + 1), lane(r)]
    every = [at(r) for r in range(ROWS)]
    for near, far, outer, inner in ((up_near, up_far, 0, 2), (down_near, down_far, 2, 0)):
        side = [row(c, inner + k) for c in (0, 2) for k in range(2)]
        fill_slots(near, cells, blocks[outer : outer + 2] + every + side, moments[outer : outer + 2])
        fill_slots(far, cells, blocks[inner : inner + 2] + [at(inner), at(inner + 1)], moments[inner : inner + 2])


WHOLE = (-2, -1, ROWS, ROWS + 1)


def row_across(cells, section, arrived):
    low_one, high_one, low_two, high_two = arrived
    masks = edge_masks()

    def value(e):
        if 0 <= e < ROWS:
            return section[cells : 2 * cells, lane(e)]
        if e < -ROWS or e >= 2 * ROWS:
            ref, k = (low_two, e + 8) if e < 0 else (high_two, e - 6)
        else:
            ref, k = (low_one, e + 6) if e < 0 else (high_one, e - 2)
        return masked(slot(ref, cells, k)[...], e, masks)

    return value


def near_source_kernel(cells, parts, section, low_one, high_one, lateral, moments, middle, held):
    masks = edge_masks()
    across = row_across(cells, section, (low_one, high_one, None, None))
    pick = lambda ref, k: slot(ref, cells, k)[...]
    given = [(low_one if e < 0 else high_one, e % 2) for e in WHOLE]
    beside = split_dot(lateral[...], jnp.concatenate([pick(ref, 8 + k) for ref, k in given], axis=1))
    for e in range(-2, ROWS + 2):
        if e in WHOLE:
            at = WHOLE.index(e)
            ref, k = given[at]
            total = stream_slope(pick(ref, 6 + k)) + beside[:cells, lane(at)]
            side = beside[cells:, lane(at)]
        else:
            total, side = parts[:cells, lane(e)], parts[cells:, lane(e)]
        for reach, factor in DIFFERENCE:
            if e in WHOLE or not 0 <= e + reach < ROWS:
                total = total + factor * across(e + reach)
        middle[:cells, lane(e + 2)] = masked(total, e, masks)
        middle[cells:, lane(e + 2)] = masked(side, e, masks)
    held[...] = added(split_dot(moments[c], section[cells * c : cells * (c + 1), :]) for c in range(3))


def first_source(cells, middle, arrived, ext):
    low_one, high_one, low_two, high_two = arrived
    masks = edge_masks()
    across = row_across(cells, None, arrived)
    ext[:, lane(FIRST.reach - 2, ROWS + 4)] = middle[...]
    for e in range(-FIRST.reach, ROWS + FIRST.reach):
        if -2 <= e < ROWS + 2:
            continue
        far = e < -ROWS or e >= 2 * ROWS
        ref = (low_two if e < 0 else high_two) if far else (low_one if e < 0 else high_one)
        top = (4 if far else 10) * cells + PAD_M * (e % 2)
        total, side = slot(ref, cells, e % 2)[...], ref[top : top + PAD_M, :]
        for reach, factor in DIFFERENCE:
            if (e + reach) // ROWS != e // ROWS:
                total = total + factor * across(e + reach)
        ext[:cells, lane(e + FIRST.reach)] = masked(total, e, masks)
        ext[cells:, lane(e + FIRST.reach)] = masked(side, e, masks)


def last_source(cells, parts, section, arrived, extra, ext):
    low_one, high_one, low_two, high_two = arrived
    masks = edge_masks()
    span, tail = slice(0, cells), slice(cells, cells + PAD_M)
    pick = lambda ref, k: slot(ref, cells, k)[...]

    def joined(e):
        if 0 <= e < ROWS:
            return parts[span, lane(e)], parts[tail, lane(e)]
        if e < -ROWS or e >= 2 * ROWS:
            ref = low_two if e < 0 else high_two
            return pick(ref, 0), ref[4 * cells :, :]
        ref, k = (low_one, e + ROWS) if e < 0 else (high_one, e - ROWS)
        top = 8 * cells + PAD_M * k
        return pick(ref, k), ref[top : top + PAD_M, :]

    def across(e, home):
        if e // ROWS == home // ROWS or home // ROWS in (-2, 2):
            return None
        if e < -ROWS:
            return masked(pick(low_two, 1 + e + ROWS + 2), e, masks)
        if e < 0:
            return masked(pick(low_one, ROWS + e + 2), e, masks)
        if e < ROWS:
            return section[cells : 2 * cells, lane(e)]
        if e < 2 * ROWS:
            return masked(pick(high_one, e), e, masks)
        return masked(pick(high_two, 1 + e - 2 * ROWS), e, masks)

    for e in range(-LAST.reach, ROWS + LAST.reach):
        total, side = joined(e)
        if e == -ROWS - 1:
            total = total + pick(low_one, 6)
        if e == 2 * ROWS:
            total = total + pick(high_one, 6)
        for reach, factor in DIFFERENCE:
            other = across(e + reach, e)
            if other is not None:
                total = total + factor * other
            if e + reach in extra and (e + reach) // ROWS == e // ROWS:
                total = total + factor * extra[e + reach]
        ext[span, lane(e + LAST.reach)] = masked(total, e, masks)
        ext[tail, lane(e + LAST.reach)] = masked(side, e, masks)


def pack_moments(extent, both, to_right, to_left):
    for side, out in enumerate((to_right, to_left)):
        top = 4 * GROUP * side
        out[:, lane(0, extent.breadth)] = both[top : top + 8]
        for k in range(extent.breadth // 2):
            out[:, lane(extent.breadth + k)] = (
                both[top + 8 : top + 16, lane(2 * k)] + both[top + 16 : top + 24, lane(2 * k + 1)]
            )


def source_kernel(
    cells, middle, held, low_one, high_one, low_two, high_two, source, ext, to_right, to_left
):
    first_source(cells, middle, (low_one, high_one, low_two, high_two), ext)
    both = split_dot(source[...], ext[...])
    pack_moments(FIRST, both, to_right, to_left)
    for side, out in enumerate((to_right, to_left)):
        top, base = 4 * GROUP * side, PAD_V * side
        out[:, lane(FIRST.packed, ROWS)] = held[base : base + 8]
        out[:, lane(FIRST.packed + ROWS, 3)] = jnp.zeros((GROUP, 3 * LANES), jnp.float32)
        for e in range(FIRST.breadth + ROWS):
            value = (
                both[top + 24 : top + 25, lane(e)]
                if e < FIRST.breadth
                else held[base + 8 : base + 9, lane(e - FIRST.breadth)]
            )
            row, tile = e % GROUP, FIRST.packed + ROWS + e // GROUP
            out[row : row + 1, lane(tile)] = value


def last_source_kernel(
    cells, parts, section, debts, low_one, high_one, low_two, high_two, source,
    ext, fixed, to_right, to_left,
):
    masks = edge_masks()
    pick = lambda ref, k: slot(ref, cells, k)[...]
    extra = {
        0: pick(low_one, 7) * masks[0],
        ROWS - 1: pick(high_one, 7) * masks[2],
        -1: pick(debts, 0),
        ROWS: pick(debts, 1),
        -ROWS: pick(low_two, 3) * masks[1],
        2 * ROWS - 1: pick(high_two, 3) * masks[3],
    }
    fixed[:cells, :] = extra[0]
    fixed[cells:, :] = extra[ROWS - 1]
    last_source(cells, parts, section, (low_one, high_one, low_two, high_two), extra, ext)
    pack_moments(LAST, split_dot(source[...], ext[...]), to_right, to_left)


def climb(extent, levels, depth):
    masks = edge_masks()
    for j in range(1, SWEEPS):
        before = slice(depth * (j - 1), depth * j)
        after = slice(depth * j, depth * (j + 1))
        for e in range(-extent.reach + j, ROWS + extent.reach - j):
            k = e + extent.reach
            here = levels[before, lane(k)]
            beside = (
                turned(here, 1) + turned(here, -1) + levels[before, lane(k + 1)] + levels[before, lane(k - 1)]
            )
            levels[after, lane(k)] = masked(beside, e, masks)
    return levels[:, lane(SWEEPS - 1, extent.found)]


def home_kernel(extent, ext, solve, partial, levels):
    depth = ext.shape[0]
    levels[:depth, :] = ext[...]
    partial[...] = dot(solve[...], climb(extent, levels, depth))


def spare(given, e):
    row, tile = e % GROUP, FIRST.packed + ROWS + e // GROUP
    return given[row : row + 1, lane(tile)]


def finish(extent, partial, left, right, solve, levels):
    for side, given in enumerate((left, right)):
        top = PAD_S * side
        levels[top : top + 8, :] = given[:, lane(0, extent.breadth)]
        for e in range(extent.breadth):
            tile = given[:, lane(extent.breadth + e // 2)]
            levels[top + 8 : top + 16, lane(e)] = pltpu.roll(tile, 4, 0) if e % 2 else tile
            if extent is FIRST:
                levels[top + 12 : top + 13, lane(e)] = spare(given, e)
    return partial[...] + split_dot(solve[...], climb(extent, levels, 2 * PAD_S))


def gradient(extent, found, c, rows, slope_rows, r):
    masks = edge_masks()
    phi = lambda r: masked(found[rows, lane(r + extent.margin)], r, masks)
    if c == 0:
        return stream_slope(phi(r))
    if c == 1:
        inside = lambda r: -extent.margin <= r < ROWS + extent.margin
        return added(factor * phi(r + reach) for reach, factor in DIFFERENCE if inside(r + reach))
    return found[slope_rows, lane(r + extent.margin)]


def middle_kernel(
    cells, partial, left, right, section, solve, low_one, high_one, low, high, start, thick, full, lateral,
    following, parts, debts, up_near, down_near, up_far, down_far, levels, flat, rim, sides,
):
    masks = edge_masks()
    found = finish(FIRST, partial, left, right, solve, levels)
    home, home_slope = slice(0, cells), slice(cells, 2 * cells)
    outer = (-2, -1, ROWS, ROWS + 1)
    for c in range(3):
        rows = slice(cells * c, cells * (c + 1))
        for r in range(ROWS):
            flat[rows, lane(r)] = section[rows, lane(r)] - gradient(FIRST, found, c, home, home_slope, r)
        for k, r in enumerate(outer):
            first = (6, 4 if r < 0 else 2, 8)[c]
            value = slot(low_one if r < 0 else high_one, cells, first + k % 2)[...]
            value = value - gradient(FIRST, found, c, home, home_slope, r)
            rim[rows, lane(k)] = masked(value, r, masks)
    sides[...] = jnp.zeros(sides.shape, jnp.float32)
    for side, given in enumerate((left, right)):
        top = 2 * cells + 2 * GROUP * side
        phi_rows, slope_rows = slice(top, top + GROUP), slice(top + GROUP, top + 2 * GROUP)
        for r in range(ROWS):
            for c in range(3):
                change = gradient(FIRST, found, c, phi_rows, slope_rows, r)
                base = GROUP * c + RANK_V * side
                count = min(RANK_V, GROUP - RANK_V * c)
                held = given[RANK_V * c : RANK_V * c + count, lane(FIRST.packed + r)]
                sides[base : base + count, lane(r)] = held - change[:count]
                if count < RANK_V:
                    held = spare(given, FIRST.breadth + r)
                    sides[base + count : base + RANK_V, lane(r)] = held - change[count:RANK_V]

    def tile(c, r):
        rows = slice(cells * c, cells * (c + 1))
        return flat[rows, lane(r)] if 0 <= r < ROWS else rim[rows, lane(r + 2 if r < 0 else r - 2)]

    for c in range(3):
        rows = slice(cells * c, cells * (c + 1))
        spanned = split_dot(
            full[...], jnp.concatenate([flat[rows, :], sides[GROUP * c : GROUP * (c + 1), :]], axis=0)
        )
        for r in range(ROWS):
            here = tile(c, r)
            up_one, down_one = turned(here, 1), turned(here, -1)
            up_two, down_two = turned(here, 2), turned(here, -2)
            carried = (
                tile(0, r) * first_diff(up_one, down_one, up_two, down_two)
                + tile(1, r) * added(factor * tile(c, r + reach) for reach, factor in DIFFERENCE)
                + tile(2, r) * spanned[:cells, lane(r)]
            )
            spread = (
                (4.0 / 3.0) * (up_one + down_one)
                - (1.0 / 12.0) * (up_two + down_two)
                - 5.0 * here
                + added(factor * tile(c, r + reach) for reach, factor in CURVE)
                + spanned[cells:, lane(r)]
            )
            change = (0.5 * time_step) * (thick[:, lane(r)] * spread - carried)
            following[rows, lane(r)] = 0.5 * (start[rows, lane(r)] + here) + change
    phi = lambda r: found[:cells, lane(r + FIRST.margin)]
    scale = 0.5 * time_step / 144.0
    owed = {
        -1: scale * (tile(1, -1) - slot(low, cells, 6)[...]) * phi(ROWS - 1) * masks[0],
        ROWS: scale * (tile(1, ROWS) + slot(high, cells, 6)[...]) * phi(0) * masks[2],
    }
    slot(debts, cells, 0)[...] = owed[-1]
    slot(debts, cells, 1)[...] = owed[ROWS]
    blocks, moments, at, up, down = own_source(cells, following, lateral, parts, owed)
    fill_slots(up_near, cells, blocks + [at(2), at(3), up, owed[ROWS]], moments)
    fill_slots(down_near, cells, blocks + [at(0), at(1), down, owed[-1]], moments)
    fill_slots(up_far, cells, [blocks[3], at(2), at(3), owed[ROWS]], moments[3:])
    fill_slots(down_far, cells, [blocks[0], at(0), at(1), owed[-1]], moments[:1])


def last_kernel(cells, partial, left, right, section, fixed, solve, out, levels, staged, sems):
    found = finish(LAST, partial, left, right, solve, levels)
    copies = []
    for c in (2, 0, 1):
        rows = slice(cells * c, cells * (c + 1))
        for r in range(ROWS):
            value = section[rows, lane(r)]
            if c == 1 and r in (0, ROWS - 1):
                value = value + fixed[cells * (r > 0) : cells * (1 + (r > 0)), :]
            value = value - gradient(LAST, found, c, slice(0, cells), slice(cells, 2 * cells), r)
            staged[rows, lane(r)] = value
            copies.append(
                pltpu.make_async_copy(staged.at[rows, lane(r)], out.at[c, :, r, :], sems.at[len(copies)])
            )
            copies[-1].start()
    for copy in copies:
        copy.wait()


def call(body, shapes, *args, scratch=(), **options):
    return pl.pallas_call(
        body,
        out_shape=[jax.ShapeDtypeStruct(s, jnp.float32) for s in shapes],
        scratch_shapes=scratch,
        compiler_params=pltpu.CompilerParams(vmem_limit_bytes=40 * 1024 * 1024),
        **options,
    )(*args)


def shifted(block, axis, step):
    count = lax.axis_size(axis)
    return lax.ppermute(block, axis, [(i, (i + step) % count) for i in range(count)])


def per_device(velocity, viscosity):
    components, cells, row_cells, columns = velocity.shape
    length = cells * lax.axis_size("span")
    own, first_own, slopes, full, moments, lateral, *first = (
        jnp.asarray(t) for t in tables(length, cells, False)
    )
    _, last_own, _, _, _, _, *last = (jnp.asarray(t) for t in tables(length, cells, True))
    width = row_cells * columns
    near = cells + PAD_M
    whole, edge, rim = (components * cells, width), (PAD_V, width), (7 * cells, columns)

    def across(up_near, down_near, up_far, down_far):
        return (
            shifted(up_near, "cross", 1), shifted(down_near, "cross", -1),
            shifted(up_far, "cross", 2), shifted(down_far, "cross", -2),
        )

    def message(near_slots, near_rows, far_slots, far_rows):
        near_shape = (near_slots * cells + near_rows * PAD_M, columns)
        far_shape = (far_slots * cells + far_rows * PAD_M, columns)
        return [near_shape] * 2 + [far_shape] * 2

    def levels(extent, depth):
        return pltpu.VMEM((SWEEPS * depth, extent.breadth * columns), jnp.float32)

    start, thick, to_right, to_left, upward, downward = call(
        functools.partial(open_kernel, cells),
        [whole, (cells, width), edge, edge, rim, rim],
        *(pltpu.with_memory_space_constraint(x, pltpu.HBM) for x in (velocity, viscosity, moments)),
        in_specs=[pl.BlockSpec(memory_space=pltpu.HBM)] * 3,
        scratch=[pltpu.VMEM(moments.shape, moments.dtype), pltpu.SemaphoreType.DMA((1 + 4 * ROWS,))],
    )
    left = shifted(to_right, "span", 1)
    right = shifted(to_left, "span", -1)
    low = shifted(upward, "cross", 1)
    high = shifted(downward, "cross", -1)
    (rough,) = call(functools.partial(rough_kernel, cells), [whole], start, thick, own)
    section, parts, *sent = call(
        functools.partial(tendency_kernel, cells),
        [whole, (near, width)] + message(10, 2, 4, 2),
        rough, start, thick, left, right, low, high, slopes, lateral,
    )
    arrived = across(*sent)
    middle, held = call(
        functools.partial(near_source_kernel, cells),
        [(near, 2 * width), (2 * PAD_V, width)],
        parts, section, *arrived[:2], lateral, moments,
    )
    ext, to_right, to_left = call(
        functools.partial(source_kernel, cells),
        [(near, FIRST.breadth * columns)] + [(GROUP, (FIRST.packed + ROWS + 3) * columns)] * 2,
        middle, held, *arrived, first[0],
    )
    left = shifted(to_right, "span", 1)
    right = shifted(to_left, "span", -1)
    (partial,) = call(
        functools.partial(home_kernel, FIRST),
        [(first_own.shape[0], FIRST.found * columns)],
        ext, first_own,
        scratch=[levels(FIRST, near)],
    )

    section, parts, debts, *sent = call(
        functools.partial(middle_kernel, cells),
        [whole, (near, width), (2 * cells, columns)] + message(8, 4, 4, 1),
        partial, left, right, section, first[1], *arrived[:2], low, high, start, thick, full, lateral,
        scratch=[
            levels(FIRST, 2 * PAD_S),
            pltpu.VMEM(whole, jnp.float32),
            pltpu.VMEM((components * cells, 4 * columns), jnp.float32),
            pltpu.VMEM((components * GROUP, width), jnp.float32),
        ],
    )
    arrived = across(*sent)
    ext, fixed, to_right, to_left = call(
        functools.partial(last_source_kernel, cells),
        [(near, LAST.breadth * columns), (2 * cells, columns)] + [(GROUP, LAST.packed * columns)] * 2,
        parts, section, debts, *arrived, last[0],
    )
    left = shifted(to_right, "span", 1)
    right = shifted(to_left, "span", -1)
    (partial,) = call(
        functools.partial(home_kernel, LAST),
        [(last_own.shape[0], LAST.found * columns)],
        ext, last_own,
        scratch=[levels(LAST, near)],
    )
    (out,) = call(
        functools.partial(last_kernel, cells),
        [velocity.shape],
        partial, left, right, section, fixed, last[1],
        scratch=[
            levels(LAST, 2 * PAD_S),
            pltpu.VMEM(whole, jnp.float32),
            pltpu.SemaphoreType.DMA((3 * ROWS,)),
        ],
        out_specs=[pl.BlockSpec(memory_space=pltpu.HBM)],
    )
    return out


def solution(mesh):
    in_specs = (P(None, "span", "cross", None), P("span", "cross", None))
    out_specs = P(None, "span", "cross", None)
    return jax.shard_map(
        per_device, mesh=mesh, in_specs=in_specs, out_specs=out_specs, check_vma=False
    )
```

```python
import functools

import jax
import jax.numpy as jnp
import ml_dtypes
import numpy as np
from jax import lax
from jax.experimental import pallas as pl
from jax.experimental.pallas import tpu as pltpu
from jax.sharding import PartitionSpec as P

SWEEPS = 4
ROWS = 4
LANES = 128
time_step = 0.1
highest = lax.Precision.HIGHEST
PAD_V = 16
PAD_S = 16
PAD_M = 8
GROUP = 8
PACK = 16
RANK_V = 3
RANK_M = 2


def symbols(length):
    w = 2.0 * np.pi * np.arange(length) / length
    first = (14.0 / 9.0 * np.sin(w) + np.sin(2.0 * w) / 18.0) / (1.0 + 2.0 / 3.0 * np.cos(w))
    second = (24.0 / 11.0 * (1.0 - np.cos(w)) + 3.0 / 22.0 * (1.0 - np.cos(2.0 * w))) / (
        1.0 + 4.0 / 11.0 * np.cos(w)
    )
    return 1j * first, -second, 1.0 / (4.0 + second)


def block_of(symbol, cells, offset):
    kernel = np.fft.ifft(symbol).real
    at = np.arange(cells)
    return kernel[(at[:, None] - (at[None, :] + offset * cells)) % len(kernel)]


def low_rank(stack, rank):
    left, scale, right = np.linalg.svd(stack, full_matrices=False)
    return left[:, :rank] * scale[:rank], right[:rank]


@functools.lru_cache(None)
def tables(length, cells, last):
    first, second, inverse = symbols(length)
    at = lambda symbol, offset: block_of(symbol, cells, offset)
    from_left, take_left = low_rank(np.concatenate([at(first, -1), at(second, -1)]), RANK_V)
    from_right, take_right = low_rank(np.concatenate([at(first, 1), at(second, 1)]), RANK_V)
    own = np.concatenate([at(first, 0), at(second, 0)])
    slopes = np.zeros((3, 2 * cells, 2 * PAD_V))
    moments = np.zeros((3, 2 * PAD_V, cells))
    for c in range(3):
        rows = slice(RANK_V * c, RANK_V * (c + 1))
        slopes[c, :, :PAD_V][:, rows] = from_left
        slopes[c, :, PAD_V:][:, rows] = from_right
        moments[c, rows] = take_left
        moments[c, PAD_V:][rows] = take_right
    m_left, t_left = low_rank(at(first, -1), RANK_M)
    m_right, t_right = low_rank(at(first, 1), RANK_M)
    lateral = np.zeros((cells + PAD_M, cells))
    lateral[:cells] = at(first, 0)
    lateral[cells : cells + RANK_M] = t_left
    lateral[cells + RANK_M : cells + 2 * RANK_M] = t_right
    powers = [inverse ** (j + 1) for j in range(SWEEPS)]
    stacked = [p for p in powers] + [first * p for p in powers]
    count = len(stacked)
    RANK_S = 2 * SWEEPS + (1 if last else 3)
    kept = [] if last else stacked
    s_left, q_left = low_rank(
        np.concatenate([at(p, -1) for p in stacked] + [take_left @ at(p, 0) for p in kept]), RANK_S
    )
    s_right, q_right = low_rank(
        np.concatenate([at(p, 1) for p in stacked] + [take_right @ at(p, 0) for p in kept]), RANK_S
    )
    e_left, e_right = s_left[count * cells :], s_right[count * cells :]
    source = np.zeros((8 * GROUP, cells + PAD_M))
    for side, q in enumerate((q_left, q_right)):
        rows = np.zeros((PAD_S, cells + PAD_M))
        rows[:RANK_S, :cells] = q
        at_m = cells + RANK_M * side
        rows[RANK_S : RANK_S + RANK_M, at_m : at_m + RANK_M] = np.eye(RANK_M)
        top = 4 * GROUP * side
        source[top : top + 8] = rows[:8]
        source[top + 8 : top + 12] = rows[8:12]
        source[top + 20 : top + 24] = rows[8:12]
        source[top + 24] = rows[12]
    near, wide = cells + PAD_M, 2 * PAD_S
    height = 2 * cells + (0 if last else 4 * GROUP)
    solve_own = np.zeros((height, SWEEPS * near))
    solve_sides = np.zeros((height, SWEEPS * wide))
    for j in range(SWEEPS):
        for half in range(2):
            index = half * SWEEPS + j
            rows = slice(cells * index, cells * (index + 1))
            edge = slice(RANK_V * index, RANK_V * (index + 1))
            center = at(stacked[index], 0)
            by_left, by_right = s_left[rows], s_right[rows]
            mine, sides = np.zeros((cells, near)), np.zeros((cells, wide))
            mine[:, :cells] = center
            mine[:, cells : cells + RANK_M] = by_right @ (q_right @ m_left)
            mine[:, cells + RANK_M : cells + 2 * RANK_M] = by_left @ (q_left @ m_right)
            sides[:, :RANK_S] = by_left
            sides[:, RANK_S : RANK_S + RANK_M] = center @ m_left
            sides[:, PAD_S : PAD_S + RANK_S] = by_right
            sides[:, PAD_S + RANK_S : PAD_S + RANK_S + RANK_M] = center @ m_right
            solve_own[cells * half : cells * (half + 1), near * j : near * (j + 1)] = -mine
            solve_sides[cells * half : cells * (half + 1), wide * j : wide * (j + 1)] = -sides
            for side in range(0 if last else 2):
                mine, sides = np.zeros((RANK_V, near)), np.zeros((RANK_V, wide))
                if side == 0:
                    back = take_left @ by_right @ q_right
                    mine[:, cells + RANK_M : cells + 2 * RANK_M] = take_left @ center @ m_right
                    sides[:, :RANK_S] = e_left[edge]
                else:
                    back = take_right @ by_left @ q_left
                    mine[:, cells : cells + RANK_M] = take_right @ center @ m_left
                    sides[:, PAD_S : PAD_S + RANK_S] = e_right[edge]
                mine[:, :cells] = back
                sides[:, RANK_S : RANK_S + RANK_M] = back @ m_left
                sides[:, PAD_S + RANK_S : PAD_S + RANK_S + RANK_M] = back @ m_right
                top = 2 * cells + GROUP * (2 * side + half)
                solve_own[top : top + RANK_V, near * j : near * (j + 1)] = -mine
                solve_sides[top : top + RANK_V, wide * j : wide * (j + 1)] = -sides
    full = np.concatenate([own, from_left, from_right], axis=1)
    full = np.pad(full, [(0, 0), (0, GROUP - 2 * RANK_V)])
    plain, split = (own, solve_own), (slopes, full, moments, lateral, source, solve_sides)
    return [x.astype(np.float32) for x in plain] + [split_table(x.astype(np.float32)) for x in split]


def dot(a, b):
    return jnp.dot(a, b, precision=highest, preferred_element_type=jnp.float32)


def halves(x):
    high = x.astype(jnp.bfloat16)
    return high, (x - high.astype(jnp.float32)).astype(jnp.bfloat16)


def split_table(table):
    gap = -table.shape[-1] % PACK
    table = np.pad(table, [(0, 0)] * (table.ndim - 1) + [(0, gap)])
    high = table.astype(ml_dtypes.bfloat16)
    low = (table - high.astype(np.float32)).astype(ml_dtypes.bfloat16)
    return np.concatenate([high, high, low], axis=-1)


def split_dot(table, x):
    gap = -x.shape[0] % PACK
    if gap:
        x = jnp.concatenate([x, jnp.zeros((gap, x.shape[1]), x.dtype)], axis=0)
    high, low = halves(x)
    return jnp.dot(table, jnp.concatenate([high, low, high], axis=0), preferred_element_type=jnp.float32)


class Extent:
    def __init__(self, margin):
        self.margin = margin
        self.reach = margin + SWEEPS - 1
        self.breadth = ROWS + 2 * self.reach
        self.packed = self.breadth + self.breadth // 2
        self.found = ROWS + 2 * margin


FIRST, LAST = Extent(3), Extent(2)


DIFFERENCE = ((1, 2.0 / 3.0), (-1, -2.0 / 3.0), (2, -1.0 / 12.0), (-2, 1.0 / 12.0))
CURVE = ((1, 4.0 / 3.0), (-1, 4.0 / 3.0), (2, -1.0 / 12.0), (-2, -1.0 / 12.0))


def lane(r, count=1):
    return slice(r * LANES, (r + count) * LANES)


def turned(tile, step):
    return pltpu.roll(tile, (-step) % LANES, 1)


def edge_masks():
    at = lax.axis_index("cross")
    last = lax.axis_size("cross") - 1
    flag = lambda test: jnp.where(test, 1.0, 0.0).astype(jnp.float32)
    return (flag(at >= 1), flag(at >= 2), flag(at <= last - 1), flag(at <= last - 2))


def masked(tile, e, masks):
    if e < -ROWS:
        return tile * masks[1]
    if e < 0:
        return tile * masks[0]
    if e >= 2 * ROWS:
        return tile * masks[3]
    if e >= ROWS:
        return tile * masks[2]
    return tile


def first_diff(up_one, down_one, up_two, down_two):
    return (8.0 * (up_one - down_one) - (up_two - down_two)) * (1.0 / 12.0)


def second_diff(middle, up_one, down_one, up_two, down_two):
    return (16.0 * (up_one + down_one) - (up_two + down_two) - 30.0 * middle) * (1.0 / 12.0)


def stream_slope(tile):
    return first_diff(turned(tile, 1), turned(tile, -1), turned(tile, 2), turned(tile, -2))


def open_kernel(
    cells, velocity, viscosity, moments, flat, thick, to_right, to_left, upward, downward, weights, sems
):
    copies = [pltpu.make_async_copy(moments, weights, sems.at[0])]
    for c in range(3):
        rows = slice(cells * c, cells * (c + 1))
        for r in range(ROWS):
            copies.append(
                pltpu.make_async_copy(velocity.at[c, :, r, :], flat.at[rows, lane(r)], sems.at[len(copies)])
            )
    for r in range(ROWS):
        copies.append(pltpu.make_async_copy(viscosity.at[:, r, :], thick.at[:, lane(r)], sems.at[len(copies)]))
    for copy in copies[1:] + copies[:1]:
        copy.start()
    copies[0].wait()
    both = None
    for c in range(3):
        for copy in copies[1 + ROWS * c : 1 + ROWS * (c + 1)]:
            copy.wait()
        rows = slice(cells * c, cells * (c + 1))
        for k in range(2):
            slot(upward, cells, 2 * c + k)[...] = flat[rows, lane(2 + k)]
            slot(downward, cells, 2 * c + k)[...] = flat[rows, lane(k)]
        part = split_dot(weights[c], flat[rows, :])
        both = part if both is None else both + part
    to_right[...] = both[:PAD_V]
    to_left[...] = both[PAD_V:]
    for copy in copies[1 + 3 * ROWS :]:
        copy.wait()
    slot(upward, cells, 6)[...] = thick[:, lane(ROWS - 1)]
    slot(downward, cells, 6)[...] = thick[:, lane(0)]


def weighed(weights, value_at, r, home):
    total = None
    for reach, factor in weights:
        if (0 <= r + reach < ROWS) == home:
            part = factor * value_at(r + reach)
            total = part if total is None else total + part
    return total


def rough_kernel(cells, flat, thick, own, rough):
    for c in range(3):
        rows = slice(cells * c, cells * (c + 1))
        at = lambda r: flat[rows, lane(r)]
        spanned = dot(own[...], flat[rows, :])
        for r in range(ROWS):
            here = at(r)
            up_one, down_one = turned(here, 1), turned(here, -1)
            up_two, down_two = turned(here, 2), turned(here, -2)
            carried = (
                flat[:cells, lane(r)] * first_diff(up_one, down_one, up_two, down_two)
                + flat[cells : 2 * cells, lane(r)] * weighed(DIFFERENCE, at, r, True)
                + flat[2 * cells :, lane(r)] * spanned[:cells, lane(r)]
            )
            spread = (
                (4.0 / 3.0) * (up_one + down_one)
                - (1.0 / 12.0) * (up_two + down_two)
                - 5.0 * here
                + weighed(CURVE, at, r, True)
                + spanned[cells:, lane(r)]
            )
            rough[rows, lane(r)] = here + time_step * (thick[:, lane(r)] * spread - carried)


def add_beyond(cells, rough, flat, thick, left, right, low, high, slopes, section):
    masks = edge_masks()
    sides = jnp.concatenate([left[...], right[...]], axis=0)
    for c in range(3):
        rows = slice(cells * c, cells * (c + 1))
        spanned = split_dot(slopes[c], sides)

        def beyond(r):
            if r < 0:
                return masked(slot(low, cells, 2 * c + r + 2)[...], r, masks)
            return masked(slot(high, cells, 2 * c + r - ROWS)[...], r, masks)

        for r in range(ROWS):
            spread = spanned[cells:, lane(r)] + weighed(CURVE, beyond, r, False)
            carried = flat[cells : 2 * cells, lane(r)] * weighed(DIFFERENCE, beyond, r, False)
            carried = carried + flat[2 * cells :, lane(r)] * spanned[:cells, lane(r)]
            section[rows, lane(r)] = rough[rows, lane(r)] + time_step * (thick[:, lane(r)] * spread - carried)


def slot(ref, cells, k):
    return ref.at[cells * k : cells * (k + 1), :]


def fill_slots(ref, cells, blocks, moments):
    for k, block in enumerate(blocks):
        slot(ref, cells, k)[...] = block
    for k, block in enumerate(moments):
        top = cells * len(blocks) + PAD_M * k
        ref[top : top + PAD_M, :] = block


def own_source(cells, section, lateral, parts, owed={}):
    side = split_dot(lateral[...], section[2 * cells :, :])
    at = lambda r: section[cells : 2 * cells, lane(r)]
    blocks = []
    for r in range(ROWS):
        total = stream_slope(section[:cells, lane(r)]) + side[:cells, lane(r)] + weighed(DIFFERENCE, at, r, True)
        for reach, factor in DIFFERENCE:
            if r + reach in owed:
                total = total + factor * owed[r + reach]
        parts[:cells, lane(r)] = total
        blocks.append(total)
    parts[cells:, :] = side[cells:]
    moments = [side[cells:, lane(r)] for r in range(ROWS)]
    up = (2.0 / 3.0) * at(0) - (1.0 / 12.0) * at(1)
    down = (1.0 / 12.0) * at(ROWS - 2) - (2.0 / 3.0) * at(ROWS - 1)
    return blocks, moments, at, up, down


def tendency_kernel(
    cells, rough, flat, thick, left, right, low, high, slopes, lateral,
    section, parts, up_near, down_near, up_far, down_far,
):
    add_beyond(cells, rough, flat, thick, left, right, low, high, slopes, section)
    blocks, moments, at, _, _ = own_source(cells, section, lateral, parts)
    row = lambda c, r: section[cells * c : cells * (c + 1), lane(r)]
    every = [at(r) for r in range(ROWS)]
    for near, far, outer, inner in ((up_near, up_far, 0, 2), (down_near, down_far, 2, 0)):
        side = [row(c, inner + k) for c in (0, 2) for k in range(2)]
        fill_slots(near, cells, blocks[outer : outer + 2] + every + side, moments[outer : outer + 2])
        fill_slots(far, cells, blocks[inner : inner + 2] + [at(inner), at(inner + 1)], moments[inner : inner + 2])


WHOLE = (-2, -1, ROWS, ROWS + 1)


def row_across(cells, section, arrived):
    low_one, high_one, low_two, high_two = arrived
    masks = edge_masks()

    def value(e):
        if 0 <= e < ROWS:
            return section[cells : 2 * cells, lane(e)]
        if e < -ROWS or e >= 2 * ROWS:
            ref, k = (low_two, e + 8) if e < 0 else (high_two, e - 6)
        else:
            ref, k = (low_one, e + 6) if e < 0 else (high_one, e - 2)
        return masked(slot(ref, cells, k)[...], e, masks)

    return value


def near_source_kernel(cells, parts, section, low_one, high_one, lateral, moments, middle, held):
    masks = edge_masks()
    across = row_across(cells, section, (low_one, high_one, None, None))
    pick = lambda ref, k: slot(ref, cells, k)[...]
    given = [(low_one if e < 0 else high_one, e % 2) for e in WHOLE]
    beside = split_dot(lateral[...], jnp.concatenate([pick(ref, 8 + k) for ref, k in given], axis=1))
    for e in range(-2, ROWS + 2):
        if e in WHOLE:
            at = WHOLE.index(e)
            ref, k = given[at]
            total = stream_slope(pick(ref, 6 + k)) + beside[:cells, lane(at)]
            side = beside[cells:, lane(at)]
        else:
            total, side = parts[:cells, lane(e)], parts[cells:, lane(e)]
        for reach, factor in DIFFERENCE:
            if e in WHOLE or not 0 <= e + reach < ROWS:
                total = total + factor * across(e + reach)
        middle[:cells, lane(e + 2)] = masked(total, e, masks)
        middle[cells:, lane(e + 2)] = masked(side, e, masks)
    held[...] = sum(split_dot(moments[c], section[cells * c : cells * (c + 1), :]) for c in range(3))


def first_source(cells, middle, arrived, ext):
    low_one, high_one, low_two, high_two = arrived
    masks = edge_masks()
    across = row_across(cells, None, arrived)
    ext[:, lane(FIRST.reach - 2, ROWS + 4)] = middle[...]
    for e in range(-FIRST.reach, ROWS + FIRST.reach):
        if -2 <= e < ROWS + 2:
            continue
        far = e < -ROWS or e >= 2 * ROWS
        ref = (low_two if e < 0 else high_two) if far else (low_one if e < 0 else high_one)
        top = (4 if far else 10) * cells + PAD_M * (e % 2)
        total, side = slot(ref, cells, e % 2)[...], ref[top : top + PAD_M, :]
        for reach, factor in DIFFERENCE:
            if (e + reach) // ROWS != e // ROWS:
                total = total + factor * across(e + reach)
        ext[:cells, lane(e + FIRST.reach)] = masked(total, e, masks)
        ext[cells:, lane(e + FIRST.reach)] = masked(side, e, masks)


def last_source(cells, parts, section, arrived, extra, ext):
    low_one, high_one, low_two, high_two = arrived
    masks = edge_masks()
    span, tail = slice(0, cells), slice(cells, cells + PAD_M)
    pick = lambda ref, k: slot(ref, cells, k)[...]

    def joined(e):
        if 0 <= e < ROWS:
            return parts[span, lane(e)], parts[tail, lane(e)]
        if e < -ROWS or e >= 2 * ROWS:
            ref = low_two if e < 0 else high_two
            return pick(ref, 0), ref[4 * cells :, :]
        ref, k = (low_one, e + ROWS) if e < 0 else (high_one, e - ROWS)
        top = 8 * cells + PAD_M * k
        return pick(ref, k), ref[top : top + PAD_M, :]

    def across(e, home):
        if e // ROWS == home // ROWS or home // ROWS in (-2, 2):
            return None
        if e < -ROWS:
            return masked(pick(low_two, 1 + e + ROWS + 2), e, masks)
        if e < 0:
            return masked(pick(low_one, ROWS + e + 2), e, masks)
        if e < ROWS:
            return section[cells : 2 * cells, lane(e)]
        if e < 2 * ROWS:
            return masked(pick(high_one, e), e, masks)
        return masked(pick(high_two, 1 + e - 2 * ROWS), e, masks)

    for e in range(-LAST.reach, ROWS + LAST.reach):
        total, side = joined(e)
        if e == -ROWS - 1:
            total = total + pick(low_one, 6)
        if e == 2 * ROWS:
            total = total + pick(high_one, 6)
        for reach, factor in DIFFERENCE:
            other = across(e + reach, e)
            if other is not None:
                total = total + factor * other
            if e + reach in extra and (e + reach) // ROWS == e // ROWS:
                total = total + factor * extra[e + reach]
        ext[span, lane(e + LAST.reach)] = masked(total, e, masks)
        ext[tail, lane(e + LAST.reach)] = masked(side, e, masks)


def pack_moments(extent, both, to_right, to_left):
    for side, out in enumerate((to_right, to_left)):
        top = 4 * GROUP * side
        out[:, lane(0, extent.breadth)] = both[top : top + 8]
        for k in range(extent.breadth // 2):
            out[:, lane(extent.breadth + k)] = (
                both[top + 8 : top + 16, lane(2 * k)] + both[top + 16 : top + 24, lane(2 * k + 1)]
            )


def source_kernel(
    cells, middle, held, low_one, high_one, low_two, high_two, source, ext, to_right, to_left
):
    first_source(cells, middle, (low_one, high_one, low_two, high_two), ext)
    both = split_dot(source[...], ext[...])
    pack_moments(FIRST, both, to_right, to_left)
    for side, out in enumerate((to_right, to_left)):
        top, base = 4 * GROUP * side, PAD_V * side
        out[:, lane(FIRST.packed, ROWS)] = held[base : base + 8]
        out[:, lane(FIRST.packed + ROWS, 3)] = jnp.zeros((GROUP, 3 * LANES), jnp.float32)
        for e in range(FIRST.breadth + ROWS):
            value = (
                both[top + 24 : top + 25, lane(e)]
                if e < FIRST.breadth
                else held[base + 8 : base + 9, lane(e - FIRST.breadth)]
            )
            row, tile = e % GROUP, FIRST.packed + ROWS + e // GROUP
            out[row : row + 1, lane(tile)] = value


def last_source_kernel(
    cells, parts, section, debts, low_one, high_one, low_two, high_two, source,
    ext, fixed, to_right, to_left,
):
    masks = edge_masks()
    pick = lambda ref, k: slot(ref, cells, k)[...]
    extra = {
        0: pick(low_one, 7) * masks[0],
        ROWS - 1: pick(high_one, 7) * masks[2],
        -1: pick(debts, 0),
        ROWS: pick(debts, 1),
        -ROWS: pick(low_two, 3) * masks[1],
        2 * ROWS - 1: pick(high_two, 3) * masks[3],
    }
    fixed[:cells, :] = extra[0]
    fixed[cells:, :] = extra[ROWS - 1]
    last_source(cells, parts, section, (low_one, high_one, low_two, high_two), extra, ext)
    pack_moments(LAST, split_dot(source[...], ext[...]), to_right, to_left)


def climb(extent, levels, depth):
    masks = edge_masks()
    for j in range(1, SWEEPS):
        before = slice(depth * (j - 1), depth * j)
        after = slice(depth * j, depth * (j + 1))
        for e in range(-extent.reach + j, ROWS + extent.reach - j):
            k = e + extent.reach
            here = levels[before, lane(k)]
            beside = (
                turned(here, 1) + turned(here, -1) + levels[before, lane(k + 1)] + levels[before, lane(k - 1)]
            )
            levels[after, lane(k)] = masked(beside, e, masks)
    return levels[:, lane(SWEEPS - 1, extent.found)]


def home_kernel(extent, ext, solve, partial, levels):
    depth = ext.shape[0]
    levels[:depth, :] = ext[...]
    partial[...] = dot(solve[...], climb(extent, levels, depth))


def spare(given, e):
    row, tile = e % GROUP, FIRST.packed + ROWS + e // GROUP
    return given[row : row + 1, lane(tile)]


def finish(extent, partial, left, right, solve, levels):
    for side, given in enumerate((left, right)):
        top = PAD_S * side
        levels[top : top + 8, :] = given[:, lane(0, extent.breadth)]
        for e in range(extent.breadth):
            tile = given[:, lane(extent.breadth + e // 2)]
            levels[top + 8 : top + 16, lane(e)] = pltpu.roll(tile, 4, 0) if e % 2 else tile
            if extent is FIRST:
                levels[top + 12 : top + 13, lane(e)] = spare(given, e)
    return partial[...] + split_dot(solve[...], climb(extent, levels, 2 * PAD_S))


def gradient(extent, found, c, rows, slope_rows, r):
    masks = edge_masks()
    phi = lambda r: masked(found[rows, lane(r + extent.margin)], r, masks)
    if c == 0:
        return stream_slope(phi(r))
    if c == 1:
        inside = lambda r: -extent.margin <= r < ROWS + extent.margin
        return sum(factor * phi(r + reach) for reach, factor in DIFFERENCE if inside(r + reach))
    return found[slope_rows, lane(r + extent.margin)]


def middle_kernel(
    cells, partial, left, right, section, solve, low_one, high_one, low, high, start, thick, full, lateral,
    following, parts, debts, up_near, down_near, up_far, down_far, levels, flat, rim, sides,
):
    masks = edge_masks()
    found = finish(FIRST, partial, left, right, solve, levels)
    home, home_slope = slice(0, cells), slice(cells, 2 * cells)
    outer = (-2, -1, ROWS, ROWS + 1)
    for c in range(3):
        rows = slice(cells * c, cells * (c + 1))
        for r in range(ROWS):
            flat[rows, lane(r)] = section[rows, lane(r)] - gradient(FIRST, found, c, home, home_slope, r)
        for k, r in enumerate(outer):
            first = (6, 4 if r < 0 else 2, 8)[c]
            value = slot(low_one if r < 0 else high_one, cells, first + k % 2)[...]
            value = value - gradient(FIRST, found, c, home, home_slope, r)
            rim[rows, lane(k)] = masked(value, r, masks)
    sides[...] = jnp.zeros(sides.shape, jnp.float32)
    for side, given in enumerate((left, right)):
        top = 2 * cells + 2 * GROUP * side
        phi_rows, slope_rows = slice(top, top + GROUP), slice(top + GROUP, top + 2 * GROUP)
        for r in range(ROWS):
            for c in range(3):
                change = gradient(FIRST, found, c, phi_rows, slope_rows, r)
                base = GROUP * c + RANK_V * side
                count = min(RANK_V, GROUP - RANK_V * c)
                held = given[RANK_V * c : RANK_V * c + count, lane(FIRST.packed + r)]
                sides[base : base + count, lane(r)] = held - change[:count]
                if count < RANK_V:
                    held = spare(given, FIRST.breadth + r)
                    sides[base + count : base + RANK_V, lane(r)] = held - change[count:RANK_V]

    def tile(c, r):
        rows = slice(cells * c, cells * (c + 1))
        return flat[rows, lane(r)] if 0 <= r < ROWS else rim[rows, lane(r + 2 if r < 0 else r - 2)]

    for c in range(3):
        rows = slice(cells * c, cells * (c + 1))
        spanned = split_dot(
            full[...], jnp.concatenate([flat[rows, :], sides[GROUP * c : GROUP * (c + 1), :]], axis=0)
        )
        for r in range(ROWS):
            here = tile(c, r)
            up_one, down_one = turned(here, 1), turned(here, -1)
            up_two, down_two = turned(here, 2), turned(here, -2)
            carried = (
                tile(0, r) * first_diff(up_one, down_one, up_two, down_two)
                + tile(1, r) * sum(factor * tile(c, r + reach) for reach, factor in DIFFERENCE)
                + tile(2, r) * spanned[:cells, lane(r)]
            )
            spread = (
                (4.0 / 3.0) * (up_one + down_one)
                - (1.0 / 12.0) * (up_two + down_two)
                - 5.0 * here
                + sum(factor * tile(c, r + reach) for reach, factor in CURVE)
                + spanned[cells:, lane(r)]
            )
            moved = here + time_step * (thick[:, lane(r)] * spread - carried)
            following[rows, lane(r)] = 0.5 * start[rows, lane(r)] + 0.5 * moved
    phi = lambda r: found[:cells, lane(r + FIRST.margin)]
    scale = 0.5 * time_step / 144.0
    owed = {
        -1: scale * (tile(1, -1) - slot(low, cells, 6)[...]) * phi(ROWS - 1) * masks[0],
        ROWS: scale * (tile(1, ROWS) + slot(high, cells, 6)[...]) * phi(0) * masks[2],
    }
    slot(debts, cells, 0)[...] = owed[-1]
    slot(debts, cells, 1)[...] = owed[ROWS]
    blocks, moments, at, up, down = own_source(cells, following, lateral, parts, owed)
    fill_slots(up_near, cells, blocks + [at(2), at(3), up, owed[ROWS]], moments)
    fill_slots(down_near, cells, blocks + [at(0), at(1), down, owed[-1]], moments)
    fill_slots(up_far, cells, [blocks[3], at(2), at(3), owed[ROWS]], moments[3:])
    fill_slots(down_far, cells, [blocks[0], at(0), at(1), owed[-1]], moments[:1])


def last_kernel(cells, partial, left, right, section, fixed, solve, out, levels, staged, sems):
    found = finish(LAST, partial, left, right, solve, levels)
    copies = []
    for c in (2, 0, 1):
        rows = slice(cells * c, cells * (c + 1))
        for r in range(ROWS):
            value = section[rows, lane(r)]
            if c == 1 and r in (0, ROWS - 1):
                value = value + fixed[cells * (r > 0) : cells * (1 + (r > 0)), :]
            value = value - gradient(LAST, found, c, slice(0, cells), slice(cells, 2 * cells), r)
            staged[rows, lane(r)] = value
            copies.append(
                pltpu.make_async_copy(staged.at[rows, lane(r)], out.at[c, :, r, :], sems.at[len(copies)])
            )
            copies[-1].start()
    for copy in copies:
        copy.wait()


def call(body, shapes, *args, scratch=(), **options):
    return pl.pallas_call(
        body,
        out_shape=[jax.ShapeDtypeStruct(s, jnp.float32) for s in shapes],
        scratch_shapes=scratch,
        compiler_params=pltpu.CompilerParams(vmem_limit_bytes=40 * 1024 * 1024),
        **options,
    )(*args)


def shifted(block, axis, step):
    count = lax.axis_size(axis)
    return lax.ppermute(block, axis, [(i, (i + step) % count) for i in range(count)])


def per_device(velocity, viscosity):
    components, cells, row_cells, columns = velocity.shape
    length = cells * lax.axis_size("span")
    own, first_own, slopes, full, moments, lateral, *first = (
        jnp.asarray(t) for t in tables(length, cells, False)
    )
    _, last_own, _, _, _, _, *last = (jnp.asarray(t) for t in tables(length, cells, True))
    width = row_cells * columns
    near = cells + PAD_M
    whole, edge, rim = (components * cells, width), (PAD_V, width), (7 * cells, columns)

    def across(up_near, down_near, up_far, down_far):
        return (
            shifted(up_near, "cross", 1), shifted(down_near, "cross", -1),
            shifted(up_far, "cross", 2), shifted(down_far, "cross", -2),
        )

    def message(near_slots, near_rows, far_slots, far_rows):
        near_shape = (near_slots * cells + near_rows * PAD_M, columns)
        far_shape = (far_slots * cells + far_rows * PAD_M, columns)
        return [near_shape] * 2 + [far_shape] * 2

    def levels(extent, depth):
        return pltpu.VMEM((SWEEPS * depth, extent.breadth * columns), jnp.float32)

    start, thick, to_right, to_left, upward, downward = call(
        functools.partial(open_kernel, cells),
        [whole, (cells, width), edge, edge, rim, rim],
        *(pltpu.with_memory_space_constraint(x, pltpu.HBM) for x in (velocity, viscosity, moments)),
        in_specs=[pl.BlockSpec(memory_space=pltpu.HBM)] * 3,
        scratch=[pltpu.VMEM(moments.shape, moments.dtype), pltpu.SemaphoreType.DMA((1 + 4 * ROWS,))],
    )
    left = shifted(to_right, "span", 1)
    right = shifted(to_left, "span", -1)
    low = shifted(upward, "cross", 1)
    high = shifted(downward, "cross", -1)
    (rough,) = call(functools.partial(rough_kernel, cells), [whole], start, thick, own)
    section, parts, *sent = call(
        functools.partial(tendency_kernel, cells),
        [whole, (near, width)] + message(10, 2, 4, 2),
        rough, start, thick, left, right, low, high, slopes, lateral,
    )
    arrived = across(*sent)
    middle, held = call(
        functools.partial(near_source_kernel, cells),
        [(near, 2 * width), (2 * PAD_V, width)],
        parts, section, *arrived[:2], lateral, moments,
    )
    ext, to_right, to_left = call(
        functools.partial(source_kernel, cells),
        [(near, FIRST.breadth * columns)] + [(GROUP, (FIRST.packed + ROWS + 3) * columns)] * 2,
        middle, held, *arrived, first[0],
    )
    left = shifted(to_right, "span", 1)
    right = shifted(to_left, "span", -1)
    (partial,) = call(
        functools.partial(home_kernel, FIRST),
        [(first_own.shape[0], FIRST.found * columns)],
        ext, first_own,
        scratch=[levels(FIRST, near)],
    )

    section, parts, debts, *sent = call(
        functools.partial(middle_kernel, cells),
        [whole, (near, width), (2 * cells, columns)] + message(8, 4, 4, 1),
        partial, left, right, section, first[1], *arrived[:2], low, high, start, thick, full, lateral,
        scratch=[
            levels(FIRST, 2 * PAD_S),
            pltpu.VMEM(whole, jnp.float32),
            pltpu.VMEM((components * cells, 4 * columns), jnp.float32),
            pltpu.VMEM((components * GROUP, width), jnp.float32),
        ],
    )
    arrived = across(*sent)
    ext, fixed, to_right, to_left = call(
        functools.partial(last_source_kernel, cells),
        [(near, LAST.breadth * columns), (2 * cells, columns)] + [(GROUP, LAST.packed * columns)] * 2,
        parts, section, debts, *arrived, last[0],
    )
    left = shifted(to_right, "span", 1)
    right = shifted(to_left, "span", -1)
    (partial,) = call(
        functools.partial(home_kernel, LAST),
        [(last_own.shape[0], LAST.found * columns)],
        ext, last_own,
        scratch=[levels(LAST, near)],
    )
    (out,) = call(
        functools.partial(last_kernel, cells),
        [velocity.shape],
        partial, left, right, section, fixed, last[1],
        scratch=[
            levels(LAST, 2 * PAD_S),
            pltpu.VMEM(whole, jnp.float32),
            pltpu.SemaphoreType.DMA((3 * ROWS,)),
        ],
        out_specs=[pl.BlockSpec(memory_space=pltpu.HBM)],
    )
    return out


def solution(mesh):
    in_specs = (P(None, "span", "cross", None), P("span", "cross", None))
    out_specs = P(None, "span", "cross", None)
    return jax.shard_map(
        per_device, mesh=mesh, in_specs=in_specs, out_specs=out_specs, check_vma=False
    )
```
